32 devices in a mesh: rep: 8 (over y, x, core), fsdp: 4 (over z).
Axes of the slice: x: 2, y: 2, z: 4, core: 2. Of those that a mesh axis runs over, the one named last changes fastest.
Arguments:
- tokens: bfloat16 [16384, 960], P(('rep', 'fsdp')), may hold values from -6 to 6
- sequence_ids: int32 [16384], P(('rep', 'fsdp')), may hold values from 0 to 7, as said below
- cotangent: bfloat16 [16384, 960], P(('rep', 'fsdp')), may hold values from -6 to 6
- norm_gains: float32 [2, 960], P(None, 'fsdp'), may hold values from 0.5 to 1.5
- qkv_weight: float32 [960, 1600], P('fsdp'), as said below
- out_weight: float32 [960, 960], P('fsdp'), may hold values from -0.5 to 0.5
- gate_up_weight: float32 [960, 5120], P('fsdp'), may hold values from -0.1875 to 0.1875
- down_weight: float32 [2560, 960], P('fsdp'), may hold values from -0.125 to 0.125
- gains_first: float32 [2, 960], P(None, 'fsdp'), may hold values from -40 to 40
- qkv_first: float32 [960, 1600], P('fsdp'), may hold values from -40 to 40
- out_first: float32 [960, 960], P('fsdp'), may hold values from -40 to 40
- gate_up_first: float32 [960, 5120], P('fsdp'), may hold values from -40 to 40
- down_first: float32 [2560, 960], P('fsdp'), may hold values from -40 to 40
- gains_second: float32 [2, 960], P(None, 'fsdp'), may hold values from 32.768 to 491.52
- qkv_second: float32 [960, 1600], P('fsdp'), may hold values from 32.768 to 491.52
- out_second: float32 [960, 960], P('fsdp'), may hold values from 32.768 to 491.52
- gate_up_second: float32 [960, 5120], P('fsdp'), may hold values from 32.768 to 491.52
- down_second: float32 [2560, 960], P('fsdp'), may hold values from 32.768 to 491.52
Outputs:
- block_out: bfloat16 [16384, 960], P(('rep', 'fsdp'))
- tokens_grad: bfloat16 [16384, 960], P(('rep', 'fsdp'))
- gains_grad: float32 [2, 960], P(None, 'fsdp')
- qkv_grad: float32 [960, 1600], P('fsdp')
- out_grad: float32 [960, 960], P('fsdp')
- gate_up_grad: float32 [960, 5120], P('fsdp')
- down_grad: float32 [2560, 960], P('fsdp')
- gains_delta: float32 [2, 960], P(None, 'fsdp')
- qkv_delta: float32 [960, 1600], P('fsdp')
- out_delta: float32 [960, 960], P('fsdp')
- gate_up_delta: float32 [960, 5120], P('fsdp')
- down_delta: float32 [2560, 960], P('fsdp')
- gains_first_new: float32 [2, 960], P(None, 'fsdp')
- qkv_first_new: float32 [960, 1600], P('fsdp')
- out_first_new: float32 [960, 960], P('fsdp')
- gate_up_first_new: float32 [960, 5120], P('fsdp')
- down_first_new: float32 [2560, 960], P('fsdp')
- gains_second_new: float32 [2, 960], P(None, 'fsdp')
- qkv_second_new: float32 [960, 1600], P('fsdp')
- out_second_new: float32 [960, 960], P('fsdp')
- gate_up_second_new: float32 [960, 5120], P('fsdp')
- down_second_new: float32 [2560, 960], P('fsdp')
The draws below stay inside these ranges and needn't reach their ends.
Inputs may be any that keep to these rules, and one draw needn't show every extreme that they name: `sequence_ids`: along each device's 512 tokens the numbers start at 0 and never fall; some device holds a single sequence of 512 tokens, and some device holds 8 sequences of 64 tokens each. `qkv_weight`: float32 weights.
All inputs are finite; a program needn't handle non-finite values.
Results may differ from the reference program's by a relative error of at most 0.022.
The reference program's roundings to bfloat16 on the way count: a program that leaves them out, or rounds other values in their place, can miss the bound.
Values may be sent and summed in bfloat16 or wider, within the bound.
A program may use at most 256 MiB of HBM per device.

```python
import math
import jax
import jax.numpy as jnp
from jax import lax

D = 960
HEADS = 15
KV_HEADS = 5
HEAD = 64
FF = 2560
ROWS_DEV = 512
STEP = 4
QKV = 1600
TOKENS = 16384
N_REP = 8
N_FSDP = 4


def draw_sequence_ids(key, part):
    buffer_count = TOKENS // ROWS_DEV
    key_level, key_cut, key_full = jax.random.split(key, 3)
    level_draw = jax.random.randint(key_level, (buffer_count, 1), 0, 4)
    full_index = jax.random.randint(key_full, (), 0, buffer_count)
    split_index = (full_index + 1) % buffer_count
    rate_table = jnp.array([0, 1, 2, 4], dtype=jnp.int32)
    cut_rate = rate_table[level_draw]
    buffer_index = jnp.arange(buffer_count, dtype=jnp.int32)[:, None]
    cut_rate = jnp.where((buffer_index == full_index) | (buffer_index == split_index), 0, cut_rate)
    cut_draw = jax.random.randint(key_cut, (buffer_count, ROWS_DEV), 0, 256)
    row_index = jnp.arange(ROWS_DEV, dtype=jnp.int32)[None, :]
    even_start = (buffer_index == split_index) & (row_index % (ROWS_DEV // 8) == 0)
    is_start = ((cut_draw < cut_rate) | even_start) & (row_index > 0)
    sequence_ids = jnp.minimum(jnp.cumsum(is_start.astype(jnp.int32), axis=1), 7)
    return sequence_ids.reshape(-1).astype(jnp.int32)


def draw_qkv_weight(key, part):
    total_width = D + 2 * KV_HEADS * HEAD
    base_draw = jax.random.normal(key, (D, total_width), jnp.float32) * (1.0 / math.sqrt(D))
    return base_draw


def level_of(own_key, extent, cuts, least, largest):
    def one(dim, blocks):
        steps = jax.random.uniform(jax.random.fold_in(jax.random.fold_in(own_key, 6), dim), (blocks,), jnp.float32, least / len(cuts), largest / len(cuts))
        return jnp.repeat(jnp.exp(steps), extent[dim] // blocks).reshape((-1,) + (1,) * (len(extent) - dim - 1))

    loudness = one(*cuts[0])
    for cut in cuts[1:]:
        loudness = loudness * one(*cut)
    return loudness


def centred(rng, shape, scale, limit, shards=(), kind=jnp.bfloat16):
    drawn = jax.random.normal(rng, shape, jnp.float32) * scale
    if len(shards) > 0:
        drawn = level_of(rng, shape, shards, -0.22, 0.18) * drawn
    return jnp.clip(drawn, min=-limit, max=limit).astype(kind)


def setup_inputs(seed: int = 0) -> dict:
    key_list = jax.random.split(jax.random.key(seed), 19)
    tokens = centred(key_list[0], (TOKENS, D), 1.0, 6.0, ((0, 32),))
    sequence_ids = draw_sequence_ids(jax.random.fold_in(key_list[18], 71), 0)
    cotangent = centred(key_list[2], (TOKENS, D), 1.0, 6.0, ((0, 32),))
    norm_gains = jnp.clip(1.0 + 0.1 * jax.random.normal(key_list[3], (2, D), jnp.float32), 0.5, 1.5)
    qkv_weight = draw_qkv_weight(jax.random.fold_in(key_list[18], 71), 0)
    out_weight = centred(key_list[5], (D, D), (D // 8) ** -0.5, 0.5, ((0, 4),), jnp.float32)
    gate_up_weight = centred(key_list[6], (D, 2 * FF), D ** -0.5, 0.1875, ((0, 4),), jnp.float32)
    down_weight = centred(key_list[7], (FF, D), FF ** -0.5, 0.125, ((0, 4),), jnp.float32)
    gains_first = centred(key_list[8], (2, D), (0.05 * TOKENS ** 0.5), 40.0, ((1, 4),), jnp.float32)
    qkv_first = centred(key_list[9], (D, QKV), (0.05 * TOKENS ** 0.5), 40.0, ((0, 4),), jnp.float32)
    out_first = centred(key_list[10], (D, D), (0.05 * TOKENS ** 0.5), 40.0, ((0, 4),), jnp.float32)
    gate_up_first = centred(key_list[11], (D, 2 * FF), (0.05 * TOKENS ** 0.5), 40.0, ((0, 4),), jnp.float32)
    down_first = centred(key_list[12], (FF, D), (0.05 * TOKENS ** 0.5), 40.0, ((0, 4),), jnp.float32)
    gains_second = jnp.clip(jnp.exp(math.log(491.52) - 2.70805 * jax.random.uniform(key_list[13], (2, D), jnp.float32) ** level_of(key_list[13], (2, D), ((1, 4),), -0.2, 0.2)), 32.768, 491.52)
    qkv_second = jnp.clip(jnp.exp(math.log(491.52) - 2.70805 * jax.random.uniform(key_list[14], (D, QKV), jnp.float32) ** level_of(key_list[14], (D, QKV), ((0, 4),), -0.2, 0.2)), 32.768, 491.52)
    out_second = jnp.clip(jnp.exp(math.log(491.52) - 2.70805 * jax.random.uniform(key_list[15], (D, D), jnp.float32) ** level_of(key_list[15], (D, D), ((0, 4),), -0.2, 0.2)), 32.768, 491.52)
    gate_up_second = jnp.clip(jnp.exp(math.log(491.52) - 2.70805 * jax.random.uniform(key_list[16], (D, 2 * FF), jnp.float32) ** level_of(key_list[16], (D, 2 * FF), ((0, 4),), -0.2, 0.2)), 32.768, 491.52)
    down_second = jnp.clip(jnp.exp(math.log(491.52) - 2.70805 * jax.random.uniform(key_list[17], (FF, D), jnp.float32) ** level_of(key_list[17], (FF, D), ((0, 4),), -0.2, 0.2)), 32.768, 491.52)
    return {"tokens": tokens, "sequence_ids": sequence_ids, "cotangent": cotangent, "norm_gains": norm_gains, "qkv_weight": qkv_weight, "out_weight": out_weight, "gate_up_weight": gate_up_weight, "down_weight": down_weight, "gains_first": gains_first, "qkv_first": qkv_first, "out_first": out_first, "gate_up_first": gate_up_first, "down_first": down_first, "gains_second": gains_second, "qkv_second": qkv_second, "out_second": out_second, "gate_up_second": gate_up_second, "down_second": down_second}


NORM_EPS = 1e-05
ROPE_BASE = 100000.0
LEARN_RATE = 0.03
BETA_ONE = 0.9
BETA_TWO = 0.95
ADAM_EPS = 1e-08
DECAY_RATE = 0.1
NEG_LARGE = -1e+30
PRECISE = lax.Precision.HIGHEST

@jax.custom_vjp
def low(v):
    return lax.optimization_barrier(v.astype(jnp.bfloat16)).astype(jnp.float32)

@jax.custom_vjp
def low_back(v):
    return v

def low_keep(v):
    return (low(v), None)

def low_pass(kept, grad):
    return (grad,)

def back_keep(v):
    return (v, None)

def back_low(kept, grad):
    return (low(grad),)
low.defvjp(low_keep, low_pass)
low_back.defvjp(back_keep, back_low)

def positions(sequence_ids):
    row_index = jnp.arange(sequence_ids.shape[0], dtype=jnp.int32)
    prior_ids = jnp.concatenate([jnp.full((1,), -1, jnp.int32), sequence_ids[:-1].astype(jnp.int32)])
    seq_starts = jnp.where(sequence_ids != prior_ids, row_index, 0)
    first_row = lax.cummax(seq_starts, axis=0)
    return (row_index - first_row).astype(jnp.float32)

def causal_mask(sequence_ids):
    row_index = jnp.arange(sequence_ids.shape[0], dtype=jnp.int32)
    return (sequence_ids[:, None] == sequence_ids[None, :]) & (row_index[None, :] <= row_index[:, None])

def rope_tables(places):
    half_size = HEAD // 2
    freq_table = ROPE_BASE ** (-2.0 * jnp.arange(half_size, dtype=jnp.float32) / HEAD)
    angles = places[:, None] * freq_table[None, :]
    return (jnp.cos(angles), jnp.sin(angles))

def rotate(vectors, cosine_table, sine_table):
    half_size = vectors.shape[-1] // 2
    first_half = vectors[..., :half_size]
    second_half = vectors[..., half_size:]
    cosine_wide = cosine_table[:, None, :]
    sine_wide = sine_table[:, None, :]
    return jnp.concatenate([first_half * cosine_wide - second_half * sine_wide, second_half * cosine_wide + first_half * sine_wide], axis=-1)

def rms_norm(values, gain_row):
    row_scale = lax.rsqrt(lax.optimization_barrier(jnp.mean(values * values, axis=-1, keepdims=True)) + NORM_EPS)
    return values * row_scale * gain_row

def swiglu(gate_part, up_part):
    return gate_part * jax.nn.sigmoid(gate_part) * up_part

def adamw_update(weight, moment_one, moment_two, gradient, decay_rate):
    first_new = BETA_ONE * moment_one + (1.0 - BETA_ONE) * gradient
    second_new = BETA_TWO * moment_two + (1.0 - BETA_TWO) * gradient * gradient
    fix_one = 1.0 - BETA_ONE ** STEP
    fix_two = 1.0 - BETA_TWO ** STEP
    update_dir = first_new / fix_one / (jnp.sqrt(second_new / fix_two) + ADAM_EPS) + decay_rate * weight
    return (-LEARN_RATE * update_dir, first_new, second_new)

def block_layer(inputs, sequence_ids, norm_gains, qkv_weight, out_weight, gate_up_weight, down_weight):
    count_rows = inputs.shape[0]
    kv_width = KV_HEADS * HEAD
    group_size = HEADS // KV_HEADS
    scale_factor = 1.0 / math.sqrt(HEAD)
    gain_rows = low(norm_gains)
    qkv_low = low(qkv_weight)
    out_low = low(out_weight)
    gate_up_low = low(gate_up_weight)
    down_low = low(down_weight)
    normed = low(rms_norm(inputs, gain_rows[0]))
    mixed_cols = low_back(jnp.dot(normed, qkv_low, precision=PRECISE))
    cosine_table, sine_table = rope_tables(positions(sequence_ids))
    queries = low(rotate(mixed_cols[:, :D].reshape(count_rows, HEADS, HEAD), cosine_table, sine_table))
    keys_rot = low(rotate(mixed_cols[:, D:D + kv_width].reshape(count_rows, KV_HEADS, HEAD), cosine_table, sine_table))
    values_kv = low(mixed_cols[:, D + kv_width:].reshape(count_rows, KV_HEADS, HEAD))
    keys_wide = jnp.repeat(keys_rot, group_size, axis=1)
    values_wide = jnp.repeat(values_kv, group_size, axis=1)
    scores = low_back(jnp.einsum('qhd,khd->hqk', queries, keys_wide, precision=PRECISE) * scale_factor)
    scores = jnp.where(causal_mask(sequence_ids)[None], scores, NEG_LARGE)
    top_score = lax.optimization_barrier(jnp.max(scores, axis=-1, keepdims=True))
    weights = jnp.exp(scores - top_score)
    prob_table = low(weights / lax.optimization_barrier(jnp.sum(weights, axis=-1, keepdims=True)))
    context = low(low_back(jnp.einsum('hqk,khd->qhd', prob_table, values_wide, precision=PRECISE)))
    middle = inputs + low_back(jnp.dot(context.reshape(count_rows, D), out_low, precision=PRECISE))
    normed_two = low(rms_norm(middle, gain_rows[1]))
    gate_up = low_back(jnp.dot(normed_two, gate_up_low, precision=PRECISE))
    hidden = low(swiglu(gate_up[:, :FF], gate_up[:, FF:]))
    return middle + low_back(jnp.dot(hidden, down_low, precision=PRECISE))

def reference(tokens, sequence_ids, cotangent, norm_gains, qkv_weight, out_weight, gate_up_weight, down_weight, gains_first, qkv_first, out_first, gate_up_first, down_first, gains_second, qkv_second, out_second, gate_up_second, down_second):
    buffer_count = N_REP * N_FSDP
    token_blocks = tokens.reshape(buffer_count, ROWS_DEV, D)
    id_blocks = sequence_ids.reshape(buffer_count, ROWS_DEV)
    cot_blocks = cotangent.reshape(buffer_count, ROWS_DEV, D)
    params = (norm_gains, qkv_weight, out_weight, gate_up_weight, down_weight)

    def one_block(grad_total, members):
        token_one, ids_one, cot_one = members

        def local_layer(inputs, gains_in, qkv_in, out_in, gate_up_in, down_in):
            return block_layer(inputs, ids_one, gains_in, qkv_in, out_in, gate_up_in, down_in)
        result, pull_back = jax.vjp(local_layer, token_one.astype(jnp.float32), *params)
        grad_parts = pull_back(cot_one.astype(jnp.float32))
        grad_total = jax.tree.map(jnp.add, grad_total, tuple(grad_parts[1:]))
        return (grad_total, (result.astype(jnp.bfloat16), grad_parts[0].astype(jnp.bfloat16)))
    zero_grads = tuple((jnp.zeros(param_one.shape, jnp.float32) for param_one in params))
    grad_total, (out_blocks, grad_blocks) = lax.scan(one_block, zero_grads, (token_blocks, id_blocks, cot_blocks))
    block_out = out_blocks.reshape(-1, D)
    tokens_grad = grad_blocks.reshape(-1, D)
    gains_grad, qkv_grad, out_grad, gate_up_grad, down_grad = grad_total
    gains_delta, gains_first_new, gains_second_new = adamw_update(norm_gains, gains_first, gains_second, gains_grad, 0.0)
    qkv_delta, qkv_first_new, qkv_second_new = adamw_update(qkv_weight, qkv_first, qkv_second, qkv_grad, DECAY_RATE)
    out_delta, out_first_new, out_second_new = adamw_update(out_weight, out_first, out_second, out_grad, DECAY_RATE)
    gate_up_delta, gate_up_first_new, gate_up_second_new = adamw_update(gate_up_weight, gate_up_first, gate_up_second, gate_up_grad, DECAY_RATE)
    down_delta, down_first_new, down_second_new = adamw_update(down_weight, down_first, down_second, down_grad, DECAY_RATE)
    return (block_out, tokens_grad, gains_grad, qkv_grad, out_grad, gate_up_grad, down_grad, gains_delta, qkv_delta, out_delta, gate_up_delta, down_delta, gains_first_new, qkv_first_new, out_first_new, gate_up_first_new, down_first_new, gains_second_new, qkv_second_new, out_second_new, gate_up_second_new, down_second_new)
```

```python
import math

import jax
import jax.numpy as jnp
from jax import lax
from jax.experimental import pallas as pl
from jax.experimental.pallas import tpu as pltpu
from jax.sharding import PartitionSpec as P
D = 960
HEADS = 15
KV_HEADS = 5
HEAD = 64
FF = 2560
STEP = 4


NORM_EPS = 1e-05
ROPE_BASE = 100000.0
LEARN_RATE = 0.03
BETA_ONE = 0.9
BETA_TWO = 0.95
ADAM_EPS = 1e-08
DECAY_RATE = 0.1
NEG_LARGE = -1e30


def positions(sequence_ids):
    row_index = jnp.arange(sequence_ids.shape[0], dtype=jnp.int32)
    prior_ids = jnp.concatenate([jnp.full((1,), -1, jnp.int32), sequence_ids[:-1]])
    seq_starts = jnp.where(sequence_ids != prior_ids, row_index, 0)
    first_row = lax.cummax(seq_starts, axis=0)
    return (row_index - first_row).astype(jnp.float32)


def causal_mask(sequence_ids):
    row_index = jnp.arange(sequence_ids.shape[0], dtype=jnp.int32)
    return (sequence_ids[:, None] == sequence_ids[None, :]) & (
        row_index[None, :] <= row_index[:, None]
    )


def rope_tables(places):
    half_size = HEAD // 2
    freq_table = ROPE_BASE ** (-2.0 * jnp.arange(half_size, dtype=jnp.float32) / HEAD)
    angles = places[:, None] * freq_table[None, :]
    return (jnp.cos(angles), jnp.sin(angles))


def rotate(vectors, cosine_table, sine_table):
    half_size = vectors.shape[-1] // 2
    first_half = vectors[..., :half_size]
    second_half = vectors[..., half_size:]
    cosine_wide = cosine_table[:, None, :]
    sine_wide = sine_table[:, None, :]
    return jnp.concatenate(
        [
            first_half * cosine_wide - second_half * sine_wide,
            second_half * cosine_wide + first_half * sine_wide,
        ],
        axis=-1,
    )


def rms_norm(values, gain_row):
    row_scale = lax.rsqrt(jnp.mean(values * values, axis=-1, keepdims=True) + NORM_EPS)
    return values * row_scale * gain_row


def swiglu(gate_part, up_part):
    return gate_part * jax.nn.sigmoid(gate_part) * up_part


def adamw_update(weight, moment_one, moment_two, gradient, decay_rate):
    first_new = BETA_ONE * moment_one + (1.0 - BETA_ONE) * gradient
    second_new = BETA_TWO * moment_two + (1.0 - BETA_TWO) * gradient * gradient
    fix_one = 1.0 - BETA_ONE**STEP
    fix_two = 1.0 - BETA_TWO**STEP
    update_dir = (
        first_new / fix_one / (jnp.sqrt(second_new / fix_two) + ADAM_EPS) + decay_rate * weight
    )
    return (-LEARN_RATE * update_dir, first_new, second_new)


def split_groups(queries, keys_rot, values_kv):
    count_rows = queries.shape[0]
    group_size = HEADS // KV_HEADS
    query_groups = queries.reshape(count_rows, KV_HEADS, group_size, HEAD).transpose(1, 2, 0, 3)
    return (query_groups, keys_rot.transpose(1, 0, 2), values_kv.transpose(1, 0, 2))


def attend(queries, keys_rot, values_kv, mask_table):
    count_rows = queries.shape[0]
    scale_factor = 1.0 / math.sqrt(HEAD)
    query_groups, key_groups, value_groups = split_groups(queries, keys_rot, values_kv)

    def one_group(members):
        query_one, key_one, value_one = members
        scores = (
            jnp.einsum("gqd,kd->gqk", query_one, key_one, preferred_element_type=jnp.float32)
            * scale_factor
        )
        scores = jnp.where(mask_table[None], scores, NEG_LARGE)
        top_score = jnp.max(scores, axis=-1, keepdims=True)
        weights = jnp.exp(scores - top_score)
        total_sum = jnp.sum(weights, axis=-1, keepdims=True)
        prob_table = (weights / total_sum).astype(jnp.bfloat16)
        context_one = jnp.einsum(
            "gqk,kd->gqd", prob_table, value_one, preferred_element_type=jnp.float32
        )
        return (context_one.astype(jnp.bfloat16), (top_score + jnp.log(total_sum))[..., 0])

    context_groups, log_total = lax.map(one_group, (query_groups, key_groups, value_groups))
    context = context_groups.transpose(2, 0, 1, 3).reshape(count_rows, HEADS, HEAD)
    return (context, log_total)


def attend_back(queries, keys_rot, values_kv, mask_table, log_total, grad_context):
    count_rows = queries.shape[0]
    group_size = HEADS // KV_HEADS
    scale_factor = 1.0 / math.sqrt(HEAD)
    query_groups, key_groups, value_groups = split_groups(queries, keys_rot, values_kv)
    grad_groups = grad_context.reshape(count_rows, KV_HEADS, group_size, HEAD).transpose(1, 2, 0, 3)

    def one_group(members):
        query_one, key_one, value_one, log_one, grad_one = members
        scores = (
            jnp.einsum("gqd,kd->gqk", query_one, key_one, preferred_element_type=jnp.float32)
            * scale_factor
        )
        scores = jnp.where(mask_table[None], scores, NEG_LARGE)
        prob_table = jnp.exp(scores - log_one[..., None])
        grad_probs = jnp.einsum(
            "gqd,kd->gqk", grad_one, value_one, preferred_element_type=jnp.float32
        )
        grad_value = jnp.einsum(
            "gqk,gqd->kd",
            prob_table.astype(jnp.bfloat16),
            grad_one,
            preferred_element_type=jnp.float32,
        )
        row_delta = jnp.sum(prob_table * grad_probs, axis=-1, keepdims=True)
        grad_scores = (prob_table * (grad_probs - row_delta)).astype(jnp.bfloat16)
        grad_query = (
            jnp.einsum("gqk,kd->gqd", grad_scores, key_one, preferred_element_type=jnp.float32)
            * scale_factor
        )
        grad_key = (
            jnp.einsum("gqk,gqd->kd", grad_scores, query_one, preferred_element_type=jnp.float32)
            * scale_factor
        )
        return (grad_query, grad_key, grad_value)

    grad_q_groups, grad_k_groups, grad_v_groups = lax.map(
        one_group, (query_groups, key_groups, value_groups, log_total, grad_groups)
    )
    grad_queries = grad_q_groups.transpose(2, 0, 1, 3).reshape(count_rows, HEADS, HEAD)
    return (grad_queries, grad_k_groups.transpose(1, 0, 2), grad_v_groups.transpose(1, 0, 2))


def forward(tokens, sequence_ids, attn_set, mlp_set):
    gain_half, qkv_half, out_half = attn_set
    gate_up_half, down_half = mlp_set
    count_rows = tokens.shape[0]
    kv_width = KV_HEADS * HEAD
    inputs = tokens.astype(jnp.float32)
    gain_rows = gain_half.astype(jnp.float32)
    normed = rms_norm(inputs, gain_rows[0]).astype(jnp.bfloat16)
    mixed_cols = jnp.dot(normed, qkv_half, preferred_element_type=jnp.float32)
    cosine_table, sine_table = rope_tables(positions(sequence_ids))
    queries = rotate(
        mixed_cols[:, :D].reshape(count_rows, HEADS, HEAD), cosine_table, sine_table
    ).astype(jnp.bfloat16)
    keys_rot = rotate(
        mixed_cols[:, D : D + kv_width].reshape(count_rows, KV_HEADS, HEAD),
        cosine_table,
        sine_table,
    ).astype(jnp.bfloat16)
    values_kv = (
        mixed_cols[:, D + kv_width :].reshape(count_rows, KV_HEADS, HEAD).astype(jnp.bfloat16)
    )
    context, log_total = attend(queries, keys_rot, values_kv, causal_mask(sequence_ids))
    middle = inputs + jnp.dot(
        context.reshape(count_rows, D), out_half, preferred_element_type=jnp.float32
    )
    normed_two = rms_norm(middle, gain_rows[1]).astype(jnp.bfloat16)
    gate_up = jnp.dot(normed_two, gate_up_half, preferred_element_type=jnp.float32)
    hidden = swiglu(gate_up[:, :FF], gate_up[:, FF:]).astype(jnp.bfloat16)
    result = middle + jnp.dot(hidden, down_half, preferred_element_type=jnp.float32)
    kept_state = (
        inputs,
        normed,
        queries,
        keys_rot,
        values_kv,
        context,
        log_total,
        middle,
        normed_two,
        gate_up,
        hidden,
    )
    return (kept_state, result)


def mlp_backward(kept_state, cotangent, attn_set, mlp_set):
    middle, normed_two, gate_up, hidden = (
        kept_state[7],
        kept_state[8],
        kept_state[9],
        kept_state[10],
    )
    gain_rows = attn_set[0].astype(jnp.float32)
    gate_up_half, down_half = mlp_set
    grad_result = cotangent.astype(jnp.float32)
    grad_branch = grad_result.astype(jnp.bfloat16)
    down_grad = jnp.einsum("rf,rd->fd", hidden, grad_branch, preferred_element_type=jnp.float32)
    grad_hidden = jnp.einsum(
        "rd,fd->rf", grad_branch, down_half, preferred_element_type=jnp.float32
    )
    _, act_back = jax.vjp(swiglu, gate_up[:, :FF], gate_up[:, FF:])
    grad_gate, grad_up = act_back(grad_hidden)
    grad_mix_two = jnp.concatenate([grad_gate, grad_up], axis=1).astype(jnp.bfloat16)
    gate_up_grad = jnp.einsum(
        "rd,rf->df", normed_two, grad_mix_two, preferred_element_type=jnp.float32
    )
    grad_normed_two = jnp.einsum(
        "rf,df->rd", grad_mix_two, gate_up_half, preferred_element_type=jnp.float32
    )
    _, norm_back_two = jax.vjp(rms_norm, middle, gain_rows[1])
    grad_middle_norm, gain_two_grad = norm_back_two(grad_normed_two)
    grad_middle = grad_result + grad_middle_norm
    return ((gate_up_grad, down_grad), (grad_middle, gain_two_grad))


def attn_backward(kept_state, carried, sequence_ids, attn_set):
    inputs, normed, queries, keys_rot, values_kv, context, log_total = kept_state[:7]
    grad_middle, gain_two_grad = carried
    gain_half, qkv_half, out_half = attn_set
    gain_rows = gain_half.astype(jnp.float32)
    count_rows = inputs.shape[0]
    kv_width = KV_HEADS * HEAD
    grad_attn = grad_middle.astype(jnp.bfloat16)
    flat_context = context.reshape(count_rows, D)
    out_grad = jnp.einsum("rc,rd->cd", flat_context, grad_attn, preferred_element_type=jnp.float32)
    grad_context = jnp.einsum("rd,cd->rc", grad_attn, out_half, preferred_element_type=jnp.float32)
    grad_context = grad_context.astype(jnp.bfloat16).reshape(count_rows, HEADS, HEAD)
    grad_queries, grad_keys, grad_values = attend_back(
        queries, keys_rot, values_kv, causal_mask(sequence_ids), log_total, grad_context
    )
    cosine_table, sine_table = rope_tables(positions(sequence_ids))
    grad_q_raw = rotate(grad_queries, cosine_table, -sine_table).reshape(count_rows, D)
    grad_k_raw = rotate(grad_keys, cosine_table, -sine_table).reshape(count_rows, kv_width)
    grad_mixed = jnp.concatenate(
        [grad_q_raw, grad_k_raw, grad_values.reshape(count_rows, kv_width)], axis=1
    )
    grad_mixed = grad_mixed.astype(jnp.bfloat16)
    qkv_grad = jnp.einsum("rd,rc->dc", normed, grad_mixed, preferred_element_type=jnp.float32)
    grad_normed = jnp.einsum("rc,dc->rd", grad_mixed, qkv_half, preferred_element_type=jnp.float32)
    _, norm_back_one = jax.vjp(rms_norm, inputs, gain_rows[0])
    grad_inputs_norm, gain_one_grad = norm_back_one(grad_normed)
    tokens_grad = (grad_middle + grad_inputs_norm).astype(jnp.bfloat16)
    gains_grad = jnp.stack([gain_one_grad, gain_two_grad])
    return (tokens_grad, (gains_grad, qkv_grad, out_grad))


def on_device_any(
    tokens,
    sequence_ids,
    cotangent,
    norm_gains,
    qkv_weight,
    out_weight,
    gate_up_weight,
    down_weight,
    gains_first,
    qkv_first,
    out_first,
    gate_up_first,
    down_first,
    gains_second,
    qkv_second,
    out_second,
    gate_up_second,
    down_second,
):
    shares = lax.axis_size("rep")
    share = lax.axis_index("rep")
    both = ("fsdp", "rep")
    group = lax.axis_size("fsdp")

    def collect(shard):
        flat = shard.astype(jnp.bfloat16).reshape(shares, -1)
        piece = lax.dynamic_index_in_dim(flat, share, 0, keepdims=False)
        whole = lax.all_gather(piece, both, axis=0, tiled=True)
        return whole.reshape(shard.shape[0] * group, shard.shape[1])

    def total(gradient, shard):
        piece = lax.psum_scatter(
            gradient.astype(jnp.bfloat16).reshape(-1), both, scatter_dimension=0, tiled=True
        )
        flat = lax.all_gather(piece, "rep", axis=0, tiled=True)
        return flat.reshape(shard.shape).astype(jnp.float32)

    gain_full = lax.all_gather(norm_gains.astype(jnp.bfloat16), "fsdp", axis=1, tiled=True)
    qkv_full = collect(qkv_weight)
    out_full = collect(out_weight)
    mlp_set = (collect(gate_up_weight), collect(down_weight))
    attn_set = (gain_full, qkv_full, out_full)
    kept_state, result = forward(tokens, sequence_ids, attn_set, mlp_set)
    block_out = result.astype(jnp.bfloat16)
    mlp_grads, carried = mlp_backward(kept_state, cotangent, attn_set, mlp_set)
    down_total = total(mlp_grads[1], down_weight)
    gate_up_total = total(mlp_grads[0], gate_up_weight)
    tokens_grad, attn_grads = attn_backward(kept_state, carried, sequence_ids, attn_set)
    gains_part = lax.psum_scatter(attn_grads[0], "fsdp", scatter_dimension=1, tiled=True)
    gains_total = lax.psum(gains_part, "rep")
    qkv_total = total(attn_grads[1], qkv_weight)
    out_total = total(attn_grads[2], out_weight)
    gains_delta, gains_first_new, gains_second_new = adamw_update(
        norm_gains, gains_first, gains_second, gains_total, 0.0
    )
    qkv_delta, qkv_first_new, qkv_second_new = adamw_update(
        qkv_weight, qkv_first, qkv_second, qkv_total, DECAY_RATE
    )
    out_delta, out_first_new, out_second_new = adamw_update(
        out_weight, out_first, out_second, out_total, DECAY_RATE
    )
    gate_up_delta, gate_up_first_new, gate_up_second_new = adamw_update(
        gate_up_weight, gate_up_first, gate_up_second, gate_up_total, DECAY_RATE
    )
    down_delta, down_first_new, down_second_new = adamw_update(
        down_weight, down_first, down_second, down_total, DECAY_RATE
    )
    return (
        block_out,
        tokens_grad,
        gains_total,
        qkv_total,
        out_total,
        gate_up_total,
        down_total,
        gains_delta,
        qkv_delta,
        out_delta,
        gate_up_delta,
        down_delta,
        gains_first_new,
        qkv_first_new,
        out_first_new,
        gate_up_first_new,
        down_first_new,
        gains_second_new,
        qkv_second_new,
        out_second_new,
        gate_up_second_new,
        down_second_new,
    )


MESH = pl.DeviceIdType.MESH
UNITS = [(0,240,128),(240,240,128),(480,240,128)] + [(720+368*j,368,192) for j in range(5)]
NU = len(UNITS); ROWS = 2560

def place():
    rep = lax.axis_index("rep"); z = lax.axis_index("fsdp")
    c = rep % 2; x = (rep // 2) % 2; y = rep // 4
    return dict(rep=rep, z=z, c=c, x=x, y=y, q=rep//2,
      k=c*4 + rep//2, pa={"rep": rep + 1 - 2*c}, xn={"rep": rep + 2 - 4*x}, yn={"rep": rep + 4 - 8*y},
      zn=[{"fsdp": (z+d)%4} for d in (1,2,3)],
      kp=(1-c)*4+rep//2, kx=c*4+y*2+1-x, ky=c*4+(1-y)*2+x, kd=c*4+(1-y)*2+1-x,
      kpx=(1-c)*4+y*2+1-x, kpy=(1-c)*4+(1-y)*2+x, kpd=(1-c)*4+(1-y)*2+1-x)

def greet(w):
    bar = pltpu.get_barrier_semaphore()
    peers = [w["pa"], w["xn"], w["yn"]] + w["zn"]
    for p in peers: pl.semaphore_signal(bar, inc=1, device_id=p, device_id_type=MESH)
    pl.semaphore_wait(bar, len(peers))

class Gather:
    def __init__(g, w, own, W, ss, rz, rx, ry, rp):
        g.w, g.own, g.W, g.ss, g.rz, g.rx, g.ry, g.rp = w, own, W, ss, rz, rx, ry, rp
        g.sent = []
    def copy(g, src, dst, s, r, dev):
        return pltpu.make_async_remote_copy(src_ref=src, dst_ref=dst, send_sem=s, recv_sem=r, device_id=dev, device_id_type=MESH)
    def send(g, u, i, src, dst, r, dev):
        cp = g.copy(src, dst, g.ss.at[u, i], r, dev); cp.start(); g.sent.append(cp)
    def got(g, ref, r):
        g.copy(ref, ref, g.ss.at[0,0], r, g.w["pa"]).wait_recv()
    def reg(g, k, u, a=None, b=None):
        r0, n, h = UNITS[u]
        lo = r0 + (a or 0); m = (b if b is not None else n) - (a or 0)
        return g.W.at[k, :, pl.ds(lo, m)]
    def stage0(g, u):
        r0, n, h = UNITS[u]; w = g.w
        for d in range(3):
            g.send(u, d, g.own.at[w["k"], pl.ds(r0, n)], g.W.at[w["k"], d, pl.ds(r0, n)], g.rz.at[u, d], w["zn"][d])
    def stage1(g, u):
        r0, n, h = UNITS[u]; w = g.w
        for d in range(3):
            g.got(g.W.at[w["k"], d, pl.ds(r0, n)], g.rz.at[u, d])
        b = g.reg(w["k"], u)
        g.send(u, 3, b, b, g.rx.at[u, 0], w["xn"])
        g.send(u, 4, b, b, g.ry.at[u, 0], w["yn"])
        g.send(u, 5, b, b, g.rp.at[u, 0], w["pa"])
    def stage2(g, u):
        r0, n, h = UNITS[u]; w = g.w
        g.got(g.reg(w["kx"], u), g.rx.at[u, 0])
        b = g.reg(w["kx"], u, 0, h); g.send(u, 6, b, b, g.ry.at[u, 1], w["yn"])
        b = g.reg(w["kx"], u); g.send(u, 7, b, b, g.rp.at[u, 1], w["pa"])
        g.got(g.reg(w["ky"], u), g.ry.at[u, 0])
        b = g.reg(w["ky"], u, h, n); g.send(u, 8, b, b, g.rx.at[u, 1], w["xn"])
        b = g.reg(w["ky"], u); g.send(u, 9, b, b, g.rp.at[u, 2], w["pa"])
    def stage3(g, u):
        r0, n, h = UNITS[u]; w = g.w
        g.got(g.reg(w["kd"], u, 0, h), g.ry.at[u, 1])
        g.got(g.reg(w["kd"], u, h, n), g.rx.at[u, 1])
        b = g.reg(w["kd"], u); g.send(u, 10, b, b, g.rp.at[u, 3], w["pa"])
    def stage4(g, u):
        w = g.w
        for i, k in enumerate(("kp", "kpx", "kpy", "kpd")):
            g.got(g.reg(w[k], u), g.rp.at[u, i])
    def slot(g, s):
        if s < NU: g.stage1(s)
        if 0 <= s-1 < NU: g.stage2(s-1)
        if 0 <= s-2 < NU: g.stage3(s-2)
    def finish(g):
        for cp in g.sent: cp.wait_send()

GSEMS = lambda: [pltpu.SemaphoreType.DMA((NU, 11)), pltpu.SemaphoreType.DMA((NU, 3)), pltpu.SemaphoreType.DMA((NU, 2)), pltpu.SemaphoreType.DMA((NU, 2)), pltpu.SemaphoreType.DMA((NU, 4))]

bf16, f32 = jnp.bfloat16, jnp.float32
NEG=NEG_LARGE; EPS=NORM_EPS
NT = (((1,),(1,)),((),())); NN = (((1,),(0,)),((),())); TN = (((0,),(0,)),((),()))
def mm(a, b, dims=NN): return lax.dot_general(a, b, dims, preferred_element_type=f32)

def pack(norm_gains, qkv, out, gu, down):
    qb, g = qkv.astype(bf16), norm_gains.astype(bf16)
    col = lambda i: jnp.pad(g[i][:, None], ((0,0),(0,127)))
    q = jnp.concatenate([qb[:, :896], col(0), qb[:, 896:], jnp.zeros((240,192), bf16), col(1)], axis=1)
    q = q.reshape(240, 8, 2, 128).transpose(1,2,0,3).reshape(8, 480, 128)
    o = jnp.pad(out.astype(bf16), ((0,0),(0,64))).reshape(240,8,128).transpose(1,0,2)
    gg = gu.astype(bf16).reshape(240,2,4,5,128).transpose(1,2,3,0,4).reshape(8,5,240,128)
    dd = jnp.pad(down.astype(bf16), ((0,0),(0,64))).reshape(5,128,8,128).transpose(2,0,1,3)
    m = jnp.concatenate([gg, dd], axis=2).reshape(8, 1840, 128)
    return jnp.concatenate([q, o, m], axis=1)

def tables(ids):
    place = jnp.sum((ids[None,:] < ids[:,None]).astype(f32), axis=1)
    place = jnp.arange(512, dtype=f32) - place
    freq = 100000.0 ** (-2.0*jnp.arange(32, dtype=f32)/64)
    ang = place[:,None]*freq[None,:]
    c, s = jnp.cos(ang), jnp.sin(ang)
    return jnp.concatenate([c,c,c,c],1), jnp.concatenate([-s,s,-s,s],1)

def load_unit(w, own, W, dst, sem, u0, n, tiles, col0=0):
    for k in range(8):
        cs = pl.ds(col0 + k*tiles*128, 128)
        pltpu.make_async_copy(own.at[k, pl.ds(u0,n)], dst.at[pl.ds(pl.multiple_of(w["z"]*n, 16), n), cs], sem).start()
        for d in range(3):
            zs = (w["z"] + 3 - d) % 4
            pltpu.make_async_copy(W.at[k, d, pl.ds(u0,n)], dst.at[pl.ds(pl.multiple_of(zs*n, 16), n), cs], sem).start()

def lanes(n=128): return lax.broadcasted_iota(jnp.int32, (1,n), 1)
def rope(t, c, s):
    first = (lanes() % 64) < 32
    sw = jnp.where(first, pltpu.roll(t, 96, 1), pltpu.roll(t, 32, 1))
    return t*c + sw*s
def dup(t, half):
    sw = pltpu.roll(t, 64, 1)
    return jnp.where((lanes() < 64) == (half == 0), t, sw)

def gain_row(tile):
    sel = ((lax.broadcasted_iota(jnp.int32,(8,128),0)==0)&(lax.broadcasted_iota(jnp.int32,(8,128),1)==0)).astype(f32).astype(bf16)
    return mm(sel, tile, NT)[0:1]
def norm(v, g):
    r = lax.rsqrt(jnp.mean(v*v, axis=1, keepdims=True) + EPS)
    return v * r * g
KV = [(7,1),(8,0),(8,1),(9,0),(9,1)]
VV = [(10,0),(10,1),(11,0),(11,1),(12,0)]

def make_bias(seqc, seqr, bias):
    for i in range(2):
        rows = lax.broadcasted_iota(jnp.int32,(256,512),0)+256*i
        cols = lax.broadcasted_iota(jnp.int32,(256,512),1)
        ok = (seqc[pl.ds(256*i,256)] == seqr[...]) & (cols <= rows)
        bias[pl.ds(256*i,256)] = jnp.where(ok, 0.0, NEG).astype(bf16)

def head_fwd(h, qk, k2, v2, bias, ctx, lse):
    t, half, g = h//2, h%2, h//3
    col = pl.ds(pl.multiple_of(t*128,128),128)
    mine = (lanes()//64) == half
    hm = jnp.where(mine, 0.125, 0.0).astype(bf16)
    for i in range(2):
        rows, n = pl.ds(256*i,256), 256*(i+1)
        s = mm(qk[rows, col]*hm, k2[g, pl.ds(0,n)], NT) + bias[rows, pl.ds(0,n)].astype(f32)
        m = jnp.max(s, axis=1, keepdims=True)
        p = jnp.exp(s-m)
        l = jnp.sum(p, axis=1, keepdims=True)
        o = mm((p*(1.0/l)).astype(bf16), v2[g, pl.ds(0,n)])
        ctx[rows, col] = jnp.where(mine, o, ctx[rows, col].astype(f32)).astype(bf16)
        lse[rows] = jnp.where(lanes()==h, m+jnp.log(l), lse[rows])

def k1_body(tok, seqc, seqr, cos, sin, own, W, n1T, qk, k2, v2, ctxT, lse, mid, n2, n2T, gains, wq, wo, n1, ctx, bias, lsem, *sems):
    w = place(); greet(w)
    g = Gather(w, own, W, *sems)
    LA=3
    for u in range(LA): g.stage0(u)
    def slot(s):
        if s+LA<NU: g.stage0(s+LA)
        g.slot(s)
    ctx[...] = jnp.zeros_like(ctx); lse[...] = jnp.zeros_like(lse)
    make_bias(seqc, seqr, bias)
    for s in range(4): slot(s)
    g.stage4(0); g.stage4(1)
    load_unit(w, own, W, wq, lsem.at[0], 0, 240, 2, 0)
    load_unit(w, own, W, wq, lsem.at[0], 240, 240, 2, 128)
    pltpu.make_async_copy(wq, wq, lsem.at[0]).wait()
    x = tok[...].astype(f32)
    g0 = gain_row(wq[:, 896:1024]); g1 = gain_row(wq[:, 1920:2048])
    gains[...] = jnp.zeros_like(gains)
    gains[0:1] = g0; gains[1:2] = g1
    n1[...] = norm(x, g0).astype(bf16)
    for half, (lo, hi) in enumerate(((0,7),(7,13))):
        for t in range(lo, hi):
            c0 = (t*128) if half==0 else 1024+(t-7)*128
            pass
        base = 0 if half==0 else 1024
        res = mm(n1[...], wq[:, base:base+(hi-lo)*128])
        for t in range(lo, hi):
            tile = res[:, (t-lo)*128:(t-lo+1)*128]
            if t < 10:
                tile = rope(tile, cos[...], sin[...])
                qk[:, t*128:(t+1)*128] = tile.astype(bf16)
            else:
                pass
            for i,(tt,hh) in enumerate(KV):
                if tt==t: k2[i] = dup(tile, hh).astype(bf16)
            for i,(tt,hh) in enumerate(VV):
                if tt==t: v2[i] = dup(tile, hh).astype(bf16)
    n1T[...] = jnp.swapaxes(n1[...],0,1)
    slot(4)
    g.stage4(2); load_unit(w, own, W, wo, lsem.at[1], 480, 240, 1)
    for i in range(5):
        def one(h, _): head_fwd(h, qk, k2, v2, bias, ctx, lse); return 0
        lax.fori_loop(3*i, 3*i+3, one, 0)
        if 5+i < NU+2: slot(5+i)
    pltpu.make_async_copy(wo, wo, lsem.at[1]).wait()
    for i in range(2):
        rows = pl.ds(256*i,256)
        m = tok[rows].astype(f32) + mm(ctx[rows, 0:960], wo[:, 0:960])
        mid[rows] = m
        n2[rows] = norm(m, g1).astype(bf16)
    n2T[...] = jnp.swapaxes(n2[...],0,1)
    ctxT[...] = jnp.swapaxes(ctx[:,0:960],0,1)
    for u in range(3,NU): g.stage4(u)
    g.finish()

def k1_call(tok, ids, own):
    c, s = tables(ids)
    S = jax.ShapeDtypeStruct
    vm = pl.BlockSpec(memory_space=pltpu.VMEM); hb = pl.BlockSpec(memory_space=pl.ANY)
    return pl.pallas_call(k1_body, name="front",
      out_shape=[S((8,3,ROWS,128),bf16), S((960,512),bf16), S((512,1280),bf16), S((5,512,128),bf16), S((5,512,128),bf16), S((960,512),bf16), S((512,128),f32), S((512,960),f32), S((512,960),bf16), S((960,512),bf16), S((8,960),f32)],
      in_specs=[vm]*5+[hb], out_specs=[hb]+[vm]*10,
      scratch_shapes=[pltpu.VMEM((960,2048),bf16), pltpu.VMEM((960,1024),bf16), pltpu.VMEM((512,960),bf16), pltpu.VMEM((512,1024),bf16), pltpu.VMEM((512,512),bf16), pltpu.SemaphoreType.DMA((2,))]+GSEMS(),
      compiler_params=pltpu.CompilerParams(collective_id=0, has_side_effects=True, vmem_limit_bytes=60<<20))(tok, ids[:,None], ids[None,:], c, s, own)
RU = [(720+368*j,368,192) for j in range(5)] + [(480,240,128),(0,240,128),(240,240,128)]

class Reduce:
    def __init__(g, w, S, RX3, RY3, RX, RY, RZ, FIN, ss, r3, rxy, rz, rf, lf):
        for n,v in dict(locals()).items():
            if n!="g": setattr(g,n,v)
        g.sent=[]; g.freed=set(); w=g.w
        g.q=w["rep"]//2; g.qx=w["y"]*2+1-w["x"]; g.qy=(1-w["y"])*2+w["x"]; g.qd=(1-w["y"])*2+1-w["x"]
    def copy(g, src, dst, s, r, dev):
        return pltpu.make_async_remote_copy(src_ref=src, dst_ref=dst, send_sem=s, recv_sem=r, device_id=dev, device_id_type=MESH)
    def send(g, u, i, src, dst, r, dev):
        cp = g.copy(src, dst, g.ss.at[u, i], r, dev); cp.start(); g.sent.append((u,cp))
    def got(g, ref, r):
        g.copy(ref, ref, g.ss.at[0,0], r, g.w["pa"]).wait_recv()
    def c1(g,u):
        r0,n,h = RU[u]; R=pl.ds(r0,n); S=g.S(u); w=g.w
        g.send(u,0,S.at[g.qd,0:2],g.RX3.at[:,R],g.r3.at[u,0],w["xn"])
        g.send(u,1,S.at[g.qd,2:4],g.RY3.at[:,R],g.r3.at[u,1],w["yn"])
        g.send(u,2,S.at[g.qx,0:2],g.RX.at[0:2,R],g.rxy.at[u,0],w["xn"])
        g.send(u,3,S.at[g.qy,2:4],g.RY.at[2:4,R],g.rxy.at[u,1],w["yn"])
    def c2(g,u):
        r0,n,h = RU[u]; R=pl.ds(r0,n); S=g.S(u); w=g.w
        g.got(g.RY3.at[:,R], g.r3.at[u,1])
        S[g.qx,2:4] = (S[g.qx,2:4].astype(f32)+g.RY3[:,R].astype(f32)).astype(bf16)
        g.send(u,4,S.at[g.qx,2:4],g.RX.at[2:4,R],g.rxy.at[u,2],w["xn"])
        g.got(g.RX3.at[:,R], g.r3.at[u,0])
        S[g.qy,0:2] = (S[g.qy,0:2].astype(f32)+g.RX3[:,R].astype(f32)).astype(bf16)
        g.send(u,5,S.at[g.qy,0:2],g.RY.at[0:2,R],g.rxy.at[u,3],w["yn"])
    def c3(g,u):
        r0,n,h = RU[u]; R=pl.ds(r0,n); S=g.S(u); w=g.w
        g.got(g.RX.at[0:2,R], g.rxy.at[u,0]); g.got(g.RX.at[2:4,R], g.rxy.at[u,2])
        g.got(g.RY.at[2:4,R], g.rxy.at[u,1]); g.got(g.RY.at[0:2,R], g.rxy.at[u,3])
        for b in range(4):
            S[g.q,b] = (S[g.q,b].astype(f32)+g.RX[b,R].astype(f32)+g.RY[b,R].astype(f32)).astype(bf16)
        for d in range(3):
            zt=(w["z"]+d+1)%4
            g.send(u,6+d,S.at[g.q,zt],g.RZ.at[d,R],g.rz.at[u,d],w["zn"][d])
    def c4(g,u):
        r0,n,h = RU[u]; R=pl.ds(r0,n); S=g.S(u); w=g.w
        for d in range(3): g.got(g.RZ.at[d,R], g.rz.at[u,d])
        S[g.q,w["z"]] = (S[g.q,w["z"]].astype(f32)+g.RZ[0,R].astype(f32)+g.RZ[1,R].astype(f32)+g.RZ[2,R].astype(f32)).astype(bf16)
        fb=S.at[g.q,w["z"]]; dst=g.FIN.at[w["k"],R]
        g.send(u,9,fb,dst,g.rf.at[u,0],w["xn"])
        g.send(u,10,fb,dst,g.rf.at[u,1],w["yn"])
        g.send(u,11,fb,dst,g.rf.at[u,4],w["pa"])
        pltpu.make_async_copy(fb,dst,g.lf.at[u]).start()
    def c5(g,u):
        r0,n,h = RU[u]; R=pl.ds(r0,n); w=g.w
        g.got(g.FIN.at[w["kx"],R], g.rf.at[u,0])
        b=g.FIN.at[w["kx"],pl.ds(r0,h)]; g.send(u,12,b,b,g.rf.at[u,3],w["yn"])
        b=g.FIN.at[w["kx"],R]; g.send(u,13,b,b,g.rf.at[u,5],w["pa"])
        g.got(g.FIN.at[w["ky"],R], g.rf.at[u,1])
        b=g.FIN.at[w["ky"],pl.ds(r0+h,n-h)]; g.send(u,14,b,b,g.rf.at[u,2],w["xn"])
        b=g.FIN.at[w["ky"],R]; g.send(u,15,b,b,g.rf.at[u,6],w["pa"])
    def c6(g,u):
        r0,n,h = RU[u]; R=pl.ds(r0,n); w=g.w
        g.got(g.FIN.at[w["kd"],pl.ds(r0,h)], g.rf.at[u,3])
        g.got(g.FIN.at[w["kd"],pl.ds(r0+h,n-h)], g.rf.at[u,2])
        b=g.FIN.at[w["kd"],R]; g.send(u,16,b,b,g.rf.at[u,7],w["pa"])
    def c7(g,u):
        r0,n,h = RU[u]; R=pl.ds(r0,n); w=g.w
        for i,k in enumerate(("kp","kpx","kpy","kpd")): g.got(g.FIN.at[w[k],R], g.rf.at[u,4+i])
        if u not in g.freed: pltpu.make_async_copy(g.S(u).at[g.q,w["z"]],g.FIN.at[w["k"],R],g.lf.at[u]).wait()
    def release(g,u):
        for cp in [e for e in g.sent if e[0]==u]: cp[1].wait_send(); g.sent.remove(cp)
        r0,n,h = RU[u]; R=pl.ds(r0,n); pltpu.make_async_copy(g.S(u).at[g.q,g.w["z"]],g.FIN.at[g.w["k"],R],g.lf.at[u]).wait(); g.freed.add(u)
    def step(g,i,u):
        if 0<=u<len(RU): getattr(g,"c%d"%i)(u)
    def finish(g):
        for _,cp in g.sent: cp.wait_send()
RSEMS = lambda: [pltpu.SemaphoreType.DMA((8,17)),pltpu.SemaphoreType.DMA((8,2)),pltpu.SemaphoreType.DMA((8,4)),pltpu.SemaphoreType.DMA((8,3)),pltpu.SemaphoreType.DMA((8,8)),pltpu.SemaphoreType.DMA((8,))]

def head_bwd(h, qk, k2, v2, bias, lse, dctx, dq, dk, dv):
    t, half, g = h//2, h%2, h//3
    col = pl.ds(pl.multiple_of(t*128,128),128)
    mine = (lanes()//64) == half
    hm = jnp.where(mine, 0.125, 0.0).astype(bf16)
    om = jnp.where(mine, 1.0, 0.0).astype(bf16)
    for i in range(2):
        rows, n = pl.ds(256*i,256), 256*(i+1)
        qs = qk[rows, col]*hm
        do = dctx[t//4, rows, pl.ds(pl.multiple_of((t%4)*128,128),128)]*om
        le = jnp.sum(jnp.where(lanes()==h, lse[rows], 0.0), axis=1, keepdims=True)
        s = mm(qs, k2[g, pl.ds(0,n)], NT) + bias[rows, pl.ds(0,n)].astype(f32)
        p = jnp.exp(s - le)
        dp = mm(do, v2[g, pl.ds(0,n)], NT)
        dv[g, pl.ds(0,n)] += mm(p.astype(bf16), do, TN)
        delta = jnp.sum(p*dp, axis=1, keepdims=True)
        ds = (p*(dp-delta)).astype(bf16)
        dk[g, pl.ds(0,n)] += mm(ds, qs, TN)
        o = mm(ds, k2[g, pl.ds(0,n)])*0.125
        dq[rows, col] = jnp.where(mine, o, dq[rows, col])

def norm_back(v, g, u):
    r = lax.rsqrt(jnp.mean(v*v, axis=1, keepdims=True)+EPS)
    wv = u*g
    dv = r*wv - v*(r*r*r)*jnp.mean(wv*v, axis=1, keepdims=True)
    return dv, u*v*r


def k2_kernel(cot, cos, sin, seqc, seqr, qk, k2, v2, lse, mid, n2, n2Ti, gains, tokp, n1T, ctxT, own, W,
            bo, tg, FIN, wg, wd, bias, n2T, n2pT, dypp, hid, dgu, hidp, dgup, da, acc, dacc, dk, dv, gcol, gcolp,
            SM, SO, RX3, RY3, RX, RY, RZ, lsem, ps, pr, *rsems):
    w = place(); c = w["c"]
    bar = pltpu.get_barrier_semaphore(); peers=[w["pa"],w["xn"],w["yn"]]+w["zn"]
    for p in peers: pl.semaphore_signal(bar, inc=1, device_id=p, device_id_type=MESH)
    def unit(j, slot):
        r0 = 720+368*j
        load_unit2(w, own, W, wg.at[slot], lsem.at[slot,0], r0, 240)
        load_unit2(w, own, W, wd.at[pl.ds(slot*512,512)], lsem.at[slot,1], r0+240, 128)
    unit(0,0); unit(1,1)
    make_bias(seqc, seqr, bias)
    acc[...] = jnp.zeros_like(acc); dacc[...] = jnp.zeros_like(dacc)
    dk[...] = jnp.zeros_like(dk); dv[...] = jnp.zeros_like(dv)
    pl.semaphore_wait(bar, len(peers))
    g = Reduce(w, lambda u: SM.at[u%NSM] if u<5 else SO.at[u-5], RX3, RY3, RX, RY, RZ, FIN, *rsems)
    live={}
    def psend(i, src, dst):
        cp = g.copy(src, dst, ps.at[i], pr.at[i], w["pa"]); cp.start(); live[i]=cp
    def psent(*ii):
        for i in ii: live.pop(i).wait_send()
    def pgot(i, dst): g.copy(dst, dst, ps.at[0], pr.at[i], w["pa"]).wait_recv()
    def local(src, dst, sem): cp = pltpu.make_async_copy(src, dst, sem); cp.start(); return cp
    oc = pl.ds(pl.multiple_of((1-c)*512,512),512); mc = pl.ds(pl.multiple_of(c*512,512),512)
    psend(0, n2Ti, n2pT); psend(1, cot.at[:,oc], dypp)
    local(n2Ti, n2T, lsem.at[2,0]).wait()
    def slot(s, lo=0, hi=5):
        for i in (7,6,5,4,3,2):
            if lo <= s-i+1 <= hi: g.step(i, s-i+1)
    for j in range(5):
        b = j%2
        pltpu.make_async_copy(wg.at[b],wg.at[b],lsem.at[b,0]).wait()
        pltpu.make_async_copy(wd.at[pl.ds(b*512,512)],wd.at[pl.ds(b*512,512)],lsem.at[b,1]).wait()
        if j>=2: psent(4+j-2, 9+j-2)
        for i in range(2):
            rows = pl.ds(256*i,256)
            gu = mm(n2[rows], wg[b])
            gate, up = gu[:, :512], gu[:, 512:]
            sg = jax.nn.sigmoid(gate)
            a = gate*sg
            hb = (a*up).astype(bf16)
            hid[b, rows] = hb
            acc[rows, 0:960] += mm(hb, wd[pl.ds(b*512,512), 0:960])
            dh = mm(cot[rows, 0:960], wd[pl.ds(b*512,512), 0:960], NT)
            dgt = (dh*up*(sg*(1.0+gate*(1.0-sg)))).astype(bf16)
            dup_ = (dh*a).astype(bf16)
            dgu[b,0,rows] = dgt; dgu[b,1,rows] = dup_
            dacc[rows] += mm(dgt, wg[b,:,0:512], NT) + mm(dup_, wg[b,:,512:1024], NT)
        psend(4+j, hid.at[b], hidp.at[b]); psend(9+j, dgu.at[b,1-c], dgup.at[b])
        if j+2<5: unit(j+2,b)
        if j==0: pgot(0,n2pT); pgot(1,dypp)
        slot(j)
        pgot(4+j, hidp.at[b]); pgot(9+j, dgup.at[b])
        if j>=NSM: g.release(j-NSM)
        S = g.S(j)
        G = mm(n2T[...], dgu[b,c]) + mm(n2pT[...], dgup[b])
        for qq in range(4):
            for z in range(4): S[qq,z,0:240] = G[z*240:(z+1)*240, qq*128:(qq+1)*128].astype(bf16)
        Dg = mm(hid[b], cot[:, mc], TN) + mm(hidp[b], dypp[...], TN)
        for qq in range(4):
            for z in range(4): S[qq,z,240:368] = Dg[z*128:(z+1)*128, qq*128:(qq+1)*128].astype(bf16)
        g.c1(j)
    psent(7,8,12,13,0,1)
    load_unit2(w, own, W, wd, lsem.at[0,1], 480, 240)
    load_unit2(w, own, W, None, lsem.at[0,0], 0, 240, halves=wg)
    lc = local(ctxT, n2T, lsem.at[2,0])
    g0, g1 = gains[0:1], gains[1:2]
    ones = jnp.ones((256,128),bf16)
    da[:, 896:1024] = jnp.zeros((512,128),bf16)
    gc = None
    for i in range(2):
        rows = pl.ds(256*i,256)
        m = mid[rows]
        bo[rows] = (m+acc[rows,0:960]).astype(bf16)
        dv_, gp = norm_back(m, g1, dacc[rows])
        dmid = cot[rows, 0:960].astype(f32)+dv_
        dacc[rows] = dmid
        da[rows,0:960] = dmid.astype(bf16)
        t_ = mm(gp.astype(bf16), ones, TN)
        gc = t_ if gc is None else gc+t_
    gcol[1] = gc.astype(bf16)
    psend(14, da.at[:,oc], hidp.at[1])
    pgot(14, hidp.at[1]); psend(2, ctxT, n2pT)
    slot(5)
    wov = wd.at[pl.ds(0,960)]
    pltpu.make_async_copy(wov,wov,lsem.at[0,1]).wait()
    hid[1,:,384:512] = jnp.zeros((512,128),bf16)
    hid[0] = mm(da[:,0:960], wd[pl.ds(0,512),0:960], NT).astype(bf16)
    hid[1,:,0:448] = mm(da[:,0:960], wd[pl.ds(512,448),0:960], NT).astype(bf16)
    lc.wait(); pgot(2,n2pT)
    G = mm(n2T[...], da[:,mc]) + mm(n2pT[...], hidp[1])
    for qq in range(4):
        for z in range(4): SO[0,qq,z] = G[z*240:(z+1)*240, qq*128:(qq+1)*128].astype(bf16)
    g.c1(5)
    psent(14,2)
    ln = local(n1T, n2T, lsem.at[2,0]); lt = local(tokp, da, lsem.at[2,1])
    acc[...] = jnp.zeros_like(acc)
    for i in range(5):
        def one(h,_): head_bwd(h, qk, k2, v2, bias, lse, hid, acc, dk, dv); return 0
        lax.fori_loop(3*i,3*i+3,one,0)
        slot(6+i)
    first = lanes()<64
    fold = lambda r: r + pltpu.roll(r,64,1)
    nsin = -sin[...]
    def put(half, t, tile): dgu[half, t//4, :, (t%4)*128:(t%4+1)*128] = tile.astype(bf16)
    for t in range(7): put(0,t,rope(acc[:,t*128:(t+1)*128], cos[...], nsin))
    zero = jnp.zeros((512,128),f32)
    put(0,7,zero); put(1,6,zero); put(1,7,zero)
    kk=[fold(dk[i]) for i in range(5)]
    for t,tile in enumerate((jnp.where(first,acc[:,896:1024],kk[0]), jnp.where(first,kk[1],kk[2]), jnp.where(first,kk[3],kk[4]))):
        put(1,t,rope(tile, cos[...], nsin))
    vv=[fold(dv[i]) for i in range(5)]
    for t,tile in enumerate((jnp.where(first,vv[0],vv[1]), jnp.where(first,vv[2],vv[3]), jnp.where(first,vv[4],0.0))):
        put(1,3+t,tile)
    psend(15, dgu.at[1-c], dgup)
    pltpu.make_async_copy(wg,wg,lsem.at[0,0]).wait()
    pgot(15,dgup); psend(3, n1T, n2pT)
    lt.wait()
    gc=None
    for i in range(2):
        rows = pl.ds(256*i,256)
        dn1 = mm(dgu[0,0,rows], wg[0,:,0:512], NT) + mm(dgu[0,1,rows,0:384], wg[0,:,512:896], NT) + mm(dgu[1,0,rows], wg[1,:,0:512], NT) + mm(dgu[1,1,rows,0:256], wg[1,:,512:768], NT)
        dv_, gp = norm_back(da[rows,0:960].astype(f32), g0, dn1)
        tg[rows] = (dacc[rows]+dv_).astype(bf16)
        t_ = mm(gp.astype(bf16), ones, TN)
        gc = t_ if gc is None else gc+t_
    gcol[0] = gc.astype(bf16)
    psend(16, gcol.at[1-c], gcolp)
    ln.wait(); pgot(3,n2pT); pgot(16,gcolp)
    for sub in range(2):
        for qq in range(4):
            t = 2*qq+sub; cs = slice((t%4)*128,(t%4+1)*128)
            if t==7: G = gcol[c].astype(f32)+gcolp[...].astype(f32)
            else: G = mm(n2T[...], dgu[c,t//4,:,cs]) + mm(n2pT[...], dgup[t//4,:,cs])
            for z in range(4): SO[1+sub,qq,z] = G[z*240:(z+1)*240].astype(bf16)
        g.c1(6+sub)
    slot(11)
    for s in range(7, 14): slot(s, 6, 7)
    for i in list(live): psent(i)
    g.finish()
NSM=4
def load_unit2(w, own, W, dst, sem, u0, n, halves=None):
    for k in range(8):
        subs = [(u0, dst, k*128)] if halves is None else [(u0+s*240, halves.at[k//4], (k%4)*256+s*128) for s in range(2)]
        for (r, dd, c0) in subs:
            cs = pl.ds(c0,128)
            pltpu.make_async_copy(own.at[k, pl.ds(r,n)], dd.at[pl.ds(pl.multiple_of(w["z"]*n,16), n), cs], sem).start()
            for d in range(3):
                zs = (w["z"] + 3 - d) % 4
                pltpu.make_async_copy(W.at[k, d, pl.ds(r,n)], dd.at[pl.ds(pl.multiple_of(zs*n,16), n), cs], sem).start()

def k2_call(tok, cot, ids, own, front):
    W, n1T, qk, k2, v2, ctxT, lse, mid, n2, n2T, gains = front
    c, s = tables(ids)
    padc = lambda a: jnp.pad(a, ((0,0),(0,64)))
    S = jax.ShapeDtypeStruct; V = lambda sh, dt=bf16: pltpu.VMEM(sh, dt); Dm=pltpu.SemaphoreType.DMA
    vm = pl.BlockSpec(memory_space=pltpu.VMEM); hb = pl.BlockSpec(memory_space=pl.ANY)
    return pl.pallas_call(k2_kernel, name="back",
      out_shape=[S((512,960),bf16), S((512,960),bf16), S((8,ROWS,128),bf16)],
      in_specs=[vm]*13+[hb]*5, out_specs=[vm,vm,hb],
      scratch_shapes=[V((2,960,1024)), V((1024,1024)), V((512,512)), V((960,512)), V((960,512)), V((512,512)), V((2,512,512)), V((2,2,512,512)),
        V((2,512,512)), V((2,512,512)), V((512,1024)), V((512,1024),f32), V((512,960),f32),
        V((5,512,128),f32), V((5,512,128),f32), V((2,960,128)), V((960,128)),
        V((NSM,4,4,368,128)), V((3,4,4,240,128)), V((2,ROWS,128)), V((2,ROWS,128)), V((4,ROWS,128)), V((4,ROWS,128)), V((3,ROWS,128)),
        Dm((3,2)), Dm((17,)), Dm((17,))]+RSEMS(),
      compiler_params=pltpu.CompilerParams(collective_id=1, has_side_effects=True, vmem_limit_bytes=67043328))(
        padc(cot), c, s, ids[:,None], ids[None,:], qk, k2, v2, lse, mid, n2, n2T, gains, padc(tok), n1T, ctxT, own, W)
def unpack(FIN):
    q = FIN[:, 0:480].reshape(8,2,240,128).transpose(2,0,1,3).reshape(240,2048)
    qkv = jnp.concatenate([q[:, :896], q[:, 1024:1728]], axis=1)
    gains = jnp.stack([q[:, 896], q[:, 1920]])
    out = FIN[:, 480:720].transpose(1,0,2).reshape(240,1024)[:, :960]
    m = FIN[:, 720:].reshape(2,4,5,368,128)
    gu = m[:,:,:,:240].transpose(3,0,1,2,4).reshape(240,5120)
    dn = m[:,:,:,240:].transpose(2,3,0,1,4).reshape(640,1024)[:, :960]
    return [a.astype(f32) for a in (gains, qkv, out, gu, dn)]

def on_device(tokens, sequence_ids, cotangent, norm_gains, qkv_weight, out_weight, gate_up_weight, down_weight, *moments):
    own = pack(norm_gains, qkv_weight, out_weight, gate_up_weight, down_weight)
    front = k1_call(tokens, sequence_ids, own)
    block_out, tokens_grad, packed = k2_call(tokens, cotangent, sequence_ids, own, front)
    grads = unpack(packed)
    weights = (norm_gains, qkv_weight, out_weight, gate_up_weight, down_weight)
    done = [
        adamw_update(weights[i], moments[i], moments[5 + i], grads[i], DECAY_RATE if i else 0.0)
        for i in range(5)
    ]
    return (block_out, tokens_grad, *grads, *[d[0] for d in done], *[d[1] for d in done], *[d[2] for d in done])


def solution(mesh):
    fits = mesh.shape["rep"] == 8 and mesh.shape["fsdp"] == 4
    return jax.shard_map(
        on_device if fits else on_device_any,
        mesh=mesh,
        in_specs=(
            P(("rep", "fsdp"), None),
            P(("rep", "fsdp")),
            P(("rep", "fsdp"), None),
            P(None, "fsdp"),
            P("fsdp", None),
            P("fsdp", None),
            P("fsdp", None),
            P("fsdp", None),
            P(None, "fsdp"),
            P("fsdp", None),
            P("fsdp", None),
            P("fsdp", None),
            P("fsdp", None),
            P(None, "fsdp"),
            P("fsdp", None),
            P("fsdp", None),
            P("fsdp", None),
            P("fsdp", None),
        ),
        out_specs=(
            P(("rep", "fsdp"), None),
            P(("rep", "fsdp"), None),
            P(None, "fsdp"),
            P("fsdp", None),
            P("fsdp", None),
            P("fsdp", None),
            P("fsdp", None),
            P(None, "fsdp"),
            P("fsdp", None),
            P("fsdp", None),
            P("fsdp", None),
            P("fsdp", None),
            P(None, "fsdp"),
            P("fsdp", None),
            P("fsdp", None),
            P("fsdp", None),
            P("fsdp", None),
            P(None, "fsdp"),
            P("fsdp", None),
            P("fsdp", None),
            P("fsdp", None),
            P("fsdp", None),
        ),
        check_vma=False,
    )
```

```python
import math

import jax
import jax.numpy as jnp
from jax import lax
from jax.experimental import pallas as pl
from jax.experimental.pallas import tpu as pltpu
from jax.sharding import PartitionSpec as P
D = 960
HEADS = 15
KV_HEADS = 5
HEAD = 64
FF = 2560
STEP = 4


NORM_EPS = 1e-05
ROPE_BASE = 100000.0
LEARN_RATE = 0.03
BETA_ONE = 0.9
BETA_TWO = 0.95
ADAM_EPS = 1e-08
DECAY_RATE = 0.1
NEG_LARGE = -1e30


def positions(sequence_ids):
    row_index = jnp.arange(sequence_ids.shape[0], dtype=jnp.int32)
    prior_ids = jnp.concatenate([jnp.full((1,), -1, jnp.int32), sequence_ids[:-1]])
    seq_starts = jnp.where(sequence_ids != prior_ids, row_index, 0)
    first_row = lax.cummax(seq_starts, axis=0)
    return (row_index - first_row).astype(jnp.float32)


def causal_mask(sequence_ids):
    row_index = jnp.arange(sequence_ids.shape[0], dtype=jnp.int32)
    return (sequence_ids[:, None] == sequence_ids[None, :]) & (
        row_index[None, :] <= row_index[:, None]
    )


def rope_tables(places):
    half_size = HEAD // 2
    freq_table = ROPE_BASE ** (-2.0 * jnp.arange(half_size, dtype=jnp.float32) / HEAD)
    angles = places[:, None] * freq_table[None, :]
    return (jnp.cos(angles), jnp.sin(angles))


def rotate(vectors, cosine_table, sine_table):
    half_size = vectors.shape[-1] // 2
    first_half = vectors[..., :half_size]
    second_half = vectors[..., half_size:]
    cosine_wide = cosine_table[:, None, :]
    sine_wide = sine_table[:, None, :]
    return jnp.concatenate(
        [
            first_half * cosine_wide - second_half * sine_wide,
            second_half * cosine_wide + first_half * sine_wide,
        ],
        axis=-1,
    )


def rms_norm(values, gain_row):
    row_scale = lax.rsqrt(jnp.mean(values * values, axis=-1, keepdims=True) + NORM_EPS)
    return values * row_scale * gain_row


def swiglu(gate_part, up_part):
    return gate_part * jax.nn.sigmoid(gate_part) * up_part


def adamw_update(weight, moment_one, moment_two, gradient, decay_rate):
    first_new = BETA_ONE * moment_one + (1.0 - BETA_ONE) * gradient
    second_new = BETA_TWO * moment_two + (1.0 - BETA_TWO) * gradient * gradient
    fix_one = 1.0 - BETA_ONE**STEP
    fix_two = 1.0 - BETA_TWO**STEP
    update_dir = (
        first_new / fix_one / (jnp.sqrt(second_new / fix_two) + ADAM_EPS) + decay_rate * weight
    )
    return (-LEARN_RATE * update_dir, first_new, second_new)


def split_groups(queries, keys_rot, values_kv):
    count_rows = queries.shape[0]
    group_size = HEADS // KV_HEADS
    query_groups = queries.reshape(count_rows, KV_HEADS, group_size, HEAD).transpose(1, 2, 0, 3)
    return (query_groups, keys_rot.transpose(1, 0, 2), values_kv.transpose(1, 0, 2))


def attend(queries, keys_rot, values_kv, mask_table):
    count_rows = queries.shape[0]
    scale_factor = 1.0 / math.sqrt(HEAD)
    query_groups, key_groups, value_groups = split_groups(queries, keys_rot, values_kv)

    def one_group(members):
        query_one, key_one, value_one = members
        scores = (
            jnp.einsum("gqd,kd->gqk", query_one, key_one, preferred_element_type=jnp.float32)
            * scale_factor
        )
        scores = jnp.where(mask_table[None], scores, NEG_LARGE)
        top_score = jnp.max(scores, axis=-1, keepdims=True)
        weights = jnp.exp(scores - top_score)
        total_sum = jnp.sum(weights, axis=-1, keepdims=True)
        prob_table = (weights / total_sum).astype(jnp.bfloat16)
        context_one = jnp.einsum(
            "gqk,kd->gqd", prob_table, value_one, preferred_element_type=jnp.float32
        )
        return (context_one.astype(jnp.bfloat16), (top_score + jnp.log(total_sum))[..., 0])

    context_groups, log_total = lax.map(one_group, (query_groups, key_groups, value_groups))
    context = context_groups.transpose(2, 0, 1, 3).reshape(count_rows, HEADS, HEAD)
    return (context, log_total)


def attend_back(queries, keys_rot, values_kv, mask_table, log_total, grad_context):
    count_rows = queries.shape[0]
    group_size = HEADS // KV_HEADS
    scale_factor = 1.0 / math.sqrt(HEAD)
    query_groups, key_groups, value_groups = split_groups(queries, keys_rot, values_kv)
    grad_groups = grad_context.reshape(count_rows, KV_HEADS, group_size, HEAD).transpose(1, 2, 0, 3)

    def one_group(members):
        query_one, key_one, value_one, log_one, grad_one = members
        scores = (
            jnp.einsum("gqd,kd->gqk", query_one, key_one, preferred_element_type=jnp.float32)
            * scale_factor
        )
        scores = jnp.where(mask_table[None], scores, NEG_LARGE)
        prob_table = jnp.exp(scores - log_one[..., None])
        grad_probs = jnp.einsum(
            "gqd,kd->gqk", grad_one, value_one, preferred_element_type=jnp.float32
        )
        grad_value = jnp.einsum(
            "gqk,gqd->kd",
            prob_table.astype(jnp.bfloat16),
            grad_one,
            preferred_element_type=jnp.float32,
        )
        row_delta = jnp.sum(prob_table * grad_probs, axis=-1, keepdims=True)
        grad_scores = (prob_table * (grad_probs - row_delta)).astype(jnp.bfloat16)
        grad_query = (
            jnp.einsum("gqk,kd->gqd", grad_scores, key_one, preferred_element_type=jnp.float32)
            * scale_factor
        )
        grad_key = (
            jnp.einsum("gqk,gqd->kd", grad_scores, query_one, preferred_element_type=jnp.float32)
            * scale_factor
        )
        return (grad_query, grad_key, grad_value)

    grad_q_groups, grad_k_groups, grad_v_groups = lax.map(
        one_group, (query_groups, key_groups, value_groups, log_total, grad_groups)
    )
    grad_queries = grad_q_groups.transpose(2, 0, 1, 3).reshape(count_rows, HEADS, HEAD)
    return (grad_queries, grad_k_groups.transpose(1, 0, 2), grad_v_groups.transpose(1, 0, 2))


def forward(tokens, sequence_ids, attn_set, mlp_set):
    gain_half, qkv_half, out_half = attn_set
    gate_up_half, down_half = mlp_set
    count_rows = tokens.shape[0]
    kv_width = KV_HEADS * HEAD
    inputs = tokens.astype(jnp.float32)
    gain_rows = gain_half.astype(jnp.float32)
    normed = rms_norm(inputs, gain_rows[0]).astype(jnp.bfloat16)
    mixed_cols = jnp.dot(normed, qkv_half, preferred_element_type=jnp.float32)
    cosine_table, sine_table = rope_tables(positions(sequence_ids))
    queries = rotate(
        mixed_cols[:, :D].reshape(count_rows, HEADS, HEAD), cosine_table, sine_table
    ).astype(jnp.bfloat16)
    keys_rot = rotate(
        mixed_cols[:, D : D + kv_width].reshape(count_rows, KV_HEADS, HEAD),
        cosine_table,
        sine_table,
    ).astype(jnp.bfloat16)
    values_kv = (
        mixed_cols[:, D + kv_width :].reshape(count_rows, KV_HEADS, HEAD).astype(jnp.bfloat16)
    )
    context, log_total = attend(queries, keys_rot, values_kv, causal_mask(sequence_ids))
    middle = inputs + jnp.dot(
        context.reshape(count_rows, D), out_half, preferred_element_type=jnp.float32
    )
    normed_two = rms_norm(middle, gain_rows[1]).astype(jnp.bfloat16)
    gate_up = jnp.dot(normed_two, gate_up_half, preferred_element_type=jnp.float32)
    hidden = swiglu(gate_up[:, :FF], gate_up[:, FF:]).astype(jnp.bfloat16)
    result = middle + jnp.dot(hidden, down_half, preferred_element_type=jnp.float32)
    kept_state = (
        inputs,
        normed,
        queries,
        keys_rot,
        values_kv,
        context,
        log_total,
        middle,
        normed_two,
        gate_up,
        hidden,
    )
    return (kept_state, result)


def mlp_backward(kept_state, cotangent, attn_set, mlp_set):
    middle, normed_two, gate_up, hidden = (
        kept_state[7],
        kept_state[8],
        kept_state[9],
        kept_state[10],
    )
    gain_rows = attn_set[0].astype(jnp.float32)
    gate_up_half, down_half = mlp_set
    grad_result = cotangent.astype(jnp.float32)
    grad_branch = grad_result.astype(jnp.bfloat16)
    down_grad = jnp.einsum("rf,rd->fd", hidden, grad_branch, preferred_element_type=jnp.float32)
    grad_hidden = jnp.einsum(
        "rd,fd->rf", grad_branch, down_half, preferred_element_type=jnp.float32
    )
    _, act_back = jax.vjp(swiglu, gate_up[:, :FF], gate_up[:, FF:])
    grad_gate, grad_up = act_back(grad_hidden)
    grad_mix_two = jnp.concatenate([grad_gate, grad_up], axis=1).astype(jnp.bfloat16)
    gate_up_grad = jnp.einsum(
        "rd,rf->df", normed_two, grad_mix_two, preferred_element_type=jnp.float32
    )
    grad_normed_two = jnp.einsum(
        "rf,df->rd", grad_mix_two, gate_up_half, preferred_element_type=jnp.float32
    )
    _, norm_back_two = jax.vjp(rms_norm, middle, gain_rows[1])
    grad_middle_norm, gain_two_grad = norm_back_two(grad_normed_two)
    grad_middle = grad_result + grad_middle_norm
    return ((gate_up_grad, down_grad), (grad_middle, gain_two_grad))


def attn_backward(kept_state, carried, sequence_ids, attn_set):
    inputs, normed, queries, keys_rot, values_kv, context, log_total = kept_state[:7]
    grad_middle, gain_two_grad = carried
    gain_half, qkv_half, out_half = attn_set
    gain_rows = gain_half.astype(jnp.float32)
    count_rows = inputs.shape[0]
    kv_width = KV_HEADS * HEAD
    grad_attn = grad_middle.astype(jnp.bfloat16)
    flat_context = context.reshape(count_rows, D)
    out_grad = jnp.einsum("rc,rd->cd", flat_context, grad_attn, preferred_element_type=jnp.float32)
    grad_context = jnp.einsum("rd,cd->rc", grad_attn, out_half, preferred_element_type=jnp.float32)
    grad_context = grad_context.astype(jnp.bfloat16).reshape(count_rows, HEADS, HEAD)
    grad_queries, grad_keys, grad_values = attend_back(
        queries, keys_rot, values_kv, causal_mask(sequence_ids), log_total, grad_context
    )
    cosine_table, sine_table = rope_tables(positions(sequence_ids))
    grad_q_raw = rotate(grad_queries, cosine_table, -sine_table).reshape(count_rows, D)
    grad_k_raw = rotate(grad_keys, cosine_table, -sine_table).reshape(count_rows, kv_width)
    grad_mixed = jnp.concatenate(
        [grad_q_raw, grad_k_raw, grad_values.reshape(count_rows, kv_width)], axis=1
    )
    grad_mixed = grad_mixed.astype(jnp.bfloat16)
    qkv_grad = jnp.einsum("rd,rc->dc", normed, grad_mixed, preferred_element_type=jnp.float32)
    grad_normed = jnp.einsum("rc,dc->rd", grad_mixed, qkv_half, preferred_element_type=jnp.float32)
    _, norm_back_one = jax.vjp(rms_norm, inputs, gain_rows[0])
    grad_inputs_norm, gain_one_grad = norm_back_one(grad_normed)
    tokens_grad = (grad_middle + grad_inputs_norm).astype(jnp.bfloat16)
    gains_grad = jnp.stack([gain_one_grad, gain_two_grad])
    return (tokens_grad, (gains_grad, qkv_grad, out_grad))


def on_device_any(
    tokens,
    sequence_ids,
    cotangent,
    norm_gains,
    qkv_weight,
    out_weight,
    gate_up_weight,
    down_weight,
    gains_first,
    qkv_first,
    out_first,
    gate_up_first,
    down_first,
    gains_second,
    qkv_second,
    out_second,
    gate_up_second,
    down_second,
):
    shares = lax.axis_size("rep")
    share = lax.axis_index("rep")
    both = ("fsdp", "rep")
    group = lax.axis_size("fsdp")

    def collect(shard):
        flat = shard.astype(jnp.bfloat16).reshape(shares, -1)
        piece = lax.dynamic_index_in_dim(flat, share, 0, keepdims=False)
        whole = lax.all_gather(piece, both, axis=0, tiled=True)
        return whole.reshape(shard.shape[0] * group, shard.shape[1])

    def total(gradient, shard):
        piece = lax.psum_scatter(
            gradient.astype(jnp.bfloat16).reshape(-1), both, scatter_dimension=0, tiled=True
        )
        flat = lax.all_gather(piece, "rep", axis=0, tiled=True)
        return flat.reshape(shard.shape).astype(jnp.float32)

    gain_full = lax.all_gather(norm_gains.astype(jnp.bfloat16), "fsdp", axis=1, tiled=True)
    qkv_full = collect(qkv_weight)
    out_full = collect(out_weight)
    mlp_set = (collect(gate_up_weight), collect(down_weight))
    attn_set = (gain_full, qkv_full, out_full)
    kept_state, result = forward(tokens, sequence_ids, attn_set, mlp_set)
    block_out = result.astype(jnp.bfloat16)
    mlp_grads, carried = mlp_backward(kept_state, cotangent, attn_set, mlp_set)
    down_total = total(mlp_grads[1], down_weight)
    gate_up_total = total(mlp_grads[0], gate_up_weight)
    tokens_grad, attn_grads = attn_backward(kept_state, carried, sequence_ids, attn_set)
    gains_part = lax.psum_scatter(attn_grads[0], "fsdp", scatter_dimension=1, tiled=True)
    gains_total = lax.psum(gains_part, "rep")
    qkv_total = total(attn_grads[1], qkv_weight)
    out_total = total(attn_grads[2], out_weight)
    gains_delta, gains_first_new, gains_second_new = adamw_update(
        norm_gains, gains_first, gains_second, gains_total, 0.0
    )
    qkv_delta, qkv_first_new, qkv_second_new = adamw_update(
        qkv_weight, qkv_first, qkv_second, qkv_total, DECAY_RATE
    )
    out_delta, out_first_new, out_second_new = adamw_update(
        out_weight, out_first, out_second, out_total, DECAY_RATE
    )
    gate_up_delta, gate_up_first_new, gate_up_second_new = adamw_update(
        gate_up_weight, gate_up_first, gate_up_second, gate_up_total, DECAY_RATE
    )
    down_delta, down_first_new, down_second_new = adamw_update(
        down_weight, down_first, down_second, down_total, DECAY_RATE
    )
    return (
        block_out,
        tokens_grad,
        gains_total,
        qkv_total,
        out_total,
        gate_up_total,
        down_total,
        gains_delta,
        qkv_delta,
        out_delta,
        gate_up_delta,
        down_delta,
        gains_first_new,
        qkv_first_new,
        out_first_new,
        gate_up_first_new,
        down_first_new,
        gains_second_new,
        qkv_second_new,
        out_second_new,
        gate_up_second_new,
        down_second_new,
    )


MESH = pl.DeviceIdType.MESH
bf16, f32 = jnp.bfloat16, jnp.float32
ROWS = 2560
GATHER_UNITS = [(0, 240, 128), (240, 240, 128), (480, 240, 128)] + [(720 + 368 * j, 368, 192) for j in range(5)]
REDUCE_UNITS = [(720 + 368 * j, 368, 192) for j in range(5)] + [(480, 240, 128), (0, 240, 128), (240, 240, 128)]
NT = (((1,), (1,)), ((), ()))
NN = (((1,), (0,)), ((), ()))
TN = (((0,), (0,)), ((), ()))


def mm(a, b, dims=NN):
    return lax.dot_general(a, b, dims, preferred_element_type=f32)


def lanes(n=128):
    return lax.broadcasted_iota(jnp.int32, (1, n), 1)


def spread(k):
    return jnp.where(k < 3, k, k - 1)


def param_specs():
    return [
        pl.BlockSpec((2, 240), lambda k: (0, 0)),
        pl.BlockSpec((240, 256), lambda k: (0, spread(k))),
        pl.BlockSpec((240, 128), lambda k: (0, k)),
        pl.BlockSpec((240, 640), lambda k: (0, k)),
        pl.BlockSpec((128, 640), lambda k: (k, 0)),
    ]


def pack_kernel(gains, qkv, out, gu, dnT, own):
    k = pl.program_id(0)
    own[0, 0:240] = qkv[:, 0:128].astype(bf16)
    own[0, 240:480] = qkv[:, 128:256].astype(bf16)

    @pl.when(k % 4 == 3)
    def _():
        row = jnp.where(k == 3, gains[0:1], gains[1:2])
        tile = jnp.where(lax.broadcasted_iota(jnp.int32, (128, 240), 0) == 0, row, 0.0)
        own[0, 240:480] = jnp.swapaxes(tile, 0, 1).astype(bf16)

    own[0, 480:720] = jnp.where(lanes() < 960 - k * 128, out[...], 0.0).astype(bf16)
    for j in range(5):
        own[0, 720 + 368 * j : 960 + 368 * j] = gu[:, j * 128 : (j + 1) * 128].astype(bf16)
        t = jnp.swapaxes(dnT[:, j * 128 : (j + 1) * 128], 0, 1)
        own[0, 960 + 368 * j : 1088 + 368 * j] = jnp.where(lanes() < 960 - k * 128, t, 0.0).astype(bf16)


def pack(norm_gains, qkv, out, gu, down):
    return pl.pallas_call(
        pack_kernel,
        name="pack",
        grid=(8,),
        out_shape=jax.ShapeDtypeStruct((8, ROWS, 128), bf16),
        in_specs=param_specs(),
        out_specs=pl.BlockSpec((1, ROWS, 128), lambda k: (k, 0, 0)),
    )(norm_gains, qkv, out, gu, down.T)


def adam_kernel(FIN, *refs):
    weight, first, second = refs[0:5], refs[5:10], refs[10:15]
    grad, delta, first_new, second_new = refs[15:20], refs[20:25], refs[25:30], refs[30:35]
    k = pl.program_id(0)
    every = slice(None)

    def update(i, at, g, rate):
        m = BETA_ONE * first[i][at] + (1.0 - BETA_ONE) * g
        v = BETA_TWO * second[i][at] + (1.0 - BETA_TWO) * g * g
        step = m * (1.0 / (1.0 - BETA_ONE**STEP)) / (jnp.sqrt(v * (1.0 / (1.0 - BETA_TWO**STEP))) + ADAM_EPS)
        if rate:
            step = step + rate * weight[i][at]
        grad[i][at] = g
        delta[i][at] = -LEARN_RATE * step
        first_new[i][at] = m
        second_new[i][at] = v

    def rows(a, b):
        return FIN[0, a:b].astype(f32)

    @pl.when(k != 3)
    def _():
        update(1, (every, slice(0, 128)), rows(0, 240), DECAY_RATE)
        update(1, (every, slice(128, 256)), rows(240, 480), DECAY_RATE)

    for i in range(2):

        @pl.when(k == 3 + 4 * i)
        def _():
            update(0, (slice(i, i + 1), every), jnp.swapaxes(rows(240, 480), 0, 1)[0:1], 0.0)

    update(2, (every, every), rows(480, 720), DECAY_RATE)
    for j in range(5):
        c = slice(j * 128, (j + 1) * 128)
        update(3, (every, c), rows(720 + 368 * j, 960 + 368 * j), DECAY_RATE)
        update(4, (every, c), jnp.swapaxes(rows(960 + 368 * j, 1088 + 368 * j), 0, 1), DECAY_RATE)


def adam(FIN, weights, moments):
    def five(group):
        return [*group[:4], group[4].T]

    ins = five(weights) + five(moments[:5]) + five(moments[5:])
    shapes = [jax.ShapeDtypeStruct(a.shape, f32) for a in ins[:5]] * 4
    outs = pl.pallas_call(
        adam_kernel,
        name="adam",
        grid=(8,),
        out_shape=shapes,
        in_specs=[pl.BlockSpec((1, ROWS, 128), lambda k: (k, 0, 0))] + param_specs() * 3,
        out_specs=param_specs() * 4,
    )(FIN, *ins)
    return [o.T if i % 5 == 4 else o for i, o in enumerate(outs)]


def tables(ids):
    place = jnp.sum((ids[None, :] < ids[:, None]).astype(f32), axis=1)
    place = jnp.arange(512, dtype=f32) - place
    freq = ROPE_BASE ** (-2.0 * jnp.arange(32, dtype=f32) / 64)
    ang = place[:, None] * freq[None, :]
    c, s = jnp.cos(ang), jnp.sin(ang)
    return jnp.concatenate([c, c, c, c], 1), jnp.concatenate([-s, s, -s, s], 1)


class Where:
    def __init__(w):
        rep, z = lax.axis_index("rep"), lax.axis_index("fsdp")
        c, x, y = rep % 2, (rep // 2) % 2, rep // 4
        w.rep, w.z, w.c, w.x, w.y = rep, z, c, x, y
        w.partner, w.xn, w.yn = {"rep": rep + 1 - 2 * c}, {"rep": rep + 2 - 4 * x}, {"rep": rep + 4 - 8 * y}
        w.zn = [{"fsdp": (z + d) % 4} for d in (1, 2, 3)]
        w.q, w.qx, w.qy, w.qd = y * 2 + x, y * 2 + 1 - x, (1 - y) * 2 + x, (1 - y) * 2 + 1 - x
        w.k, w.kx, w.ky, w.kd = c * 4 + w.q, c * 4 + w.qx, c * 4 + w.qy, c * 4 + w.qd
        o = (1 - c) * 4
        w.kp, w.kpx, w.kpy, w.kpd = o + w.q, o + w.qx, o + w.qy, o + w.qd

    def peers(w):
        return [w.partner, w.xn, w.yn] + w.zn


class Link:
    def __init__(g, w, sems):
        g.w, g.sems, g.sent = w, sems, []

    def copy(g, src, dst, s, r, dev):
        return pltpu.make_async_remote_copy(
            src_ref=src, dst_ref=dst, send_sem=s, recv_sem=r, device_id=dev, device_id_type=MESH
        )

    def send(g, u, i, src, dst, r, dev):
        cp = g.copy(src, dst, g.sems[0].at[u, i], r, dev)
        cp.start()
        g.sent.append((u, cp))

    def got(g, ref, r):
        g.copy(ref, ref, g.sems[0].at[0, 0], r, g.w.partner).wait_recv()

    def finish(g):
        for _, cp in g.sent:
            cp.wait_send()


class Gather(Link):
    def __init__(g, w, own, W, sems):
        super().__init__(w, sems)
        g.own, g.W = own, W
        g.rz, g.rx, g.ry, g.rp = sems[1:]

    def reg(g, k, u, a=0, b=None):
        r0, n, h = GATHER_UNITS[u]
        return g.W.at[k, :, pl.ds(r0 + a, (n if b is None else b) - a)]

    def g0(g, u):
        r0, n, h = GATHER_UNITS[u]
        for d in range(3):
            src = g.own.at[g.w.k, pl.ds(r0, n)]
            g.send(u, d, src, g.W.at[g.w.k, d, pl.ds(r0, n)], g.rz.at[u, d], g.w.zn[d])

    def g1(g, u):
        r0, n, h = GATHER_UNITS[u]
        for d in range(3):
            g.got(g.W.at[g.w.k, d, pl.ds(r0, n)], g.rz.at[u, d])
        b = g.reg(g.w.k, u)
        g.send(u, 3, b, b, g.rx.at[u, 0], g.w.xn)
        g.send(u, 4, b, b, g.ry.at[u, 0], g.w.yn)
        g.send(u, 5, b, b, g.rp.at[u, 0], g.w.partner)

    def g2a(g, u):
        h = GATHER_UNITS[u][2]
        g.got(g.reg(g.w.kx, u), g.rx.at[u, 0])
        b = g.reg(g.w.kx, u, 0, h)
        g.send(u, 6, b, b, g.ry.at[u, 1], g.w.yn)
        b = g.reg(g.w.kx, u)
        g.send(u, 7, b, b, g.rp.at[u, 1], g.w.partner)

    def g2b(g, u):
        h = GATHER_UNITS[u][2]
        g.got(g.reg(g.w.ky, u), g.ry.at[u, 0])
        b = g.reg(g.w.ky, u, h)
        g.send(u, 8, b, b, g.rx.at[u, 1], g.w.xn)
        b = g.reg(g.w.ky, u)
        g.send(u, 9, b, b, g.rp.at[u, 2], g.w.partner)

    def g3(g, u):
        h = GATHER_UNITS[u][2]
        g.got(g.reg(g.w.kd, u, 0, h), g.ry.at[u, 1])
        g.got(g.reg(g.w.kd, u, h), g.rx.at[u, 1])
        b = g.reg(g.w.kd, u)
        g.send(u, 10, b, b, g.rp.at[u, 3], g.w.partner)

    def g4(g, u):
        for i, k in enumerate((g.w.kp, g.w.kpx, g.w.kpy, g.w.kpd)):
            g.got(g.reg(k, u), g.rp.at[u, i])


def add3(*parts):
    t = parts[0].astype(f32)
    for p in parts[1:]:
        t = t + p.astype(f32)
    return t.astype(bf16)


class Reduce(Link):
    def __init__(g, w, S, RX3, RY3, RX, RY, RZ, FIN, sems):
        super().__init__(w, sems)
        g.S, g.RX3, g.RY3, g.RX, g.RY, g.RZ, g.FIN = S, RX3, RY3, RX, RY, RZ, FIN
        g.r3, g.rxy, g.rz, g.rf, g.lf = sems[1:]

    def at(g, u):
        r0, n, h = REDUCE_UNITS[u]
        return pl.ds(r0, n), g.S(u), g.w

    def c1(g, u):
        R, S, w = g.at(u)
        g.send(u, 0, S.at[w.qd, 0:2], g.RX3.at[:, R], g.r3.at[u, 0], w.xn)
        g.send(u, 1, S.at[w.qd, 2:4], g.RY3.at[:, R], g.r3.at[u, 1], w.yn)
        g.send(u, 2, S.at[w.qx, 0:2], g.RX.at[0:2, R], g.rxy.at[u, 0], w.xn)
        g.send(u, 3, S.at[w.qy, 2:4], g.RY.at[2:4, R], g.rxy.at[u, 1], w.yn)

    def c2a(g, u):
        R, S, w = g.at(u)
        g.got(g.RY3.at[:, R], g.r3.at[u, 1])
        S[w.qx, 2:4] = add3(S[w.qx, 2:4], g.RY3[:, R])
        g.send(u, 4, S.at[w.qx, 2:4], g.RX.at[2:4, R], g.rxy.at[u, 2], w.xn)

    def c2b(g, u):
        R, S, w = g.at(u)
        g.got(g.RX3.at[:, R], g.r3.at[u, 0])
        S[w.qy, 0:2] = add3(S[w.qy, 0:2], g.RX3[:, R])
        g.send(u, 5, S.at[w.qy, 0:2], g.RY.at[0:2, R], g.rxy.at[u, 3], w.yn)

    def c3(g, u):
        R, S, w = g.at(u)
        g.got(g.RX.at[0:2, R], g.rxy.at[u, 0])
        g.got(g.RX.at[2:4, R], g.rxy.at[u, 2])
        g.got(g.RY.at[2:4, R], g.rxy.at[u, 1])
        g.got(g.RY.at[0:2, R], g.rxy.at[u, 3])
        S[w.q] = add3(S[w.q], g.RX[:, R], g.RY[:, R])
        for d in range(3):
            zt = (w.z + d + 1) % 4
            g.send(u, 6 + d, S.at[w.q, zt], g.RZ.at[d, R], g.rz.at[u, d], w.zn[d])

    def c4(g, u):
        R, S, w = g.at(u)
        for d in range(3):
            g.got(g.RZ.at[d, R], g.rz.at[u, d])
        S[w.q, w.z] = add3(S[w.q, w.z], g.RZ[0, R], g.RZ[1, R], g.RZ[2, R])
        src, dst = S.at[w.q, w.z], g.FIN.at[w.k, R]
        g.send(u, 9, src, dst, g.rf.at[u, 0], w.xn)
        g.send(u, 10, src, dst, g.rf.at[u, 1], w.yn)
        g.send(u, 11, src, dst, g.rf.at[u, 4], w.partner)
        pltpu.make_async_copy(src, dst, g.lf.at[u]).start()

    def fin(g, k, u, a=0, b=None):
        r0, n, h = REDUCE_UNITS[u]
        return g.FIN.at[k, pl.ds(r0 + a, (n if b is None else b) - a)]

    def c5a(g, u):
        h, w = REDUCE_UNITS[u][2], g.w
        g.got(g.fin(w.kx, u), g.rf.at[u, 0])
        b = g.fin(w.kx, u, 0, h)
        g.send(u, 12, b, b, g.rf.at[u, 3], w.yn)
        b = g.fin(w.kx, u)
        g.send(u, 13, b, b, g.rf.at[u, 5], w.partner)

    def c5b(g, u):
        h, w = REDUCE_UNITS[u][2], g.w
        g.got(g.fin(w.ky, u), g.rf.at[u, 1])
        b = g.fin(w.ky, u, h)
        g.send(u, 14, b, b, g.rf.at[u, 2], w.xn)
        b = g.fin(w.ky, u)
        g.send(u, 15, b, b, g.rf.at[u, 6], w.partner)

    def c6(g, u):
        h, w = REDUCE_UNITS[u][2], g.w
        g.got(g.fin(w.kd, u, 0, h), g.rf.at[u, 3])
        g.got(g.fin(w.kd, u, h), g.rf.at[u, 2])
        b = g.fin(w.kd, u)
        g.send(u, 16, b, b, g.rf.at[u, 7], w.partner)

    def c7(g, u):
        R, S, w = g.at(u)
        for i, k in enumerate((w.kp, w.kpx, w.kpy, w.kpd)):
            g.got(g.fin(k, u), g.rf.at[u, 4 + i])
        pltpu.make_async_copy(S.at[w.q, w.z], g.fin(w.k, u), g.lf.at[u]).wait()


def load_unit(w, own, W, dst, sem, u0, n, row0=0, halves=False):
    def block(k, _):
        def one(r, view, c0):
            def put(src, zs):
                rows = pl.ds(pl.multiple_of(row0 + zs * n, 16), n)
                pltpu.make_async_copy(src, view.at[rows, pl.ds(pl.multiple_of(c0, 128), 128)], sem).start()

            put(own.at[k, pl.ds(r, n)], w.z)
            for d in range(3):
                put(W.at[k, d, pl.ds(r, n)], (w.z + 3 - d) % 4)

        if halves:
            for s in range(2):
                one(u0 + s * n, dst.at[k // 4], (k % 4) * 256 + s * 128)
        else:
            one(u0, dst, k * 128)
        return 0

    lax.fori_loop(0, 8, block, 0)


def rope(t, c, s):
    first = (lanes() % 64) < 32
    return t * c + jnp.where(first, pltpu.roll(t, 96, 1), pltpu.roll(t, 32, 1)) * s


def dup(t, half):
    return jnp.where((lanes() < 64) == (half == 0), t, pltpu.roll(t, 64, 1))


def gain_row(tile):
    at = (lax.broadcasted_iota(jnp.int32, (8, 128), 0) == 0) & (lax.broadcasted_iota(jnp.int32, (8, 128), 1) == 0)
    return mm(at.astype(f32).astype(bf16), tile, NT)[0:1]


def norm(v, g):
    return v * lax.rsqrt(jnp.mean(v * v, axis=1, keepdims=True) + NORM_EPS) * g


def norm_back(v, g, u):
    r = lax.rsqrt(jnp.mean(v * v, axis=1, keepdims=True) + NORM_EPS)
    wv = u * g
    return r * wv - v * (r * r * r) * jnp.mean(wv * v, axis=1, keepdims=True), u * v * r


def head_at(h):
    t, half = h // 2, h % 2
    mine = (lanes() // 64) == half
    return t, h // 3, mine, pl.ds(pl.multiple_of(t * 128, 128), 128)


def head_fwd(h, qk, k2, v2, bias, ctx, lse):
    t, g, mine, col = head_at(h)
    hm = jnp.where(mine, 0.125, 0.0).astype(bf16)
    for i in range(2):
        rows, n = pl.ds(256 * i, 256), 256 * (i + 1)
        s = mm(qk[rows, col] * hm, k2[g, pl.ds(0, n)], NT) + bias[rows, pl.ds(0, n)].astype(f32)
        m = jnp.max(s, axis=1, keepdims=True)
        p = jnp.exp(s - m)
        l = jnp.sum(p, axis=1, keepdims=True)
        o = mm((p * (1.0 / l)).astype(bf16), v2[g, pl.ds(0, n)])
        ctx[rows, col] = jnp.where(mine, o, ctx[rows, col].astype(f32)).astype(bf16)
        lse[rows] = jnp.where(lanes() == h, m + jnp.log(l), lse[rows])


def head_bwd(h, qk, k2, v2, bias, lse, dctx, dq, dk, dv):
    t, g, mine, col = head_at(h)
    hm = jnp.where(mine, 0.125, 0.0).astype(bf16)
    om = jnp.where(mine, 1.0, 0.0).astype(bf16)
    for i in range(2):
        rows, n = pl.ds(256 * i, 256), 256 * (i + 1)
        qs = qk[rows, col] * hm
        do = dctx[t // 4, rows, pl.ds(pl.multiple_of((t % 4) * 128, 128), 128)] * om
        le = jnp.sum(jnp.where(lanes() == h, lse[rows], 0.0), axis=1, keepdims=True)
        s = mm(qs, k2[g, pl.ds(0, n)], NT) + bias[rows, pl.ds(0, n)].astype(f32)
        p = jnp.exp(s - le)
        dp = mm(do, v2[g, pl.ds(0, n)], NT)
        dv[g, pl.ds(0, n)] += mm(p.astype(bf16), do, TN)
        ds = (p * (dp - jnp.sum(p * dp, axis=1, keepdims=True))).astype(bf16)
        dk[g, pl.ds(0, n)] += mm(ds, qs, TN)
        dq[rows, col] = jnp.where(mine, mm(ds, k2[g, pl.ds(0, n)]) * 0.125, dq[rows, col])


KEYS = [(7, 1), (8, 0), (8, 1), (9, 0), (9, 1)]
VALUES = [(10, 0), (10, 1), (11, 0), (11, 1), (12, 0)]


def layer_kernel(
    tokT, cotT, cos, sin, seqc, seqr, own,
    boT, tgT, FIN, W, n1H, ctxH,
    cot, qk, k2, v2, lse, mid, n2, gains,
    wg, wd, bias, n2T, n2pT, cpT, dypp, hid, dgu, hidp, dgup, da, acc, dacc, dk, dv, gcol, gcolp,
    SM, SO, RX3, RY3, RX, RY, RZ,
    lsem, ps, pr, *sems,
):
    w = Where()
    c = w.c
    bar = pltpu.get_barrier_semaphore()
    for p in w.peers():
        pl.semaphore_signal(bar, inc=1, device_id=p, device_id_type=MESH)
    tl = pltpu.make_async_copy(tokT, tgT, lsem.at[0])
    tl.start()
    cl = pltpu.make_async_copy(cotT, boT, lsem.at[1])
    cl.start()
    pl.semaphore_wait(bar, 6)
    ga = Gather(w, own, W, sems[:5])
    re = Reduce(w, lambda u: SM.at[u] if u < 5 else SO.at[u - 5], RX3, RY3, RX, RY, RZ, FIN, sems[5:])
    live, local = {}, {}

    def psend(i, src, dst):
        live[i] = ga.copy(src, dst, ps.at[i], pr.at[i], w.partner)
        live[i].start()

    def psent(*which):
        for i in which:
            live.pop(i).wait_send()

    def pgot(i, dst):
        ga.copy(dst, dst, ps.at[0], pr.at[i], w.partner).wait_recv()

    def begin(name, src, dst, sem):
        local[name] = pltpu.make_async_copy(src, dst, sem)
        local[name].start()

    def end(name):
        local.pop(name).wait()

    other = pl.ds(pl.multiple_of((1 - c) * 512, 512), 512)
    mine = pl.ds(pl.multiple_of(c * 512, 512), 512)
    half_rows = [pl.ds(256 * i, 256) for i in range(2)]

    def A0():
        for i in range(2):
            rows = lax.broadcasted_iota(jnp.int32, (256, 512), 0) + 256 * i
            cols = lax.broadcasted_iota(jnp.int32, (256, 512), 1)
            ok = (seqc[pl.ds(256 * i, 256)] == seqr[...]) & (cols <= rows)
            bias[pl.ds(256 * i, 256)] = jnp.where(ok, 0.0, NEG_LARGE).astype(bf16)
        lse[...] = jnp.zeros_like(lse)
        acc[...] = jnp.zeros_like(acc)
        dacc[...] = jnp.zeros_like(dacc)
        dk[...] = jnp.zeros_like(dk)
        dv[...] = jnp.zeros_like(dv)
        tl.wait()
        cl.wait()
        mid[...] = jnp.swapaxes(tgT[...], 0, 1).astype(f32)
        cot[:, 896:1024] = jnp.zeros((512, 128), bf16)
        cot[:, 0:960] = jnp.swapaxes(boT[...], 0, 1)

    def LQ():
        load_unit(w, own, W, wg, lsem.at[0], 0, 240, halves=True)

    def wait_q():
        pltpu.make_async_copy(wg, wg, lsem.at[0]).wait()

    def LO():
        load_unit(w, own, W, wd, lsem.at[1], 480, 240)

    def wait_o():
        view = wd.at[pl.ds(0, 960)]
        pltpu.make_async_copy(view, view, lsem.at[1]).wait()

    def A1():
        wait_q()
        gains[...] = jnp.zeros_like(gains)
        gains[0:1] = gain_row(wg[0, :, 896:1024])
        gains[1:2] = gain_row(wg[1, :, 896:1024])
        n1 = norm(mid[...], gains[0:1]).astype(bf16)
        da[:, 0:960] = n1
        tgT[...] = jnp.swapaxes(n1, 0, 1)
        for half, (lo, hi) in enumerate(((0, 6), (6, 13))):
            res = mm(da[:, 0:960], wg[half, :, 0 : (hi - lo) * 128])
            for t in range(lo, hi):
                tile = res[:, (t - lo) * 128 : (t - lo + 1) * 128]
                if t < 10:
                    tile = rope(tile, cos[...], sin[...])
                    qk[:, t * 128 : (t + 1) * 128] = tile.astype(bf16)
                for i in range(5):
                    if KEYS[i][0] == t:
                        k2[i] = dup(tile, KEYS[i][1]).astype(bf16)
                    if VALUES[i][0] == t:
                        v2[i] = dup(tile, VALUES[i][1]).astype(bf16)
        begin("n1", tgT, n1H, lsem.at[2])
        da[...] = jnp.zeros_like(da)

    def H(i):
        def one(h, _):
            head_fwd(h, qk, k2, v2, bias, da, lse)
            return 0

        lax.fori_loop(3 * i, 3 * i + 3, one, 0)

    def A3():
        wait_o()
        for rows in half_rows:
            m = mid[rows] + mm(da[rows, 0:960], wd[pl.ds(0, 960), 0:960])
            mid[rows] = m
            n2[rows] = norm(m, gains[1:2]).astype(bf16)
        n2T[...] = jnp.swapaxes(n2[...], 0, 1)
        boT[...] = jnp.swapaxes(da[:, 0:960], 0, 1)
        psend(0, n2T, n2pT)
        psend(1, cot.at[:, other], dypp)
        psend(2, boT, cpT)
        begin("ctx", boT, ctxH, lsem.at[3])

    def dslot(j):
        return pl.ds(((j + 2) % 3) * 512, 512)

    def L(j):
        load_unit(w, own, W, wg.at[j % 2], lsem.at[4 + j % 2], 720 + 368 * j, 240)
        load_unit(w, own, W, wd, lsem.at[6 + j % 2], 960 + 368 * j, 128, row0=((j + 2) % 3) * 512)

    def F(j):
        b = j % 2
        pltpu.make_async_copy(wg.at[b], wg.at[b], lsem.at[4 + b]).wait()
        view = wd.at[dslot(j)]
        pltpu.make_async_copy(view, view, lsem.at[6 + b]).wait()
        if j >= 2:
            psent(4 + j - 2, 9 + j - 2)

        def half(i, _):
            rows = pl.ds(pl.multiple_of(i * 256, 256), 256)
            gu = mm(n2[rows], wg[b])
            gate, up = gu[:, :512], gu[:, 512:]
            sg = jax.nn.sigmoid(gate)
            a = gate * sg
            hb = (a * up).astype(bf16)
            hid[b, rows] = hb
            acc[rows, 0:960] += mm(hb, wd[dslot(j), 0:960])
            dh = mm(cot[rows, 0:960], wd[dslot(j), 0:960], NT)
            dgate = (dh * up * (sg * (1.0 + gate * (1.0 - sg)))).astype(bf16)
            dup_ = (dh * a).astype(bf16)
            dgu[b, 0, rows] = dgate
            dgu[b, 1, rows] = dup_
            dacc[rows] += mm(dgate, wg[b, :, 0:512], NT) + mm(dup_, wg[b, :, 512:1024], NT)
            return 0

        lax.fori_loop(0, 2, half, 0)
        psend(4 + j, hid.at[b], hidp.at[b])
        psend(9 + j, dgu.at[b, 1 - c], dgup.at[b])

    def cut(S, G, n, r0=0):
        for q in range(4):
            for z in range(4):
                S[q, z, r0 : r0 + n] = G[z * n : (z + 1) * n, q * 128 : (q + 1) * 128].astype(bf16)

    def R(j):
        b = j % 2
        if j == 0:
            pgot(0, n2pT)
            pgot(1, dypp)
        pgot(4 + j, hidp.at[b])
        pgot(9 + j, dgup.at[b])
        cut(SM.at[j], mm(n2T[...], dgu[b, c]) + mm(n2pT[...], dgup[b]), 240)
        cut(SM.at[j], mm(hid[b], cot[:, mine], TN) + mm(hidp[b], dypp[...], TN), 128, 240)

    def B1():
        psent(7, 8, 12, 13, 0, 1, 2)
        LO()
        LQ()
        end("ctx")
        begin("ctxT", ctxH, n2T, lsem.at[3])
        ones = jnp.ones((256, 128), bf16)
        da[:, 896:1024] = jnp.zeros((512, 128), bf16)
        gc = 0.0
        for i, rows in enumerate(half_rows):
            m = mid[rows]
            boT[:, 256 * i : 256 * (i + 1)] = jnp.swapaxes((m + acc[rows, 0:960]).astype(bf16), 0, 1)
            dv_, gp = norm_back(m, gains[1:2], dacc[rows])
            dmid = cot[rows, 0:960].astype(f32) + dv_
            dacc[rows] = dmid
            da[rows, 0:960] = dmid.astype(bf16)
            gc = gc + mm(gp.astype(bf16), ones, TN)
        gcol[1] = gc.astype(bf16)
        psend(14, da.at[:, other], hidp.at[1])

    def B2():
        wait_o()
        hid[1, :, 384:512] = jnp.zeros((512, 128), bf16)
        hid[0] = mm(da[:, 0:960], wd[pl.ds(0, 512), 0:960], NT).astype(bf16)
        hid[1, :, 0:448] = mm(da[:, 0:960], wd[pl.ds(512, 448), 0:960], NT).astype(bf16)
        end("ctxT")
        pgot(2, cpT)
        pgot(14, hidp.at[1])
        end("n1")
        psend(3, n1H, n2pT)
        cut(SO.at[0], mm(n2T[...], da[:, mine]) + mm(cpT[...], hidp[1]), 240)
        acc[...] = jnp.zeros_like(acc)
        psent(14)
        begin("n1T", n1H, n2T, lsem.at[2])
        begin("tok", tokT, tgT, lsem.at[3])

    def K(i):
        def one(h, _):
            head_bwd(h, qk, k2, v2, bias, lse, hid, acc, dk, dv)
            return 0

        lax.fori_loop(3 * i, 3 * i + 3, one, 0)

    def D1():
        def put(half, t, tile):
            dgu[half, t // 4, :, (t % 4) * 128 : (t % 4 + 1) * 128] = tile.astype(bf16)

        first = lanes() < 64
        nsin = -sin[...]

        def fold(ref, i):
            return ref[i] + pltpu.roll(ref[i], 64, 1)

        for t in range(7):
            put(t // 6, t % 6, rope(acc[:, t * 128 : (t + 1) * 128], cos[...], nsin))
        zero = jnp.zeros((512, 128), f32)
        for half, t in ((0, 6), (0, 7), (1, 7)):
            put(half, t, zero)
        kk, vv = [fold(dk, i) for i in range(5)], [fold(dv, i) for i in range(5)]
        put(1, 1, rope(jnp.where(first, acc[:, 896:1024], kk[0]), cos[...], nsin))
        put(1, 2, rope(jnp.where(first, kk[1], kk[2]), cos[...], nsin))
        put(1, 3, rope(jnp.where(first, kk[3], kk[4]), cos[...], nsin))
        put(1, 4, jnp.where(first, vv[0], vv[1]))
        put(1, 5, jnp.where(first, vv[2], vv[3]))
        put(1, 6, jnp.where(first, vv[4], 0.0))
        psend(15, dgu.at[1 - c], dgup)

    def qgrad(sub):
        for q in range(4):
            t = 2 * q + sub
            if t == 7:
                G = gcol[c].astype(f32) + gcolp[...].astype(f32)
            else:
                at = slice((t % 4) * 128, (t % 4 + 1) * 128)
                G = mm(n2T[...], dgu[c, t // 4, :, at]) + mm(n2pT[...], dgup[t // 4, :, at])
            for z in range(4):
                SO[1 + sub, q, z] = G[z * 240 : (z + 1) * 240].astype(bf16)

    def D2():
        end("n1T")
        pgot(3, n2pT)
        pgot(15, dgup)
        qgrad(0)

    def D3():
        wait_q()
        end("tok")
        da[:, 0:960] = jnp.swapaxes(tgT[...], 0, 1)
        ones = jnp.ones((256, 128), bf16)
        gc = 0.0
        for i, rows in enumerate(half_rows):
            dn1 = mm(dgu[0, 0, rows], wg[0, :, 0:512], NT) + mm(dgu[0, 1, rows, 0:256], wg[0, :, 512:768], NT)
            dn1 += mm(dgu[1, 0, rows], wg[1, :, 0:512], NT) + mm(dgu[1, 1, rows, 0:384], wg[1, :, 512:896], NT)
            dv_, gp = norm_back(da[rows, 0:960].astype(f32), gains[0:1], dn1)
            tgT[:, 256 * i : 256 * (i + 1)] = jnp.swapaxes((dacc[rows] + dv_).astype(bf16), 0, 1)
            gc = gc + mm(gp.astype(bf16), ones, TN)
        gcol[0] = gc.astype(bf16)
        psend(16, gcol.at[1 - c], gcolp)

    def D4():
        pgot(16, gcolp)
        qgrad(1)

    steps = dict(A0=A0, LQ=LQ, A1=A1, LO=LO, H=H, A3=A3, L=L, F=F, R=R, B1=B1, B2=B2, K=K, D1=D1, D2=D2, D3=D3, D4=D4)
    for name, at in PROGRAM:
        if name in steps:
            steps[name](*([] if at is None else [at]))
        else:
            getattr(ga if name[0] == "g" else re, name)(at)
    for i in list(live):
        psent(i)
    ga.finish()
    re.finish()


def layer(tok, cot, ids, own):
    c, s = tables(ids)
    S, D = jax.ShapeDtypeStruct, pltpu.SemaphoreType.DMA

    def V(*shape, dt=bf16):
        return pltpu.VMEM(shape, dt)

    vm = pl.BlockSpec(memory_space=pltpu.VMEM)
    hb = pl.BlockSpec(memory_space=pl.ANY)
    outs = pl.pallas_call(
        layer_kernel,
        name="layer",
        out_shape=[
            S((960, 512), bf16), S((960, 512), bf16), S((8, ROWS, 128), bf16),
            S((8, 3, ROWS, 128), bf16), S((960, 512), bf16), S((960, 512), bf16),
        ],
        in_specs=[hb, hb, vm, vm, vm, vm, hb],
        out_specs=[vm, vm, hb, hb, hb, hb],
        scratch_shapes=[
            V(512, 1024), V(512, 1280), V(5, 512, 128), V(5, 512, 128), V(512, 128, dt=f32), V(512, 960, dt=f32),
            V(512, 960), V(8, 960, dt=f32),
            V(2, 960, 1024), V(1536, 1024), V(512, 512), V(960, 512), V(960, 512), V(960, 512), V(512, 512),
            V(2, 512, 512), V(2, 2, 512, 512), V(2, 512, 512), V(2, 512, 512), V(512, 1024),
            V(512, 1024, dt=f32), V(512, 960, dt=f32), V(5, 512, 128, dt=f32), V(5, 512, 128, dt=f32),
            V(2, 960, 128), V(960, 128),
            V(5, 4, 4, 368, 128), V(3, 4, 4, 240, 128),
            V(2, ROWS, 128), V(2, ROWS, 128), V(4, ROWS, 128), V(4, ROWS, 128), V(3, ROWS, 128),
            D((8,)), D((17,)), D((17,)),
            D((8, 11)), D((8, 3)), D((8, 2)), D((8, 2)), D((8, 4)),
            D((8, 17)), D((8, 2)), D((8, 4)), D((8, 3)), D((8, 8)), D((8,)),
        ],
        compiler_params=pltpu.CompilerParams(
            collective_id=0, has_side_effects=True, vmem_limit_bytes=67043328
        ),
    )(tok.T, cot.T, c, s, ids[:, None], ids[None, :], own)
    return outs[:3]


PROGRAM = [
    ("g0", 0), ("g0", 1), ("g0", 2), ("g0", 3), ("A0", None), ("g1", 0), ("g0", 4), ("g1", 1), ("g0", 5),
    ("g2a", 0), ("g2b", 0), ("g1", 2), ("g0", 6), ("g2a", 1), ("g2b", 1), ("g3", 0), ("g4", 0), ("g2a", 2),
    ("g2b", 2), ("g1", 3), ("g0", 7), ("g3", 1), ("g4", 1), ("LQ", None), ("g3", 2), ("g4", 2), ("LO", None),
    ("g1", 4), ("A1", None), ("g2a", 3), ("g2b", 3), ("H", 0), ("g2a", 4), ("g2b", 4), ("g1", 5), ("H", 1),
    ("g3", 3), ("H", 2), ("g3", 4), ("g1", 6), ("g4", 3), ("L", 0), ("H", 3), ("g4", 4), ("H", 4), ("g2a", 5),
    ("g2b", 5), ("A3", None), ("L", 1), ("g1", 7), ("F", 0), ("g3", 5), ("g2a", 6), ("g2b", 6), ("R", 0),
    ("c1", 0), ("g4", 5), ("L", 2), ("F", 1), ("g3", 6), ("g2a", 7), ("g2b", 7), ("R", 1), ("c2a", 0),
    ("c2b", 0), ("c1", 1), ("g4", 6), ("L", 3), ("F", 2), ("R", 2), ("g3", 7), ("c1", 2), ("F", 3), ("c3", 0),
    ("c2a", 1), ("c2b", 1), ("g4", 7), ("L", 4), ("R", 3), ("c1", 3), ("F", 4), ("c2a", 2), ("c2b", 2),
    ("R", 4), ("c4", 0), ("c1", 4), ("B1", None), ("c3", 1), ("B2", None), ("c2a", 3), ("c2b", 3), ("c1", 5),
    ("K", 0), ("K", 1), ("c4", 1), ("c5a", 0), ("c3", 2), ("K", 2), ("c5b", 0), ("c2b", 4), ("c2a", 4),
    ("K", 3), ("K", 4), ("c4", 2), ("c3", 3), ("D1", None), ("c2a", 5), ("c2b", 5), ("D2", None), ("c5a", 1),
    ("c1", 6), ("D3", None), ("c6", 0), ("c5b", 1), ("D4", None), ("c1", 7), ("c4", 3), ("c3", 4), ("c5a", 2),
    ("c7", 0), ("c5b", 2), ("c3", 5), ("c2b", 6), ("c2a", 6), ("c6", 1), ("c7", 1), ("c4", 4), ("c2b", 7),
    ("c2a", 7), ("c5a", 3), ("c4", 5), ("c5b", 3), ("c6", 2), ("c7", 2), ("c3", 6), ("c5a", 4), ("c5b", 4),
    ("c3", 7), ("c5a", 5), ("c6", 3), ("c7", 3), ("c5b", 5), ("c6", 4), ("c4", 6), ("c7", 4), ("c6", 5),
    ("c7", 5), ("c5a", 6), ("c5b", 6), ("c4", 7), ("c6", 6), ("c7", 6), ("c5a", 7), ("c5b", 7), ("c6", 7),
    ("c7", 7),
]


def on_device(tokens, sequence_ids, cotangent, norm_gains, qkv_weight, out_weight, gate_up_weight, down_weight, *moments):
    weights = (norm_gains, qkv_weight, out_weight, gate_up_weight, down_weight)
    block_out, tokens_grad, packed = layer(tokens, cotangent, sequence_ids, pack(*weights))
    return (block_out.T, tokens_grad.T, *adam(packed, weights, moments))


def solution(mesh):
    fits = mesh.shape["rep"] == 8 and mesh.shape["fsdp"] == 4
    return jax.shard_map(
        on_device if fits else on_device_any,
        mesh=mesh,
        in_specs=(
            P(("rep", "fsdp"), None),
            P(("rep", "fsdp")),
            P(("rep", "fsdp"), None),
            P(None, "fsdp"),
            P("fsdp", None),
            P("fsdp", None),
            P("fsdp", None),
            P("fsdp", None),
            P(None, "fsdp"),
            P("fsdp", None),
            P("fsdp", None),
            P("fsdp", None),
            P("fsdp", None),
            P(None, "fsdp"),
            P("fsdp", None),
            P("fsdp", None),
            P("fsdp", None),
            P("fsdp", None),
        ),
        out_specs=(
            P(("rep", "fsdp"), None),
            P(("rep", "fsdp"), None),
            P(None, "fsdp"),
            P("fsdp", None),
            P("fsdp", None),
            P("fsdp", None),
            P("fsdp", None),
            P(None, "fsdp"),
            P("fsdp", None),
            P("fsdp", None),
            P("fsdp", None),
            P("fsdp", None),
            P(None, "fsdp"),
            P("fsdp", None),
            P("fsdp", None),
            P("fsdp", None),
            P("fsdp", None),
            P(None, "fsdp"),
            P("fsdp", None),
            P("fsdp", None),
            P("fsdp", None),
            P("fsdp", None),
        ),
        check_vma=False,
    )
```

```python
import math

import jax
import jax.numpy as jnp
from jax import lax
from jax.experimental import pallas as pl
from jax.experimental.pallas import tpu as pltpu
from jax.sharding import PartitionSpec as P
D = 960
HEADS = 15
KV_HEADS = 5
HEAD = 64
FF = 2560
STEP = 4


NORM_EPS = 1e-05
ROPE_BASE = 100000.0
LEARN_RATE = 0.03
BETA_ONE = 0.9
BETA_TWO = 0.95
ADAM_EPS = 1e-08
DECAY_RATE = 0.1
NEG_LARGE = -1e30


def positions(sequence_ids):
    row_index = jnp.arange(sequence_ids.shape[0], dtype=jnp.int32)
    prior_ids = jnp.concatenate([jnp.full((1,), -1, jnp.int32), sequence_ids[:-1]])
    seq_starts = jnp.where(sequence_ids != prior_ids, row_index, 0)
    first_row = lax.cummax(seq_starts, axis=0)
    return (row_index - first_row).astype(jnp.float32)


def causal_mask(sequence_ids):
    row_index = jnp.arange(sequence_ids.shape[0], dtype=jnp.int32)
    return (sequence_ids[:, None] == sequence_ids[None, :]) & (
        row_index[None, :] <= row_index[:, None]
    )


def rope_tables(places):
    half_size = HEAD // 2
    freq_table = ROPE_BASE ** (-2.0 * jnp.arange(half_size, dtype=jnp.float32) / HEAD)
    angles = places[:, None] * freq_table[None, :]
    return (jnp.cos(angles), jnp.sin(angles))


def rotate(vectors, cosine_table, sine_table):
    half_size = vectors.shape[-1] // 2
    first_half = vectors[..., :half_size]
    second_half = vectors[..., half_size:]
    cosine_wide = cosine_table[:, None, :]
    sine_wide = sine_table[:, None, :]
    return jnp.concatenate(
        [
            first_half * cosine_wide - second_half * sine_wide,
            second_half * cosine_wide + first_half * sine_wide,
        ],
        axis=-1,
    )


def rms_norm(values, gain_row):
    row_scale = lax.rsqrt(jnp.mean(values * values, axis=-1, keepdims=True) + NORM_EPS)
    return values * row_scale * gain_row


def swiglu(gate_part, up_part):
    return gate_part * jax.nn.sigmoid(gate_part) * up_part


def adamw_update(weight, moment_one, moment_two, gradient, decay_rate):
    first_new = BETA_ONE * moment_one + (1.0 - BETA_ONE) * gradient
    second_new = BETA_TWO * moment_two + (1.0 - BETA_TWO) * gradient * gradient
    fix_one = 1.0 - BETA_ONE**STEP
    fix_two = 1.0 - BETA_TWO**STEP
    update_dir = (
        first_new / fix_one / (jnp.sqrt(second_new / fix_two) + ADAM_EPS) + decay_rate * weight
    )
    return (-LEARN_RATE * update_dir, first_new, second_new)


def split_groups(queries, keys_rot, values_kv):
    count_rows = queries.shape[0]
    group_size = HEADS // KV_HEADS
    query_groups = queries.reshape(count_rows, KV_HEADS, group_size, HEAD).transpose(1, 2, 0, 3)
    return (query_groups, keys_rot.transpose(1, 0, 2), values_kv.transpose(1, 0, 2))


def attend(queries, keys_rot, values_kv, mask_table):
    count_rows = queries.shape[0]
    scale_factor = 1.0 / math.sqrt(HEAD)
    query_groups, key_groups, value_groups = split_groups(queries, keys_rot, values_kv)

    def one_group(members):
        query_one, key_one, value_one = members
        scores = (
            jnp.einsum("gqd,kd->gqk", query_one, key_one, preferred_element_type=jnp.float32)
            * scale_factor
        )
        scores = jnp.where(mask_table[None], scores, NEG_LARGE)
        top_score = jnp.max(scores, axis=-1, keepdims=True)
        weights = jnp.exp(scores - top_score)
        total_sum = jnp.sum(weights, axis=-1, keepdims=True)
        prob_table = (weights / total_sum).astype(jnp.bfloat16)
        context_one = jnp.einsum(
            "gqk,kd->gqd", prob_table, value_one, preferred_element_type=jnp.float32
        )
        return (context_one.astype(jnp.bfloat16), (top_score + jnp.log(total_sum))[..., 0])

    context_groups, log_total = lax.map(one_group, (query_groups, key_groups, value_groups))
    context = context_groups.transpose(2, 0, 1, 3).reshape(count_rows, HEADS, HEAD)
    return (context, log_total)


def attend_back(queries, keys_rot, values_kv, mask_table, log_total, grad_context):
    count_rows = queries.shape[0]
    group_size = HEADS // KV_HEADS
    scale_factor = 1.0 / math.sqrt(HEAD)
    query_groups, key_groups, value_groups = split_groups(queries, keys_rot, values_kv)
    grad_groups = grad_context.reshape(count_rows, KV_HEADS, group_size, HEAD).transpose(1, 2, 0, 3)

    def one_group(members):
        query_one, key_one, value_one, log_one, grad_one = members
        scores = (
            jnp.einsum("gqd,kd->gqk", query_one, key_one, preferred_element_type=jnp.float32)
            * scale_factor
        )
        scores = jnp.where(mask_table[None], scores, NEG_LARGE)
        prob_table = jnp.exp(scores - log_one[..., None])
        grad_probs = jnp.einsum(
            "gqd,kd->gqk", grad_one, value_one, preferred_element_type=jnp.float32
        )
        grad_value = jnp.einsum(
            "gqk,gqd->kd",
            prob_table.astype(jnp.bfloat16),
            grad_one,
            preferred_element_type=jnp.float32,
        )
        row_delta = jnp.sum(prob_table * grad_probs, axis=-1, keepdims=True)
        grad_scores = (prob_table * (grad_probs - row_delta)).astype(jnp.bfloat16)
        grad_query = (
            jnp.einsum("gqk,kd->gqd", grad_scores, key_one, preferred_element_type=jnp.float32)
            * scale_factor
        )
        grad_key = (
            jnp.einsum("gqk,gqd->kd", grad_scores, query_one, preferred_element_type=jnp.float32)
            * scale_factor
        )
        return (grad_query, grad_key, grad_value)

    grad_q_groups, grad_k_groups, grad_v_groups = lax.map(
        one_group, (query_groups, key_groups, value_groups, log_total, grad_groups)
    )
    grad_queries = grad_q_groups.transpose(2, 0, 1, 3).reshape(count_rows, HEADS, HEAD)
    return (grad_queries, grad_k_groups.transpose(1, 0, 2), grad_v_groups.transpose(1, 0, 2))


def forward(tokens, sequence_ids, attn_set, mlp_set):
    gain_half, qkv_half, out_half = attn_set
    gate_up_half, down_half = mlp_set
    count_rows = tokens.shape[0]
    kv_width = KV_HEADS * HEAD
    inputs = tokens.astype(jnp.float32)
    gain_rows = gain_half.astype(jnp.float32)
    normed = rms_norm(inputs, gain_rows[0]).astype(jnp.bfloat16)
    mixed_cols = jnp.dot(normed, qkv_half, preferred_element_type=jnp.float32)
    cosine_table, sine_table = rope_tables(positions(sequence_ids))
    queries = rotate(
        mixed_cols[:, :D].reshape(count_rows, HEADS, HEAD), cosine_table, sine_table
    ).astype(jnp.bfloat16)
    keys_rot = rotate(
        mixed_cols[:, D : D + kv_width].reshape(count_rows, KV_HEADS, HEAD),
        cosine_table,
        sine_table,
    ).astype(jnp.bfloat16)
    values_kv = (
        mixed_cols[:, D + kv_width :].reshape(count_rows, KV_HEADS, HEAD).astype(jnp.bfloat16)
    )
    context, log_total = attend(queries, keys_rot, values_kv, causal_mask(sequence_ids))
    middle = inputs + jnp.dot(
        context.reshape(count_rows, D), out_half, preferred_element_type=jnp.float32
    )
    normed_two = rms_norm(middle, gain_rows[1]).astype(jnp.bfloat16)
    gate_up = jnp.dot(normed_two, gate_up_half, preferred_element_type=jnp.float32)
    hidden = swiglu(gate_up[:, :FF], gate_up[:, FF:]).astype(jnp.bfloat16)
    result = middle + jnp.dot(hidden, down_half, preferred_element_type=jnp.float32)
    kept_state = (
        inputs,
        normed,
        queries,
        keys_rot,
        values_kv,
        context,
        log_total,
        middle,
        normed_two,
        gate_up,
        hidden,
    )
    return (kept_state, result)


def mlp_backward(kept_state, cotangent, attn_set, mlp_set):
    middle, normed_two, gate_up, hidden = (
        kept_state[7],
        kept_state[8],
        kept_state[9],
        kept_state[10],
    )
    gain_rows = attn_set[0].astype(jnp.float32)
    gate_up_half, down_half = mlp_set
    grad_result = cotangent.astype(jnp.float32)
    grad_branch = grad_result.astype(jnp.bfloat16)
    down_grad = jnp.einsum("rf,rd->fd", hidden, grad_branch, preferred_element_type=jnp.float32)
    grad_hidden = jnp.einsum(
        "rd,fd->rf", grad_branch, down_half, preferred_element_type=jnp.float32
    )
    _, act_back = jax.vjp(swiglu, gate_up[:, :FF], gate_up[:, FF:])
    grad_gate, grad_up = act_back(grad_hidden)
    grad_mix_two = jnp.concatenate([grad_gate, grad_up], axis=1).astype(jnp.bfloat16)
    gate_up_grad = jnp.einsum(
        "rd,rf->df", normed_two, grad_mix_two, preferred_element_type=jnp.float32
    )
    grad_normed_two = jnp.einsum(
        "rf,df->rd", grad_mix_two, gate_up_half, preferred_element_type=jnp.float32
    )
    _, norm_back_two = jax.vjp(rms_norm, middle, gain_rows[1])
    grad_middle_norm, gain_two_grad = norm_back_two(grad_normed_two)
    grad_middle = grad_result + grad_middle_norm
    return ((gate_up_grad, down_grad), (grad_middle, gain_two_grad))


def attn_backward(kept_state, carried, sequence_ids, attn_set):
    inputs, normed, queries, keys_rot, values_kv, context, log_total = kept_state[:7]
    grad_middle, gain_two_grad = carried
    gain_half, qkv_half, out_half = attn_set
    gain_rows = gain_half.astype(jnp.float32)
    count_rows = inputs.shape[0]
    kv_width = KV_HEADS * HEAD
    grad_attn = grad_middle.astype(jnp.bfloat16)
    flat_context = context.reshape(count_rows, D)
    out_grad = jnp.einsum("rc,rd->cd", flat_context, grad_attn, preferred_element_type=jnp.float32)
    grad_context = jnp.einsum("rd,cd->rc", grad_attn, out_half, preferred_element_type=jnp.float32)
    grad_context = grad_context.astype(jnp.bfloat16).reshape(count_rows, HEADS, HEAD)
    grad_queries, grad_keys, grad_values = attend_back(
        queries, keys_rot, values_kv, causal_mask(sequence_ids), log_total, grad_context
    )
    cosine_table, sine_table = rope_tables(positions(sequence_ids))
    grad_q_raw = rotate(grad_queries, cosine_table, -sine_table).reshape(count_rows, D)
    grad_k_raw = rotate(grad_keys, cosine_table, -sine_table).reshape(count_rows, kv_width)
    grad_mixed = jnp.concatenate(
        [grad_q_raw, grad_k_raw, grad_values.reshape(count_rows, kv_width)], axis=1
    )
    grad_mixed = grad_mixed.astype(jnp.bfloat16)
    qkv_grad = jnp.einsum("rd,rc->dc", normed, grad_mixed, preferred_element_type=jnp.float32)
    grad_normed = jnp.einsum("rc,dc->rd", grad_mixed, qkv_half, preferred_element_type=jnp.float32)
    _, norm_back_one = jax.vjp(rms_norm, inputs, gain_rows[0])
    grad_inputs_norm, gain_one_grad = norm_back_one(grad_normed)
    tokens_grad = (grad_middle + grad_inputs_norm).astype(jnp.bfloat16)
    gains_grad = jnp.stack([gain_one_grad, gain_two_grad])
    return (tokens_grad, (gains_grad, qkv_grad, out_grad))


def on_device_any(
    tokens,
    sequence_ids,
    cotangent,
    norm_gains,
    qkv_weight,
    out_weight,
    gate_up_weight,
    down_weight,
    gains_first,
    qkv_first,
    out_first,
    gate_up_first,
    down_first,
    gains_second,
    qkv_second,
    out_second,
    gate_up_second,
    down_second,
):
    shares = lax.axis_size("rep")
    share = lax.axis_index("rep")
    both = ("fsdp", "rep")
    group = lax.axis_size("fsdp")

    def collect(shard):
        flat = shard.astype(jnp.bfloat16).reshape(shares, -1)
        piece = lax.dynamic_index_in_dim(flat, share, 0, keepdims=False)
        whole = lax.all_gather(piece, both, axis=0, tiled=True)
        return whole.reshape(shard.shape[0] * group, shard.shape[1])

    def total(gradient, shard):
        piece = lax.psum_scatter(
            gradient.astype(jnp.bfloat16).reshape(-1), both, scatter_dimension=0, tiled=True
        )
        flat = lax.all_gather(piece, "rep", axis=0, tiled=True)
        return flat.reshape(shard.shape).astype(jnp.float32)

    gain_full = lax.all_gather(norm_gains.astype(jnp.bfloat16), "fsdp", axis=1, tiled=True)
    qkv_full = collect(qkv_weight)
    out_full = collect(out_weight)
    mlp_set = (collect(gate_up_weight), collect(down_weight))
    attn_set = (gain_full, qkv_full, out_full)
    kept_state, result = forward(tokens, sequence_ids, attn_set, mlp_set)
    block_out = result.astype(jnp.bfloat16)
    mlp_grads, carried = mlp_backward(kept_state, cotangent, attn_set, mlp_set)
    down_total = total(mlp_grads[1], down_weight)
    gate_up_total = total(mlp_grads[0], gate_up_weight)
    tokens_grad, attn_grads = attn_backward(kept_state, carried, sequence_ids, attn_set)
    gains_part = lax.psum_scatter(attn_grads[0], "fsdp", scatter_dimension=1, tiled=True)
    gains_total = lax.psum(gains_part, "rep")
    qkv_total = total(attn_grads[1], qkv_weight)
    out_total = total(attn_grads[2], out_weight)
    gains_delta, gains_first_new, gains_second_new = adamw_update(
        norm_gains, gains_first, gains_second, gains_total, 0.0
    )
    qkv_delta, qkv_first_new, qkv_second_new = adamw_update(
        qkv_weight, qkv_first, qkv_second, qkv_total, DECAY_RATE
    )
    out_delta, out_first_new, out_second_new = adamw_update(
        out_weight, out_first, out_second, out_total, DECAY_RATE
    )
    gate_up_delta, gate_up_first_new, gate_up_second_new = adamw_update(
        gate_up_weight, gate_up_first, gate_up_second, gate_up_total, DECAY_RATE
    )
    down_delta, down_first_new, down_second_new = adamw_update(
        down_weight, down_first, down_second, down_total, DECAY_RATE
    )
    return (
        block_out,
        tokens_grad,
        gains_total,
        qkv_total,
        out_total,
        gate_up_total,
        down_total,
        gains_delta,
        qkv_delta,
        out_delta,
        gate_up_delta,
        down_delta,
        gains_first_new,
        qkv_first_new,
        out_first_new,
        gate_up_first_new,
        down_first_new,
        gains_second_new,
        qkv_second_new,
        out_second_new,
        gate_up_second_new,
        down_second_new,
    )


MESH = pl.DeviceIdType.MESH
bf16, f32 = jnp.bfloat16, jnp.float32
ROWS = 2560
GATHER_UNITS = [(0, 240, 128), (240, 240, 128), (480, 240, 128)] + [(720 + 368 * j, 368, 192) for j in range(5)]
REDUCE_UNITS = [(720 + 368 * j, 368, 192) for j in range(5)] + [(480, 240, 128), (0, 240, 128), (240, 240, 128)]
NT = (((1,), (1,)), ((), ()))
NN = (((1,), (0,)), ((), ()))
TN = (((0,), (0,)), ((), ()))


def mm(a, b, dims=NN):
    return lax.dot_general(a, b, dims, preferred_element_type=f32)


def lanes(n=128):
    return lax.broadcasted_iota(jnp.int32, (1, n), 1)


def spread(k):
    return jnp.where(k < 3, k, k - 1)


def param_specs():
    return [
        pl.BlockSpec((2, 240), lambda k: (0, 0)),
        pl.BlockSpec((240, 256), lambda k: (0, spread(k))),
        pl.BlockSpec((240, 128), lambda k: (0, k)),
        pl.BlockSpec((240, 640), lambda k: (0, k)),
        pl.BlockSpec((128, 640), lambda k: (k, 0)),
    ]


def pack_kernel(gains, qkv, out, gu, dnT, own):
    k = pl.program_id(0)
    own[0, 0:240] = qkv[:, 0:128].astype(bf16)
    own[0, 240:480] = qkv[:, 128:256].astype(bf16)

    @pl.when(k % 4 == 3)
    def _():
        row = jnp.where(k == 3, gains[0:1], gains[1:2])
        tile = jnp.where(lax.broadcasted_iota(jnp.int32, (128, 240), 0) == 0, row, 0.0)
        own[0, 240:480] = jnp.swapaxes(tile, 0, 1).astype(bf16)

    own[0, 480:720] = jnp.where(lanes() < 960 - k * 128, out[...], 0.0).astype(bf16)
    for j in range(5):
        own[0, 720 + 368 * j : 960 + 368 * j] = gu[:, j * 128 : (j + 1) * 128].astype(bf16)
        t = jnp.swapaxes(dnT[:, j * 128 : (j + 1) * 128], 0, 1)
        own[0, 960 + 368 * j : 1088 + 368 * j] = jnp.where(lanes() < 960 - k * 128, t, 0.0).astype(bf16)


def pack(norm_gains, qkv, out, gu, down):
    return pl.pallas_call(
        pack_kernel,
        name="pack",
        grid=(8,),
        out_shape=jax.ShapeDtypeStruct((8, ROWS, 128), bf16),
        in_specs=param_specs(),
        out_specs=pl.BlockSpec((1, ROWS, 128), lambda k: (k, 0, 0)),
    )(norm_gains, qkv, out, gu, down.T)


def adam_kernel(FIN, *refs):
    weight, first, second = refs[0:5], refs[5:10], refs[10:15]
    grad, delta, first_new, second_new = refs[15:20], refs[20:25], refs[25:30], refs[30:35]
    k = pl.program_id(0)
    every = slice(None)

    def update(i, at, g, rate):
        m = BETA_ONE * first[i][at] + (1.0 - BETA_ONE) * g
        v = BETA_TWO * second[i][at] + (1.0 - BETA_TWO) * g * g
        step = m * (1.0 / (1.0 - BETA_ONE**STEP)) / (jnp.sqrt(v * (1.0 / (1.0 - BETA_TWO**STEP))) + ADAM_EPS)
        if rate:
            step = step + rate * weight[i][at]
        grad[i][at] = g
        delta[i][at] = -LEARN_RATE * step
        first_new[i][at] = m
        second_new[i][at] = v

    def rows(a, b):
        return FIN[0, a:b].astype(f32)

    @pl.when(k != 3)
    def _():
        update(1, (every, slice(0, 128)), rows(0, 240), DECAY_RATE)
        update(1, (every, slice(128, 256)), rows(240, 480), DECAY_RATE)

    for i in range(2):

        @pl.when(k == 3 + 4 * i)
        def _():
            update(0, (slice(i, i + 1), every), jnp.swapaxes(rows(240, 480), 0, 1)[0:1], 0.0)

    update(2, (every, every), rows(480, 720), DECAY_RATE)
    for j in range(5):
        c = slice(j * 128, (j + 1) * 128)
        update(3, (every, c), rows(720 + 368 * j, 960 + 368 * j), DECAY_RATE)
        update(4, (every, c), jnp.swapaxes(rows(960 + 368 * j, 1088 + 368 * j), 0, 1), DECAY_RATE)


def adam(FIN, weights, moments):
    def five(group):
        return [*group[:4], group[4].T]

    ins = five(weights) + five(moments[:5]) + five(moments[5:])
    shapes = [jax.ShapeDtypeStruct(a.shape, f32) for a in ins[:5]] * 4
    outs = pl.pallas_call(
        adam_kernel,
        name="adam",
        grid=(8,),
        out_shape=shapes,
        in_specs=[pl.BlockSpec((1, ROWS, 128), lambda k: (k, 0, 0))] + param_specs() * 3,
        out_specs=param_specs() * 4,
    )(FIN, *ins)
    return [o.T if i % 5 == 4 else o for i, o in enumerate(outs)]


class Where:
    def __init__(w):
        rep, z = lax.axis_index("rep"), lax.axis_index("fsdp")
        c, x, y = rep % 2, (rep // 2) % 2, rep // 4
        w.rep, w.z, w.c, w.x, w.y = rep, z, c, x, y
        w.partner, w.xn, w.yn = {"rep": rep + 1 - 2 * c}, {"rep": rep + 2 - 4 * x}, {"rep": rep + 4 - 8 * y}
        w.zn = [{"fsdp": (z + d) % 4} for d in (1, 2, 3)]
        w.q, w.qx, w.qy, w.qd = y * 2 + x, y * 2 + 1 - x, (1 - y) * 2 + x, (1 - y) * 2 + 1 - x
        w.k, w.kx, w.ky, w.kd = c * 4 + w.q, c * 4 + w.qx, c * 4 + w.qy, c * 4 + w.qd
        o = (1 - c) * 4
        w.kp, w.kpx, w.kpy, w.kpd = o + w.q, o + w.qx, o + w.qy, o + w.qd

    def peers(w):
        return [w.partner, w.xn, w.yn] + w.zn


class Link:
    def __init__(g, w, sems):
        g.w, g.sems, g.ran, g.waiting = w, sems, [], False

    def copy(g, src, dst, s, r, dev):
        return pltpu.make_async_remote_copy(
            src_ref=src, dst_ref=dst, send_sem=s, recv_sem=r, device_id=dev, device_id_type=MESH
        )

    def send(g, u, i, src, dst, r, dev):
        cp = g.copy(src, dst, g.sems[0].at[u, i], r, dev)
        if g.waiting:
            cp.wait_send()
        else:
            cp.start()

    def got(g, ref, r):
        if not g.waiting:
            g.copy(ref, ref, g.sems[0].at[0, 0], r, g.w.partner).wait_recv()

    def add(g, ref, at, *parts):
        if not g.waiting:
            t = ref[at].astype(f32)
            for p, where in parts:
                t = t + p[where].astype(f32)
            ref[at] = t.astype(bf16)

    def step(g, name, u):
        getattr(g, name)(u)
        g.ran.append((name, u))

    def finish(g):
        g.waiting = True
        for name, u in g.ran:
            getattr(g, name)(u)


class Gather(Link):
    def __init__(g, w, own, W, sems):
        super().__init__(w, sems)
        g.own, g.W = own, W
        g.rz, g.rx, g.ry, g.rp = sems[1:]

    def reg(g, k, u, a=0, b=None):
        r0, n, h = GATHER_UNITS[u]
        return g.W.at[k, :, pl.ds(r0 + a, (n if b is None else b) - a)]

    def g0(g, u):
        r0, n, h = GATHER_UNITS[u]
        for d in range(3):
            src = g.own.at[g.w.k, pl.ds(r0, n)]
            g.send(u, d, src, g.W.at[g.w.k, d, pl.ds(r0, n)], g.rz.at[u, d], g.w.zn[d])

    def g1(g, u):
        r0, n, h = GATHER_UNITS[u]
        for d in range(3):
            g.got(g.W.at[g.w.k, d, pl.ds(r0, n)], g.rz.at[u, d])
        b = g.reg(g.w.k, u)
        g.send(u, 3, b, b, g.rx.at[u, 0], g.w.xn)
        g.send(u, 4, b, b, g.ry.at[u, 0], g.w.yn)
        g.send(u, 5, b, b, g.rp.at[u, 0], g.w.partner)

    def g2a(g, u):
        h = GATHER_UNITS[u][2]
        g.got(g.reg(g.w.kx, u), g.rx.at[u, 0])
        b = g.reg(g.w.kx, u, 0, h)
        g.send(u, 6, b, b, g.ry.at[u, 1], g.w.yn)
        b = g.reg(g.w.kx, u)
        g.send(u, 7, b, b, g.rp.at[u, 1], g.w.partner)

    def g2b(g, u):
        h = GATHER_UNITS[u][2]
        g.got(g.reg(g.w.ky, u), g.ry.at[u, 0])
        b = g.reg(g.w.ky, u, h)
        g.send(u, 8, b, b, g.rx.at[u, 1], g.w.xn)
        b = g.reg(g.w.ky, u)
        g.send(u, 9, b, b, g.rp.at[u, 2], g.w.partner)

    def g3(g, u):
        h = GATHER_UNITS[u][2]
        g.got(g.reg(g.w.kd, u, 0, h), g.ry.at[u, 1])
        g.got(g.reg(g.w.kd, u, h), g.rx.at[u, 1])
        b = g.reg(g.w.kd, u)
        g.send(u, 10, b, b, g.rp.at[u, 3], g.w.partner)

    def g4(g, u):
        for i, k in enumerate((g.w.kp, g.w.kpx, g.w.kpy, g.w.kpd)):
            g.got(g.reg(k, u), g.rp.at[u, i])


class Reduce(Link):
    def __init__(g, w, S, RX3, RY3, RX, RY, RZ, FIN, sems):
        super().__init__(w, sems)
        g.S, g.RX3, g.RY3, g.RX, g.RY, g.RZ, g.FIN = S, RX3, RY3, RX, RY, RZ, FIN
        g.r3, g.rxy, g.rz, g.rf, g.lf = sems[1:]

    def at(g, u):
        r0, n, h = REDUCE_UNITS[u]
        return pl.ds(r0, n), g.S(u), g.w

    def c1(g, u):
        R, S, w = g.at(u)
        g.send(u, 0, S.at[w.qd, 0:2], g.RX3.at[:, R], g.r3.at[u, 0], w.xn)
        g.send(u, 1, S.at[w.qd, 2:4], g.RY3.at[:, R], g.r3.at[u, 1], w.yn)
        g.send(u, 2, S.at[w.qx, 0:2], g.RX.at[0:2, R], g.rxy.at[u, 0], w.xn)
        g.send(u, 3, S.at[w.qy, 2:4], g.RY.at[2:4, R], g.rxy.at[u, 1], w.yn)

    def c2a(g, u):
        R, S, w = g.at(u)
        g.got(g.RY3.at[:, R], g.r3.at[u, 1])
        g.add(S, (w.qx, slice(2, 4)), (g.RY3, (slice(None), R)))
        g.send(u, 4, S.at[w.qx, 2:4], g.RX.at[2:4, R], g.rxy.at[u, 2], w.xn)

    def c2b(g, u):
        R, S, w = g.at(u)
        g.got(g.RX3.at[:, R], g.r3.at[u, 0])
        g.add(S, (w.qy, slice(0, 2)), (g.RX3, (slice(None), R)))
        g.send(u, 5, S.at[w.qy, 0:2], g.RY.at[0:2, R], g.rxy.at[u, 3], w.yn)

    def c3(g, u):
        R, S, w = g.at(u)
        g.got(g.RX.at[0:2, R], g.rxy.at[u, 0])
        g.got(g.RX.at[2:4, R], g.rxy.at[u, 2])
        g.got(g.RY.at[2:4, R], g.rxy.at[u, 1])
        g.got(g.RY.at[0:2, R], g.rxy.at[u, 3])
        g.add(S, (w.q,), (g.RX, (slice(None), R)), (g.RY, (slice(None), R)))
        for d in range(3):
            zt = (w.z + d + 1) % 4
            g.send(u, 6 + d, S.at[w.q, zt], g.RZ.at[d, R], g.rz.at[u, d], w.zn[d])

    def c4(g, u):
        R, S, w = g.at(u)
        for d in range(3):
            g.got(g.RZ.at[d, R], g.rz.at[u, d])
        g.add(S, (w.q, w.z), *[(g.RZ, (d, R)) for d in range(3)])
        src, dst = S.at[w.q, w.z], g.FIN.at[w.k, R]
        g.send(u, 9, src, dst, g.rf.at[u, 0], w.xn)
        g.send(u, 10, src, dst, g.rf.at[u, 1], w.yn)
        g.send(u, 11, src, dst, g.rf.at[u, 4], w.partner)
        if not g.waiting:
            pltpu.make_async_copy(src, dst, g.lf.at[u]).start()

    def fin(g, k, u, a=0, b=None):
        r0, n, h = REDUCE_UNITS[u]
        return g.FIN.at[k, pl.ds(r0 + a, (n if b is None else b) - a)]

    def c5a(g, u):
        h, w = REDUCE_UNITS[u][2], g.w
        g.got(g.fin(w.kx, u), g.rf.at[u, 0])
        b = g.fin(w.kx, u, 0, h)
        g.send(u, 12, b, b, g.rf.at[u, 3], w.yn)
        b = g.fin(w.kx, u)
        g.send(u, 13, b, b, g.rf.at[u, 5], w.partner)

    def c5b(g, u):
        h, w = REDUCE_UNITS[u][2], g.w
        g.got(g.fin(w.ky, u), g.rf.at[u, 1])
        b = g.fin(w.ky, u, h)
        g.send(u, 14, b, b, g.rf.at[u, 2], w.xn)
        b = g.fin(w.ky, u)
        g.send(u, 15, b, b, g.rf.at[u, 6], w.partner)

    def c6(g, u):
        h, w = REDUCE_UNITS[u][2], g.w
        g.got(g.fin(w.kd, u, 0, h), g.rf.at[u, 3])
        g.got(g.fin(w.kd, u, h), g.rf.at[u, 2])
        b = g.fin(w.kd, u)
        g.send(u, 16, b, b, g.rf.at[u, 7], w.partner)

    def c7(g, u):
        R, S, w = g.at(u)
        for i, k in enumerate((w.kp, w.kpx, w.kpy, w.kpd)):
            g.got(g.fin(k, u), g.rf.at[u, 4 + i])
        if not g.waiting:
            pltpu.make_async_copy(S.at[w.q, w.z], g.fin(w.k, u), g.lf.at[u]).wait()


def load_unit(w, own, W, dst, sem, u0, n, row0=0, halves=False):
    def block(k, _):
        def one(r, view, c0):
            def put(src, zs):
                rows = pl.ds(pl.multiple_of(row0 + zs * n, 16), n)
                pltpu.make_async_copy(src, view.at[rows, pl.ds(pl.multiple_of(c0, 128), 128)], sem).start()

            put(own.at[k, pl.ds(r, n)], w.z)
            for d in range(3):
                put(W.at[k, d, pl.ds(r, n)], (w.z + 3 - d) % 4)

        if halves:
            for s in range(2):
                one(u0 + s * n, dst.at[k // 4], (k % 4) * 256 + s * 128)
        else:
            one(u0, dst, k * 128)
        return 0

    lax.fori_loop(0, 8, block, 0)


def rope(t, c, s):
    first = (lanes() % 64) < 32
    return t * c + jnp.where(first, pltpu.roll(t, 96, 1), pltpu.roll(t, 32, 1)) * s


def dup(t, half):
    return jnp.where((lanes() < 64) == (half == 0), t, pltpu.roll(t, 64, 1))


def gain_row(tile):
    at = (lax.broadcasted_iota(jnp.int32, (8, 128), 0) == 0) & (lax.broadcasted_iota(jnp.int32, (8, 128), 1) == 0)
    return mm(at.astype(f32).astype(bf16), tile, NT)[0:1]


def norm(v, g):
    return v * lax.rsqrt(jnp.mean(v * v, axis=1, keepdims=True) + NORM_EPS) * g


def norm_back(v, g, u):
    r = lax.rsqrt(jnp.mean(v * v, axis=1, keepdims=True) + NORM_EPS)
    wv = u * g
    return r * wv - v * (r * r * r) * jnp.mean(wv * v, axis=1, keepdims=True), u * v * r


def head_at(h):
    t, half = h // 2, h % 2
    mine = (lanes() // 64) == half
    return t, h // 3, mine, pl.ds(pl.multiple_of(t * 128, 128), 128)


def head_fwd(h, qk, k2, v2, bias, ctx, lse):
    t, g, mine, col = head_at(h)
    hm = jnp.where(mine, 0.125, 0.0).astype(bf16)
    for i in range(2):
        rows, n = pl.ds(256 * i, 256), 256 * (i + 1)
        s = mm(qk[rows, col] * hm, k2[g, pl.ds(0, n)], NT) + bias[rows, pl.ds(0, n)].astype(f32)
        m = jnp.max(s, axis=1, keepdims=True)
        p = jnp.exp(s - m)
        l = jnp.sum(p, axis=1, keepdims=True)
        o = mm((p * (1.0 / l)).astype(bf16), v2[g, pl.ds(0, n)])
        ctx[rows, col] = jnp.where(mine, o, ctx[rows, col].astype(f32)).astype(bf16)
        lse[rows] = jnp.where(lanes() == h, m + jnp.log(l), lse[rows])


def head_bwd(h, qk, k2, v2, bias, lse, dctx, dq, dk, dv):
    t, g, mine, col = head_at(h)
    hm = jnp.where(mine, 0.125, 0.0).astype(bf16)
    om = jnp.where(mine, 1.0, 0.0).astype(bf16)
    for i in range(2):
        rows, n = pl.ds(256 * i, 256), 256 * (i + 1)
        qs = qk[rows, col] * hm
        do = dctx[t // 4, rows, pl.ds(pl.multiple_of((t % 4) * 128, 128), 128)] * om
        le = jnp.sum(jnp.where(lanes() == h, lse[rows], 0.0), axis=1, keepdims=True)
        s = mm(qs, k2[g, pl.ds(0, n)], NT) + bias[rows, pl.ds(0, n)].astype(f32)
        p = jnp.exp(s - le)
        dp = mm(do, v2[g, pl.ds(0, n)], NT)
        dv[g, pl.ds(0, n)] += mm(p.astype(bf16), do, TN)
        ds = (p * (dp - jnp.sum(p * dp, axis=1, keepdims=True))).astype(bf16)
        dk[g, pl.ds(0, n)] += mm(ds, qs, TN)
        dq[rows, col] = jnp.where(mine, mm(ds, k2[g, pl.ds(0, n)]) * 0.125, dq[rows, col])


KEYS = [(7, 1), (8, 0), (8, 1), (9, 0), (9, 1)]
VALUES = [(10, 0), (10, 1), (11, 0), (11, 1), (12, 0)]


def layer_kernel(
    tokT, cotT, freq, ids, own,
    boT, tgT, FIN, W, n1H, ctxH,
    cot, cos, sin, qk, k2, v2, lse, mid, n2, gains,
    wg, wd, bias, n2T, n2pT, cpT, dypp, hid, dgu, hidp, dgup, da, acc, dacc, dk, dv, gcol, gcolp,
    SM, SO, RX3, RY3, RX, RY, RZ,
    lsem, ps, pr, *sems,
):
    w = Where()
    c = w.c
    bar = pltpu.get_barrier_semaphore()
    for p in w.peers():
        pl.semaphore_signal(bar, inc=1, device_id=p, device_id_type=MESH)
    tl = pltpu.make_async_copy(tokT, tgT, lsem.at[0])
    tl.start()
    cl = pltpu.make_async_copy(cotT, boT, lsem.at[1])
    cl.start()
    pl.semaphore_wait(bar, 6)
    ga = Gather(w, own, W, sems[:5])
    re = Reduce(w, lambda u: SM.at[u] if u < 5 else SO.at[u - 5], RX3, RY3, RX, RY, RZ, FIN, sems[5:])
    live, local = {}, {}

    def psend(i, src, dst):
        live[i] = ga.copy(src, dst, ps.at[i], pr.at[i], w.partner)
        live[i].start()

    def psent(*which):
        for i in which:
            live.pop(i).wait_send()

    def pgot(i, dst):
        ga.copy(dst, dst, ps.at[0], pr.at[i], w.partner).wait_recv()

    def begin(name, src, dst, sem):
        local[name] = pltpu.make_async_copy(src, dst, sem)
        local[name].start()

    def end(name):
        local.pop(name).wait()

    other = pl.ds(pl.multiple_of((1 - c) * 512, 512), 512)
    mine = pl.ds(pl.multiple_of(c * 512, 512), 512)
    half_rows = [pl.ds(256 * i, 256) for i in range(2)]

    def A0():
        seq = ids[...].astype(f32)
        column = jnp.swapaxes(jnp.broadcast_to(seq, (8, 512)), 0, 1)[:, 0:1]
        for i in range(2):
            own_seq = column[256 * i : 256 * (i + 1)]
            rows = lax.broadcasted_iota(jnp.int32, (256, 512), 0) + 256 * i
            cols = lax.broadcasted_iota(jnp.int32, (256, 512), 1)
            ok = (own_seq == seq) & (cols <= rows)
            bias[pl.ds(256 * i, 256)] = jnp.where(ok, 0.0, NEG_LARGE).astype(bf16)
            first_row = jnp.sum(jnp.where(seq < own_seq, 1.0, 0.0), axis=1, keepdims=True)
            row = (lax.broadcasted_iota(jnp.int32, (256, 1), 0) + 256 * i).astype(f32)
            angle = (row - first_row) * freq[...]
            cos[pl.ds(256 * i, 256)] = jnp.cos(angle)
            sin[pl.ds(256 * i, 256)] = jnp.where((lanes() % 64) < 32, -1.0, 1.0) * jnp.sin(angle)
        lse[...] = jnp.zeros_like(lse)
        acc[...] = jnp.zeros_like(acc)
        dacc[...] = jnp.zeros_like(dacc)
        dk[...] = jnp.zeros_like(dk)
        dv[...] = jnp.zeros_like(dv)
        tl.wait()
        cl.wait()
        mid[...] = jnp.swapaxes(tgT[...], 0, 1).astype(f32)
        cot[:, 896:1024] = jnp.zeros((512, 128), bf16)
        cot[:, 0:960] = jnp.swapaxes(boT[...], 0, 1)

    def LQ():
        load_unit(w, own, W, wg, lsem.at[0], 0, 240, halves=True)

    def wait_q():
        pltpu.make_async_copy(wg, wg, lsem.at[0]).wait()

    def LO():
        load_unit(w, own, W, wd, lsem.at[1], 480, 240)

    def wait_o():
        view = wd.at[pl.ds(0, 960)]
        pltpu.make_async_copy(view, view, lsem.at[1]).wait()

    def A1():
        wait_q()
        gains[...] = jnp.zeros_like(gains)
        gains[0:1] = gain_row(wg[0, :, 896:1024])
        gains[1:2] = gain_row(wg[1, :, 896:1024])
        n1 = norm(mid[...], gains[0:1]).astype(bf16)
        da[:, 0:960] = n1
        tgT[...] = jnp.swapaxes(n1, 0, 1)
        for half, (lo, hi) in enumerate(((0, 6), (6, 13))):
            res = mm(da[:, 0:960], wg[half, :, 0 : (hi - lo) * 128])
            for t in range(lo, hi):
                tile = res[:, (t - lo) * 128 : (t - lo + 1) * 128]
                if t < 10:
                    tile = rope(tile, cos[...], sin[...])
                    qk[:, t * 128 : (t + 1) * 128] = tile.astype(bf16)
                for i in range(5):
                    if KEYS[i][0] == t:
                        k2[i] = dup(tile, KEYS[i][1]).astype(bf16)
                    if VALUES[i][0] == t:
                        v2[i] = dup(tile, VALUES[i][1]).astype(bf16)
        begin("n1", tgT, n1H, lsem.at[2])
        da[...] = jnp.zeros_like(da)

    def A3():
        wait_o()
        for rows in half_rows:
            m = mid[rows] + mm(da[rows, 0:960], wd[pl.ds(0, 960), 0:960])
            mid[rows] = m
            n2[rows] = norm(m, gains[1:2]).astype(bf16)
        n2T[...] = jnp.swapaxes(n2[...], 0, 1)
        boT[...] = jnp.swapaxes(da[:, 0:960], 0, 1)
        psend(0, n2T, n2pT)
        psend(1, cot.at[:, other], dypp)
        psend(2, boT, cpT)
        begin("ctx", boT, ctxH, lsem.at[3])

    def dslot(j):
        return pl.ds(pl.multiple_of(((j + 2) % 3) * 512, 512), 512)

    def L(j):
        load_unit(w, own, W, wg.at[j % 2], lsem.at[4 + j % 2], 720 + 368 * j, 240)
        load_unit(w, own, W, wd, lsem.at[6 + j % 2], 960 + 368 * j, 128, row0=((j + 2) % 3) * 512)

    def sends(j):
        b = j % 2
        return (
            ga.copy(hid.at[b], hidp.at[b], ps.at[4 + j], pr.at[4 + j], w.partner),
            ga.copy(dgu.at[b, 1 - c], dgup.at[b], ps.at[9 + j], pr.at[9 + j], w.partner),
        )

    def F(j):
        b = j % 2
        pltpu.make_async_copy(wg.at[b], wg.at[b], lsem.at[4 + b]).wait()
        view = wd.at[dslot(j)]
        pltpu.make_async_copy(view, view, lsem.at[6 + b]).wait()

        @pl.when(j >= 2)
        def _():
            sends(j - 2)[0].wait_send()
            sends(j - 2)[1].wait_send()

        def half(i, _):
            rows = pl.ds(pl.multiple_of(i * 256, 256), 256)
            gu = mm(n2[rows], wg[b])
            gate, up = gu[:, :512], gu[:, 512:]
            sg = jax.nn.sigmoid(gate)
            a = gate * sg
            hb = (a * up).astype(bf16)
            hid[b, rows] = hb
            acc[rows, 0:960] += mm(hb, wd[dslot(j), 0:960])
            dh = mm(cot[rows, 0:960], wd[dslot(j), 0:960], NT)
            dgate = (dh * up * (sg * (1.0 + gate * (1.0 - sg)))).astype(bf16)
            dup_ = (dh * a).astype(bf16)
            dgu[b, 0, rows] = dgate
            dgu[b, 1, rows] = dup_
            dacc[rows] += mm(dgate, wg[b, :, 0:512], NT) + mm(dup_, wg[b, :, 512:1024], NT)
            return 0

        lax.fori_loop(0, 2, half, 0)
        for cp in sends(j):
            cp.start()

    def cut(S, G, n, r0=0):
        for q in range(4):
            for z in range(4):
                S[q, z, r0 : r0 + n] = G[z * n : (z + 1) * n, q * 128 : (q + 1) * 128].astype(bf16)

    def R(j):
        b = j % 2

        @pl.when(j == 0)
        def _():
            pgot(0, n2pT)
            pgot(1, dypp)

        pgot(4 + j, hidp.at[b])
        pgot(9 + j, dgup.at[b])
        cut(SM.at[j], mm(n2T[...], dgu[b, c]) + mm(n2pT[...], dgup[b]), 240)
        cut(SM.at[j], mm(hid[b], cot[:, mine], TN) + mm(hidp[b], dypp[...], TN), 128, 240)

    def B1():
        for cp in sends(3) + sends(4):
            cp.wait_send()
        psent(0, 1, 2)
        LO()
        LQ()
        end("ctx")
        begin("ctxT", ctxH, n2T, lsem.at[3])
        ones = jnp.ones((256, 128), bf16)
        da[:, 896:1024] = jnp.zeros((512, 128), bf16)
        gc = 0.0
        for i, rows in enumerate(half_rows):
            m = mid[rows]
            boT[:, 256 * i : 256 * (i + 1)] = jnp.swapaxes((m + acc[rows, 0:960]).astype(bf16), 0, 1)
            dv_, gp = norm_back(m, gains[1:2], dacc[rows])
            dmid = cot[rows, 0:960].astype(f32) + dv_
            dacc[rows] = dmid
            da[rows, 0:960] = dmid.astype(bf16)
            gc = gc + mm(gp.astype(bf16), ones, TN)
        gcol[1] = gc.astype(bf16)
        psend(14, da.at[:, other], hidp.at[1])

    def B2():
        wait_o()
        hid[1, :, 384:512] = jnp.zeros((512, 128), bf16)
        hid[0] = mm(da[:, 0:960], wd[pl.ds(0, 512), 0:960], NT).astype(bf16)
        hid[1, :, 0:448] = mm(da[:, 0:960], wd[pl.ds(512, 448), 0:960], NT).astype(bf16)
        end("ctxT")
        pgot(2, cpT)
        pgot(14, hidp.at[1])
        end("n1")
        psend(3, n1H, n2pT)
        cut(SO.at[0], mm(n2T[...], da[:, mine]) + mm(cpT[...], hidp[1]), 240)
        acc[...] = jnp.zeros_like(acc)
        psent(14)
        begin("n1T", n1H, n2T, lsem.at[2])
        begin("tok", tokT, tgT, lsem.at[3])

    def D1():
        def put(half, t, tile):
            dgu[half, t // 4, :, (t % 4) * 128 : (t % 4 + 1) * 128] = tile.astype(bf16)

        first = lanes() < 64
        nsin = -sin[...]

        def fold(ref, i):
            return ref[i] + pltpu.roll(ref[i], 64, 1)

        for t in range(7):
            put(t // 6, t % 6, rope(acc[:, t * 128 : (t + 1) * 128], cos[...], nsin))
        zero = jnp.zeros((512, 128), f32)
        for half, t in ((0, 6), (0, 7), (1, 7)):
            put(half, t, zero)
        kk, vv = [fold(dk, i) for i in range(5)], [fold(dv, i) for i in range(5)]
        put(1, 1, rope(jnp.where(first, acc[:, 896:1024], kk[0]), cos[...], nsin))
        put(1, 2, rope(jnp.where(first, kk[1], kk[2]), cos[...], nsin))
        put(1, 3, rope(jnp.where(first, kk[3], kk[4]), cos[...], nsin))
        put(1, 4, jnp.where(first, vv[0], vv[1]))
        put(1, 5, jnp.where(first, vv[2], vv[3]))
        put(1, 6, jnp.where(first, vv[4], 0.0))
        psend(15, dgu.at[1 - c], dgup)

    def qgrad(sub):
        for q in range(4):
            t = 2 * q + sub
            if t == 7:
                G = gcol[c].astype(f32) + gcolp[...].astype(f32)
            else:
                at = slice((t % 4) * 128, (t % 4 + 1) * 128)
                G = mm(n2T[...], dgu[c, t // 4, :, at]) + mm(n2pT[...], dgup[t // 4, :, at])
            for z in range(4):
                SO[1 + sub, q, z] = G[z * 240 : (z + 1) * 240].astype(bf16)

    def D2():
        end("n1T")
        pgot(3, n2pT)
        pgot(15, dgup)
        qgrad(0)

    def D3():
        wait_q()
        end("tok")
        da[:, 0:960] = jnp.swapaxes(tgT[...], 0, 1)
        ones = jnp.ones((256, 128), bf16)
        gc = 0.0
        for i, rows in enumerate(half_rows):
            dn1 = mm(dgu[0, 0, rows], wg[0, :, 0:512], NT) + mm(dgu[0, 1, rows, 0:256], wg[0, :, 512:768], NT)
            dn1 += mm(dgu[1, 0, rows], wg[1, :, 0:512], NT) + mm(dgu[1, 1, rows, 0:384], wg[1, :, 512:896], NT)
            dv_, gp = norm_back(da[rows, 0:960].astype(f32), gains[0:1], dn1)
            tgT[:, 256 * i : 256 * (i + 1)] = jnp.swapaxes((dacc[rows] + dv_).astype(bf16), 0, 1)
            gc = gc + mm(gp.astype(bf16), ones, TN)
        gcol[0] = gc.astype(bf16)
        psend(16, gcol.at[1 - c], gcolp)

    def D4():
        pgot(16, gcolp)
        qgrad(1)

    steps = dict(A0=A0, LQ=LQ, A1=A1, LO=LO, A3=A3, L=L, B1=B1, B2=B2, D1=D1, D2=D2, D3=D3, D4=D4)

    def run(part):
        for name, at in part:
            if name in steps:
                steps[name](*([] if at is None else [at]))
            else:
                (ga if name[0] == "g" else re).step(name, at)

    def after(i, parts, at=None):
        for n, part in enumerate(parts):
            if part:
                pl.when(i == (n if at is None else at(n)))(lambda part=part: run(part))

    def heads(one_head, parts):
        def turn(h, _):
            one_head(h)
            after(h, parts, lambda n: 3 * n + 2)
            return 0

        lax.fori_loop(0, 15, turn, 0)

    def unit(j, _):
        F(j)
        after(j, PARTS["F"])
        R(j)
        after(j, PARTS["R"])
        return 0

    run(PARTS["start"])
    heads(lambda h: head_fwd(h, qk, k2, v2, bias, da, lse), PARTS["H"])
    run(PARTS["A3"])
    lax.fori_loop(0, 5, unit, 0)
    run(PARTS["B1"])
    heads(lambda h: head_bwd(h, qk, k2, v2, bias, lse, hid, acc, dk, dv), PARTS["K"])
    run(PARTS["D1"])
    for i in list(live):
        psent(i)
    ga.finish()
    re.finish()


def layer(tok, cot, ids, own):
    freq = ROPE_BASE ** (-2.0 * (jnp.arange(128) % 32).astype(f32) / HEAD)
    S, D = jax.ShapeDtypeStruct, pltpu.SemaphoreType.DMA

    def V(*shape, dt=bf16):
        return pltpu.VMEM(shape, dt)

    vm = pl.BlockSpec(memory_space=pltpu.VMEM)
    hb = pl.BlockSpec(memory_space=pl.ANY)
    outs = pl.pallas_call(
        layer_kernel,
        name="layer",
        out_shape=[
            S((960, 512), bf16), S((960, 512), bf16), S((8, ROWS, 128), bf16),
            S((8, 3, ROWS, 128), bf16), S((960, 512), bf16), S((960, 512), bf16),
        ],
        in_specs=[hb, hb, vm, vm, hb],
        out_specs=[vm, vm, hb, hb, hb, hb],
        scratch_shapes=[
            V(512, 1024), V(512, 128, dt=f32), V(512, 128, dt=f32), V(512, 1280), V(5, 512, 128), V(5, 512, 128), V(512, 128, dt=f32), V(512, 960, dt=f32),
            V(512, 960), V(8, 960, dt=f32),
            V(2, 960, 1024), V(1536, 1024), V(512, 512), V(960, 512), V(960, 512), V(960, 512), V(512, 512),
            V(2, 512, 512), V(2, 2, 512, 512), V(2, 512, 512), V(2, 512, 512), V(512, 1024),
            V(512, 1024, dt=f32), V(512, 960, dt=f32), V(5, 512, 128, dt=f32), V(5, 512, 128, dt=f32),
            V(2, 960, 128), V(960, 128),
            V(5, 4, 4, 368, 128), V(3, 4, 4, 240, 128),
            V(2, ROWS, 128), V(2, ROWS, 128), V(4, ROWS, 128), V(4, ROWS, 128), V(3, ROWS, 128),
            D((8,)), D((17,)), D((17,)),
            D((8, 11)), D((8, 3)), D((8, 2)), D((8, 2)), D((8, 4)),
            D((8, 17)), D((8, 2)), D((8, 4)), D((8, 3)), D((8, 8)), D((8,)),
        ],
        compiler_params=pltpu.CompilerParams(
            collective_id=0, has_side_effects=True, vmem_limit_bytes=67043328
        ),
    )(tok.T, cot.T, freq[None, :], ids[None, :], own)
    return outs[:3]


PARTS = {
    "start": [
        ("g0", 0), ("g0", 1), ("g0", 2), ("g0", 3), ("A0", None), ("g1", 0), ("g0", 4), ("g1", 1), ("g0", 5),
        ("g2a", 0), ("g2b", 0), ("g1", 2), ("g0", 6), ("g2a", 1), ("g2b", 1), ("g3", 0), ("g4", 0),
        ("g2a", 2), ("g2b", 2), ("g1", 3), ("g0", 7), ("g3", 1), ("g4", 1), ("LQ", None), ("g3", 2),
        ("g4", 2), ("LO", None), ("g1", 4), ("A1", None), ("g2a", 3), ("g2b", 3),
    ],
    "H": [
        [
            ("g2a", 4), ("g2b", 4), ("g1", 5),
        ],
        [
            ("g3", 3),
        ],
        [
            ("g3", 4), ("g1", 6), ("g4", 3), ("L", 0),
        ],
        [
            ("g4", 4),
        ],
        [
            ("g2a", 5), ("g2b", 5),
        ],
    ],
    "A3": [
        ("A3", None), ("L", 1), ("g1", 7),
    ],
    "F": [
        [
            ("g3", 5), ("g2a", 6), ("g2b", 6),
        ],
        [
            ("g3", 6), ("g2a", 7), ("g2b", 7),
        ],
        [],
        [
            ("c3", 0), ("c2a", 1), ("c2b", 1), ("g4", 7), ("L", 4),
        ],
        [
            ("c2a", 2), ("c2b", 2),
        ],
    ],
    "R": [
        [
            ("c1", 0), ("g4", 5), ("L", 2),
        ],
        [
            ("c2a", 0), ("c2b", 0), ("c1", 1), ("g4", 6), ("L", 3),
        ],
        [
            ("g3", 7), ("c1", 2),
        ],
        [
            ("c1", 3),
        ],
        [
            ("c4", 0), ("c1", 4),
        ],
    ],
    "B1": [
        ("B1", None), ("c3", 1), ("B2", None), ("c2a", 3), ("c2b", 3), ("c1", 5),
    ],
    "K": [
        [],
        [
            ("c4", 1), ("c5a", 0), ("c3", 2),
        ],
        [
            ("c5b", 0), ("c2b", 4), ("c2a", 4),
        ],
        [],
        [
            ("c4", 2), ("c3", 3),
        ],
    ],
    "D1": [
        ("D1", None), ("c2a", 5), ("c2b", 5), ("D2", None), ("c5a", 1), ("c1", 6), ("D3", None), ("c6", 0),
        ("c5b", 1), ("D4", None), ("c1", 7), ("c4", 3), ("c3", 4), ("c5a", 2), ("c7", 0), ("c5b", 2),
        ("c3", 5), ("c2b", 6), ("c2a", 6), ("c6", 1), ("c7", 1), ("c4", 4), ("c2b", 7), ("c2a", 7),
        ("c5a", 3), ("c4", 5), ("c5b", 3), ("c6", 2), ("c7", 2), ("c3", 6), ("c5a", 4), ("c5b", 4), ("c3", 7),
        ("c5a", 5), ("c6", 3), ("c7", 3), ("c5b", 5), ("c6", 4), ("c4", 6), ("c7", 4), ("c6", 5), ("c7", 5),
        ("c5a", 6), ("c5b", 6), ("c4", 7), ("c6", 6), ("c7", 6), ("c5a", 7), ("c5b", 7), ("c6", 7), ("c7", 7),
    ],
}


def on_device(tokens, sequence_ids, cotangent, norm_gains, qkv_weight, out_weight, gate_up_weight, down_weight, *moments):
    weights = (norm_gains, qkv_weight, out_weight, gate_up_weight, down_weight)
    block_out, tokens_grad, packed = layer(tokens, cotangent, sequence_ids, pack(*weights))
    return (block_out.T, tokens_grad.T, *adam(packed, weights, moments))


def solution(mesh):
    fits = mesh.shape["rep"] == 8 and mesh.shape["fsdp"] == 4
    return jax.shard_map(
        on_device if fits else on_device_any,
        mesh=mesh,
        in_specs=(
            P(("rep", "fsdp"), None),
            P(("rep", "fsdp")),
            P(("rep", "fsdp"), None),
            P(None, "fsdp"),
            P("fsdp", None),
            P("fsdp", None),
            P("fsdp", None),
            P("fsdp", None),
            P(None, "fsdp"),
            P("fsdp", None),
            P("fsdp", None),
            P("fsdp", None),
            P("fsdp", None),
            P(None, "fsdp"),
            P("fsdp", None),
            P("fsdp", None),
            P("fsdp", None),
            P("fsdp", None),
        ),
        out_specs=(
            P(("rep", "fsdp"), None),
            P(("rep", "fsdp"), None),
            P(None, "fsdp"),
            P("fsdp", None),
            P("fsdp", None),
            P("fsdp", None),
            P("fsdp", None),
            P(None, "fsdp"),
            P("fsdp", None),
            P("fsdp", None),
            P("fsdp", None),
            P("fsdp", None),
            P(None, "fsdp"),
            P("fsdp", None),
            P("fsdp", None),
            P("fsdp", None),
            P("fsdp", None),
            P(None, "fsdp"),
            P("fsdp", None),
            P("fsdp", None),
            P("fsdp", None),
            P("fsdp", None),
        ),
        check_vma=False,
    )
```

```python
import math

import jax
import jax.numpy as jnp
from jax import lax
from jax.experimental import pallas as pl
from jax.experimental.pallas import tpu as pltpu
from jax.sharding import PartitionSpec as P
D = 960
HEADS = 15
KV_HEADS = 5
HEAD = 64
FF = 2560
STEP = 4


NORM_EPS = 1e-05
ROPE_BASE = 100000.0
LEARN_RATE = 0.03
BETA_ONE = 0.9
BETA_TWO = 0.95
ADAM_EPS = 1e-08
DECAY_RATE = 0.1
NEG_LARGE = -1e30


def positions(sequence_ids):
    row_index = jnp.arange(sequence_ids.shape[0], dtype=jnp.int32)
    prior_ids = jnp.concatenate([jnp.full((1,), -1, jnp.int32), sequence_ids[:-1]])
    seq_starts = jnp.where(sequence_ids != prior_ids, row_index, 0)
    first_row = lax.cummax(seq_starts, axis=0)
    return (row_index - first_row).astype(jnp.float32)


def causal_mask(sequence_ids):
    row_index = jnp.arange(sequence_ids.shape[0], dtype=jnp.int32)
    return (sequence_ids[:, None] == sequence_ids[None, :]) & (
        row_index[None, :] <= row_index[:, None]
    )


def rope_tables(places):
    half_size = HEAD // 2
    freq_table = ROPE_BASE ** (-2.0 * jnp.arange(half_size, dtype=jnp.float32) / HEAD)
    angles = places[:, None] * freq_table[None, :]
    return (jnp.cos(angles), jnp.sin(angles))


def rotate(vectors, cosine_table, sine_table):
    half_size = vectors.shape[-1] // 2
    first_half = vectors[..., :half_size]
    second_half = vectors[..., half_size:]
    cosine_wide = cosine_table[:, None, :]
    sine_wide = sine_table[:, None, :]
    return jnp.concatenate(
        [
            first_half * cosine_wide - second_half * sine_wide,
            second_half * cosine_wide + first_half * sine_wide,
        ],
        axis=-1,
    )


def rms_norm(values, gain_row):
    row_scale = lax.rsqrt(jnp.mean(values * values, axis=-1, keepdims=True) + NORM_EPS)
    return values * row_scale * gain_row


def swiglu(gate_part, up_part):
    return gate_part * jax.nn.sigmoid(gate_part) * up_part


def adamw_update(weight, moment_one, moment_two, gradient, decay_rate):
    first_new = BETA_ONE * moment_one + (1.0 - BETA_ONE) * gradient
    second_new = BETA_TWO * moment_two + (1.0 - BETA_TWO) * gradient * gradient
    fix_one = 1.0 - BETA_ONE**STEP
    fix_two = 1.0 - BETA_TWO**STEP
    update_dir = (
        first_new / fix_one / (jnp.sqrt(second_new / fix_two) + ADAM_EPS) + decay_rate * weight
    )
    return (-LEARN_RATE * update_dir, first_new, second_new)


def split_groups(queries, keys_rot, values_kv):
    count_rows = queries.shape[0]
    group_size = HEADS // KV_HEADS
    query_groups = queries.reshape(count_rows, KV_HEADS, group_size, HEAD).transpose(1, 2, 0, 3)
    return (query_groups, keys_rot.transpose(1, 0, 2), values_kv.transpose(1, 0, 2))


def attend(queries, keys_rot, values_kv, mask_table):
    count_rows = queries.shape[0]
    scale_factor = 1.0 / math.sqrt(HEAD)
    query_groups, key_groups, value_groups = split_groups(queries, keys_rot, values_kv)

    def one_group(members):
        query_one, key_one, value_one = members
        scores = (
            jnp.einsum("gqd,kd->gqk", query_one, key_one, preferred_element_type=jnp.float32)
            * scale_factor
        )
        scores = jnp.where(mask_table[None], scores, NEG_LARGE)
        top_score = jnp.max(scores, axis=-1, keepdims=True)
        weights = jnp.exp(scores - top_score)
        total_sum = jnp.sum(weights, axis=-1, keepdims=True)
        prob_table = (weights / total_sum).astype(jnp.bfloat16)
        context_one = jnp.einsum(
            "gqk,kd->gqd", prob_table, value_one, preferred_element_type=jnp.float32
        )
        return (context_one.astype(jnp.bfloat16), (top_score + jnp.log(total_sum))[..., 0])

    context_groups, log_total = lax.map(one_group, (query_groups, key_groups, value_groups))
    context = context_groups.transpose(2, 0, 1, 3).reshape(count_rows, HEADS, HEAD)
    return (context, log_total)


def attend_back(queries, keys_rot, values_kv, mask_table, log_total, grad_context):
    count_rows = queries.shape[0]
    group_size = HEADS // KV_HEADS
    scale_factor = 1.0 / math.sqrt(HEAD)
    query_groups, key_groups, value_groups = split_groups(queries, keys_rot, values_kv)
    grad_groups = grad_context.reshape(count_rows, KV_HEADS, group_size, HEAD).transpose(1, 2, 0, 3)

    def one_group(members):
        query_one, key_one, value_one, log_one, grad_one = members
        scores = (
            jnp.einsum("gqd,kd->gqk", query_one, key_one, preferred_element_type=jnp.float32)
            * scale_factor
        )
        scores = jnp.where(mask_table[None], scores, NEG_LARGE)
        prob_table = jnp.exp(scores - log_one[..., None])
        grad_probs = jnp.einsum(
            "gqd,kd->gqk", grad_one, value_one, preferred_element_type=jnp.float32
        )
        grad_value = jnp.einsum(
            "gqk,gqd->kd",
            prob_table.astype(jnp.bfloat16),
            grad_one,
            preferred_element_type=jnp.float32,
        )
        row_delta = jnp.sum(prob_table * grad_probs, axis=-1, keepdims=True)
        grad_scores = (prob_table * (grad_probs - row_delta)).astype(jnp.bfloat16)
        grad_query = (
            jnp.einsum("gqk,kd->gqd", grad_scores, key_one, preferred_element_type=jnp.float32)
            * scale_factor
        )
        grad_key = (
            jnp.einsum("gqk,gqd->kd", grad_scores, query_one, preferred_element_type=jnp.float32)
            * scale_factor
        )
        return (grad_query, grad_key, grad_value)

    grad_q_groups, grad_k_groups, grad_v_groups = lax.map(
        one_group, (query_groups, key_groups, value_groups, log_total, grad_groups)
    )
    grad_queries = grad_q_groups.transpose(2, 0, 1, 3).reshape(count_rows, HEADS, HEAD)
    return (grad_queries, grad_k_groups.transpose(1, 0, 2), grad_v_groups.transpose(1, 0, 2))


def forward(tokens, sequence_ids, attn_set, mlp_set):
    gain_half, qkv_half, out_half = attn_set
    gate_up_half, down_half = mlp_set
    count_rows = tokens.shape[0]
    kv_width = KV_HEADS * HEAD
    inputs = tokens.astype(jnp.float32)
    gain_rows = gain_half.astype(jnp.float32)
    normed = rms_norm(inputs, gain_rows[0]).astype(jnp.bfloat16)
    mixed_cols = jnp.dot(normed, qkv_half, preferred_element_type=jnp.float32)
    cosine_table, sine_table = rope_tables(positions(sequence_ids))
    queries = rotate(
        mixed_cols[:, :D].reshape(count_rows, HEADS, HEAD), cosine_table, sine_table
    ).astype(jnp.bfloat16)
    keys_rot = rotate(
        mixed_cols[:, D : D + kv_width].reshape(count_rows, KV_HEADS, HEAD),
        cosine_table,
        sine_table,
    ).astype(jnp.bfloat16)
    values_kv = (
        mixed_cols[:, D + kv_width :].reshape(count_rows, KV_HEADS, HEAD).astype(jnp.bfloat16)
    )
    context, log_total = attend(queries, keys_rot, values_kv, causal_mask(sequence_ids))
    middle = inputs + jnp.dot(
        context.reshape(count_rows, D), out_half, preferred_element_type=jnp.float32
    )
    normed_two = rms_norm(middle, gain_rows[1]).astype(jnp.bfloat16)
    gate_up = jnp.dot(normed_two, gate_up_half, preferred_element_type=jnp.float32)
    hidden = swiglu(gate_up[:, :FF], gate_up[:, FF:]).astype(jnp.bfloat16)
    result = middle + jnp.dot(hidden, down_half, preferred_element_type=jnp.float32)
    kept_state = (
        inputs,
        normed,
        queries,
        keys_rot,
        values_kv,
        context,
        log_total,
        middle,
        normed_two,
        gate_up,
        hidden,
    )
    return (kept_state, result)


def mlp_backward(kept_state, cotangent, attn_set, mlp_set):
    middle, normed_two, gate_up, hidden = (
        kept_state[7],
        kept_state[8],
        kept_state[9],
        kept_state[10],
    )
    gain_rows = attn_set[0].astype(jnp.float32)
    gate_up_half, down_half = mlp_set
    grad_result = cotangent.astype(jnp.float32)
    grad_branch = grad_result.astype(jnp.bfloat16)
    down_grad = jnp.einsum("rf,rd->fd", hidden, grad_branch, preferred_element_type=jnp.float32)
    grad_hidden = jnp.einsum(
        "rd,fd->rf", grad_branch, down_half, preferred_element_type=jnp.float32
    )
    _, act_back = jax.vjp(swiglu, gate_up[:, :FF], gate_up[:, FF:])
    grad_gate, grad_up = act_back(grad_hidden)
    grad_mix_two = jnp.concatenate([grad_gate, grad_up], axis=1).astype(jnp.bfloat16)
    gate_up_grad = jnp.einsum(
        "rd,rf->df", normed_two, grad_mix_two, preferred_element_type=jnp.float32
    )
    grad_normed_two = jnp.einsum(
        "rf,df->rd", grad_mix_two, gate_up_half, preferred_element_type=jnp.float32
    )
    _, norm_back_two = jax.vjp(rms_norm, middle, gain_rows[1])
    grad_middle_norm, gain_two_grad = norm_back_two(grad_normed_two)
    grad_middle = grad_result + grad_middle_norm
    return ((gate_up_grad, down_grad), (grad_middle, gain_two_grad))


def attn_backward(kept_state, carried, sequence_ids, attn_set):
    inputs, normed, queries, keys_rot, values_kv, context, log_total = kept_state[:7]
    grad_middle, gain_two_grad = carried
    gain_half, qkv_half, out_half = attn_set
    gain_rows = gain_half.astype(jnp.float32)
    count_rows = inputs.shape[0]
    kv_width = KV_HEADS * HEAD
    grad_attn = grad_middle.astype(jnp.bfloat16)
    flat_context = context.reshape(count_rows, D)
    out_grad = jnp.einsum("rc,rd->cd", flat_context, grad_attn, preferred_element_type=jnp.float32)
    grad_context = jnp.einsum("rd,cd->rc", grad_attn, out_half, preferred_element_type=jnp.float32)
    grad_context = grad_context.astype(jnp.bfloat16).reshape(count_rows, HEADS, HEAD)
    grad_queries, grad_keys, grad_values = attend_back(
        queries, keys_rot, values_kv, causal_mask(sequence_ids), log_total, grad_context
    )
    cosine_table, sine_table = rope_tables(positions(sequence_ids))
    grad_q_raw = rotate(grad_queries, cosine_table, -sine_table).reshape(count_rows, D)
    grad_k_raw = rotate(grad_keys, cosine_table, -sine_table).reshape(count_rows, kv_width)
    grad_mixed = jnp.concatenate(
        [grad_q_raw, grad_k_raw, grad_values.reshape(count_rows, kv_width)], axis=1
    )
    grad_mixed = grad_mixed.astype(jnp.bfloat16)
    qkv_grad = jnp.einsum("rd,rc->dc", normed, grad_mixed, preferred_element_type=jnp.float32)
    grad_normed = jnp.einsum("rc,dc->rd", grad_mixed, qkv_half, preferred_element_type=jnp.float32)
    _, norm_back_one = jax.vjp(rms_norm, inputs, gain_rows[0])
    grad_inputs_norm, gain_one_grad = norm_back_one(grad_normed)
    tokens_grad = (grad_middle + grad_inputs_norm).astype(jnp.bfloat16)
    gains_grad = jnp.stack([gain_one_grad, gain_two_grad])
    return (tokens_grad, (gains_grad, qkv_grad, out_grad))


def on_device_any(
    tokens,
    sequence_ids,
    cotangent,
    norm_gains,
    qkv_weight,
    out_weight,
    gate_up_weight,
    down_weight,
    gains_first,
    qkv_first,
    out_first,
    gate_up_first,
    down_first,
    gains_second,
    qkv_second,
    out_second,
    gate_up_second,
    down_second,
):
    shares = lax.axis_size("rep")
    share = lax.axis_index("rep")
    both = ("fsdp", "rep")
    group = lax.axis_size("fsdp")

    def collect(shard):
        flat = shard.astype(jnp.bfloat16).reshape(shares, -1)
        piece = lax.dynamic_index_in_dim(flat, share, 0, keepdims=False)
        whole = lax.all_gather(piece, both, axis=0, tiled=True)
        return whole.reshape(shard.shape[0] * group, shard.shape[1])

    def total(gradient, shard):
        piece = lax.psum_scatter(
            gradient.astype(jnp.bfloat16).reshape(-1), both, scatter_dimension=0, tiled=True
        )
        flat = lax.all_gather(piece, "rep", axis=0, tiled=True)
        return flat.reshape(shard.shape).astype(jnp.float32)

    gain_full = lax.all_gather(norm_gains.astype(jnp.bfloat16), "fsdp", axis=1, tiled=True)
    qkv_full = collect(qkv_weight)
    out_full = collect(out_weight)
    mlp_set = (collect(gate_up_weight), collect(down_weight))
    attn_set = (gain_full, qkv_full, out_full)
    kept_state, result = forward(tokens, sequence_ids, attn_set, mlp_set)
    block_out = result.astype(jnp.bfloat16)
    mlp_grads, carried = mlp_backward(kept_state, cotangent, attn_set, mlp_set)
    down_total = total(mlp_grads[1], down_weight)
    gate_up_total = total(mlp_grads[0], gate_up_weight)
    tokens_grad, attn_grads = attn_backward(kept_state, carried, sequence_ids, attn_set)
    gains_part = lax.psum_scatter(attn_grads[0], "fsdp", scatter_dimension=1, tiled=True)
    gains_total = lax.psum(gains_part, "rep")
    qkv_total = total(attn_grads[1], qkv_weight)
    out_total = total(attn_grads[2], out_weight)
    gains_delta, gains_first_new, gains_second_new = adamw_update(
        norm_gains, gains_first, gains_second, gains_total, 0.0
    )
    qkv_delta, qkv_first_new, qkv_second_new = adamw_update(
        qkv_weight, qkv_first, qkv_second, qkv_total, DECAY_RATE
    )
    out_delta, out_first_new, out_second_new = adamw_update(
        out_weight, out_first, out_second, out_total, DECAY_RATE
    )
    gate_up_delta, gate_up_first_new, gate_up_second_new = adamw_update(
        gate_up_weight, gate_up_first, gate_up_second, gate_up_total, DECAY_RATE
    )
    down_delta, down_first_new, down_second_new = adamw_update(
        down_weight, down_first, down_second, down_total, DECAY_RATE
    )
    return (
        block_out,
        tokens_grad,
        gains_total,
        qkv_total,
        out_total,
        gate_up_total,
        down_total,
        gains_delta,
        qkv_delta,
        out_delta,
        gate_up_delta,
        down_delta,
        gains_first_new,
        qkv_first_new,
        out_first_new,
        gate_up_first_new,
        down_first_new,
        gains_second_new,
        qkv_second_new,
        out_second_new,
        gate_up_second_new,
        down_second_new,
    )


MESH = pl.DeviceIdType.MESH
bf16, f32 = jnp.bfloat16, jnp.float32
ROWS = 2560
GATHER_UNITS = [(0, 128, 64), (128, 112, 64), (240, 240, 128), (480, 240, 128)] + [(720 + 368 * j, 368, 192) for j in range(5)]
REDUCE_UNITS = [(720 + 368 * j, 368, 192) for j in range(5)] + [(480, 240, 128), (0, 240, 128), (240, 128, 64), (368, 112, 64)]
NT = (((1,), (1,)), ((), ()))
NN = (((1,), (0,)), ((), ()))
TN = (((0,), (0,)), ((), ()))


def mm(a, b, dims=NN):
    return lax.dot_general(a, b, dims, preferred_element_type=f32)


def lanes(n=128):
    return lax.broadcasted_iota(jnp.int32, (1, n), 1)


def spread(k):
    return jnp.where(k < 3, k, k - 1)


def param_specs():
    return [
        pl.BlockSpec((2, 240), lambda k: (0, 0)),
        pl.BlockSpec((240, 256), lambda k: (0, spread(k))),
        pl.BlockSpec((240, 128), lambda k: (0, k)),
        pl.BlockSpec((240, 640), lambda k: (0, k)),
        pl.BlockSpec((128, 640), lambda k: (k, 0)),
    ]


def pack_kernel(gains, qkv, out, gu, dnT, own):
    k = pl.program_id(0)
    own[0, 0:240] = qkv[:, 0:128].astype(bf16)
    own[0, 240:480] = qkv[:, 128:256].astype(bf16)

    @pl.when(k % 4 == 3)
    def _():
        row = jnp.where(k == 3, gains[0:1], gains[1:2])
        tile = jnp.where(lax.broadcasted_iota(jnp.int32, (128, 240), 0) == 0, row, 0.0)
        own[0, 240:480] = jnp.swapaxes(tile, 0, 1).astype(bf16)

    own[0, 480:720] = jnp.where(lanes() < 960 - k * 128, out[...], 0.0).astype(bf16)
    for j in range(5):
        own[0, 720 + 368 * j : 960 + 368 * j] = gu[:, j * 128 : (j + 1) * 128].astype(bf16)
        t = jnp.swapaxes(dnT[:, j * 128 : (j + 1) * 128].astype(bf16), 0, 1)
        own[0, 960 + 368 * j : 1088 + 368 * j] = jnp.where(lanes() < 960 - k * 128, t.astype(f32), 0.0).astype(bf16)


def pack(norm_gains, qkv, out, gu, down):
    return pl.pallas_call(
        pack_kernel,
        name="pack",
        grid=(8,),
        out_shape=jax.ShapeDtypeStruct((8, ROWS, 128), bf16),
        in_specs=param_specs(),
        out_specs=pl.BlockSpec((1, ROWS, 128), lambda k: (k, 0, 0)),
    )(norm_gains, qkv, out, gu, down.T)


def adam_kernel(FIN, *refs):
    weight, first, second = refs[0:5], refs[5:10], refs[10:15]
    grad, delta, first_new, second_new = refs[15:20], refs[20:25], refs[25:30], refs[30:35]
    k = pl.program_id(0)
    every = slice(None)

    def update(i, at, g, rate):
        m = BETA_ONE * first[i][at] + (1.0 - BETA_ONE) * g
        v = BETA_TWO * second[i][at] + (1.0 - BETA_TWO) * g * g
        fixed = v * (1.0 / (1.0 - BETA_TWO**STEP))
        root = fixed * lax.rsqrt(fixed)
        step = m * (1.0 / (1.0 - BETA_ONE**STEP)) / (root + ADAM_EPS)
        if rate:
            step = step + rate * weight[i][at]
        grad[i][at] = g
        delta[i][at] = -LEARN_RATE * step
        first_new[i][at] = m
        second_new[i][at] = v

    def rows(a, b):
        return FIN[0, a:b].astype(f32)

    @pl.when(k != 3)
    def _():
        update(1, (every, slice(0, 128)), rows(0, 240), DECAY_RATE)
        update(1, (every, slice(128, 256)), rows(240, 480), DECAY_RATE)

    for i in range(2):

        @pl.when(k == 3 + 4 * i)
        def _():
            update(0, (slice(i, i + 1), every), jnp.swapaxes(rows(240, 480), 0, 1)[0:1], 0.0)

    update(2, (every, every), rows(480, 720), DECAY_RATE)
    for j in range(5):
        c = slice(j * 128, (j + 1) * 128)
        update(3, (every, c), rows(720 + 368 * j, 960 + 368 * j), DECAY_RATE)
        turned = jnp.swapaxes(FIN[0, 960 + 368 * j : 1088 + 368 * j], 0, 1).astype(f32)
        update(4, (every, c), turned, DECAY_RATE)


def adam(FIN, weights, moments):
    def five(group):
        return [*group[:4], group[4].T]

    ins = five(weights) + five(moments[:5]) + five(moments[5:])
    shapes = [jax.ShapeDtypeStruct(a.shape, f32) for a in ins[:5]] * 4
    outs = pl.pallas_call(
        adam_kernel,
        name="adam",
        grid=(8,),
        out_shape=shapes,
        in_specs=[pl.BlockSpec((1, ROWS, 128), lambda k: (k, 0, 0))] + param_specs() * 3,
        out_specs=param_specs() * 4,
    )(FIN, *ins)
    return [o.T if i % 5 == 4 else o for i, o in enumerate(outs)]


class Where:
    def __init__(w):
        rep, z = lax.axis_index("rep"), lax.axis_index("fsdp")
        c, x, y = rep % 2, (rep // 2) % 2, rep // 4
        w.rep, w.z, w.c, w.x, w.y = rep, z, c, x, y
        w.partner, w.xn, w.yn = {"rep": rep + 1 - 2 * c}, {"rep": rep + 2 - 4 * x}, {"rep": rep + 4 - 8 * y}
        w.dn = {"rep": rep + 6 - 4 * x - 8 * y}
        w.zn = [{"fsdp": (z + d) % 4} for d in (1, 2, 3)]
        w.q, w.qx, w.qy, w.qd = y * 2 + x, y * 2 + 1 - x, (1 - y) * 2 + x, (1 - y) * 2 + 1 - x
        w.k, w.kx, w.ky, w.kd = c * 4 + w.q, c * 4 + w.qx, c * 4 + w.qy, c * 4 + w.qd
        o = (1 - c) * 4
        w.kp, w.kpx, w.kpy, w.kpd = o + w.q, o + w.qx, o + w.qy, o + w.qd

    def peers(w):
        return [w.partner, w.xn, w.yn, w.dn] + w.zn


class Link:
    def __init__(g, w, sems):
        g.w, g.sems, g.ran, g.waiting = w, sems, [], False

    def copy(g, src, dst, s, r, dev):
        return pltpu.make_async_remote_copy(
            src_ref=src, dst_ref=dst, send_sem=s, recv_sem=r, device_id=dev, device_id_type=MESH
        )

    def send(g, u, i, src, dst, r, dev):
        cp = g.copy(src, dst, g.sems[0].at[u, i], r, dev)
        if g.waiting:
            cp.wait_send()
        else:
            cp.start()

    def got(g, ref, r):
        if not g.waiting:
            g.copy(ref, ref, g.sems[0].at[0, 0], r, g.w.partner).wait_recv()

    def add(g, ref, at, *parts):
        if not g.waiting:
            t = ref[at].astype(f32)
            for p, where in parts:
                t = t + p[where].astype(f32)
            ref[at] = t.astype(bf16)

    def step(g, name, u):
        getattr(g, name)(u)
        g.ran.append((name, u))

    def finish(g):
        g.waiting = True
        for name, u in g.ran:
            getattr(g, name)(u)


class Gather(Link):
    def __init__(g, w, own, W, sems):
        super().__init__(w, sems)
        g.own, g.W = own, W
        g.rz, g.rx, g.ry, g.rp = sems[1:]

    def reg(g, k, u, a=0, b=None):
        r0, n, h = GATHER_UNITS[u]
        return g.W.at[k, :, pl.ds(r0 + a, (n if b is None else b) - a)]

    def g0(g, u):
        r0, n, h = GATHER_UNITS[u]
        for d in range(3):
            src = g.own.at[g.w.k, pl.ds(r0, n)]
            g.send(u, d, src, g.W.at[g.w.k, d, pl.ds(r0, n)], g.rz.at[u, d], g.w.zn[d])

    def g1(g, u):
        r0, n, h = GATHER_UNITS[u]
        for d in range(3):
            g.got(g.W.at[g.w.k, d, pl.ds(r0, n)], g.rz.at[u, d])
        b = g.reg(g.w.k, u)
        g.send(u, 3, b, b, g.rx.at[u, 0], g.w.xn)
        g.send(u, 4, b, b, g.ry.at[u, 0], g.w.yn)
        g.send(u, 5, b, b, g.rp.at[u, 0], g.w.partner)

    def g2a(g, u):
        h = GATHER_UNITS[u][2]
        g.got(g.reg(g.w.kx, u), g.rx.at[u, 0])
        b = g.reg(g.w.kx, u, 0, h)
        g.send(u, 6, b, b, g.ry.at[u, 1], g.w.yn)
        b = g.reg(g.w.kx, u)
        g.send(u, 7, b, b, g.rp.at[u, 1], g.w.partner)

    def g2b(g, u):
        h = GATHER_UNITS[u][2]
        g.got(g.reg(g.w.ky, u), g.ry.at[u, 0])
        b = g.reg(g.w.ky, u, h)
        g.send(u, 8, b, b, g.rx.at[u, 1], g.w.xn)
        b = g.reg(g.w.ky, u)
        g.send(u, 9, b, b, g.rp.at[u, 2], g.w.partner)

    def g3(g, u):
        h = GATHER_UNITS[u][2]
        g.got(g.reg(g.w.kd, u, 0, h), g.ry.at[u, 1])
        g.got(g.reg(g.w.kd, u, h), g.rx.at[u, 1])
        b = g.reg(g.w.kd, u)
        g.send(u, 10, b, b, g.rp.at[u, 3], g.w.partner)

    def g4(g, u):
        for i, k in enumerate((g.w.kp, g.w.kpx, g.w.kpy, g.w.kpd)):
            g.got(g.reg(k, u), g.rp.at[u, i])


class Reduce(Link):
    def __init__(g, w, S, RX3, RY3, RX, RY, RZ, FIN, sems):
        super().__init__(w, sems)
        g.S, g.RX3, g.RY3, g.RX, g.RY, g.RZ, g.FIN = S, RX3, RY3, RX, RY, RZ, FIN
        g.r3, g.rxy, g.rz, g.rf, g.lf = sems[1:]

    def at(g, u):
        r0, n, h = REDUCE_UNITS[u]
        return pl.ds(r0, n), g.S(u), g.w

    def z1(g, u):
        R, S, w = g.at(u)
        landing = ((slice(0, 4), g.RX), (slice(0, 4), g.RY), (slice(0, 2), g.RX3), (slice(2, 4), g.RY3))
        for i, (part, buf) in enumerate(landing):
            d = min(i, 2)
            g.send(u, i, S.at[part, (w.z + d + 1) % 4], buf.at[:, R], g.rxy.at[u, i], w.zn[d])

    def z2(g, u):
        r0, n, h = REDUCE_UNITS[u]
        R, S, w = g.at(u)
        for i, buf in enumerate((g.RX, g.RY, g.RX3, g.RY3)):
            g.got(buf.at[:, R], g.rxy.at[u, i])
        for a, third in ((0, g.RX3), (2, g.RY3)):
            part = slice(a, a + 2)
            g.add(S, (part, w.z), (g.RX, (part, R)), (g.RY, (part, R)), (third, (slice(None), R)))
        up, low = (pl.ds(0, h), pl.ds(r0, h)), (pl.ds(h, n - h), pl.ds(r0 + h, n - h))
        g.send(u, 4, S.at[w.qd, w.z, up[0]], g.RZ.at[0, up[1]], g.r3.at[u, 0], w.xn)
        g.send(u, 5, S.at[w.qd, w.z, low[0]], g.RZ.at[0, low[1]], g.r3.at[u, 1], w.yn)
        g.send(u, 6, S.at[w.qx, w.z, up[0]], g.RZ.at[1, up[1]], g.rz.at[u, 0], w.xn)
        g.send(u, 7, S.at[w.qy, w.z, low[0]], g.RZ.at[2, low[1]], g.rz.at[u, 1], w.yn)

    def z3a(g, u):
        r0, n, h = REDUCE_UNITS[u]
        R, S, w = g.at(u)
        low = (pl.ds(h, n - h), pl.ds(r0 + h, n - h))
        g.got(g.RZ.at[0, low[1]], g.r3.at[u, 1])
        g.add(S, (w.qx, w.z, low[0]), (g.RZ, (0, low[1])))
        g.send(u, 8, S.at[w.qx, w.z, low[0]], g.RZ.at[1, low[1]], g.rz.at[u, 2], w.xn)

    def z3b(g, u):
        r0, n, h = REDUCE_UNITS[u]
        R, S, w = g.at(u)
        up = (pl.ds(0, h), pl.ds(r0, h))
        g.got(g.RZ.at[0, up[1]], g.r3.at[u, 0])
        g.add(S, (w.qy, w.z, up[0]), (g.RZ, (0, up[1])))
        g.send(u, 17, S.at[w.qy, w.z, up[0]], g.RZ.at[2, up[1]], g.rz.at[u, 3], w.yn)

    def z4(g, u):
        r0, n, h = REDUCE_UNITS[u]
        R, S, w = g.at(u)
        up, low = pl.ds(r0, h), pl.ds(r0 + h, n - h)
        g.got(g.RZ.at[1, up], g.rz.at[u, 0])
        g.got(g.RZ.at[1, low], g.rz.at[u, 2])
        g.got(g.RZ.at[2, low], g.rz.at[u, 1])
        g.got(g.RZ.at[2, up], g.rz.at[u, 3])
        g.add(S, (w.q, w.z), (g.RZ, (1, R)), (g.RZ, (2, R)))
        g.share(u)

    def c1(g, u):
        R, S, w = g.at(u)
        g.send(u, 0, S.at[w.qd, 0:2], g.RX3.at[:, R], g.r3.at[u, 0], w.xn)
        g.send(u, 1, S.at[w.qd, 2:4], g.RY3.at[:, R], g.r3.at[u, 1], w.yn)
        g.send(u, 2, S.at[w.qx, 0:2], g.RX.at[0:2, R], g.rxy.at[u, 0], w.xn)
        g.send(u, 3, S.at[w.qy, 2:4], g.RY.at[2:4, R], g.rxy.at[u, 1], w.yn)

    def c2a(g, u):
        R, S, w = g.at(u)
        g.got(g.RY3.at[:, R], g.r3.at[u, 1])
        g.add(S, (w.qx, slice(2, 4)), (g.RY3, (slice(None), R)))
        g.send(u, 4, S.at[w.qx, 2:4], g.RX.at[2:4, R], g.rxy.at[u, 2], w.xn)

    def c2b(g, u):
        R, S, w = g.at(u)
        g.got(g.RX3.at[:, R], g.r3.at[u, 0])
        g.add(S, (w.qy, slice(0, 2)), (g.RX3, (slice(None), R)))
        g.send(u, 5, S.at[w.qy, 0:2], g.RY.at[0:2, R], g.rxy.at[u, 3], w.yn)

    def c3(g, u):
        R, S, w = g.at(u)
        g.got(g.RX.at[0:2, R], g.rxy.at[u, 0])
        g.got(g.RX.at[2:4, R], g.rxy.at[u, 2])
        g.got(g.RY.at[2:4, R], g.rxy.at[u, 1])
        g.got(g.RY.at[0:2, R], g.rxy.at[u, 3])
        g.add(S, (w.q,), (g.RX, (slice(None), R)), (g.RY, (slice(None), R)))
        for d in range(3):
            zt = (w.z + d + 1) % 4
            g.send(u, 6 + d, S.at[w.q, zt], g.RZ.at[d, R], g.rz.at[u, d], w.zn[d])

    def c4(g, u):
        R, S, w = g.at(u)
        for d in range(3):
            g.got(g.RZ.at[d, R], g.rz.at[u, d])
        g.add(S, (w.q, w.z), *[(g.RZ, (d, R)) for d in range(3)])
        g.share(u)

    def share(g, u):
        R, S, w = g.at(u)
        src, dst = S.at[w.q, w.z], g.FIN.at[w.k, R]
        if u in DIAGONAL:
            g.send(u, 12, src, dst, g.rf.at[u, 2], w.dn)
        g.send(u, 9, src, dst, g.rf.at[u, 0], w.xn)
        g.send(u, 10, src, dst, g.rf.at[u, 1], w.yn)
        g.send(u, 11, src, dst, g.rf.at[u, 4], w.partner)
        if not g.waiting:
            pltpu.make_async_copy(src, dst, g.lf.at[u]).start()

    def fin(g, k, u, a=0, b=None):
        r0, n, h = REDUCE_UNITS[u]
        return g.FIN.at[k, pl.ds(r0 + a, (n if b is None else b) - a)]

    def c5a(g, u):
        h, w = REDUCE_UNITS[u][2], g.w
        g.got(g.fin(w.kx, u), g.rf.at[u, 0])
        if u not in DIAGONAL:
            b = g.fin(w.kx, u, 0, h)
            g.send(u, 12, b, b, g.rf.at[u, 3], w.yn)
        b = g.fin(w.kx, u)
        g.send(u, 13, b, b, g.rf.at[u, 5], w.partner)

    def c5b(g, u):
        h, w = REDUCE_UNITS[u][2], g.w
        g.got(g.fin(w.ky, u), g.rf.at[u, 1])
        if u not in DIAGONAL:
            b = g.fin(w.ky, u, h)
            g.send(u, 14, b, b, g.rf.at[u, 2], w.xn)
        b = g.fin(w.ky, u)
        g.send(u, 15, b, b, g.rf.at[u, 6], w.partner)

    def c6(g, u):
        h, w = REDUCE_UNITS[u][2], g.w
        if u in DIAGONAL:
            g.got(g.fin(w.kd, u), g.rf.at[u, 2])
        else:
            g.got(g.fin(w.kd, u, 0, h), g.rf.at[u, 3])
            g.got(g.fin(w.kd, u, h), g.rf.at[u, 2])
        b = g.fin(w.kd, u)
        g.send(u, 16, b, b, g.rf.at[u, 7], w.partner)

    def c7(g, u):
        R, S, w = g.at(u)
        for i, k in enumerate((w.kp, w.kpx, w.kpy, w.kpd)):
            g.got(g.fin(k, u), g.rf.at[u, 4 + i])
        if not g.waiting:
            pltpu.make_async_copy(S.at[w.q, w.z], g.fin(w.k, u), g.lf.at[u]).wait()


def load_unit(w, own, W, dst, sem, u0, n, row0=0, halves=False):
    def block(k, _):
        def one(r, view, c0):
            def put(src, zs):
                rows = pl.ds(pl.multiple_of(row0 + zs * n, 16), n)
                pltpu.make_async_copy(src, view.at[rows, pl.ds(pl.multiple_of(c0, 128), 128)], sem).start()

            put(own.at[k, pl.ds(r, n)], w.z)
            for d in range(3):
                put(W.at[k, d, pl.ds(r, n)], (w.z + 3 - d) % 4)

        if halves:
            for s in range(2):
                one(u0 + s * n, dst.at[k // 4], (k % 4) * 256 + s * 128)
        else:
            one(u0, dst, k * 128)
        return 0

    lax.fori_loop(0, 8, block, 0)


def rope(t, c, s):
    first = (lanes() % 64) < 32
    return t * c + jnp.where(first, pltpu.roll(t, 96, 1), pltpu.roll(t, 32, 1)) * s


def dup(t, half):
    return jnp.where((lanes() < 64) == (half == 0), t, pltpu.roll(t, 64, 1))


def gain_row(tile):
    at = (lax.broadcasted_iota(jnp.int32, (8, 128), 0) == 0) & (lax.broadcasted_iota(jnp.int32, (8, 128), 1) == 0)
    return mm(at.astype(f32).astype(bf16), tile, NT)[0:1]


def norm(v, g):
    return v * lax.rsqrt(jnp.mean(v * v, axis=1, keepdims=True) + NORM_EPS) * g


def norm_back(v, g, u):
    r = lax.rsqrt(jnp.mean(v * v, axis=1, keepdims=True) + NORM_EPS)
    wv = u * g
    return r * wv - v * (r * r * r) * jnp.mean(wv * v, axis=1, keepdims=True), u * v * r


def head_at(h):
    t, half = h // 2, h % 2
    mine = (lanes() // 64) == half
    return t, mine, pl.ds(pl.multiple_of(t * 128, 128), 128)


def group_fwd(g, qk, k2, v2, bias, ctx, lse):
    for i in range(2):
        rows, n = pl.ds(256 * i, 256), 256 * (i + 1)
        sums = lse[rows]
        for h in (3 * g, 3 * g + 1, 3 * g + 2):
            t, mine, col = head_at(h)
            hm = jnp.where(mine, 0.125, 0.0).astype(bf16)
            s = mm(qk[rows, col] * hm, k2[g, pl.ds(0, n)], NT) + bias[rows, pl.ds(0, n)].astype(f32)
            m = jnp.max(s, axis=1, keepdims=True)
            p = jnp.exp(s - m)
            l = jnp.sum(p, axis=1, keepdims=True)
            o = mm((p * (1.0 / l)).astype(bf16), v2[g, pl.ds(0, n)])
            ctx[rows, col] = jnp.where(mine, o, ctx[rows, col].astype(f32)).astype(bf16)
            sums = jnp.where(lanes() == h, m + jnp.log(l), sums)
        lse[rows] = sums


def group_bwd(g, qk, k2, v2, bias, lse, dctx, dq, dk, dv):
    for i in range(2):
        rows, n = pl.ds(256 * i, 256), 256 * (i + 1)
        dk_part, dv_part = 0.0, 0.0
        for h in (3 * g, 3 * g + 1, 3 * g + 2):
            t, mine, col = head_at(h)
            hm = jnp.where(mine, 0.125, 0.0).astype(bf16)
            om = jnp.where(mine, 1.0, 0.0).astype(bf16)
            qs = qk[rows, col] * hm
            do = dctx[t // 4, rows, pl.ds(pl.multiple_of((t % 4) * 128, 128), 128)] * om
            le = jnp.sum(jnp.where(lanes() == h, lse[rows], 0.0), axis=1, keepdims=True)
            s = mm(qs, k2[g, pl.ds(0, n)], NT) + bias[rows, pl.ds(0, n)].astype(f32)
            p = jnp.exp(s - le)
            dp = mm(do, v2[g, pl.ds(0, n)], NT)
            dv_part += mm(p.astype(bf16), do, TN)
            ds = (p * (dp - jnp.sum(p * dp, axis=1, keepdims=True))).astype(bf16)
            dk_part += mm(ds, qs, TN)
            dq[rows, col] = jnp.where(mine, mm(ds, k2[g, pl.ds(0, n)]) * 0.125, dq[rows, col])
        if i == 0:
            dk[g] = jnp.zeros_like(dk[g])
            dv[g] = jnp.zeros_like(dv[g])
        dk[g, pl.ds(0, n)] += dk_part
        dv[g, pl.ds(0, n)] += dv_part


KEYS = [(7, 1), (8, 0), (8, 1), (9, 0), (9, 1)]
VALUES = [(10, 0), (10, 1), (11, 0), (11, 1), (12, 0)]


def layer_kernel(
    tokT, cotT, freq, ids, own,
    boT, tgT, FIN, W, n1H, ctxH,
    cot, cos, sin, qk, k2, v2, lse, mid, n2, gains,
    wg, wd, bias, n2T, n2pT, cpT, dypp, hid, dgu, hidp, dgup, da, acc, dacc, dk, dv, gcol, gcolp,
    SM, SO, RX3, RY3, RX, RY, RZ,
    lsem, ps, pr, *sems,
):
    w = Where()
    c = w.c
    bar = pltpu.get_barrier_semaphore()
    for p in w.peers():
        pl.semaphore_signal(bar, inc=1, device_id=p, device_id_type=MESH)
    tl = pltpu.make_async_copy(tokT, tgT, lsem.at[0])
    tl.start()
    cl = pltpu.make_async_copy(cotT, boT, lsem.at[1])
    cl.start()
    pl.semaphore_wait(bar, len(w.peers()))

    def summed(u):
        if u < 5:
            return SM.at[u]
        return SO.at[u - 5] if u < 7 else SO.at[2, :, :, slice(*((0, 128), (128, 240))[u - 7])]

    ga = Gather(w, own, W, sems[:5])
    re = Reduce(w, summed, RX3, RY3, RX, RY, RZ, FIN, sems[5:])
    live, local = {}, {}

    def psend(i, src, dst):
        live[i] = ga.copy(src, dst, ps.at[i], pr.at[i], w.partner)
        live[i].start()

    def psent(*which):
        for i in which:
            live.pop(i).wait_send()

    def pgot(i, dst):
        ga.copy(dst, dst, ps.at[0], pr.at[i], w.partner).wait_recv()

    def begin(name, src, dst, sem):
        local[name] = pltpu.make_async_copy(src, dst, sem)
        local[name].start()

    def end(name):
        local.pop(name).wait()

    other = pl.ds(pl.multiple_of((1 - c) * 512, 512), 512)
    mine = pl.ds(pl.multiple_of(c * 512, 512), 512)
    half_rows = [pl.ds(256 * i, 256) for i in range(2)]

    def A0():
        seq = ids[...].astype(f32)
        column = jnp.swapaxes(jnp.broadcast_to(seq, (8, 512)), 0, 1)[:, 0:1]
        for i in range(2):
            own_seq = column[256 * i : 256 * (i + 1)]
            rows = lax.broadcasted_iota(jnp.int32, (256, 512), 0) + 256 * i
            cols = lax.broadcasted_iota(jnp.int32, (256, 512), 1)
            ok = (own_seq == seq) & (cols <= rows)
            bias[pl.ds(256 * i, 256)] = jnp.where(ok, 0.0, NEG_LARGE).astype(bf16)
            first_row = jnp.sum(jnp.where(seq < own_seq, 1.0, 0.0), axis=1, keepdims=True)
            row = (lax.broadcasted_iota(jnp.int32, (256, 1), 0) + 256 * i).astype(f32)
            angle = (row - first_row) * freq[...]
            cos[pl.ds(256 * i, 256)] = jnp.cos(angle)
            sin[pl.ds(256 * i, 256)] = jnp.where((lanes() % 64) < 32, -1.0, 1.0) * jnp.sin(angle)
        lse[...] = jnp.zeros_like(lse)
        acc[...] = jnp.zeros_like(acc)
        dacc[...] = jnp.zeros_like(dacc)
        tl.wait()
        cl.wait()
        mid[...] = jnp.swapaxes(tgT[...], 0, 1).astype(f32)
        cot[:, 896:1024] = jnp.zeros((512, 128), bf16)
        cot[:, 0:960] = jnp.swapaxes(boT[...], 0, 1)

    def LQ():
        load_unit(w, own, W, wg, lsem.at[0], 0, 240, halves=True)

    def wait_q():
        pltpu.make_async_copy(wg, wg, lsem.at[0]).wait()

    def LO():
        load_unit(w, own, W, wd, lsem.at[1], 480, 240)

    def wait_o():
        view = wd.at[pl.ds(0, 960)]
        pltpu.make_async_copy(view, view, lsem.at[1]).wait()

    def A1():
        wait_q()
        gains[...] = jnp.zeros_like(gains)
        gains[0:1] = gain_row(wg[0, :, 896:1024])
        gains[1:2] = gain_row(wg[1, :, 896:1024])
        n1 = norm(mid[...], gains[0:1]).astype(bf16)
        da[:, 0:960] = n1
        tgT[...] = jnp.swapaxes(n1, 0, 1)
        for half, (lo, hi) in enumerate(((0, 6), (6, 13))):
            res = mm(da[:, 0:960], wg[half, :, 0 : (hi - lo) * 128])
            for t in range(lo, hi):
                tile = res[:, (t - lo) * 128 : (t - lo + 1) * 128]
                if t < 10:
                    tile = rope(tile, cos[...], sin[...])
                    qk[:, t * 128 : (t + 1) * 128] = tile.astype(bf16)
                for i in range(5):
                    if KEYS[i][0] == t:
                        k2[i] = dup(tile, KEYS[i][1]).astype(bf16)
                    if VALUES[i][0] == t:
                        v2[i] = dup(tile, VALUES[i][1]).astype(bf16)
        begin("n1", tgT, n1H, lsem.at[2])
        da[...] = jnp.zeros_like(da)

    def A3():
        wait_o()
        for rows in half_rows:
            m = mid[rows] + mm(da[rows, 0:960], wd[pl.ds(0, 960), 0:960])
            mid[rows] = m
            n2[rows] = norm(m, gains[1:2]).astype(bf16)
        n2T[...] = jnp.swapaxes(n2[...], 0, 1)
        boT[...] = jnp.swapaxes(da[:, 0:960], 0, 1)
        psend(0, n2T, n2pT)
        psend(1, cot.at[:, other], dypp)
        psend(2, boT, cpT)
        begin("ctx", boT, ctxH, lsem.at[3])

    def dslot(j):
        return pl.ds(pl.multiple_of(((j + 2) % 3) * 512, 512), 512)

    def L(j):
        load_unit(w, own, W, wg.at[j % 2], lsem.at[4 + j % 2], 720 + 368 * j, 240)
        load_unit(w, own, W, wd, lsem.at[6 + j % 2], 960 + 368 * j, 128, row0=((j + 2) % 3) * 512)

    def sends(j):
        b = j % 2
        return (
            ga.copy(hid.at[b], hidp.at[b], ps.at[4 + j], pr.at[4 + j], w.partner),
            ga.copy(dgu.at[b, 1 - c], dgup.at[b], ps.at[9 + j], pr.at[9 + j], w.partner),
        )

    def F(j):
        b = j % 2
        pltpu.make_async_copy(wg.at[b], wg.at[b], lsem.at[4 + b]).wait()
        view = wd.at[dslot(j)]
        pltpu.make_async_copy(view, view, lsem.at[6 + b]).wait()

        @pl.when(j >= 2)
        def _():
            sends(j - 2)[0].wait_send()
            sends(j - 2)[1].wait_send()

        def half(i, _):
            rows = pl.ds(pl.multiple_of(i * 256, 256), 256)
            gu = mm(n2[rows], wg[b])
            gate, up = gu[:, :512], gu[:, 512:]
            sg = jax.nn.sigmoid(gate)
            a = gate * sg
            hb = (a * up).astype(bf16)
            hid[b, rows] = hb
            acc[rows, 0:960] += mm(hb, wd[dslot(j), 0:960])
            dh = mm(cot[rows, 0:960], wd[dslot(j), 0:960], NT)
            dgate = (dh * up * (sg * (1.0 + gate * (1.0 - sg)))).astype(bf16)
            dup_ = (dh * a).astype(bf16)
            dgu[b, 0, rows] = dgate
            dgu[b, 1, rows] = dup_
            dacc[rows] += mm(dgate, wg[b, :, 0:512], NT) + mm(dup_, wg[b, :, 512:1024], NT)
            return 0

        lax.fori_loop(0, 2, half, 0)
        for cp in sends(j):
            cp.start()

    def cut(S, G, n, r0=0):
        for q in range(4):
            for z in range(4):
                S[q, z, r0 : r0 + n] = G[z * n : (z + 1) * n, q * 128 : (q + 1) * 128].astype(bf16)

    def R(j):
        b = j % 2

        @pl.when(j == 0)
        def _():
            pgot(0, n2pT)
            pgot(1, dypp)

        pgot(4 + j, hidp.at[b])
        pgot(9 + j, dgup.at[b])
        cut(SM.at[j], mm(n2T[...], dgu[b, c]) + mm(n2pT[...], dgup[b]), 240)
        cut(SM.at[j], mm(hid[b], cot[:, mine], TN) + mm(hidp[b], dypp[...], TN), 128, 240)

    def B1():
        for cp in sends(3) + sends(4):
            cp.wait_send()
        psent(0, 1, 2)
        LO()
        LQ()
        end("ctx")
        begin("ctxT", ctxH, n2T, lsem.at[3])
        ones = jnp.ones((256, 128), bf16)
        da[:, 896:1024] = jnp.zeros((512, 128), bf16)
        gc = 0.0
        for i, rows in enumerate(half_rows):
            m = mid[rows]
            boT[:, 256 * i : 256 * (i + 1)] = jnp.swapaxes((m + acc[rows, 0:960]).astype(bf16), 0, 1)
            dv_, gp = norm_back(m, gains[1:2], dacc[rows])
            dmid = cot[rows, 0:960].astype(f32) + dv_
            dacc[rows] = dmid
            da[rows, 0:960] = dmid.astype(bf16)
            gc = gc + mm(gp.astype(bf16), ones, TN)
        gcol[1] = gc.astype(bf16)
        psend(14, da.at[:, other], hidp.at[1])

    def B2():
        wait_o()
        hid[1, :, 384:512] = jnp.zeros((512, 128), bf16)
        hid[0] = mm(da[:, 0:960], wd[pl.ds(0, 512), 0:960], NT).astype(bf16)
        hid[1, :, 0:448] = mm(da[:, 0:960], wd[pl.ds(512, 448), 0:960], NT).astype(bf16)
        end("ctxT")
        pgot(2, cpT)
        pgot(14, hidp.at[1])
        end("n1")
        psend(3, n1H, n2pT)
        cut(SO.at[0], mm(n2T[...], da[:, mine]) + mm(cpT[...], hidp[1]), 240)
        acc[...] = jnp.zeros_like(acc)
        psent(14)
        begin("n1T", n1H, n2T, lsem.at[2])
        begin("tok", tokT, tgT, lsem.at[3])

    def D1():
        def put(half, t, tile):
            dgu[half, t // 4, :, (t % 4) * 128 : (t % 4 + 1) * 128] = tile.astype(bf16)

        first = lanes() < 64
        nsin = -sin[...]

        def fold(ref, i):
            return ref[i] + pltpu.roll(ref[i], 64, 1)

        for t in range(7):
            put(t // 6, t % 6, rope(acc[:, t * 128 : (t + 1) * 128], cos[...], nsin))
        zero = jnp.zeros((512, 128), f32)
        for half, t in ((0, 6), (0, 7), (1, 7)):
            put(half, t, zero)
        kk, vv = [fold(dk, i) for i in range(5)], [fold(dv, i) for i in range(5)]
        put(1, 1, rope(jnp.where(first, acc[:, 896:1024], kk[0]), cos[...], nsin))
        put(1, 2, rope(jnp.where(first, kk[1], kk[2]), cos[...], nsin))
        put(1, 3, rope(jnp.where(first, kk[3], kk[4]), cos[...], nsin))
        put(1, 4, jnp.where(first, vv[0], vv[1]))
        put(1, 5, jnp.where(first, vv[2], vv[3]))
        put(1, 6, jnp.where(first, vv[4], 0.0))
        psend(15, dgu.at[1 - c], dgup)

    def qgrad(sub):
        for q in range(4):
            t = 2 * q + sub
            if t == 7:
                G = gcol[c].astype(f32) + gcolp[...].astype(f32)
            else:
                at = slice((t % 4) * 128, (t % 4 + 1) * 128)
                G = mm(n2T[...], dgu[c, t // 4, :, at]) + mm(n2pT[...], dgup[t // 4, :, at])
            for z in range(4):
                SO[1 + sub, q, z] = G[z * 240 : (z + 1) * 240].astype(bf16)

    def D2():
        end("n1T")
        pgot(3, n2pT)
        pgot(15, dgup)
        qgrad(0)

    def D3():
        wait_q()
        end("tok")
        da[:, 0:960] = jnp.swapaxes(tgT[...], 0, 1)
        ones = jnp.ones((256, 128), bf16)
        gc = 0.0
        for i, rows in enumerate(half_rows):
            dn1 = mm(dgu[0, 0, rows], wg[0, :, 0:512], NT) + mm(dgu[0, 1, rows, 0:256], wg[0, :, 512:768], NT)
            dn1 += mm(dgu[1, 0, rows], wg[1, :, 0:512], NT) + mm(dgu[1, 1, rows, 0:384], wg[1, :, 512:896], NT)
            dv_, gp = norm_back(da[rows, 0:960].astype(f32), gains[0:1], dn1)
            tgT[:, 256 * i : 256 * (i + 1)] = jnp.swapaxes((dacc[rows] + dv_).astype(bf16), 0, 1)
            gc = gc + mm(gp.astype(bf16), ones, TN)
        gcol[0] = gc.astype(bf16)
        psend(16, gcol.at[1 - c], gcolp)

    def D4():
        pgot(16, gcolp)
        qgrad(1)

    steps = dict(A0=A0, LQ=LQ, A1=A1, LO=LO, A3=A3, L=L, B1=B1, B2=B2, D1=D1, D2=D2, D3=D3, D4=D4)

    def run(part):
        for name, at in part:
            if name in steps:
                steps[name](*([] if at is None else [at]))
            else:
                (ga if name[0] == "g" else re).step(name, at)

    def after(i, parts):
        for n, part in enumerate(parts):
            if part:
                pl.when(i == n)(lambda part=part: run(part))

    def heads(group, parts):
        def turn(g, _):
            group(g)
            after(g, parts)
            return 0

        lax.fori_loop(0, 5, turn, 0)

    def unit(j, _):
        F(j)
        after(j, PARTS["F"])
        R(j)
        after(j, PARTS["R"])
        return 0

    run(PARTS["start"])
    heads(lambda g: group_fwd(g, qk, k2, v2, bias, da, lse), PARTS["H"])
    run(PARTS["A3"])
    lax.fori_loop(0, 5, unit, 0)
    run(PARTS["B1"])
    heads(lambda g: group_bwd(g, qk, k2, v2, bias, lse, hid, acc, dk, dv), PARTS["K"])
    run(PARTS["D1"])
    for i in list(live):
        psent(i)
    ga.finish()
    re.finish()


def layer(tok, cot, ids, own):
    freq = ROPE_BASE ** (-2.0 * (jnp.arange(128) % 32).astype(f32) / HEAD)
    S, D = jax.ShapeDtypeStruct, pltpu.SemaphoreType.DMA

    def V(*shape, dt=bf16):
        return pltpu.VMEM(shape, dt)

    vm = pl.BlockSpec(memory_space=pltpu.VMEM)
    hb = pl.BlockSpec(memory_space=pl.ANY)
    outs = pl.pallas_call(
        layer_kernel,
        name="layer",
        out_shape=[
            S((960, 512), bf16), S((960, 512), bf16), S((8, ROWS, 128), bf16),
            S((8, 3, ROWS, 128), bf16), S((960, 512), bf16), S((960, 512), bf16),
        ],
        in_specs=[hb, hb, vm, vm, hb],
        out_specs=[vm, vm, hb, hb, hb, hb],
        scratch_shapes=[
            V(512, 1024), V(512, 128, dt=f32), V(512, 128, dt=f32), V(512, 1280), V(5, 512, 128), V(5, 512, 128), V(512, 128, dt=f32), V(512, 960, dt=f32),
            V(512, 960), V(8, 960, dt=f32),
            V(2, 960, 1024), V(1536, 1024), V(512, 512), V(960, 512), V(960, 512), V(960, 512), V(512, 512),
            V(2, 512, 512), V(2, 2, 512, 512), V(2, 512, 512), V(2, 512, 512), V(512, 1024),
            V(512, 1024, dt=f32), V(512, 960, dt=f32), V(5, 512, 128, dt=f32), V(5, 512, 128, dt=f32),
            V(2, 960, 128), V(960, 128),
            V(5, 4, 4, 368, 128), V(3, 4, 4, 240, 128),
            V(2, ROWS, 128), V(2, ROWS, 128), V(4, ROWS, 128), V(4, ROWS, 128), V(3, ROWS, 128),
            D((8,)), D((17,)), D((17,)),
            D((9, 11)), D((9, 3)), D((9, 2)), D((9, 2)), D((9, 4)),
            D((9, 18)), D((9, 2)), D((9, 4)), D((9, 4)), D((9, 8)), D((9,)),
        ],
        compiler_params=pltpu.CompilerParams(
            collective_id=0, has_side_effects=True, vmem_limit_bytes=67043328
        ),
    )(tok.T, cot.T, freq[None, :], ids[None, :], own)
    return outs[:3]


PARTS = {
    "start": [
        ("g0", 0), ("g0", 1), ("g0", 2), ("g0", 3), ("A0", None), ("g1", 0), ("g0", 4), ("g1", 1), ("g0", 5),
        ("g2a", 0), ("g2b", 0), ("g1", 2), ("g2a", 1), ("g2b", 1), ("g0", 6), ("g3", 0), ("g4", 0), ("g1", 3),
        ("g0", 7), ("g2a", 2), ("g2b", 2), ("g3", 1), ("g4", 1), ("g2a", 3), ("g2b", 3), ("g1", 4), ("g0", 8),
        ("g3", 2), ("g4", 2), ("LQ", None), ("g3", 3), ("g4", 3), ("LO", None), ("g1", 5), ("A1", None),
        ("g2a", 4), ("g2b", 4),
    ],
    "H": [
        [
            ("g2a", 5), ("g2b", 5), ("g1", 6),
        ],
        [],
        [
            ("g3", 4), ("g1", 7),
        ],
        [
            ("g3", 5), ("g4", 4), ("L", 0),
        ],
        [
            ("g2a", 6), ("g2b", 6), ("g4", 5),
        ],
    ],
    "A3": [
        ("A3", None), ("L", 1), ("g1", 8),
    ],
    "F": [
        [
            ("g3", 6), ("g2a", 7), ("g2b", 7),
        ],
        [
            ("g3", 7), ("g2a", 8), ("g2b", 8),
        ],
        [
            ("g3", 8),
        ],
        [],
        [
            ("c2a", 2), ("c2b", 2),
        ],
    ],
    "R": [
        [
            ("z1", 0), ("g4", 6), ("L", 2),
        ],
        [
            ("c1", 1), ("g4", 7), ("L", 3),
        ],
        [
            ("c2a", 1), ("c2b", 1), ("c1", 2), ("g4", 8), ("L", 4),
        ],
        [
            ("c3", 1), ("c1", 3),
        ],
        [
            ("z2", 0), ("c1", 4),
        ],
    ],
    "B1": [
        ("B1", None), ("c2a", 3), ("c2b", 3), ("B2", None), ("c1", 5),
    ],
    "K": [
        [
            ("c4", 1), ("c3", 2), ("z3a", 0), ("z3b", 0),
        ],
        [
            ("c2a", 4), ("c2b", 4),
        ],
        [],
        [
            ("c4", 2), ("c3", 3),
        ],
        [
            ("c2a", 5), ("c2b", 5),
        ],
    ],
    "D1": [
        ("D1", None), ("c5a", 1), ("c5b", 1), ("D3", None), ("z4", 0), ("D2", None), ("c5a", 2), ("c5b", 2),
        ("c4", 3), ("c3", 4), ("c1", 6), ("D4", None), ("c6", 1), ("c3", 5), ("c1", 7), ("c1", 8), ("c7", 1),
        ("c5a", 0), ("c5b", 0), ("c6", 2), ("c7", 2), ("c5a", 3), ("c5b", 3), ("c2b", 6), ("c2a", 6),
        ("c4", 4), ("c2b", 7), ("c2a", 7), ("c2b", 8), ("c2a", 8), ("c4", 5), ("c6", 0), ("c6", 3), ("c7", 0),
        ("c7", 3), ("c3", 6), ("c5a", 4), ("c5b", 4), ("c3", 7), ("c3", 8), ("c5a", 5), ("c5b", 5), ("c6", 4),
        ("c7", 4), ("c4", 6), ("c6", 5), ("c7", 5), ("c4", 7), ("c5a", 6), ("c5b", 6), ("c4", 8), ("c6", 6),
        ("c5a", 7), ("c5b", 7), ("c7", 6), ("c6", 7), ("c7", 7), ("c5a", 8), ("c5b", 8), ("c6", 8), ("c7", 8),
    ],
}

DIAGONAL = (6, 7, 8)

def on_device(tokens, sequence_ids, cotangent, norm_gains, qkv_weight, out_weight, gate_up_weight, down_weight, *moments):
    weights = (norm_gains, qkv_weight, out_weight, gate_up_weight, down_weight)
    block_out, tokens_grad, packed = layer(tokens, cotangent, sequence_ids, pack(*weights))
    return (block_out.T, tokens_grad.T, *adam(packed, weights, moments))


def solution(mesh):
    fits = mesh.shape["rep"] == 8 and mesh.shape["fsdp"] == 4
    return jax.shard_map(
        on_device if fits else on_device_any,
        mesh=mesh,
        in_specs=(
            P(("rep", "fsdp"), None),
            P(("rep", "fsdp")),
            P(("rep", "fsdp"), None),
            P(None, "fsdp"),
            P("fsdp", None),
            P("fsdp", None),
            P("fsdp", None),
            P("fsdp", None),
            P(None, "fsdp"),
            P("fsdp", None),
            P("fsdp", None),
            P("fsdp", None),
            P("fsdp", None),
            P(None, "fsdp"),
            P("fsdp", None),
            P("fsdp", None),
            P("fsdp", None),
            P("fsdp", None),
        ),
        out_specs=(
            P(("rep", "fsdp"), None),
            P(("rep", "fsdp"), None),
            P(None, "fsdp"),
            P("fsdp", None),
            P("fsdp", None),
            P("fsdp", None),
            P("fsdp", None),
            P(None, "fsdp"),
            P("fsdp", None),
            P("fsdp", None),
            P("fsdp", None),
            P("fsdp", None),
            P(None, "fsdp"),
            P("fsdp", None),
            P("fsdp", None),
            P("fsdp", None),
            P("fsdp", None),
            P(None, "fsdp"),
            P("fsdp", None),
            P("fsdp", None),
            P("fsdp", None),
            P("fsdp", None),
        ),
        check_vma=False,
    )
```

```python
import math

import jax
import jax.numpy as jnp
from jax import lax
from jax.experimental import pallas as pl
from jax.experimental.pallas import tpu as pltpu
from jax.sharding import PartitionSpec as P
D = 960
HEADS = 15
KV_HEADS = 5
HEAD = 64
FF = 2560
STEP = 4


NORM_EPS = 1e-05
ROPE_BASE = 100000.0
LEARN_RATE = 0.03
BETA_ONE = 0.9
BETA_TWO = 0.95
ADAM_EPS = 1e-08
DECAY_RATE = 0.1
NEG_LARGE = -1e30


def positions(sequence_ids):
    row_index = jnp.arange(sequence_ids.shape[0], dtype=jnp.int32)
    prior_ids = jnp.concatenate([jnp.full((1,), -1, jnp.int32), sequence_ids[:-1]])
    seq_starts = jnp.where(sequence_ids != prior_ids, row_index, 0)
    first_row = lax.cummax(seq_starts, axis=0)
    return (row_index - first_row).astype(jnp.float32)


def causal_mask(sequence_ids):
    row_index = jnp.arange(sequence_ids.shape[0], dtype=jnp.int32)
    return (sequence_ids[:, None] == sequence_ids[None, :]) & (
        row_index[None, :] <= row_index[:, None]
    )


def rope_tables(places):
    half_size = HEAD // 2
    freq_table = ROPE_BASE ** (-2.0 * jnp.arange(half_size, dtype=jnp.float32) / HEAD)
    angles = places[:, None] * freq_table[None, :]
    return (jnp.cos(angles), jnp.sin(angles))


def rotate(vectors, cosine_table, sine_table):
    half_size = vectors.shape[-1] // 2
    first_half = vectors[..., :half_size]
    second_half = vectors[..., half_size:]
    cosine_wide = cosine_table[:, None, :]
    sine_wide = sine_table[:, None, :]
    return jnp.concatenate(
        [
            first_half * cosine_wide - second_half * sine_wide,
            second_half * cosine_wide + first_half * sine_wide,
        ],
        axis=-1,
    )


def rms_norm(values, gain_row):
    row_scale = lax.rsqrt(jnp.mean(values * values, axis=-1, keepdims=True) + NORM_EPS)
    return values * row_scale * gain_row


def swiglu(gate_part, up_part):
    return gate_part * jax.nn.sigmoid(gate_part) * up_part


def adamw_update(weight, moment_one, moment_two, gradient, decay_rate):
    first_new = BETA_ONE * moment_one + (1.0 - BETA_ONE) * gradient
    second_new = BETA_TWO * moment_two + (1.0 - BETA_TWO) * gradient * gradient
    fix_one = 1.0 - BETA_ONE**STEP
    fix_two = 1.0 - BETA_TWO**STEP
    update_dir = (
        first_new / fix_one / (jnp.sqrt(second_new / fix_two) + ADAM_EPS) + decay_rate * weight
    )
    return (-LEARN_RATE * update_dir, first_new, second_new)


def split_groups(queries, keys_rot, values_kv):
    count_rows = queries.shape[0]
    group_size = HEADS // KV_HEADS
    query_groups = queries.reshape(count_rows, KV_HEADS, group_size, HEAD).transpose(1, 2, 0, 3)
    return (query_groups, keys_rot.transpose(1, 0, 2), values_kv.transpose(1, 0, 2))


def attend(queries, keys_rot, values_kv, mask_table):
    count_rows = queries.shape[0]
    scale_factor = 1.0 / math.sqrt(HEAD)
    query_groups, key_groups, value_groups = split_groups(queries, keys_rot, values_kv)

    def one_group(members):
        query_one, key_one, value_one = members
        scores = (
            jnp.einsum("gqd,kd->gqk", query_one, key_one, preferred_element_type=jnp.float32)
            * scale_factor
        )
        scores = jnp.where(mask_table[None], scores, NEG_LARGE)
        top_score = jnp.max(scores, axis=-1, keepdims=True)
        weights = jnp.exp(scores - top_score)
        total_sum = jnp.sum(weights, axis=-1, keepdims=True)
        prob_table = (weights / total_sum).astype(jnp.bfloat16)
        context_one = jnp.einsum(
            "gqk,kd->gqd", prob_table, value_one, preferred_element_type=jnp.float32
        )
        return (context_one.astype(jnp.bfloat16), (top_score + jnp.log(total_sum))[..., 0])

    context_groups, log_total = lax.map(one_group, (query_groups, key_groups, value_groups))
    context = context_groups.transpose(2, 0, 1, 3).reshape(count_rows, HEADS, HEAD)
    return (context, log_total)


def attend_back(queries, keys_rot, values_kv, mask_table, log_total, grad_context):
    count_rows = queries.shape[0]
    group_size = HEADS // KV_HEADS
    scale_factor = 1.0 / math.sqrt(HEAD)
    query_groups, key_groups, value_groups = split_groups(queries, keys_rot, values_kv)
    grad_groups = grad_context.reshape(count_rows, KV_HEADS, group_size, HEAD).transpose(1, 2, 0, 3)

    def one_group(members):
        query_one, key_one, value_one, log_one, grad_one = members
        scores = (
            jnp.einsum("gqd,kd->gqk", query_one, key_one, preferred_element_type=jnp.float32)
            * scale_factor
        )
        scores = jnp.where(mask_table[None], scores, NEG_LARGE)
        prob_table = jnp.exp(scores - log_one[..., None])
        grad_probs = jnp.einsum(
            "gqd,kd->gqk", grad_one, value_one, preferred_element_type=jnp.float32
        )
        grad_value = jnp.einsum(
            "gqk,gqd->kd",
            prob_table.astype(jnp.bfloat16),
            grad_one,
            preferred_element_type=jnp.float32,
        )
        row_delta = jnp.sum(prob_table * grad_probs, axis=-1, keepdims=True)
        grad_scores = (prob_table * (grad_probs - row_delta)).astype(jnp.bfloat16)
        grad_query = (
            jnp.einsum("gqk,kd->gqd", grad_scores, key_one, preferred_element_type=jnp.float32)
            * scale_factor
        )
        grad_key = (
            jnp.einsum("gqk,gqd->kd", grad_scores, query_one, preferred_element_type=jnp.float32)
            * scale_factor
        )
        return (grad_query, grad_key, grad_value)

    grad_q_groups, grad_k_groups, grad_v_groups = lax.map(
        one_group, (query_groups, key_groups, value_groups, log_total, grad_groups)
    )
    grad_queries = grad_q_groups.transpose(2, 0, 1, 3).reshape(count_rows, HEADS, HEAD)
    return (grad_queries, grad_k_groups.transpose(1, 0, 2), grad_v_groups.transpose(1, 0, 2))


def forward(tokens, sequence_ids, attn_set, mlp_set):
    gain_half, qkv_half, out_half = attn_set
    gate_up_half, down_half = mlp_set
    count_rows = tokens.shape[0]
    kv_width = KV_HEADS * HEAD
    inputs = tokens.astype(jnp.float32)
    gain_rows = gain_half.astype(jnp.float32)
    normed = rms_norm(inputs, gain_rows[0]).astype(jnp.bfloat16)
    mixed_cols = jnp.dot(normed, qkv_half, preferred_element_type=jnp.float32)
    cosine_table, sine_table = rope_tables(positions(sequence_ids))
    queries = rotate(
        mixed_cols[:, :D].reshape(count_rows, HEADS, HEAD), cosine_table, sine_table
    ).astype(jnp.bfloat16)
    keys_rot = rotate(
        mixed_cols[:, D : D + kv_width].reshape(count_rows, KV_HEADS, HEAD),
        cosine_table,
        sine_table,
    ).astype(jnp.bfloat16)
    values_kv = (
        mixed_cols[:, D + kv_width :].reshape(count_rows, KV_HEADS, HEAD).astype(jnp.bfloat16)
    )
    context, log_total = attend(queries, keys_rot, values_kv, causal_mask(sequence_ids))
    middle = inputs + jnp.dot(
        context.reshape(count_rows, D), out_half, preferred_element_type=jnp.float32
    )
    normed_two = rms_norm(middle, gain_rows[1]).astype(jnp.bfloat16)
    gate_up = jnp.dot(normed_two, gate_up_half, preferred_element_type=jnp.float32)
    hidden = swiglu(gate_up[:, :FF], gate_up[:, FF:]).astype(jnp.bfloat16)
    result = middle + jnp.dot(hidden, down_half, preferred_element_type=jnp.float32)
    kept_state = (
        inputs,
        normed,
        queries,
        keys_rot,
        values_kv,
        context,
        log_total,
        middle,
        normed_two,
        gate_up,
        hidden,
    )
    return (kept_state, result)


def mlp_backward(kept_state, cotangent, attn_set, mlp_set):
    middle, normed_two, gate_up, hidden = (
        kept_state[7],
        kept_state[8],
        kept_state[9],
        kept_state[10],
    )
    gain_rows = attn_set[0].astype(jnp.float32)
    gate_up_half, down_half = mlp_set
    grad_result = cotangent.astype(jnp.float32)
    grad_branch = grad_result.astype(jnp.bfloat16)
    down_grad = jnp.einsum("rf,rd->fd", hidden, grad_branch, preferred_element_type=jnp.float32)
    grad_hidden = jnp.einsum(
        "rd,fd->rf", grad_branch, down_half, preferred_element_type=jnp.float32
    )
    _, act_back = jax.vjp(swiglu, gate_up[:, :FF], gate_up[:, FF:])
    grad_gate, grad_up = act_back(grad_hidden)
    grad_mix_two = jnp.concatenate([grad_gate, grad_up], axis=1).astype(jnp.bfloat16)
    gate_up_grad = jnp.einsum(
        "rd,rf->df", normed_two, grad_mix_two, preferred_element_type=jnp.float32
    )
    grad_normed_two = jnp.einsum(
        "rf,df->rd", grad_mix_two, gate_up_half, preferred_element_type=jnp.float32
    )
    _, norm_back_two = jax.vjp(rms_norm, middle, gain_rows[1])
    grad_middle_norm, gain_two_grad = norm_back_two(grad_normed_two)
    grad_middle = grad_result + grad_middle_norm
    return ((gate_up_grad, down_grad), (grad_middle, gain_two_grad))


def attn_backward(kept_state, carried, sequence_ids, attn_set):
    inputs, normed, queries, keys_rot, values_kv, context, log_total = kept_state[:7]
    grad_middle, gain_two_grad = carried
    gain_half, qkv_half, out_half = attn_set
    gain_rows = gain_half.astype(jnp.float32)
    count_rows = inputs.shape[0]
    kv_width = KV_HEADS * HEAD
    grad_attn = grad_middle.astype(jnp.bfloat16)
    flat_context = context.reshape(count_rows, D)
    out_grad = jnp.einsum("rc,rd->cd", flat_context, grad_attn, preferred_element_type=jnp.float32)
    grad_context = jnp.einsum("rd,cd->rc", grad_attn, out_half, preferred_element_type=jnp.float32)
    grad_context = grad_context.astype(jnp.bfloat16).reshape(count_rows, HEADS, HEAD)
    grad_queries, grad_keys, grad_values = attend_back(
        queries, keys_rot, values_kv, causal_mask(sequence_ids), log_total, grad_context
    )
    cosine_table, sine_table = rope_tables(positions(sequence_ids))
    grad_q_raw = rotate(grad_queries, cosine_table, -sine_table).reshape(count_rows, D)
    grad_k_raw = rotate(grad_keys, cosine_table, -sine_table).reshape(count_rows, kv_width)
    grad_mixed = jnp.concatenate(
        [grad_q_raw, grad_k_raw, grad_values.reshape(count_rows, kv_width)], axis=1
    )
    grad_mixed = grad_mixed.astype(jnp.bfloat16)
    qkv_grad = jnp.einsum("rd,rc->dc", normed, grad_mixed, preferred_element_type=jnp.float32)
    grad_normed = jnp.einsum("rc,dc->rd", grad_mixed, qkv_half, preferred_element_type=jnp.float32)
    _, norm_back_one = jax.vjp(rms_norm, inputs, gain_rows[0])
    grad_inputs_norm, gain_one_grad = norm_back_one(grad_normed)
    tokens_grad = (grad_middle + grad_inputs_norm).astype(jnp.bfloat16)
    gains_grad = jnp.stack([gain_one_grad, gain_two_grad])
    return (tokens_grad, (gains_grad, qkv_grad, out_grad))


def on_device_any(
    tokens,
    sequence_ids,
    cotangent,
    norm_gains,
    qkv_weight,
    out_weight,
    gate_up_weight,
    down_weight,
    gains_first,
    qkv_first,
    out_first,
    gate_up_first,
    down_first,
    gains_second,
    qkv_second,
    out_second,
    gate_up_second,
    down_second,
):
    shares = lax.axis_size("rep")
    share = lax.axis_index("rep")
    both = ("fsdp", "rep")
    group = lax.axis_size("fsdp")

    def collect(shard):
        flat = shard.astype(jnp.bfloat16).reshape(shares, -1)
        piece = lax.dynamic_index_in_dim(flat, share, 0, keepdims=False)
        whole = lax.all_gather(piece, both, axis=0, tiled=True)
        return whole.reshape(shard.shape[0] * group, shard.shape[1])

    def total(gradient, shard):
        piece = lax.psum_scatter(
            gradient.astype(jnp.bfloat16).reshape(-1), both, scatter_dimension=0, tiled=True
        )
        flat = lax.all_gather(piece, "rep", axis=0, tiled=True)
        return flat.reshape(shard.shape).astype(jnp.float32)

    gain_full = lax.all_gather(norm_gains.astype(jnp.bfloat16), "fsdp", axis=1, tiled=True)
    qkv_full = collect(qkv_weight)
    out_full = collect(out_weight)
    mlp_set = (collect(gate_up_weight), collect(down_weight))
    attn_set = (gain_full, qkv_full, out_full)
    kept_state, result = forward(tokens, sequence_ids, attn_set, mlp_set)
    block_out = result.astype(jnp.bfloat16)
    mlp_grads, carried = mlp_backward(kept_state, cotangent, attn_set, mlp_set)
    down_total = total(mlp_grads[1], down_weight)
    gate_up_total = total(mlp_grads[0], gate_up_weight)
    tokens_grad, attn_grads = attn_backward(kept_state, carried, sequence_ids, attn_set)
    gains_part = lax.psum_scatter(attn_grads[0], "fsdp", scatter_dimension=1, tiled=True)
    gains_total = lax.psum(gains_part, "rep")
    qkv_total = total(attn_grads[1], qkv_weight)
    out_total = total(attn_grads[2], out_weight)
    gains_delta, gains_first_new, gains_second_new = adamw_update(
        norm_gains, gains_first, gains_second, gains_total, 0.0
    )
    qkv_delta, qkv_first_new, qkv_second_new = adamw_update(
        qkv_weight, qkv_first, qkv_second, qkv_total, DECAY_RATE
    )
    out_delta, out_first_new, out_second_new = adamw_update(
        out_weight, out_first, out_second, out_total, DECAY_RATE
    )
    gate_up_delta, gate_up_first_new, gate_up_second_new = adamw_update(
        gate_up_weight, gate_up_first, gate_up_second, gate_up_total, DECAY_RATE
    )
    down_delta, down_first_new, down_second_new = adamw_update(
        down_weight, down_first, down_second, down_total, DECAY_RATE
    )
    return (
        block_out,
        tokens_grad,
        gains_total,
        qkv_total,
        out_total,
        gate_up_total,
        down_total,
        gains_delta,
        qkv_delta,
        out_delta,
        gate_up_delta,
        down_delta,
        gains_first_new,
        qkv_first_new,
        out_first_new,
        gate_up_first_new,
        down_first_new,
        gains_second_new,
        qkv_second_new,
        out_second_new,
        gate_up_second_new,
        down_second_new,
    )


MESH = pl.DeviceIdType.MESH
bf16, f32 = jnp.bfloat16, jnp.float32
ROWS = 2560
GATHER_UNITS = [(0, 128, 64), (128, 112, 64), (240, 240, 128), (480, 240, 128)] + [(720 + 368 * j, 368, 192) for j in range(5)]
REDUCE_UNITS = [(720 + 368 * j, 368, 192) for j in range(5)] + [(480, 240, 128), (0, 240, 128), (240, 128, 64), (368, 112, 64)]
NT = (((1,), (1,)), ((), ()))
NN = (((1,), (0,)), ((), ()))
TN = (((0,), (0,)), ((), ()))


def mm(a, b, dims=NN):
    return lax.dot_general(a, b, dims, preferred_element_type=f32)


def lanes(n=128):
    return lax.broadcasted_iota(jnp.int32, (1, n), 1)


def spread(k):
    return jnp.where(k < 3, k, k - 1)


def param_specs():
    return [
        pl.BlockSpec((2, 240), lambda k: (0, 0)),
        pl.BlockSpec((240, 256), lambda k: (0, spread(k))),
        pl.BlockSpec((240, 128), lambda k: (0, k)),
        pl.BlockSpec((240, 640), lambda k: (0, k)),
        pl.BlockSpec((128, 640), lambda k: (k, 0)),
    ]


def adam_kernel(FIN, *refs):
    weight, first, second = refs[0:5], refs[5:10], refs[10:15]
    grad, delta, first_new, second_new = refs[15:20], refs[20:25], refs[25:30], refs[30:35]
    k = pl.program_id(0)
    every = slice(None)

    def update(i, at, g, rate):
        m = BETA_ONE * first[i][at] + (1.0 - BETA_ONE) * g
        v = BETA_TWO * second[i][at] + (1.0 - BETA_TWO) * g * g
        fixed = v * (1.0 / (1.0 - BETA_TWO**STEP))
        root = fixed * lax.rsqrt(fixed)
        step = m * (1.0 / (1.0 - BETA_ONE**STEP)) / (root + ADAM_EPS)
        if rate:
            step = step + rate * weight[i][at]
        grad[i][at] = g
        delta[i][at] = -LEARN_RATE * step
        first_new[i][at] = m
        second_new[i][at] = v

    def rows(a, b):
        return FIN[0, a:b].astype(f32)

    @pl.when(k != 3)
    def _():
        update(1, (every, slice(0, 128)), rows(0, 240), DECAY_RATE)
        update(1, (every, slice(128, 256)), rows(240, 480), DECAY_RATE)

    for i in range(2):

        @pl.when(k == 3 + 4 * i)
        def _():
            update(0, (slice(i, i + 1), every), jnp.swapaxes(rows(240, 480), 0, 1)[0:1], 0.0)

    update(2, (every, every), rows(480, 720), DECAY_RATE)
    for j in range(5):
        c = slice(j * 128, (j + 1) * 128)
        update(3, (every, c), rows(720 + 368 * j, 960 + 368 * j), DECAY_RATE)
        turned = jnp.swapaxes(FIN[0, 960 + 368 * j : 1088 + 368 * j], 0, 1).astype(f32)
        update(4, (every, c), turned, DECAY_RATE)


def adam(FIN, weights, moments):
    def five(group):
        return [*group[:4], group[4].T]

    ins = five(weights) + five(moments[:5]) + five(moments[5:])
    shapes = [jax.ShapeDtypeStruct(a.shape, f32) for a in ins[:5]] * 4
    outs = pl.pallas_call(
        adam_kernel,
        name="adam",
        grid=(8,),
        out_shape=shapes,
        in_specs=[pl.BlockSpec((1, ROWS, 128), lambda k: (k, 0, 0))] + param_specs() * 3,
        out_specs=param_specs() * 4,
    )(FIN, *ins)
    return [o.T if i % 5 == 4 else o for i, o in enumerate(outs)]


class Where:
    def __init__(w):
        rep, z = lax.axis_index("rep"), lax.axis_index("fsdp")
        c, x, y = rep % 2, (rep // 2) % 2, rep // 4
        w.rep, w.z, w.c, w.x, w.y = rep, z, c, x, y
        w.partner, w.xn, w.yn = {"rep": rep + 1 - 2 * c}, {"rep": rep + 2 - 4 * x}, {"rep": rep + 4 - 8 * y}
        w.dn = {"rep": rep + 6 - 4 * x - 8 * y}
        w.zn = [{"fsdp": (z + d) % 4} for d in (1, 2, 3)]
        w.q, w.qx, w.qy, w.qd = y * 2 + x, y * 2 + 1 - x, (1 - y) * 2 + x, (1 - y) * 2 + 1 - x
        w.k, w.kx, w.ky, w.kd = c * 4 + w.q, c * 4 + w.qx, c * 4 + w.qy, c * 4 + w.qd
        o = (1 - c) * 4
        w.kp, w.kpx, w.kpy, w.kpd = o + w.q, o + w.qx, o + w.qy, o + w.qd

    def peers(w):
        return [w.partner, w.xn, w.yn, w.dn] + w.zn


class Link:
    def __init__(g, w, sems):
        g.w, g.sems, g.ran, g.waiting = w, sems, [], False

    def copy(g, src, dst, s, r, dev):
        return pltpu.make_async_remote_copy(
            src_ref=src, dst_ref=dst, send_sem=s, recv_sem=r, device_id=dev, device_id_type=MESH
        )

    def send(g, u, i, src, dst, r, dev):
        cp = g.copy(src, dst, g.sems[0].at[u, i], r, dev)
        if g.waiting:
            cp.wait_send()
        else:
            cp.start()

    def got(g, ref, r):
        if not g.waiting:
            g.copy(ref, ref, g.sems[0].at[0, 0], r, g.w.partner).wait_recv()

    def add(g, ref, at, *parts):
        if not g.waiting:
            t = ref[at].astype(f32)
            for p, where in parts:
                t = t + p[where].astype(f32)
            ref[at] = t.astype(bf16)

    def step(g, name, u):
        getattr(g, name)(u)
        if name != "g0":
            g.ran.append((name, u))

    def finish(g):
        g.waiting = True
        for name, u in g.ran:
            getattr(g, name)(u)


class Gather(Link):
    def __init__(g, w, own, W, sems):
        super().__init__(w, sems)
        g.own, g.W = own, W
        g.rz, g.rx, g.ry, g.rp = sems[1:]

    def reg(g, k, u, a=0, b=None):
        r0, n, h = GATHER_UNITS[u]
        return g.W.at[k, :, pl.ds(r0 + a, (n if b is None else b) - a)]

    def g0(g, u):
        r0, n, h = GATHER_UNITS[u]
        for d in range(3):
            g.send(u, d, g.own(u, g.w.k), g.W.at[g.w.k, d, pl.ds(r0, n)], g.rz.at[u, d], g.w.zn[d])

    def g1(g, u):
        r0, n, h = GATHER_UNITS[u]
        for d in range(3):
            g.got(g.W.at[g.w.k, d, pl.ds(r0, n)], g.rz.at[u, d])
        b = g.reg(g.w.k, u)
        g.send(u, 3, b, b, g.rx.at[u, 0], g.w.xn)
        g.send(u, 4, b, b, g.ry.at[u, 0], g.w.yn)
        g.send(u, 5, b, b, g.rp.at[u, 0], g.w.partner)

    def g2a(g, u):
        h = GATHER_UNITS[u][2]
        g.got(g.reg(g.w.kx, u), g.rx.at[u, 0])
        b = g.reg(g.w.kx, u, 0, h)
        g.send(u, 6, b, b, g.ry.at[u, 1], g.w.yn)
        b = g.reg(g.w.kx, u)
        g.send(u, 7, b, b, g.rp.at[u, 1], g.w.partner)

    def g2b(g, u):
        h = GATHER_UNITS[u][2]
        g.got(g.reg(g.w.ky, u), g.ry.at[u, 0])
        b = g.reg(g.w.ky, u, h)
        g.send(u, 8, b, b, g.rx.at[u, 1], g.w.xn)
        b = g.reg(g.w.ky, u)
        g.send(u, 9, b, b, g.rp.at[u, 2], g.w.partner)

    def g3(g, u):
        h = GATHER_UNITS[u][2]
        g.got(g.reg(g.w.kd, u, 0, h), g.ry.at[u, 1])
        g.got(g.reg(g.w.kd, u, h), g.rx.at[u, 1])
        b = g.reg(g.w.kd, u)
        g.send(u, 10, b, b, g.rp.at[u, 3], g.w.partner)

    def g4(g, u):
        for i, k in enumerate((g.w.kp, g.w.kpx, g.w.kpy, g.w.kpd)):
            g.got(g.reg(k, u), g.rp.at[u, i])


class Reduce(Link):
    def __init__(g, w, S, RX3, RY3, RX, RY, RZ, FIN, sems):
        super().__init__(w, sems)
        g.S, g.RX3, g.RY3, g.RX, g.RY, g.RZ, g.FIN = S, RX3, RY3, RX, RY, RZ, FIN
        g.r3, g.rxy, g.rz, g.rf, g.lf = sems[1:]

    def at(g, u):
        r0, n, h = REDUCE_UNITS[u]
        return pl.ds(r0, n), g.S(u), g.w

    def z1(g, u):
        R, S, w = g.at(u)
        landing = ((slice(0, 4), g.RX), (slice(0, 4), g.RY), (slice(0, 2), g.RX3), (slice(2, 4), g.RY3))
        for i, (part, buf) in enumerate(landing):
            d = min(i, 2)
            g.send(u, i, S.at[part, (w.z + d + 1) % 4], buf.at[:, R], g.rxy.at[u, i], w.zn[d])

    def z2(g, u):
        r0, n, h = REDUCE_UNITS[u]
        R, S, w = g.at(u)
        for i, buf in enumerate((g.RX, g.RY, g.RX3, g.RY3)):
            g.got(buf.at[:, R], g.rxy.at[u, i])
        for a, third in ((0, g.RX3), (2, g.RY3)):
            part = slice(a, a + 2)
            g.add(S, (part, w.z), (g.RX, (part, R)), (g.RY, (part, R)), (third, (slice(None), R)))
        up, low = (pl.ds(0, h), pl.ds(r0, h)), (pl.ds(h, n - h), pl.ds(r0 + h, n - h))
        g.send(u, 4, S.at[w.qd, w.z, up[0]], g.RZ.at[0, up[1]], g.r3.at[u, 0], w.xn)
        g.send(u, 5, S.at[w.qd, w.z, low[0]], g.RZ.at[0, low[1]], g.r3.at[u, 1], w.yn)
        g.send(u, 6, S.at[w.qx, w.z, up[0]], g.RZ.at[1, up[1]], g.rz.at[u, 0], w.xn)
        g.send(u, 7, S.at[w.qy, w.z, low[0]], g.RZ.at[2, low[1]], g.rz.at[u, 1], w.yn)

    def z3a(g, u):
        r0, n, h = REDUCE_UNITS[u]
        R, S, w = g.at(u)
        low = (pl.ds(h, n - h), pl.ds(r0 + h, n - h))
        g.got(g.RZ.at[0, low[1]], g.r3.at[u, 1])
        g.add(S, (w.qx, w.z, low[0]), (g.RZ, (0, low[1])))
        g.send(u, 8, S.at[w.qx, w.z, low[0]], g.RZ.at[1, low[1]], g.rz.at[u, 2], w.xn)

    def z3b(g, u):
        r0, n, h = REDUCE_UNITS[u]
        R, S, w = g.at(u)
        up = (pl.ds(0, h), pl.ds(r0, h))
        g.got(g.RZ.at[0, up[1]], g.r3.at[u, 0])
        g.add(S, (w.qy, w.z, up[0]), (g.RZ, (0, up[1])))
        g.send(u, 17, S.at[w.qy, w.z, up[0]], g.RZ.at[2, up[1]], g.rz.at[u, 3], w.yn)

    def z4(g, u):
        r0, n, h = REDUCE_UNITS[u]
        R, S, w = g.at(u)
        up, low = pl.ds(r0, h), pl.ds(r0 + h, n - h)
        g.got(g.RZ.at[1, up], g.rz.at[u, 0])
        g.got(g.RZ.at[1, low], g.rz.at[u, 2])
        g.got(g.RZ.at[2, low], g.rz.at[u, 1])
        g.got(g.RZ.at[2, up], g.rz.at[u, 3])
        g.add(S, (w.q, w.z), (g.RZ, (1, R)), (g.RZ, (2, R)))
        g.share(u)

    def c1(g, u):
        R, S, w = g.at(u)
        g.send(u, 0, S.at[w.qd, 0:2], g.RX3.at[:, R], g.r3.at[u, 0], w.xn)
        g.send(u, 1, S.at[w.qd, 2:4], g.RY3.at[:, R], g.r3.at[u, 1], w.yn)
        g.send(u, 2, S.at[w.qx, 0:2], g.RX.at[0:2, R], g.rxy.at[u, 0], w.xn)
        g.send(u, 3, S.at[w.qy, 2:4], g.RY.at[2:4, R], g.rxy.at[u, 1], w.yn)

    def c2a(g, u):
        R, S, w = g.at(u)
        g.got(g.RY3.at[:, R], g.r3.at[u, 1])
        g.add(S, (w.qx, slice(2, 4)), (g.RY3, (slice(None), R)))
        g.send(u, 4, S.at[w.qx, 2:4], g.RX.at[2:4, R], g.rxy.at[u, 2], w.xn)

    def c2b(g, u):
        R, S, w = g.at(u)
        g.got(g.RX3.at[:, R], g.r3.at[u, 0])
        g.add(S, (w.qy, slice(0, 2)), (g.RX3, (slice(None), R)))
        g.send(u, 5, S.at[w.qy, 0:2], g.RY.at[0:2, R], g.rxy.at[u, 3], w.yn)

    def c3(g, u):
        R, S, w = g.at(u)
        g.got(g.RX.at[0:2, R], g.rxy.at[u, 0])
        g.got(g.RX.at[2:4, R], g.rxy.at[u, 2])
        g.got(g.RY.at[2:4, R], g.rxy.at[u, 1])
        g.got(g.RY.at[0:2, R], g.rxy.at[u, 3])
        g.add(S, (w.q,), (g.RX, (slice(None), R)), (g.RY, (slice(None), R)))
        for d in range(3):
            zt = (w.z + d + 1) % 4
            g.send(u, 6 + d, S.at[w.q, zt], g.RZ.at[d, R], g.rz.at[u, d], w.zn[d])

    def c4(g, u):
        R, S, w = g.at(u)
        for d in range(3):
            g.got(g.RZ.at[d, R], g.rz.at[u, d])
        g.add(S, (w.q, w.z), *[(g.RZ, (d, R)) for d in range(3)])
        g.share(u)

    def share(g, u):
        R, S, w = g.at(u)
        src, dst = S.at[w.q, w.z], g.FIN.at[w.k, R]
        if u in DIAGONAL:
            g.send(u, 12, src, dst, g.rf.at[u, 2], w.dn)
        g.send(u, 9, src, dst, g.rf.at[u, 0], w.xn)
        g.send(u, 10, src, dst, g.rf.at[u, 1], w.yn)
        g.send(u, 11, src, dst, g.rf.at[u, 4], w.partner)
        if not g.waiting:
            pltpu.make_async_copy(src, dst, g.lf.at[u]).start()

    def fin(g, k, u, a=0, b=None):
        r0, n, h = REDUCE_UNITS[u]
        return g.FIN.at[k, pl.ds(r0 + a, (n if b is None else b) - a)]

    def c5a(g, u):
        h, w = REDUCE_UNITS[u][2], g.w
        g.got(g.fin(w.kx, u), g.rf.at[u, 0])
        if u not in DIAGONAL:
            b = g.fin(w.kx, u, 0, h)
            g.send(u, 12, b, b, g.rf.at[u, 3], w.yn)
        b = g.fin(w.kx, u)
        g.send(u, 13, b, b, g.rf.at[u, 5], w.partner)

    def c5b(g, u):
        h, w = REDUCE_UNITS[u][2], g.w
        g.got(g.fin(w.ky, u), g.rf.at[u, 1])
        if u not in DIAGONAL:
            b = g.fin(w.ky, u, h)
            g.send(u, 14, b, b, g.rf.at[u, 2], w.xn)
        b = g.fin(w.ky, u)
        g.send(u, 15, b, b, g.rf.at[u, 6], w.partner)

    def c6(g, u):
        h, w = REDUCE_UNITS[u][2], g.w
        if u in DIAGONAL:
            g.got(g.fin(w.kd, u), g.rf.at[u, 2])
        else:
            g.got(g.fin(w.kd, u, 0, h), g.rf.at[u, 3])
            g.got(g.fin(w.kd, u, h), g.rf.at[u, 2])
        b = g.fin(w.kd, u)
        g.send(u, 16, b, b, g.rf.at[u, 7], w.partner)

    def c7(g, u):
        R, S, w = g.at(u)
        for i, k in enumerate((w.kp, w.kpx, w.kpy, w.kpd)):
            g.got(g.fin(k, u), g.rf.at[u, 4 + i])
        if not g.waiting:
            pltpu.make_async_copy(S.at[w.q, w.z], g.fin(w.k, u), g.lf.at[u]).wait()


def load_unit(w, own, W, dst, sem, u0, n, row0=0, halves=False):
    def block(k, _):
        def one(r, s, view, c0):
            def put(src, zs):
                rows = pl.ds(pl.multiple_of(row0 + zs * n, 16), n)
                pltpu.make_async_copy(src, view.at[rows, pl.ds(pl.multiple_of(c0, 128), 128)], sem).start()

            put(own(k, s), w.z)
            for d in range(3):
                put(W.at[k, d, pl.ds(r, n)], (w.z + 3 - d) % 4)

        if halves:
            for s in range(2):
                one(u0 + s * n, s, dst.at[k // 4], (k % 4) * 256 + s * 128)
        else:
            one(u0, 0, dst, k * 128)
        return 0

    lax.fori_loop(0, 8, block, 0)


def rope(t, c, s):
    first = (lanes() % 64) < 32
    return t * c + jnp.where(first, pltpu.roll(t, 96, 1), pltpu.roll(t, 32, 1)) * s


def dup(t, half):
    return jnp.where((lanes() < 64) == (half == 0), t, pltpu.roll(t, 64, 1))


def gain_row(tile):
    at = (lax.broadcasted_iota(jnp.int32, (8, 128), 0) == 0) & (lax.broadcasted_iota(jnp.int32, (8, 128), 1) == 0)
    return mm(at.astype(f32).astype(bf16), tile, NT)[0:1]


def norm(v, g):
    return v * lax.rsqrt(jnp.mean(v * v, axis=1, keepdims=True) + NORM_EPS) * g


def norm_back(v, g, u):
    r = lax.rsqrt(jnp.mean(v * v, axis=1, keepdims=True) + NORM_EPS)
    wv = u * g
    return r * wv - v * (r * r * r) * jnp.mean(wv * v, axis=1, keepdims=True), u * v * r


def head_at(h):
    t, half = h // 2, h % 2
    mine = (lanes() // 64) == half
    return t, mine, pl.ds(pl.multiple_of(t * 128, 128), 128)


def group_fwd(g, qk, k2, v2, bias, ctx, lse):
    for i in range(2):
        rows, n = pl.ds(256 * i, 256), 256 * (i + 1)
        sums = lse[rows]
        for h in (3 * g, 3 * g + 1, 3 * g + 2):
            t, mine, col = head_at(h)
            hm = jnp.where(mine, 0.125, 0.0).astype(bf16)
            s = mm(qk[rows, col] * hm, k2[g, pl.ds(0, n)], NT) + bias[rows, pl.ds(0, n)].astype(f32)
            m = jnp.max(s, axis=1, keepdims=True)
            p = jnp.exp(s - m)
            l = jnp.sum(p, axis=1, keepdims=True)
            o = mm((p * (1.0 / l)).astype(bf16), v2[g, pl.ds(0, n)])
            ctx[rows, col] = jnp.where(mine, o, ctx[rows, col].astype(f32)).astype(bf16)
            sums = jnp.where(lanes() == h, m + jnp.log(l), sums)
        lse[rows] = sums


def group_bwd(g, qk, k2, v2, bias, lse, dctx, dq, dk, dv):
    for i in range(2):
        rows, n = pl.ds(256 * i, 256), 256 * (i + 1)
        dk_part, dv_part = 0.0, 0.0
        for h in (3 * g, 3 * g + 1, 3 * g + 2):
            t, mine, col = head_at(h)
            hm = jnp.where(mine, 0.125, 0.0).astype(bf16)
            om = jnp.where(mine, 1.0, 0.0).astype(bf16)
            qs = qk[rows, col] * hm
            do = dctx[t // 4, rows, pl.ds(pl.multiple_of((t % 4) * 128, 128), 128)] * om
            le = jnp.sum(jnp.where(lanes() == h, lse[rows], 0.0), axis=1, keepdims=True)
            s = mm(qs, k2[g, pl.ds(0, n)], NT) + bias[rows, pl.ds(0, n)].astype(f32)
            p = jnp.exp(s - le)
            dp = mm(do, v2[g, pl.ds(0, n)], NT)
            dv_part += mm(p.astype(bf16), do, TN)
            ds = (p * (dp - jnp.sum(p * dp, axis=1, keepdims=True))).astype(bf16)
            dk_part += mm(ds, qs, TN)
            dq[rows, col] = jnp.where(mine, mm(ds, k2[g, pl.ds(0, n)]) * 0.125, dq[rows, col])
        if i == 0:
            dk[g] = jnp.zeros_like(dk[g])
            dv[g] = jnp.zeros_like(dv[g])
        dk[g, pl.ds(0, n)] += dk_part
        dv[g, pl.ds(0, n)] += dv_part


KEYS = [(7, 1), (8, 0), (8, 1), (9, 0), (9, 1)]
VALUES = [(10, 0), (10, 1), (11, 0), (11, 1), (12, 0)]


def layer_kernel(
    tokT, cotT, freq, ids, norm_gains, qkv, out, gate_up, downT,
    boT, tgT, FIN, W, n1H, ctxH,
    cot, cos, sin, qk, k2, v2, lse, mid, n2, gains,
    wg, wd, bias, n2T, n2pT, cpT, dypp, hid, dgu, hidp, dgup, da, acc, dacc, dk, dv, gcol, gcolp,
    SM, SO, RX3, RY3, RX, RY, RZ, stage,
    lsem, wsem, ps, pr, *sems,
):
    w = Where()
    c = w.c
    bar = pltpu.get_barrier_semaphore()
    for p in w.peers():
        pl.semaphore_signal(bar, inc=1, device_id=p, device_id_type=MESH)
    loads = {}

    def fetch(name, *pairs):
        loads[name] = [pltpu.make_async_copy(src, dst, wsem.at[len(loads)]) for src, dst in pairs]
        for cp in loads[name]:
            cp.start()

    def fetch_unit(j):
        rows = slice(256 * (j % 2), 256 * (j % 2) + 240)
        cols = [(gate_up.at[:, k * 640 + j * 128 : k * 640 + (j + 1) * 128], acc.at[rows, k * 128 : (k + 1) * 128]) for k in range(8)]
        for k in range(8):
            pltpu.make_async_copy(*cols[k], wsem.at[2 + j]).start()
        part = downT.at[:, j * 128 : (j + 1) * 128]
        turned = (dk, dv)[j % 2]
        pltpu.make_async_copy(part.at[0:512], turned.at[0], wsem.at[7 + j]).start()
        pltpu.make_async_copy(part.at[512:960], turned.at[1, 0:448], wsem.at[12 + j]).start()

    fetch("qkv", (qkv, stage))
    fetch("out", (out, dacc.at[0:240]))
    fetch_unit(0)
    fetch_unit(1)
    tl = pltpu.make_async_copy(tokT, tgT, lsem.at[0])
    tl.start()
    cl = pltpu.make_async_copy(cotT, boT, lsem.at[1])
    cl.start()
    pl.semaphore_wait(bar, len(w.peers()))

    def summed(u):
        if u < 5:
            return SM.at[u]
        return SO.at[u - 5] if u < 7 else SO.at[2, :, :, slice(*((0, 128), (128, 240))[u - 7])]

    def held(u, k):
        at = (k // 4, k % 4)
        if u >= 4:
            return SM.at[u - 4, *at]
        return (SO.at[1, *at, 0:128], SO.at[1, *at, 128:240], SO.at[2, *at], SO.at[0, *at])[u]

    ga = Gather(w, held, W, sems[:5])
    re = Reduce(w, summed, RX3, RY3, RX, RY, RZ, FIN, sems[5:])
    live, local = {}, {}

    def psend(i, src, dst):
        live[i] = ga.copy(src, dst, ps.at[i], pr.at[i], w.partner)
        live[i].start()

    def psent(*which):
        for i in which:
            live.pop(i).wait_send()

    def pgot(i, dst):
        ga.copy(dst, dst, ps.at[0], pr.at[i], w.partner).wait_recv()

    def begin(name, src, dst, sem):
        local[name] = pltpu.make_async_copy(src, dst, sem)
        local[name].start()

    def end(name):
        local.pop(name).wait()

    other = pl.ds(pl.multiple_of((1 - c) * 512, 512), 512)
    mine = pl.ds(pl.multiple_of(c * 512, 512), 512)
    half_rows = [pl.ds(256 * i, 256) for i in range(2)]

    zero = jnp.zeros((240, 128), bf16)

    def PQ():
        loads["qkv"][0].wait()
        for t in range(13):
            k, sub = (t // 2, t % 2) if t < 6 else (4 + (t - 6) // 2, (t - 6) % 2)
            tile = SO.at[1 + sub, k // 4, k % 4]
            if t < 12:
                tile[...] = stage[:, t * 128 : (t + 1) * 128].astype(bf16)
            else:
                tile[...] = zero
                tile[:, 0:64] = stage[:, 1536:1600].astype(bf16)
        SO[1, 0, 3] = zero
        for i in range(2):
            at = lax.broadcasted_iota(jnp.int32, (128, 240), 0) == 0
            tile = jnp.where(at, norm_gains[i : i + 1], 0.0)
            SO[2, i, 3] = jnp.swapaxes(tile, 0, 1).astype(bf16)

    def PO():
        loads["out"][0].wait()
        SO[0, 1, 3] = zero
        for k in range(8):
            width = 128 if k < 7 else 64
            SO[0, k // 4, k % 4, :, 0:width] = dacc[0:240, k * 128 : k * 128 + width].astype(bf16)

    def PM(j):
        rows = slice(256 * (j % 2), 256 * (j % 2) + 240)
        turned = (dk, dv)[j % 2]
        view = acc.at[rows]
        pltpu.make_async_copy(view, view, wsem.at[2 + j]).wait()
        for i, part in enumerate((turned.at[0], turned.at[1, 0:448])):
            pltpu.make_async_copy(part, part, wsem.at[7 + 5 * i + j]).wait()
        SM[j, 1, 3, 240:368] = jnp.zeros((128, 128), bf16)
        for k in range(8):
            width = 128 if k < 7 else 64
            SM[j, k // 4, k % 4, 0:240] = acc[rows, k * 128 : (k + 1) * 128].astype(bf16)
            block = turned[k // 4, (k % 4) * 128 : (k % 4) * 128 + width].astype(bf16)
            SM[j, k // 4, k % 4, 240:368, 0:width] = jnp.swapaxes(block, 0, 1)
        if j + 2 < 5:
            fetch_unit(j + 2)

    def A0():
        seq = ids[...].astype(f32)
        column = jnp.swapaxes(jnp.broadcast_to(seq, (8, 512)), 0, 1)[:, 0:1]
        for i in range(2):
            own_seq = column[256 * i : 256 * (i + 1)]
            rows = lax.broadcasted_iota(jnp.int32, (256, 512), 0) + 256 * i
            cols = lax.broadcasted_iota(jnp.int32, (256, 512), 1)
            ok = (own_seq == seq) & (cols <= rows)
            bias[pl.ds(256 * i, 256)] = jnp.where(ok, 0.0, NEG_LARGE).astype(bf16)
            first_row = jnp.sum(jnp.where(seq < own_seq, 1.0, 0.0), axis=1, keepdims=True)
            row = (lax.broadcasted_iota(jnp.int32, (256, 1), 0) + 256 * i).astype(f32)
            angle = (row - first_row) * freq[...]
            cos[pl.ds(256 * i, 256)] = jnp.cos(angle)
            sin[pl.ds(256 * i, 256)] = jnp.where((lanes() % 64) < 32, -1.0, 1.0) * jnp.sin(angle)
        lse[...] = jnp.zeros_like(lse)
        tl.wait()
        cl.wait()
        mid[...] = jnp.swapaxes(tgT[...], 0, 1).astype(f32)
        cot[:, 896:1024] = jnp.zeros((512, 128), bf16)
        cot[:, 0:960] = jnp.swapaxes(boT[...], 0, 1)

    def LQ():
        load_unit(w, lambda k, s: SO.at[1 + s, k // 4, k % 4], W, wg, lsem.at[0], 0, 240, halves=True)

    def wait_q():
        pltpu.make_async_copy(wg, wg, lsem.at[0]).wait()

    def LO():
        load_unit(w, lambda k, s: SO.at[0, k // 4, k % 4], W, wd, lsem.at[1], 480, 240)

    def wait_o():
        view = wd.at[pl.ds(0, 960)]
        pltpu.make_async_copy(view, view, lsem.at[1]).wait()

    def A1():
        wait_q()
        acc[...] = jnp.zeros_like(acc)
        dacc[...] = jnp.zeros_like(dacc)
        gains[...] = jnp.zeros_like(gains)
        gains[0:1] = gain_row(wg[0, :, 896:1024])
        gains[1:2] = gain_row(wg[1, :, 896:1024])
        n1 = norm(mid[...], gains[0:1]).astype(bf16)
        da[:, 0:960] = n1
        tgT[...] = jnp.swapaxes(n1, 0, 1)
        for half, (lo, hi) in enumerate(((0, 6), (6, 13))):
            res = mm(da[:, 0:960], wg[half, :, 0 : (hi - lo) * 128])
            for t in range(lo, hi):
                tile = res[:, (t - lo) * 128 : (t - lo + 1) * 128]
                if t < 10:
                    tile = rope(tile, cos[...], sin[...])
                    qk[:, t * 128 : (t + 1) * 128] = tile.astype(bf16)
                for i in range(5):
                    if KEYS[i][0] == t:
                        k2[i] = dup(tile, KEYS[i][1]).astype(bf16)
                    if VALUES[i][0] == t:
                        v2[i] = dup(tile, VALUES[i][1]).astype(bf16)
        begin("n1", tgT, n1H, lsem.at[2])
        da[...] = jnp.zeros_like(da)

    def A3():
        wait_o()
        for rows in half_rows:
            m = mid[rows] + mm(da[rows, 0:960], wd[pl.ds(0, 960), 0:960])
            mid[rows] = m
            n2[rows] = norm(m, gains[1:2]).astype(bf16)
        n2T[...] = jnp.swapaxes(n2[...], 0, 1)
        boT[...] = jnp.swapaxes(da[:, 0:960], 0, 1)
        psend(0, n2T, n2pT)
        psend(1, cot.at[:, other], dypp)
        psend(2, boT, cpT)
        begin("ctx", boT, ctxH, lsem.at[3])

    def dslot(j):
        return pl.ds(pl.multiple_of(((j + 2) % 3) * 512, 512), 512)

    def L(j):
        def rows(a, b):
            return lambda k, s: SM.at[j, k // 4, k % 4, a:b]

        load_unit(w, rows(0, 240), W, wg.at[j % 2], lsem.at[4 + j % 2], 720 + 368 * j, 240)
        load_unit(w, rows(240, 368), W, wd, lsem.at[6 + j % 2], 960 + 368 * j, 128, row0=((j + 2) % 3) * 512)

    def sends(j):
        b = j % 2
        return (
            ga.copy(hid.at[b], hidp.at[b], ps.at[4 + j], pr.at[4 + j], w.partner),
            ga.copy(dgu.at[b, 1 - c], dgup.at[b], ps.at[9 + j], pr.at[9 + j], w.partner),
        )

    def F(j):
        b = j % 2
        pltpu.make_async_copy(wg.at[b], wg.at[b], lsem.at[4 + b]).wait()
        view = wd.at[dslot(j)]
        pltpu.make_async_copy(view, view, lsem.at[6 + b]).wait()

        @pl.when(j >= 2)
        def _():
            sends(j - 2)[0].wait_send()
            sends(j - 2)[1].wait_send()

        def half(i, _):
            rows = pl.ds(pl.multiple_of(i * 256, 256), 256)
            gu = mm(n2[rows], wg[b])
            gate, up = gu[:, :512], gu[:, 512:]
            sg = jax.nn.sigmoid(gate)
            a = gate * sg
            hb = (a * up).astype(bf16)
            hid[b, rows] = hb
            acc[rows, 0:960] += mm(hb, wd[dslot(j), 0:960])
            dh = mm(cot[rows, 0:960], wd[dslot(j), 0:960], NT)
            dgate = (dh * up * (sg * (1.0 + gate * (1.0 - sg)))).astype(bf16)
            dup_ = (dh * a).astype(bf16)
            dgu[b, 0, rows] = dgate
            dgu[b, 1, rows] = dup_
            dacc[rows] += mm(dgate, wg[b, :, 0:512], NT) + mm(dup_, wg[b, :, 512:1024], NT)
            return 0

        lax.fori_loop(0, 2, half, 0)
        for cp in sends(j):
            cp.start()

    def cut(S, G, n, r0=0):
        for q in range(4):
            for z in range(4):
                S[q, z, r0 : r0 + n] = G[z * n : (z + 1) * n, q * 128 : (q + 1) * 128].astype(bf16)

    def R(j):
        b = j % 2

        @pl.when(j == 0)
        def _():
            pgot(0, n2pT)
            pgot(1, dypp)

        pgot(4 + j, hidp.at[b])
        pgot(9 + j, dgup.at[b])
        cut(SM.at[j], mm(n2T[...], dgu[b, c]) + mm(n2pT[...], dgup[b]), 240)
        cut(SM.at[j], mm(hid[b], cot[:, mine], TN) + mm(hidp[b], dypp[...], TN), 128, 240)

    def B1():
        for cp in sends(3) + sends(4):
            cp.wait_send()
        psent(0, 1, 2)
        LO()
        LQ()
        end("ctx")
        begin("ctxT", ctxH, n2T, lsem.at[3])
        ones = jnp.ones((256, 128), bf16)
        da[:, 896:1024] = jnp.zeros((512, 128), bf16)
        gc = 0.0
        for i, rows in enumerate(half_rows):
            m = mid[rows]
            boT[:, 256 * i : 256 * (i + 1)] = jnp.swapaxes((m + acc[rows, 0:960]).astype(bf16), 0, 1)
            dv_, gp = norm_back(m, gains[1:2], dacc[rows])
            dmid = cot[rows, 0:960].astype(f32) + dv_
            dacc[rows] = dmid
            da[rows, 0:960] = dmid.astype(bf16)
            gc = gc + mm(gp.astype(bf16), ones, TN)
        gcol[1] = gc.astype(bf16)
        psend(14, da.at[:, other], hidp.at[1])

    def B2():
        wait_o()
        hid[1, :, 384:512] = jnp.zeros((512, 128), bf16)
        hid[0] = mm(da[:, 0:960], wd[pl.ds(0, 512), 0:960], NT).astype(bf16)
        hid[1, :, 0:448] = mm(da[:, 0:960], wd[pl.ds(512, 448), 0:960], NT).astype(bf16)
        end("ctxT")
        pgot(2, cpT)
        pgot(14, hidp.at[1])
        end("n1")
        psend(3, n1H, n2pT)
        cut(SO.at[0], mm(n2T[...], da[:, mine]) + mm(cpT[...], hidp[1]), 240)
        acc[...] = jnp.zeros_like(acc)
        psent(14)
        begin("n1T", n1H, n2T, lsem.at[2])
        begin("tok", tokT, tgT, lsem.at[3])

    def D1():
        def put(half, t, tile):
            dgu[half, t // 4, :, (t % 4) * 128 : (t % 4 + 1) * 128] = tile.astype(bf16)

        first = lanes() < 64
        nsin = -sin[...]

        def fold(ref, i):
            return ref[i] + pltpu.roll(ref[i], 64, 1)

        for t in range(7):
            put(t // 6, t % 6, rope(acc[:, t * 128 : (t + 1) * 128], cos[...], nsin))
        zero = jnp.zeros((512, 128), f32)
        for half, t in ((0, 6), (0, 7), (1, 7)):
            put(half, t, zero)
        kk, vv = [fold(dk, i) for i in range(5)], [fold(dv, i) for i in range(5)]
        put(1, 1, rope(jnp.where(first, acc[:, 896:1024], kk[0]), cos[...], nsin))
        put(1, 2, rope(jnp.where(first, kk[1], kk[2]), cos[...], nsin))
        put(1, 3, rope(jnp.where(first, kk[3], kk[4]), cos[...], nsin))
        put(1, 4, jnp.where(first, vv[0], vv[1]))
        put(1, 5, jnp.where(first, vv[2], vv[3]))
        put(1, 6, jnp.where(first, vv[4], 0.0))
        psend(15, dgu.at[1 - c], dgup)

    def qgrad(sub):
        for q in range(4):
            t = 2 * q + sub
            if t == 7:
                G = gcol[c].astype(f32) + gcolp[...].astype(f32)
            else:
                at = slice((t % 4) * 128, (t % 4 + 1) * 128)
                G = mm(n2T[...], dgu[c, t // 4, :, at]) + mm(n2pT[...], dgup[t // 4, :, at])
            for z in range(4):
                SO[1 + sub, q, z] = G[z * 240 : (z + 1) * 240].astype(bf16)

    def D2():
        end("n1T")
        pgot(3, n2pT)
        pgot(15, dgup)
        qgrad(0)

    def D3():
        wait_q()
        end("tok")
        da[:, 0:960] = jnp.swapaxes(tgT[...], 0, 1)
        ones = jnp.ones((256, 128), bf16)
        gc = 0.0
        for i, rows in enumerate(half_rows):
            dn1 = mm(dgu[0, 0, rows], wg[0, :, 0:512], NT) + mm(dgu[0, 1, rows, 0:256], wg[0, :, 512:768], NT)
            dn1 += mm(dgu[1, 0, rows], wg[1, :, 0:512], NT) + mm(dgu[1, 1, rows, 0:384], wg[1, :, 512:896], NT)
            dv_, gp = norm_back(da[rows, 0:960].astype(f32), gains[0:1], dn1)
            tgT[:, 256 * i : 256 * (i + 1)] = jnp.swapaxes((dacc[rows] + dv_).astype(bf16), 0, 1)
            gc = gc + mm(gp.astype(bf16), ones, TN)
        gcol[0] = gc.astype(bf16)
        psend(16, gcol.at[1 - c], gcolp)

    def D4():
        pgot(16, gcolp)
        qgrad(1)

    steps = dict(PQ=PQ, PO=PO, PM=PM, A0=A0, LQ=LQ, A1=A1, LO=LO, A3=A3, L=L, B1=B1, B2=B2, D1=D1, D2=D2, D3=D3, D4=D4)

    def run(part):
        for name, at in part:
            if name in steps:
                steps[name](*([] if at is None else [at]))
            else:
                (ga if name[0] == "g" else re).step(name, at)

    def after(i, parts):
        for n, part in enumerate(parts):
            if part:
                pl.when(i == n)(lambda part=part: run(part))

    def heads(group, parts):
        def turn(g, _):
            group(g)
            after(g, parts)
            return 0

        lax.fori_loop(0, 5, turn, 0)

    def unit(j, _):
        F(j)
        after(j, PARTS["F"])
        R(j)
        after(j, PARTS["R"])
        return 0

    run(PARTS["start"])
    heads(lambda g: group_fwd(g, qk, k2, v2, bias, da, lse), PARTS["H"])
    run(PARTS["A3"])
    ga.waiting = True
    for u in range(len(GATHER_UNITS)):
        ga.g0(u)
    ga.waiting = False
    lax.fori_loop(0, 5, unit, 0)
    run(PARTS["B1"])
    heads(lambda g: group_bwd(g, qk, k2, v2, bias, lse, hid, acc, dk, dv), PARTS["K"])
    run(PARTS["D1"])
    for i in list(live):
        psent(i)
    ga.finish()
    re.finish()


def layer(tok, cot, ids, weights):
    freq = ROPE_BASE ** (-2.0 * (jnp.arange(128) % 32).astype(f32) / HEAD)
    S, D = jax.ShapeDtypeStruct, pltpu.SemaphoreType.DMA

    def V(*shape, dt=bf16):
        return pltpu.VMEM(shape, dt)

    vm = pl.BlockSpec(memory_space=pltpu.VMEM)
    hb = pl.BlockSpec(memory_space=pl.ANY)
    outs = pl.pallas_call(
        layer_kernel,
        name="layer",
        out_shape=[
            S((960, 512), bf16), S((960, 512), bf16), S((8, ROWS, 128), bf16),
            S((8, 3, ROWS, 128), bf16), S((960, 512), bf16), S((960, 512), bf16),
        ],
        in_specs=[hb, hb, vm, vm, vm, hb, hb, hb, hb],
        out_specs=[vm, vm, hb, hb, hb, hb],
        scratch_shapes=[
            V(512, 1024), V(512, 128, dt=f32), V(512, 128, dt=f32), V(512, 1280), V(5, 512, 128), V(5, 512, 128), V(512, 128, dt=f32), V(512, 960, dt=f32),
            V(512, 960), V(8, 960, dt=f32),
            V(2, 960, 1024), V(1536, 1024), V(512, 512), V(960, 512), V(960, 512), V(960, 512), V(512, 512),
            V(2, 512, 512), V(2, 2, 512, 512), V(2, 512, 512), V(2, 512, 512), V(512, 1024),
            V(512, 1024, dt=f32), V(512, 960, dt=f32), V(5, 512, 128, dt=f32), V(5, 512, 128, dt=f32),
            V(2, 960, 128), V(960, 128),
            V(5, 4, 4, 368, 128), V(3, 4, 4, 240, 128),
            V(2, ROWS, 128), V(2, ROWS, 128), V(4, ROWS, 128), V(4, ROWS, 128), V(3, ROWS, 128), V(240, 1600, dt=f32),
            D((8,)), D((17,)), D((17,)), D((17,)),
            D((9, 11)), D((9, 3)), D((9, 2)), D((9, 2)), D((9, 4)),
            D((9, 18)), D((9, 2)), D((9, 4)), D((9, 4)), D((9, 8)), D((9,)),
        ],
        compiler_params=pltpu.CompilerParams(
            collective_id=0, has_side_effects=True, vmem_limit_bytes=67043328
        ),
    )(tok.T, cot.T, freq[None, :], ids[None, :], *weights[:4], weights[4].T)
    return outs[:3]


PARTS = {
    "start": [
        ("PQ", None), ("g0", 0), ("g0", 1), ("g0", 2), ("PO", None), ("g0", 3), ("PM", 0), ("PM", 1),
        ("A0", None), ("PM", 2), ("g1", 0), ("g0", 4), ("PM", 3), ("PM", 4), ("g1", 1), ("g0", 5), ("g2a", 0),
        ("g2b", 0), ("g1", 2), ("g2a", 1), ("g2b", 1), ("g0", 6), ("g3", 0), ("g4", 0), ("g1", 3), ("g0", 7),
        ("g2a", 2), ("g2b", 2), ("g3", 1), ("g4", 1), ("g2a", 3), ("g2b", 3), ("g1", 4), ("g0", 8), ("g3", 2),
        ("g4", 2), ("LQ", None), ("g3", 3), ("g4", 3), ("LO", None), ("g1", 5), ("A1", None), ("g2a", 4),
        ("g2b", 4),
    ],
    "H": [
        [
            ("g2a", 5), ("g2b", 5), ("g1", 6),
        ],
        [],
        [
            ("g3", 4), ("g1", 7),
        ],
        [
            ("g3", 5), ("g4", 4), ("L", 0),
        ],
        [
            ("g2a", 6), ("g2b", 6), ("g4", 5),
        ],
    ],
    "A3": [
        ("A3", None), ("L", 1), ("g1", 8),
    ],
    "F": [
        [
            ("g3", 6), ("g2a", 7), ("g2b", 7),
        ],
        [
            ("g3", 7), ("g2a", 8), ("g2b", 8),
        ],
        [
            ("g3", 8),
        ],
        [],
        [
            ("c2a", 2), ("c2b", 2),
        ],
    ],
    "R": [
        [
            ("z1", 0), ("g4", 6), ("L", 2),
        ],
        [
            ("c1", 1), ("g4", 7), ("L", 3),
        ],
        [
            ("c2a", 1), ("c2b", 1), ("c1", 2), ("g4", 8), ("L", 4),
        ],
        [
            ("c3", 1), ("c1", 3),
        ],
        [
            ("z2", 0), ("c1", 4),
        ],
    ],
    "B1": [
        ("B1", None), ("c2a", 3), ("c2b", 3), ("B2", None), ("c1", 5),
    ],
    "K": [
        [
            ("c4", 1), ("c3", 2), ("z3a", 0), ("z3b", 0),
        ],
        [
            ("c2a", 4), ("c2b", 4),
        ],
        [],
        [
            ("c4", 2), ("c3", 3),
        ],
        [
            ("c2a", 5), ("c2b", 5),
        ],
    ],
    "D1": [
        ("D1", None), ("c5a", 1), ("c5b", 1), ("D3", None), ("z4", 0), ("D2", None), ("c5a", 2), ("c5b", 2),
        ("c4", 3), ("c3", 4), ("c1", 6), ("D4", None), ("c6", 1), ("c3", 5), ("c1", 7), ("c1", 8), ("c7", 1),
        ("c5a", 0), ("c5b", 0), ("c6", 2), ("c7", 2), ("c5a", 3), ("c5b", 3), ("c2b", 6), ("c2a", 6),
        ("c4", 4), ("c2b", 7), ("c2a", 7), ("c2b", 8), ("c2a", 8), ("c4", 5), ("c6", 0), ("c6", 3), ("c7", 0),
        ("c7", 3), ("c3", 6), ("c5a", 4), ("c5b", 4), ("c3", 7), ("c3", 8), ("c5a", 5), ("c5b", 5), ("c6", 4),
        ("c7", 4), ("c4", 6), ("c6", 5), ("c7", 5), ("c4", 7), ("c5a", 6), ("c5b", 6), ("c4", 8), ("c6", 6),
        ("c5a", 7), ("c5b", 7), ("c7", 6), ("c6", 7), ("c7", 7), ("c5a", 8), ("c5b", 8), ("c6", 8), ("c7", 8),
    ],
}

DIAGONAL = (6, 7, 8)

def on_device(tokens, sequence_ids, cotangent, norm_gains, qkv_weight, out_weight, gate_up_weight, down_weight, *moments):
    weights = (norm_gains, qkv_weight, out_weight, gate_up_weight, down_weight)
    block_out, tokens_grad, packed = layer(tokens, cotangent, sequence_ids, weights)
    return (block_out.T, tokens_grad.T, *adam(packed, weights, moments))


def solution(mesh):
    fits = mesh.shape["rep"] == 8 and mesh.shape["fsdp"] == 4
    return jax.shard_map(
        on_device if fits else on_device_any,
        mesh=mesh,
        in_specs=(
            P(("rep", "fsdp"), None),
            P(("rep", "fsdp")),
            P(("rep", "fsdp"), None),
            P(None, "fsdp"),
            P("fsdp", None),
            P("fsdp", None),
            P("fsdp", None),
            P("fsdp", None),
            P(None, "fsdp"),
            P("fsdp", None),
            P("fsdp", None),
            P("fsdp", None),
            P("fsdp", None),
            P(None, "fsdp"),
            P("fsdp", None),
            P("fsdp", None),
            P("fsdp", None),
            P("fsdp", None),
        ),
        out_specs=(
            P(("rep", "fsdp"), None),
            P(("rep", "fsdp"), None),
            P(None, "fsdp"),
            P("fsdp", None),
            P("fsdp", None),
            P("fsdp", None),
            P("fsdp", None),
            P(None, "fsdp"),
            P("fsdp", None),
            P("fsdp", None),
            P("fsdp", None),
            P("fsdp", None),
            P(None, "fsdp"),
            P("fsdp", None),
            P("fsdp", None),
            P("fsdp", None),
            P("fsdp", None),
            P(None, "fsdp"),
            P("fsdp", None),
            P("fsdp", None),
            P("fsdp", None),
            P("fsdp", None),
        ),
        check_vma=False,
    )
```

```python
import math

import jax
import jax.numpy as jnp
from jax import lax
from jax.experimental import pallas as pl
from jax.experimental.pallas import tpu as pltpu
from jax.sharding import PartitionSpec as P
D = 960
HEADS = 15
KV_HEADS = 5
HEAD = 64
FF = 2560
STEP = 4


NORM_EPS = 1e-05
ROPE_BASE = 100000.0
LEARN_RATE = 0.03
BETA_ONE = 0.9
BETA_TWO = 0.95
ADAM_EPS = 1e-08
DECAY_RATE = 0.1
NEG_LARGE = -1e30


def positions(sequence_ids):
    row_index = jnp.arange(sequence_ids.shape[0], dtype=jnp.int32)
    prior_ids = jnp.concatenate([jnp.full((1,), -1, jnp.int32), sequence_ids[:-1]])
    seq_starts = jnp.where(sequence_ids != prior_ids, row_index, 0)
    first_row = lax.cummax(seq_starts, axis=0)
    return (row_index - first_row).astype(jnp.float32)


def causal_mask(sequence_ids):
    row_index = jnp.arange(sequence_ids.shape[0], dtype=jnp.int32)
    return (sequence_ids[:, None] == sequence_ids[None, :]) & (
        row_index[None, :] <= row_index[:, None]
    )


def rope_tables(places):
    half_size = HEAD // 2
    freq_table = ROPE_BASE ** (-2.0 * jnp.arange(half_size, dtype=jnp.float32) / HEAD)
    angles = places[:, None] * freq_table[None, :]
    return (jnp.cos(angles), jnp.sin(angles))


def rotate(vectors, cosine_table, sine_table):
    half_size = vectors.shape[-1] // 2
    first_half = vectors[..., :half_size]
    second_half = vectors[..., half_size:]
    cosine_wide = cosine_table[:, None, :]
    sine_wide = sine_table[:, None, :]
    return jnp.concatenate(
        [
            first_half * cosine_wide - second_half * sine_wide,
            second_half * cosine_wide + first_half * sine_wide,
        ],
        axis=-1,
    )


def rms_norm(values, gain_row):
    row_scale = lax.rsqrt(jnp.mean(values * values, axis=-1, keepdims=True) + NORM_EPS)
    return values * row_scale * gain_row


def swiglu(gate_part, up_part):
    return gate_part * jax.nn.sigmoid(gate_part) * up_part


def adamw_update(weight, moment_one, moment_two, gradient, decay_rate):
    first_new = BETA_ONE * moment_one + (1.0 - BETA_ONE) * gradient
    second_new = BETA_TWO * moment_two + (1.0 - BETA_TWO) * gradient * gradient
    fix_one = 1.0 - BETA_ONE**STEP
    fix_two = 1.0 - BETA_TWO**STEP
    update_dir = (
        first_new / fix_one / (jnp.sqrt(second_new / fix_two) + ADAM_EPS) + decay_rate * weight
    )
    return (-LEARN_RATE * update_dir, first_new, second_new)


def split_groups(queries, keys_rot, values_kv):
    count_rows = queries.shape[0]
    group_size = HEADS // KV_HEADS
    query_groups = queries.reshape(count_rows, KV_HEADS, group_size, HEAD).transpose(1, 2, 0, 3)
    return (query_groups, keys_rot.transpose(1, 0, 2), values_kv.transpose(1, 0, 2))


def attend(queries, keys_rot, values_kv, mask_table):
    count_rows = queries.shape[0]
    scale_factor = 1.0 / math.sqrt(HEAD)
    query_groups, key_groups, value_groups = split_groups(queries, keys_rot, values_kv)

    def one_group(members):
        query_one, key_one, value_one = members
        scores = (
            jnp.einsum("gqd,kd->gqk", query_one, key_one, preferred_element_type=jnp.float32)
            * scale_factor
        )
        scores = jnp.where(mask_table[None], scores, NEG_LARGE)
        top_score = jnp.max(scores, axis=-1, keepdims=True)
        weights = jnp.exp(scores - top_score)
        total_sum = jnp.sum(weights, axis=-1, keepdims=True)
        prob_table = (weights / total_sum).astype(jnp.bfloat16)
        context_one = jnp.einsum(
            "gqk,kd->gqd", prob_table, value_one, preferred_element_type=jnp.float32
        )
        return (context_one.astype(jnp.bfloat16), (top_score + jnp.log(total_sum))[..., 0])

    context_groups, log_total = lax.map(one_group, (query_groups, key_groups, value_groups))
    context = context_groups.transpose(2, 0, 1, 3).reshape(count_rows, HEADS, HEAD)
    return (context, log_total)


def attend_back(queries, keys_rot, values_kv, mask_table, log_total, grad_context):
    count_rows = queries.shape[0]
    group_size = HEADS // KV_HEADS
    scale_factor = 1.0 / math.sqrt(HEAD)
    query_groups, key_groups, value_groups = split_groups(queries, keys_rot, values_kv)
    grad_groups = grad_context.reshape(count_rows, KV_HEADS, group_size, HEAD).transpose(1, 2, 0, 3)

    def one_group(members):
        query_one, key_one, value_one, log_one, grad_one = members
        scores = (
            jnp.einsum("gqd,kd->gqk", query_one, key_one, preferred_element_type=jnp.float32)
            * scale_factor
        )
        scores = jnp.where(mask_table[None], scores, NEG_LARGE)
        prob_table = jnp.exp(scores - log_one[..., None])
        grad_probs = jnp.einsum(
            "gqd,kd->gqk", grad_one, value_one, preferred_element_type=jnp.float32
        )
        grad_value = jnp.einsum(
            "gqk,gqd->kd",
            prob_table.astype(jnp.bfloat16),
            grad_one,
            preferred_element_type=jnp.float32,
        )
        row_delta = jnp.sum(prob_table * grad_probs, axis=-1, keepdims=True)
        grad_scores = (prob_table * (grad_probs - row_delta)).astype(jnp.bfloat16)
        grad_query = (
            jnp.einsum("gqk,kd->gqd", grad_scores, key_one, preferred_element_type=jnp.float32)
            * scale_factor
        )
        grad_key = (
            jnp.einsum("gqk,gqd->kd", grad_scores, query_one, preferred_element_type=jnp.float32)
            * scale_factor
        )
        return (grad_query, grad_key, grad_value)

    grad_q_groups, grad_k_groups, grad_v_groups = lax.map(
        one_group, (query_groups, key_groups, value_groups, log_total, grad_groups)
    )
    grad_queries = grad_q_groups.transpose(2, 0, 1, 3).reshape(count_rows, HEADS, HEAD)
    return (grad_queries, grad_k_groups.transpose(1, 0, 2), grad_v_groups.transpose(1, 0, 2))


def forward(tokens, sequence_ids, attn_set, mlp_set):
    gain_half, qkv_half, out_half = attn_set
    gate_up_half, down_half = mlp_set
    count_rows = tokens.shape[0]
    kv_width = KV_HEADS * HEAD
    inputs = tokens.astype(jnp.float32)
    gain_rows = gain_half.astype(jnp.float32)
    normed = rms_norm(inputs, gain_rows[0]).astype(jnp.bfloat16)
    mixed_cols = jnp.dot(normed, qkv_half, preferred_element_type=jnp.float32)
    cosine_table, sine_table = rope_tables(positions(sequence_ids))
    queries = rotate(
        mixed_cols[:, :D].reshape(count_rows, HEADS, HEAD), cosine_table, sine_table
    ).astype(jnp.bfloat16)
    keys_rot = rotate(
        mixed_cols[:, D : D + kv_width].reshape(count_rows, KV_HEADS, HEAD),
        cosine_table,
        sine_table,
    ).astype(jnp.bfloat16)
    values_kv = (
        mixed_cols[:, D + kv_width :].reshape(count_rows, KV_HEADS, HEAD).astype(jnp.bfloat16)
    )
    context, log_total = attend(queries, keys_rot, values_kv, causal_mask(sequence_ids))
    middle = inputs + jnp.dot(
        context.reshape(count_rows, D), out_half, preferred_element_type=jnp.float32
    )
    normed_two = rms_norm(middle, gain_rows[1]).astype(jnp.bfloat16)
    gate_up = jnp.dot(normed_two, gate_up_half, preferred_element_type=jnp.float32)
    hidden = swiglu(gate_up[:, :FF], gate_up[:, FF:]).astype(jnp.bfloat16)
    result = middle + jnp.dot(hidden, down_half, preferred_element_type=jnp.float32)
    kept_state = (
        inputs,
        normed,
        queries,
        keys_rot,
        values_kv,
        context,
        log_total,
        middle,
        normed_two,
        gate_up,
        hidden,
    )
    return (kept_state, result)


def mlp_backward(kept_state, cotangent, attn_set, mlp_set):
    middle, normed_two, gate_up, hidden = (
        kept_state[7],
        kept_state[8],
        kept_state[9],
        kept_state[10],
    )
    gain_rows = attn_set[0].astype(jnp.float32)
    gate_up_half, down_half = mlp_set
    grad_result = cotangent.astype(jnp.float32)
    grad_branch = grad_result.astype(jnp.bfloat16)
    down_grad = jnp.einsum("rf,rd->fd", hidden, grad_branch, preferred_element_type=jnp.float32)
    grad_hidden = jnp.einsum(
        "rd,fd->rf", grad_branch, down_half, preferred_element_type=jnp.float32
    )
    _, act_back = jax.vjp(swiglu, gate_up[:, :FF], gate_up[:, FF:])
    grad_gate, grad_up = act_back(grad_hidden)
    grad_mix_two = jnp.concatenate([grad_gate, grad_up], axis=1).astype(jnp.bfloat16)
    gate_up_grad = jnp.einsum(
        "rd,rf->df", normed_two, grad_mix_two, preferred_element_type=jnp.float32
    )
    grad_normed_two = jnp.einsum(
        "rf,df->rd", grad_mix_two, gate_up_half, preferred_element_type=jnp.float32
    )
    _, norm_back_two = jax.vjp(rms_norm, middle, gain_rows[1])
    grad_middle_norm, gain_two_grad = norm_back_two(grad_normed_two)
    grad_middle = grad_result + grad_middle_norm
    return ((gate_up_grad, down_grad), (grad_middle, gain_two_grad))


def attn_backward(kept_state, carried, sequence_ids, attn_set):
    inputs, normed, queries, keys_rot, values_kv, context, log_total = kept_state[:7]
    grad_middle, gain_two_grad = carried
    gain_half, qkv_half, out_half = attn_set
    gain_rows = gain_half.astype(jnp.float32)
    count_rows = inputs.shape[0]
    kv_width = KV_HEADS * HEAD
    grad_attn = grad_middle.astype(jnp.bfloat16)
    flat_context = context.reshape(count_rows, D)
    out_grad = jnp.einsum("rc,rd->cd", flat_context, grad_attn, preferred_element_type=jnp.float32)
    grad_context = jnp.einsum("rd,cd->rc", grad_attn, out_half, preferred_element_type=jnp.float32)
    grad_context = grad_context.astype(jnp.bfloat16).reshape(count_rows, HEADS, HEAD)
    grad_queries, grad_keys, grad_values = attend_back(
        queries, keys_rot, values_kv, causal_mask(sequence_ids), log_total, grad_context
    )
    cosine_table, sine_table = rope_tables(positions(sequence_ids))
    grad_q_raw = rotate(grad_queries, cosine_table, -sine_table).reshape(count_rows, D)
    grad_k_raw = rotate(grad_keys, cosine_table, -sine_table).reshape(count_rows, kv_width)
    grad_mixed = jnp.concatenate(
        [grad_q_raw, grad_k_raw, grad_values.reshape(count_rows, kv_width)], axis=1
    )
    grad_mixed = grad_mixed.astype(jnp.bfloat16)
    qkv_grad = jnp.einsum("rd,rc->dc", normed, grad_mixed, preferred_element_type=jnp.float32)
    grad_normed = jnp.einsum("rc,dc->rd", grad_mixed, qkv_half, preferred_element_type=jnp.float32)
    _, norm_back_one = jax.vjp(rms_norm, inputs, gain_rows[0])
    grad_inputs_norm, gain_one_grad = norm_back_one(grad_normed)
    tokens_grad = (grad_middle + grad_inputs_norm).astype(jnp.bfloat16)
    gains_grad = jnp.stack([gain_one_grad, gain_two_grad])
    return (tokens_grad, (gains_grad, qkv_grad, out_grad))


def on_device_any(
    tokens,
    sequence_ids,
    cotangent,
    norm_gains,
    qkv_weight,
    out_weight,
    gate_up_weight,
    down_weight,
    gains_first,
    qkv_first,
    out_first,
    gate_up_first,
    down_first,
    gains_second,
    qkv_second,
    out_second,
    gate_up_second,
    down_second,
):
    shares = lax.axis_size("rep")
    share = lax.axis_index("rep")
    both = ("fsdp", "rep")
    group = lax.axis_size("fsdp")

    def collect(shard):
        flat = shard.astype(jnp.bfloat16).reshape(shares, -1)
        piece = lax.dynamic_index_in_dim(flat, share, 0, keepdims=False)
        whole = lax.all_gather(piece, both, axis=0, tiled=True)
        return whole.reshape(shard.shape[0] * group, shard.shape[1])

    def total(gradient, shard):
        piece = lax.psum_scatter(
            gradient.astype(jnp.bfloat16).reshape(-1), both, scatter_dimension=0, tiled=True
        )
        flat = lax.all_gather(piece, "rep", axis=0, tiled=True)
        return flat.reshape(shard.shape).astype(jnp.float32)

    gain_full = lax.all_gather(norm_gains.astype(jnp.bfloat16), "fsdp", axis=1, tiled=True)
    qkv_full = collect(qkv_weight)
    out_full = collect(out_weight)
    mlp_set = (collect(gate_up_weight), collect(down_weight))
    attn_set = (gain_full, qkv_full, out_full)
    kept_state, result = forward(tokens, sequence_ids, attn_set, mlp_set)
    block_out = result.astype(jnp.bfloat16)
    mlp_grads, carried = mlp_backward(kept_state, cotangent, attn_set, mlp_set)
    down_total = total(mlp_grads[1], down_weight)
    gate_up_total = total(mlp_grads[0], gate_up_weight)
    tokens_grad, attn_grads = attn_backward(kept_state, carried, sequence_ids, attn_set)
    gains_part = lax.psum_scatter(attn_grads[0], "fsdp", scatter_dimension=1, tiled=True)
    gains_total = lax.psum(gains_part, "rep")
    qkv_total = total(attn_grads[1], qkv_weight)
    out_total = total(attn_grads[2], out_weight)
    gains_delta, gains_first_new, gains_second_new = adamw_update(
        norm_gains, gains_first, gains_second, gains_total, 0.0
    )
    qkv_delta, qkv_first_new, qkv_second_new = adamw_update(
        qkv_weight, qkv_first, qkv_second, qkv_total, DECAY_RATE
    )
    out_delta, out_first_new, out_second_new = adamw_update(
        out_weight, out_first, out_second, out_total, DECAY_RATE
    )
    gate_up_delta, gate_up_first_new, gate_up_second_new = adamw_update(
        gate_up_weight, gate_up_first, gate_up_second, gate_up_total, DECAY_RATE
    )
    down_delta, down_first_new, down_second_new = adamw_update(
        down_weight, down_first, down_second, down_total, DECAY_RATE
    )
    return (
        block_out,
        tokens_grad,
        gains_total,
        qkv_total,
        out_total,
        gate_up_total,
        down_total,
        gains_delta,
        qkv_delta,
        out_delta,
        gate_up_delta,
        down_delta,
        gains_first_new,
        qkv_first_new,
        out_first_new,
        gate_up_first_new,
        down_first_new,
        gains_second_new,
        qkv_second_new,
        out_second_new,
        gate_up_second_new,
        down_second_new,
    )


MESH = pl.DeviceIdType.MESH
bf16, f32 = jnp.bfloat16, jnp.float32
ROWS = 2560
GATHER_UNITS = [(0, 128, 64), (128, 112, 64), (240, 240, 128), (480, 240, 128)] + [(720 + 368 * j, 368, 192) for j in range(5)]
REDUCE_UNITS = [(720 + 368 * j, 368, 192) for j in range(5)] + [(480, 240, 128), (0, 240, 128), (240, 128, 64), (368, 112, 64)]
NT = (((1,), (1,)), ((), ()))
NN = (((1,), (0,)), ((), ()))
TN = (((0,), (0,)), ((), ()))


def mm(a, b, dims=NN):
    return lax.dot_general(a, b, dims, preferred_element_type=f32)


def lanes(n=128):
    return lax.broadcasted_iota(jnp.int32, (1, n), 1)


def spread(k):
    return jnp.where(k < 3, k, k - 1)


def param_specs():
    return [
        pl.BlockSpec((2, 240), lambda k: (0, 0)),
        pl.BlockSpec((240, 256), lambda k: (0, spread(k))),
        pl.BlockSpec((240, 128), lambda k: (0, k)),
        pl.BlockSpec((240, 640), lambda k: (0, k)),
        pl.BlockSpec((128, 640), lambda k: (k, 0)),
    ]


def adam_kernel(FIN, *refs):
    weight, first, second = refs[0:5], refs[5:10], refs[10:15]
    grad, delta, first_new, second_new = refs[15:20], refs[20:25], refs[25:30], refs[30:35]
    k = pl.program_id(0)
    every = slice(None)

    def update(i, at, g, rate):
        m = BETA_ONE * first[i][at] + (1.0 - BETA_ONE) * g
        v = BETA_TWO * second[i][at] + (1.0 - BETA_TWO) * g * g
        fixed = v * (1.0 / (1.0 - BETA_TWO**STEP))
        root = fixed * lax.rsqrt(fixed)
        step = m * (1.0 / (1.0 - BETA_ONE**STEP)) / (root + ADAM_EPS)
        if rate:
            step = step + rate * weight[i][at]
        grad[i][at] = g
        delta[i][at] = -LEARN_RATE * step
        first_new[i][at] = m
        second_new[i][at] = v

    def rows(a, b):
        return FIN[0, a:b].astype(f32)

    @pl.when(k != 3)
    def _():
        update(1, (every, slice(0, 128)), rows(0, 240), DECAY_RATE)
        update(1, (every, slice(128, 256)), rows(240, 480), DECAY_RATE)

    for i in range(2):

        @pl.when(k == 3 + 4 * i)
        def _():
            update(0, (slice(i, i + 1), every), jnp.swapaxes(rows(240, 480), 0, 1)[0:1], 0.0)

    update(2, (every, every), rows(480, 720), DECAY_RATE)
    for j in range(5):
        c = slice(j * 128, (j + 1) * 128)
        update(3, (every, c), rows(720 + 368 * j, 960 + 368 * j), DECAY_RATE)
        turned = jnp.swapaxes(FIN[0, 960 + 368 * j : 1088 + 368 * j], 0, 1).astype(f32)
        update(4, (every, c), turned, DECAY_RATE)


def adam(FIN, weights, moments):
    def five(group):
        return [*group[:4], group[4].T]

    ins = five(weights) + five(moments[:5]) + five(moments[5:])
    shapes = [jax.ShapeDtypeStruct(a.shape, f32) for a in ins[:5]] * 4
    outs = pl.pallas_call(
        adam_kernel,
        name="adam",
        grid=(8,),
        out_shape=shapes,
        in_specs=[pl.BlockSpec((1, ROWS, 128), lambda k: (k, 0, 0))] + param_specs() * 3,
        out_specs=param_specs() * 4,
    )(FIN, *ins)
    return [o.T if i % 5 == 4 else o for i, o in enumerate(outs)]


class Where:
    def __init__(w):
        rep, z = lax.axis_index("rep"), lax.axis_index("fsdp")
        c, x, y = rep % 2, (rep // 2) % 2, rep // 4
        w.rep, w.z, w.c, w.x, w.y = rep, z, c, x, y
        w.partner, w.xn, w.yn = {"rep": rep + 1 - 2 * c}, {"rep": rep + 2 - 4 * x}, {"rep": rep + 4 - 8 * y}
        w.dn = {"rep": rep + 6 - 4 * x - 8 * y}
        w.zn = [{"fsdp": (z + d) % 4} for d in (1, 2, 3)]
        w.q, w.qx, w.qy, w.qd = y * 2 + x, y * 2 + 1 - x, (1 - y) * 2 + x, (1 - y) * 2 + 1 - x
        w.k, w.kx, w.ky, w.kd = c * 4 + w.q, c * 4 + w.qx, c * 4 + w.qy, c * 4 + w.qd
        o = (1 - c) * 4
        w.kp, w.kpx, w.kpy, w.kpd = o + w.q, o + w.qx, o + w.qy, o + w.qd

    def peers(w):
        return [w.partner, w.xn, w.yn, w.dn] + w.zn


class Link:
    def __init__(g, w, sems):
        g.w, g.sems, g.ran, g.waiting = w, sems, [], False

    def copy(g, src, dst, s, r, dev):
        return pltpu.make_async_remote_copy(
            src_ref=src, dst_ref=dst, send_sem=s, recv_sem=r, device_id=dev, device_id_type=MESH
        )

    def send(g, u, i, src, dst, r, dev):
        cp = g.copy(src, dst, g.sems[0].at[u, i], r, dev)
        if g.waiting:
            cp.wait_send()
        else:
            cp.start()

    def got(g, ref, r):
        if not g.waiting:
            g.copy(ref, ref, g.sems[0].at[0, 0], r, g.w.partner).wait_recv()

    def add(g, ref, at, *parts):
        if not g.waiting:
            t = ref[at].astype(f32)
            for p, where in parts:
                t = t + p[where].astype(f32)
            ref[at] = t.astype(bf16)

    def step(g, name, u):
        getattr(g, name)(u)
        if name != "g0":
            g.ran.append((name, u))

    def finish(g):
        g.waiting = True
        for name, u in g.ran:
            getattr(g, name)(u)


class Gather(Link):
    def __init__(g, w, own, W, sems):
        super().__init__(w, sems)
        g.own, g.W = own, W
        g.rz, g.rx, g.ry, g.rp = sems[1:]

    def reg(g, k, u, a=0, b=None):
        r0, n, h = GATHER_UNITS[u]
        return g.W.at[k, :, pl.ds(r0 + a, (n if b is None else b) - a)]

    def g0(g, u):
        r0, n, h = GATHER_UNITS[u]

        def out(d):
            g.send(u, d, g.own(u, g.w.k), g.W.at[g.w.k, d, pl.ds(r0, n)], g.rz.at[u, d], g.w.zn[d])

        pl.when(g.w.z != 3)(lambda: out(0))
        out(1)
        pl.when(g.w.z != 0)(lambda: out(2))

    def gr(g, u):
        r0, n, h = GATHER_UNITS[u]
        z = g.w.z

        @pl.when((z == 1) | (z == 2))
        def _():
            src = g.W.at[g.w.k, 1, pl.ds(r0, n)]
            g.got(src, g.rz.at[u, 1])
            d = 2 * (z - 1)
            g.send(u, 11, src, g.W.at[g.w.k, d, pl.ds(r0, n)], g.rz.at[u, d], {"fsdp": 3 * (z - 1)})

    def g1(g, u):
        r0, n, h = GATHER_UNITS[u]

        def block(d):
            g.got(g.W.at[g.w.k, d, pl.ds(r0, n)], g.rz.at[u, d])

        block(0)
        pl.when((g.w.z == 0) | (g.w.z == 3))(lambda: block(1))
        block(2)
        b = g.reg(g.w.k, u)
        g.send(u, 3, b, b, g.rx.at[u, 0], g.w.xn)
        g.send(u, 4, b, b, g.ry.at[u, 0], g.w.yn)
        g.send(u, 5, b, b, g.rp.at[u, 0], g.w.partner)

    def g2a(g, u):
        h = GATHER_UNITS[u][2]
        g.got(g.reg(g.w.kx, u), g.rx.at[u, 0])
        b = g.reg(g.w.kx, u, 0, h)
        g.send(u, 6, b, b, g.ry.at[u, 1], g.w.yn)
        b = g.reg(g.w.kx, u)
        g.send(u, 7, b, b, g.rp.at[u, 1], g.w.partner)

    def g2b(g, u):
        h = GATHER_UNITS[u][2]
        g.got(g.reg(g.w.ky, u), g.ry.at[u, 0])
        b = g.reg(g.w.ky, u, h)
        g.send(u, 8, b, b, g.rx.at[u, 1], g.w.xn)
        b = g.reg(g.w.ky, u)
        g.send(u, 9, b, b, g.rp.at[u, 2], g.w.partner)

    def g3(g, u):
        h = GATHER_UNITS[u][2]
        g.got(g.reg(g.w.kd, u, 0, h), g.ry.at[u, 1])
        g.got(g.reg(g.w.kd, u, h), g.rx.at[u, 1])
        b = g.reg(g.w.kd, u)
        g.send(u, 10, b, b, g.rp.at[u, 3], g.w.partner)

    def g4(g, u):
        for i, k in enumerate((g.w.kp, g.w.kpx, g.w.kpy, g.w.kpd)):
            g.got(g.reg(k, u), g.rp.at[u, i])


class Reduce(Link):
    def __init__(g, w, S, RX3, RY3, RX, RY, RZ, FIN, sems):
        super().__init__(w, sems)
        g.S, g.RX3, g.RY3, g.RX, g.RY, g.RZ, g.FIN = S, RX3, RY3, RX, RY, RZ, FIN
        g.r3, g.rxy, g.rz, g.rf, g.lf = sems[1:]

    def at(g, u):
        r0, n, h = REDUCE_UNITS[u]
        return pl.ds(r0, n), g.S(u), g.w

    def z1(g, u):
        R, S, w = g.at(u)
        landing = ((slice(0, 4), g.RX), (slice(0, 4), g.RY), (slice(0, 2), g.RX3), (slice(2, 4), g.RY3))
        for i, (part, buf) in enumerate(landing):
            d = min(i, 2)
            g.send(u, i, S.at[part, (w.z + d + 1) % 4], buf.at[:, R], g.rxy.at[u, i], w.zn[d])

    def z2(g, u):
        r0, n, h = REDUCE_UNITS[u]
        R, S, w = g.at(u)
        for i, buf in enumerate((g.RX, g.RY, g.RX3, g.RY3)):
            g.got(buf.at[:, R], g.rxy.at[u, i])
        for a, third in ((0, g.RX3), (2, g.RY3)):
            part = slice(a, a + 2)
            g.add(S, (part, w.z), (g.RX, (part, R)), (g.RY, (part, R)), (third, (slice(None), R)))
        up, low = (pl.ds(0, h), pl.ds(r0, h)), (pl.ds(h, n - h), pl.ds(r0 + h, n - h))
        g.send(u, 4, S.at[w.qd, w.z, up[0]], g.RZ.at[0, up[1]], g.r3.at[u, 0], w.xn)
        g.send(u, 5, S.at[w.qd, w.z, low[0]], g.RZ.at[0, low[1]], g.r3.at[u, 1], w.yn)
        g.send(u, 6, S.at[w.qx, w.z, up[0]], g.RZ.at[1, up[1]], g.rz.at[u, 0], w.xn)
        g.send(u, 7, S.at[w.qy, w.z, low[0]], g.RZ.at[2, low[1]], g.rz.at[u, 1], w.yn)

    def z3a(g, u):
        r0, n, h = REDUCE_UNITS[u]
        R, S, w = g.at(u)
        low = (pl.ds(h, n - h), pl.ds(r0 + h, n - h))
        g.got(g.RZ.at[0, low[1]], g.r3.at[u, 1])
        g.add(S, (w.qx, w.z, low[0]), (g.RZ, (0, low[1])))
        g.send(u, 8, S.at[w.qx, w.z, low[0]], g.RZ.at[1, low[1]], g.rz.at[u, 2], w.xn)

    def z3b(g, u):
        r0, n, h = REDUCE_UNITS[u]
        R, S, w = g.at(u)
        up = (pl.ds(0, h), pl.ds(r0, h))
        g.got(g.RZ.at[0, up[1]], g.r3.at[u, 0])
        g.add(S, (w.qy, w.z, up[0]), (g.RZ, (0, up[1])))
        g.send(u, 17, S.at[w.qy, w.z, up[0]], g.RZ.at[2, up[1]], g.rz.at[u, 3], w.yn)

    def z4(g, u):
        r0, n, h = REDUCE_UNITS[u]
        R, S, w = g.at(u)
        up, low = pl.ds(r0, h), pl.ds(r0 + h, n - h)
        g.got(g.RZ.at[1, up], g.rz.at[u, 0])
        g.got(g.RZ.at[1, low], g.rz.at[u, 2])
        g.got(g.RZ.at[2, low], g.rz.at[u, 1])
        g.got(g.RZ.at[2, up], g.rz.at[u, 3])
        g.add(S, (w.q, w.z), (g.RZ, (1, R)), (g.RZ, (2, R)))
        g.share(u)

    def c1(g, u):
        R, S, w = g.at(u)
        g.send(u, 0, S.at[w.qd, 0:2], g.RX3.at[:, R], g.r3.at[u, 0], w.xn)
        g.send(u, 1, S.at[w.qd, 2:4], g.RY3.at[:, R], g.r3.at[u, 1], w.yn)
        g.send(u, 2, S.at[w.qx, 0:2], g.RX.at[0:2, R], g.rxy.at[u, 0], w.xn)
        g.send(u, 3, S.at[w.qy, 2:4], g.RY.at[2:4, R], g.rxy.at[u, 1], w.yn)

    def c2a(g, u):
        R, S, w = g.at(u)
        g.got(g.RY3.at[:, R], g.r3.at[u, 1])
        g.add(S, (w.qx, slice(2, 4)), (g.RY3, (slice(None), R)))
        g.send(u, 4, S.at[w.qx, 2:4], g.RX.at[2:4, R], g.rxy.at[u, 2], w.xn)

    def c2b(g, u):
        R, S, w = g.at(u)
        g.got(g.RX3.at[:, R], g.r3.at[u, 0])
        g.add(S, (w.qy, slice(0, 2)), (g.RX3, (slice(None), R)))
        g.send(u, 5, S.at[w.qy, 0:2], g.RY.at[0:2, R], g.rxy.at[u, 3], w.yn)

    def c3(g, u):
        R, S, w = g.at(u)
        g.got(g.RX.at[0:2, R], g.rxy.at[u, 0])
        g.got(g.RX.at[2:4, R], g.rxy.at[u, 2])
        g.got(g.RY.at[2:4, R], g.rxy.at[u, 1])
        g.got(g.RY.at[0:2, R], g.rxy.at[u, 3])
        g.add(S, (w.q,), (g.RX, (slice(None), R)), (g.RY, (slice(None), R)))
        for d in range(3):
            zt = (w.z + d + 1) % 4
            g.send(u, 6 + d, S.at[w.q, zt], g.RZ.at[d, R], g.rz.at[u, d], w.zn[d])

    def c4(g, u):
        R, S, w = g.at(u)
        for d in range(3):
            g.got(g.RZ.at[d, R], g.rz.at[u, d])
        g.add(S, (w.q, w.z), *[(g.RZ, (d, R)) for d in range(3)])
        g.share(u)

    def share(g, u):
        R, S, w = g.at(u)
        src, dst = S.at[w.q, w.z], g.FIN.at[w.k, R]
        if u in DIAGONAL:
            g.send(u, 12, src, dst, g.rf.at[u, 2], w.dn)
        g.send(u, 9, src, dst, g.rf.at[u, 0], w.xn)
        g.send(u, 10, src, dst, g.rf.at[u, 1], w.yn)
        g.send(u, 11, src, dst, g.rf.at[u, 4], w.partner)
        if not g.waiting:
            pltpu.make_async_copy(src, dst, g.lf.at[u]).start()

    def fin(g, k, u, a=0, b=None):
        r0, n, h = REDUCE_UNITS[u]
        return g.FIN.at[k, pl.ds(r0 + a, (n if b is None else b) - a)]

    def c5a(g, u):
        h, w = REDUCE_UNITS[u][2], g.w
        g.got(g.fin(w.kx, u), g.rf.at[u, 0])
        if u not in DIAGONAL:
            b = g.fin(w.kx, u, 0, h)
            g.send(u, 12, b, b, g.rf.at[u, 3], w.yn)
        b = g.fin(w.kx, u)
        g.send(u, 13, b, b, g.rf.at[u, 5], w.partner)

    def c5b(g, u):
        h, w = REDUCE_UNITS[u][2], g.w
        g.got(g.fin(w.ky, u), g.rf.at[u, 1])
        if u not in DIAGONAL:
            b = g.fin(w.ky, u, h)
            g.send(u, 14, b, b, g.rf.at[u, 2], w.xn)
        b = g.fin(w.ky, u)
        g.send(u, 15, b, b, g.rf.at[u, 6], w.partner)

    def c6(g, u):
        h, w = REDUCE_UNITS[u][2], g.w
        if u in DIAGONAL:
            g.got(g.fin(w.kd, u), g.rf.at[u, 2])
        else:
            g.got(g.fin(w.kd, u, 0, h), g.rf.at[u, 3])
            g.got(g.fin(w.kd, u, h), g.rf.at[u, 2])
        b = g.fin(w.kd, u)
        g.send(u, 16, b, b, g.rf.at[u, 7], w.partner)

    def c7(g, u):
        R, S, w = g.at(u)
        for i, k in enumerate((w.kp, w.kpx, w.kpy, w.kpd)):
            g.got(g.fin(k, u), g.rf.at[u, 4 + i])
        if not g.waiting:
            pltpu.make_async_copy(S.at[w.q, w.z], g.fin(w.k, u), g.lf.at[u]).wait()


def load_unit(w, own, W, dst, sem, u0, n, row0=0, halves=False):
    def block(k, _):
        def one(r, s, view, c0):
            def put(src, zs):
                rows = pl.ds(pl.multiple_of(row0 + zs * n, 16), n)
                pltpu.make_async_copy(src, view.at[rows, pl.ds(pl.multiple_of(c0, 128), 128)], sem).start()

            put(own(k, s), w.z)
            for d in range(3):
                put(W.at[k, d, pl.ds(r, n)], (w.z + 3 - d) % 4)

        if halves:
            for s in range(2):
                one(u0 + s * n, s, dst.at[k // 4], (k % 4) * 256 + s * 128)
        else:
            one(u0, 0, dst, k * 128)
        return 0

    lax.fori_loop(0, 8, block, 0)


def rope(t, c, s):
    first = (lanes() % 64) < 32
    return t * c + jnp.where(first, pltpu.roll(t, 96, 1), pltpu.roll(t, 32, 1)) * s


def dup(t, half):
    return jnp.where((lanes() < 64) == (half == 0), t, pltpu.roll(t, 64, 1))


def gain_row(tile):
    at = (lax.broadcasted_iota(jnp.int32, (8, 128), 0) == 0) & (lax.broadcasted_iota(jnp.int32, (8, 128), 1) == 0)
    return mm(at.astype(f32).astype(bf16), tile, NT)[0:1]


def norm(v, g):
    return v * lax.rsqrt(jnp.mean(v * v, axis=1, keepdims=True) + NORM_EPS) * g


def norm_back(v, g, u):
    r = lax.rsqrt(jnp.mean(v * v, axis=1, keepdims=True) + NORM_EPS)
    wv = u * g
    return r * wv - v * (r * r * r) * jnp.mean(wv * v, axis=1, keepdims=True), u * v * r


def head_at(h):
    t, half = h // 2, h % 2
    mine = (lanes() // 64) == half
    return t, mine, pl.ds(pl.multiple_of(t * 128, 128), 128)


def group_fwd(g, qk, k2, v2, bias, ctx, lse):
    for i in range(2):
        rows, n = pl.ds(256 * i, 256), 256 * (i + 1)
        sums = lse[rows]
        for h in (3 * g, 3 * g + 1, 3 * g + 2):
            t, mine, col = head_at(h)
            hm = jnp.where(mine, 0.125, 0.0).astype(bf16)
            s = mm(qk[rows, col] * hm, k2[g, pl.ds(0, n)], NT) + bias[rows, pl.ds(0, n)].astype(f32)
            m = jnp.max(s, axis=1, keepdims=True)
            p = jnp.exp(s - m)
            l = jnp.sum(p, axis=1, keepdims=True)
            o = mm((p * (1.0 / l)).astype(bf16), v2[g, pl.ds(0, n)])
            ctx[rows, col] = jnp.where(mine, o, ctx[rows, col].astype(f32)).astype(bf16)
            sums = jnp.where(lanes() == h, m + jnp.log(l), sums)
        lse[rows] = sums


def group_bwd(g, qk, k2, v2, bias, lse, dctx, dq, dk, dv):
    for i in range(2):
        rows, n = pl.ds(256 * i, 256), 256 * (i + 1)
        dk_part, dv_part = 0.0, 0.0
        for h in (3 * g, 3 * g + 1, 3 * g + 2):
            t, mine, col = head_at(h)
            hm = jnp.where(mine, 0.125, 0.0).astype(bf16)
            om = jnp.where(mine, 1.0, 0.0).astype(bf16)
            qs = qk[rows, col] * hm
            do = dctx[t // 4, rows, pl.ds(pl.multiple_of((t % 4) * 128, 128), 128)] * om
            le = jnp.sum(jnp.where(lanes() == h, lse[rows], 0.0), axis=1, keepdims=True)
            s = mm(qs, k2[g, pl.ds(0, n)], NT) + bias[rows, pl.ds(0, n)].astype(f32)
            p = jnp.exp(s - le)
            dp = mm(do, v2[g, pl.ds(0, n)], NT)
            dv_part += mm(p.astype(bf16), do, TN)
            ds = (p * (dp - jnp.sum(p * dp, axis=1, keepdims=True))).astype(bf16)
            dk_part += mm(ds, qs, TN)
            dq[rows, col] = jnp.where(mine, mm(ds, k2[g, pl.ds(0, n)]) * 0.125, dq[rows, col])
        if i == 0:
            dk[g] = jnp.zeros_like(dk[g])
            dv[g] = jnp.zeros_like(dv[g])
        dk[g, pl.ds(0, n)] += dk_part
        dv[g, pl.ds(0, n)] += dv_part


KEYS = [(7, 1), (8, 0), (8, 1), (9, 0), (9, 1)]
VALUES = [(10, 0), (10, 1), (11, 0), (11, 1), (12, 0)]


def layer_kernel(
    tokT, cotT, freq, ids, norm_gains, qkv, out, gate_up, downT,
    boT, tgT, FIN, W, n1H, ctxH,
    cot, cos, sin, qk, k2, v2, lse, mid, n2, gains,
    wg, wd, bias, n2T, n2pT, cpT, dypp, hid, dgu, hidp, dgup, da, acc, dacc, dk, dv, gcol, gcolp,
    SM, SO, RX3, RY3, RX, RY, RZ, stage,
    lsem, wsem, ps, pr, *sems,
):
    w = Where()
    c = w.c
    bar = pltpu.get_barrier_semaphore()
    for p in w.peers():
        pl.semaphore_signal(bar, inc=1, device_id=p, device_id_type=MESH)
    loads = {}

    def fetch(name, *pairs):
        loads[name] = [pltpu.make_async_copy(src, dst, wsem.at[len(loads)]) for src, dst in pairs]
        for cp in loads[name]:
            cp.start()

    def fetch_unit(j):
        rows = slice(256 * (j % 2), 256 * (j % 2) + 240)
        cols = [(gate_up.at[:, k * 640 + j * 128 : k * 640 + (j + 1) * 128], acc.at[rows, k * 128 : (k + 1) * 128]) for k in range(8)]
        for k in range(8):
            pltpu.make_async_copy(*cols[k], wsem.at[2 + j]).start()
        part = downT.at[:, j * 128 : (j + 1) * 128]
        turned = (dk, dv)[j % 2]
        pltpu.make_async_copy(part.at[0:512], turned.at[0], wsem.at[7 + j]).start()
        pltpu.make_async_copy(part.at[512:960], turned.at[1, 0:448], wsem.at[12 + j]).start()

    fetch("qkv", (qkv, stage))
    fetch("out", (out, dacc.at[0:240]))
    fetch_unit(0)
    fetch_unit(1)
    tl = pltpu.make_async_copy(tokT, tgT, lsem.at[0])
    tl.start()
    cl = pltpu.make_async_copy(cotT, boT, lsem.at[1])
    cl.start()
    pl.semaphore_wait(bar, len(w.peers()))

    def summed(u):
        if u < 5:
            return SM.at[u]
        return SO.at[u - 5] if u < 7 else SO.at[2, :, :, slice(*((0, 128), (128, 240))[u - 7])]

    def held(u, k):
        at = (k // 4, k % 4)
        if u >= 4:
            return SM.at[u - 4, *at]
        return (SO.at[1, *at, 0:128], SO.at[1, *at, 128:240], SO.at[2, *at], SO.at[0, *at])[u]

    ga = Gather(w, held, W, sems[:5])
    re = Reduce(w, summed, RX3, RY3, RX, RY, RZ, FIN, sems[5:])
    live, local = {}, {}

    def psend(i, src, dst):
        live[i] = ga.copy(src, dst, ps.at[i], pr.at[i], w.partner)
        live[i].start()

    def psent(*which):
        for i in which:
            live.pop(i).wait_send()

    def pgot(i, dst):
        ga.copy(dst, dst, ps.at[0], pr.at[i], w.partner).wait_recv()

    def begin(name, src, dst, sem):
        local[name] = pltpu.make_async_copy(src, dst, sem)
        local[name].start()

    def end(name):
        local.pop(name).wait()

    other = pl.ds(pl.multiple_of((1 - c) * 512, 512), 512)
    mine = pl.ds(pl.multiple_of(c * 512, 512), 512)
    half_rows = [pl.ds(256 * i, 256) for i in range(2)]

    zero = jnp.zeros((240, 128), bf16)

    def PQ():
        loads["qkv"][0].wait()
        for t in range(13):
            k, sub = (t // 2, t % 2) if t < 6 else (4 + (t - 6) // 2, (t - 6) % 2)
            tile = SO.at[1 + sub, k // 4, k % 4]
            if t < 12:
                tile[...] = stage[:, t * 128 : (t + 1) * 128].astype(bf16)
            else:
                tile[...] = zero
                tile[:, 0:64] = stage[:, 1536:1600].astype(bf16)
        SO[1, 0, 3] = zero
        for i in range(2):
            at = lax.broadcasted_iota(jnp.int32, (128, 240), 0) == 0
            tile = jnp.where(at, norm_gains[i : i + 1], 0.0)
            SO[2, i, 3] = jnp.swapaxes(tile, 0, 1).astype(bf16)

    def PO():
        loads["out"][0].wait()
        SO[0, 1, 3] = zero
        for k in range(8):
            width = 128 if k < 7 else 64
            SO[0, k // 4, k % 4, :, 0:width] = dacc[0:240, k * 128 : k * 128 + width].astype(bf16)

    def PM(j):
        rows = slice(256 * (j % 2), 256 * (j % 2) + 240)
        turned = (dk, dv)[j % 2]
        view = acc.at[rows]
        pltpu.make_async_copy(view, view, wsem.at[2 + j]).wait()
        for i, part in enumerate((turned.at[0], turned.at[1, 0:448])):
            pltpu.make_async_copy(part, part, wsem.at[7 + 5 * i + j]).wait()
        SM[j, 1, 3, 240:368] = jnp.zeros((128, 128), bf16)
        for k in range(8):
            width = 128 if k < 7 else 64
            SM[j, k // 4, k % 4, 0:240] = acc[rows, k * 128 : (k + 1) * 128].astype(bf16)
            block = turned[k // 4, (k % 4) * 128 : (k % 4) * 128 + width].astype(bf16)
            SM[j, k // 4, k % 4, 240:368, 0:width] = jnp.swapaxes(block, 0, 1)
        if j + 2 < 5:
            fetch_unit(j + 2)

    def A0():
        seq = ids[...].astype(f32)
        column = jnp.swapaxes(jnp.broadcast_to(seq, (8, 512)), 0, 1)[:, 0:1]
        for i in range(2):
            own_seq = column[256 * i : 256 * (i + 1)]
            rows = lax.broadcasted_iota(jnp.int32, (256, 512), 0) + 256 * i
            cols = lax.broadcasted_iota(jnp.int32, (256, 512), 1)
            ok = (own_seq == seq) & (cols <= rows)
            bias[pl.ds(256 * i, 256)] = jnp.where(ok, 0.0, NEG_LARGE).astype(bf16)
            first_row = jnp.sum(jnp.where(seq < own_seq, 1.0, 0.0), axis=1, keepdims=True)
            row = (lax.broadcasted_iota(jnp.int32, (256, 1), 0) + 256 * i).astype(f32)
            angle = (row - first_row) * freq[...]
            cos[pl.ds(256 * i, 256)] = jnp.cos(angle)
            sin[pl.ds(256 * i, 256)] = jnp.where((lanes() % 64) < 32, -1.0, 1.0) * jnp.sin(angle)
        lse[...] = jnp.zeros_like(lse)
        tl.wait()
        cl.wait()
        mid[...] = jnp.swapaxes(tgT[...], 0, 1).astype(f32)
        cot[:, 896:1024] = jnp.zeros((512, 128), bf16)
        cot[:, 0:960] = jnp.swapaxes(boT[...], 0, 1)

    def LQ():
        load_unit(w, lambda k, s: SO.at[1 + s, k // 4, k % 4], W, wg, lsem.at[0], 0, 240, halves=True)

    def wait_q():
        pltpu.make_async_copy(wg, wg, lsem.at[0]).wait()

    def LO():
        load_unit(w, lambda k, s: SO.at[0, k // 4, k % 4], W, wd, lsem.at[1], 480, 240)

    def wait_o():
        view = wd.at[pl.ds(0, 960)]
        pltpu.make_async_copy(view, view, lsem.at[1]).wait()

    def A1():
        wait_q()
        acc[...] = jnp.zeros_like(acc)
        dacc[...] = jnp.zeros_like(dacc)
        gains[...] = jnp.zeros_like(gains)
        gains[0:1] = gain_row(wg[0, :, 896:1024])
        gains[1:2] = gain_row(wg[1, :, 896:1024])
        n1 = norm(mid[...], gains[0:1]).astype(bf16)
        da[:, 0:960] = n1
        tgT[...] = jnp.swapaxes(n1, 0, 1)
        for half, (lo, hi) in enumerate(((0, 6), (6, 13))):
            res = mm(da[:, 0:960], wg[half, :, 0 : (hi - lo) * 128])
            for t in range(lo, hi):
                tile = res[:, (t - lo) * 128 : (t - lo + 1) * 128]
                if t < 10:
                    tile = rope(tile, cos[...], sin[...])
                    qk[:, t * 128 : (t + 1) * 128] = tile.astype(bf16)
                for i in range(5):
                    if KEYS[i][0] == t:
                        k2[i] = dup(tile, KEYS[i][1]).astype(bf16)
                    if VALUES[i][0] == t:
                        v2[i] = dup(tile, VALUES[i][1]).astype(bf16)
        begin("n1", tgT, n1H, lsem.at[2])
        da[...] = jnp.zeros_like(da)

    def A3():
        wait_o()
        for rows in half_rows:
            m = mid[rows] + mm(da[rows, 0:960], wd[pl.ds(0, 960), 0:960])
            mid[rows] = m
            n2[rows] = norm(m, gains[1:2]).astype(bf16)
        n2T[...] = jnp.swapaxes(n2[...], 0, 1)
        boT[...] = jnp.swapaxes(da[:, 0:960], 0, 1)
        psend(0, n2T, n2pT)
        psend(1, cot.at[:, other], dypp)
        psend(2, boT, cpT)
        begin("ctx", boT, ctxH, lsem.at[3])

    def dslot(j):
        return pl.ds(pl.multiple_of(((j + 2) % 3) * 512, 512), 512)

    def L(j):
        def rows(a, b):
            return lambda k, s: SM.at[j, k // 4, k % 4, a:b]

        load_unit(w, rows(0, 240), W, wg.at[j % 2], lsem.at[4 + j % 2], 720 + 368 * j, 240)
        load_unit(w, rows(240, 368), W, wd, lsem.at[6 + j % 2], 960 + 368 * j, 128, row0=((j + 2) % 3) * 512)

    def sends(j):
        b = j % 2
        return (
            ga.copy(hid.at[b], hidp.at[b], ps.at[4 + j], pr.at[4 + j], w.partner),
            ga.copy(dgu.at[b, 1 - c], dgup.at[b], ps.at[9 + j], pr.at[9 + j], w.partner),
        )

    def F(j):
        b = j % 2
        pltpu.make_async_copy(wg.at[b], wg.at[b], lsem.at[4 + b]).wait()
        view = wd.at[dslot(j)]
        pltpu.make_async_copy(view, view, lsem.at[6 + b]).wait()

        @pl.when(j >= 2)
        def _():
            sends(j - 2)[0].wait_send()
            sends(j - 2)[1].wait_send()

        def half(i, _):
            rows = pl.ds(pl.multiple_of(i * 256, 256), 256)
            gu = mm(n2[rows], wg[b])
            gate, up = gu[:, :512], gu[:, 512:]
            sg = jax.nn.sigmoid(gate)
            a = gate * sg
            hb = (a * up).astype(bf16)
            hid[b, rows] = hb
            acc[rows, 0:960] += mm(hb, wd[dslot(j), 0:960])
            dh = mm(cot[rows, 0:960], wd[dslot(j), 0:960], NT)
            dgate = (dh * up * (sg * (1.0 + gate * (1.0 - sg)))).astype(bf16)
            dup_ = (dh * a).astype(bf16)
            dgu[b, 0, rows] = dgate
            dgu[b, 1, rows] = dup_
            dacc[rows] += mm(dgate, wg[b, :, 0:512], NT) + mm(dup_, wg[b, :, 512:1024], NT)
            return 0

        lax.fori_loop(0, 2, half, 0)
        for cp in sends(j):
            cp.start()

    def cut(S, G, n, r0=0):
        for q in range(4):
            for z in range(4):
                S[q, z, r0 : r0 + n] = G[z * n : (z + 1) * n, q * 128 : (q + 1) * 128].astype(bf16)

    def R(j):
        b = j % 2

        @pl.when(j == 0)
        def _():
            pgot(0, n2pT)
            pgot(1, dypp)

        pgot(4 + j, hidp.at[b])
        pgot(9 + j, dgup.at[b])
        cut(SM.at[j], mm(n2T[...], dgu[b, c]) + mm(n2pT[...], dgup[b]), 240)
        cut(SM.at[j], mm(hid[b], cot[:, mine], TN) + mm(hidp[b], dypp[...], TN), 128, 240)

    def B1():
        for cp in sends(3) + sends(4):
            cp.wait_send()
        psent(0, 1, 2)
        LO()
        LQ()
        end("ctx")
        begin("ctxT", ctxH, n2T, lsem.at[3])
        ones = jnp.ones((256, 128), bf16)
        da[:, 896:1024] = jnp.zeros((512, 128), bf16)
        gc = 0.0
        for i, rows in enumerate(half_rows):
            m = mid[rows]
            boT[:, 256 * i : 256 * (i + 1)] = jnp.swapaxes((m + acc[rows, 0:960]).astype(bf16), 0, 1)
            dv_, gp = norm_back(m, gains[1:2], dacc[rows])
            dmid = cot[rows, 0:960].astype(f32) + dv_
            dacc[rows] = dmid
            da[rows, 0:960] = dmid.astype(bf16)
            gc = gc + mm(gp.astype(bf16), ones, TN)
        gcol[1] = gc.astype(bf16)
        psend(14, da.at[:, other], hidp.at[1])

    def B2():
        wait_o()
        hid[1, :, 384:512] = jnp.zeros((512, 128), bf16)
        hid[0] = mm(da[:, 0:960], wd[pl.ds(0, 512), 0:960], NT).astype(bf16)
        hid[1, :, 0:448] = mm(da[:, 0:960], wd[pl.ds(512, 448), 0:960], NT).astype(bf16)
        end("ctxT")
        pgot(2, cpT)
        pgot(14, hidp.at[1])
        end("n1")
        psend(3, n1H, n2pT)
        cut(SO.at[0], mm(n2T[...], da[:, mine]) + mm(cpT[...], hidp[1]), 240)
        acc[...] = jnp.zeros_like(acc)
        psent(14)
        begin("n1T", n1H, n2T, lsem.at[2])
        begin("tok", tokT, tgT, lsem.at[3])

    def D1():
        def put(half, t, tile):
            dgu[half, t // 4, :, (t % 4) * 128 : (t % 4 + 1) * 128] = tile.astype(bf16)

        first = lanes() < 64
        nsin = -sin[...]

        def fold(ref, i):
            return ref[i] + pltpu.roll(ref[i], 64, 1)

        for t in range(7):
            put(t // 6, t % 6, rope(acc[:, t * 128 : (t + 1) * 128], cos[...], nsin))
        zero = jnp.zeros((512, 128), f32)
        for half, t in ((0, 6), (0, 7), (1, 7)):
            put(half, t, zero)
        kk, vv = [fold(dk, i) for i in range(5)], [fold(dv, i) for i in range(5)]
        put(1, 1, rope(jnp.where(first, acc[:, 896:1024], kk[0]), cos[...], nsin))
        put(1, 2, rope(jnp.where(first, kk[1], kk[2]), cos[...], nsin))
        put(1, 3, rope(jnp.where(first, kk[3], kk[4]), cos[...], nsin))
        put(1, 4, jnp.where(first, vv[0], vv[1]))
        put(1, 5, jnp.where(first, vv[2], vv[3]))
        put(1, 6, jnp.where(first, vv[4], 0.0))
        psend(15, dgu.at[1 - c], dgup)

    def qgrad(sub):
        for q in range(4):
            t = 2 * q + sub
            if t == 7:
                G = gcol[c].astype(f32) + gcolp[...].astype(f32)
            else:
                at = slice((t % 4) * 128, (t % 4 + 1) * 128)
                G = mm(n2T[...], dgu[c, t // 4, :, at]) + mm(n2pT[...], dgup[t // 4, :, at])
            for z in range(4):
                SO[1 + sub, q, z] = G[z * 240 : (z + 1) * 240].astype(bf16)

    def D2():
        end("n1T")
        pgot(3, n2pT)
        pgot(15, dgup)
        qgrad(0)

    def D3():
        wait_q()
        end("tok")
        da[:, 0:960] = jnp.swapaxes(tgT[...], 0, 1)
        ones = jnp.ones((256, 128), bf16)
        gc = 0.0
        for i, rows in enumerate(half_rows):
            dn1 = mm(dgu[0, 0, rows], wg[0, :, 0:512], NT) + mm(dgu[0, 1, rows, 0:256], wg[0, :, 512:768], NT)
            dn1 += mm(dgu[1, 0, rows], wg[1, :, 0:512], NT) + mm(dgu[1, 1, rows, 0:384], wg[1, :, 512:896], NT)
            dv_, gp = norm_back(da[rows, 0:960].astype(f32), gains[0:1], dn1)
            tgT[:, 256 * i : 256 * (i + 1)] = jnp.swapaxes((dacc[rows] + dv_).astype(bf16), 0, 1)
            gc = gc + mm(gp.astype(bf16), ones, TN)
        gcol[0] = gc.astype(bf16)
        psend(16, gcol.at[1 - c], gcolp)

    def D4():
        pgot(16, gcolp)
        qgrad(1)

    steps = dict(PQ=PQ, PO=PO, PM=PM, A0=A0, LQ=LQ, A1=A1, LO=LO, A3=A3, L=L, B1=B1, B2=B2, D1=D1, D2=D2, D3=D3, D4=D4)

    def run(part):
        for name, at in part:
            if name in steps:
                steps[name](*([] if at is None else [at]))
            else:
                (ga if name[0] == "g" else re).step(name, at)

    def after(i, parts):
        for n, part in enumerate(parts):
            if part:
                pl.when(i == n)(lambda part=part: run(part))

    def heads(group, parts):
        def turn(g, _):
            group(g)
            after(g, parts)
            return 0

        lax.fori_loop(0, 5, turn, 0)

    def unit(j, _):
        F(j)
        after(j, PARTS["F"])
        R(j)
        after(j, PARTS["R"])
        return 0

    run(PARTS["start"])
    heads(lambda g: group_fwd(g, qk, k2, v2, bias, da, lse), PARTS["H"])
    run(PARTS["A3"])
    ga.waiting = True
    for u in range(len(GATHER_UNITS)):
        ga.g0(u)
    ga.waiting = False
    lax.fori_loop(0, 5, unit, 0)
    run(PARTS["B1"])
    heads(lambda g: group_bwd(g, qk, k2, v2, bias, lse, hid, acc, dk, dv), PARTS["K"])
    run(PARTS["D1"])
    for i in list(live):
        psent(i)
    ga.finish()
    re.finish()


def layer(tok, cot, ids, weights):
    freq = ROPE_BASE ** (-2.0 * (jnp.arange(128) % 32).astype(f32) / HEAD)
    S, D = jax.ShapeDtypeStruct, pltpu.SemaphoreType.DMA

    def V(*shape, dt=bf16):
        return pltpu.VMEM(shape, dt)

    vm = pl.BlockSpec(memory_space=pltpu.VMEM)
    hb = pl.BlockSpec(memory_space=pl.ANY)
    outs = pl.pallas_call(
        layer_kernel,
        name="layer",
        out_shape=[
            S((960, 512), bf16), S((960, 512), bf16), S((8, ROWS, 128), bf16),
            S((8, 3, ROWS, 128), bf16), S((960, 512), bf16), S((960, 512), bf16),
        ],
        in_specs=[hb, hb, vm, vm, vm, hb, hb, hb, hb],
        out_specs=[vm, vm, hb, hb, hb, hb],
        scratch_shapes=[
            V(512, 1024), V(512, 128, dt=f32), V(512, 128, dt=f32), V(512, 1280), V(5, 512, 128), V(5, 512, 128), V(512, 128, dt=f32), V(512, 960, dt=f32),
            V(512, 960), V(8, 960, dt=f32),
            V(2, 960, 1024), V(1536, 1024), V(512, 512), V(960, 512), V(960, 512), V(960, 512), V(512, 512),
            V(2, 512, 512), V(2, 2, 512, 512), V(2, 512, 512), V(2, 512, 512), V(512, 1024),
            V(512, 1024, dt=f32), V(512, 960, dt=f32), V(5, 512, 128, dt=f32), V(5, 512, 128, dt=f32),
            V(2, 960, 128), V(960, 128),
            V(5, 4, 4, 368, 128), V(3, 4, 4, 240, 128),
            V(2, ROWS, 128), V(2, ROWS, 128), V(4, ROWS, 128), V(4, ROWS, 128), V(3, ROWS, 128), V(240, 1600, dt=f32),
            D((8,)), D((17,)), D((17,)), D((17,)),
            D((9, 12)), D((9, 3)), D((9, 2)), D((9, 2)), D((9, 4)),
            D((9, 18)), D((9, 2)), D((9, 4)), D((9, 4)), D((9, 8)), D((9,)),
        ],
        compiler_params=pltpu.CompilerParams(
            collective_id=0, has_side_effects=True, vmem_limit_bytes=67043328
        ),
    )(tok.T, cot.T, freq[None, :], ids[None, :], *weights[:4], weights[4].T)
    return outs[:3]


PARTS = {
    "start": [
        ("PQ", None), ("g0", 0), ("g0", 1), ("g0", 2), ("PO", None), ("PM", 0), ("PM", 1), ("A0", None),
        ("gr", 0), ("PM", 2), ("gr", 1), ("PM", 3), ("PM", 4), ("gr", 2), ("g1", 0), ("g0", 3), ("g1", 1),
        ("g0", 4), ("g1", 2), ("g0", 5), ("g2a", 0), ("g2b", 0), ("gr", 3), ("g2a", 1), ("g2b", 1), ("gr", 4),
        ("g2a", 2), ("g2b", 2), ("g3", 0), ("g3", 1), ("g4", 0), ("gr", 5), ("g4", 1), ("g1", 3), ("g0", 6),
        ("g3", 2), ("g1", 4), ("g0", 7), ("g4", 2), ("LQ", None), ("g1", 5), ("g0", 8), ("g2a", 3),
        ("g2b", 3), ("A1", None), ("gr", 6), ("gr", 7), ("g2a", 4), ("g2b", 4),
    ],
    "H": [
        [
            ("gr", 8),
        ],
        [
            ("g2a", 5), ("g2b", 5), ("g1", 6),
        ],
        [
            ("g3", 3), ("g1", 7), ("g1", 8),
        ],
        [
            ("g3", 4), ("g4", 3), ("LO", None), ("g3", 5),
        ],
        [
            ("g4", 4), ("L", 0), ("g4", 5),
        ],
    ],
    "A3": [
        ("A3", None), ("L", 1), ("g2a", 6), ("g2b", 6),
    ],
    "F": [
        [
            ("g2a", 7), ("g2b", 7),
        ],
        [
            ("g3", 6), ("g2a", 8), ("g2b", 8),
        ],
        [
            ("L", 4), ("c2a", 1), ("c2b", 1),
        ],
        [
            ("c3", 1),
        ],
        [
            ("z2", 0),
        ],
    ],
    "R": [
        [
            ("z1", 0),
        ],
        [
            ("g3", 7), ("c1", 1), ("g4", 6), ("L", 2), ("g4", 7), ("L", 3), ("g3", 8), ("g4", 8),
        ],
        [
            ("c1", 2),
        ],
        [
            ("c2a", 2), ("c2b", 2), ("c1", 3),
        ],
        [
            ("c3", 2), ("c1", 4),
        ],
    ],
    "B1": [
        ("B1", None), ("c4", 1), ("c2a", 3), ("c2b", 3), ("B2", None), ("c1", 5),
    ],
    "K": [
        [
            ("z3a", 0), ("z3b", 0),
        ],
        [
            ("c4", 2), ("c2a", 4), ("c2b", 4),
        ],
        [
            ("c5a", 1), ("c5b", 1),
        ],
        [
            ("c3", 3), ("c2a", 5), ("c2b", 5),
        ],
        [
            ("z4", 0),
        ],
    ],
    "D1": [
        ("D1", None), ("c5a", 2), ("c5b", 2), ("D3", None), ("c3", 4), ("c6", 1), ("c4", 3), ("D2", None),
        ("c3", 5), ("c1", 6), ("D4", None), ("c5a", 0), ("c5b", 0), ("c6", 2), ("c1", 7), ("c1", 8),
        ("c7", 1), ("c5a", 3), ("c5b", 3), ("c7", 2), ("c2b", 6), ("c2a", 6), ("c4", 4), ("c6", 0),
        ("c2b", 7), ("c7", 0), ("c2a", 7), ("c4", 5), ("c2b", 8), ("c2a", 8), ("c6", 3), ("c7", 3), ("c3", 6),
        ("c5a", 4), ("c5b", 4), ("c3", 7), ("c5a", 5), ("c5b", 5), ("c3", 8), ("c6", 4), ("c7", 4), ("c6", 5),
        ("c4", 6), ("c7", 5), ("c4", 7), ("c5a", 6), ("c5b", 6), ("c4", 8), ("c6", 6), ("c5a", 7), ("c5b", 7),
        ("c7", 6), ("c6", 7), ("c7", 7), ("c5a", 8), ("c5b", 8), ("c6", 8), ("c7", 8),
    ],
}

DIAGONAL = (6, 7, 8)

def on_device(tokens, sequence_ids, cotangent, norm_gains, qkv_weight, out_weight, gate_up_weight, down_weight, *moments):
    weights = (norm_gains, qkv_weight, out_weight, gate_up_weight, down_weight)
    block_out, tokens_grad, packed = layer(tokens, cotangent, sequence_ids, weights)
    return (block_out.T, tokens_grad.T, *adam(packed, weights, moments))


def solution(mesh):
    fits = mesh.shape["rep"] == 8 and mesh.shape["fsdp"] == 4
    return jax.shard_map(
        on_device if fits else on_device_any,
        mesh=mesh,
        in_specs=(
            P(("rep", "fsdp"), None),
            P(("rep", "fsdp")),
            P(("rep", "fsdp"), None),
            P(None, "fsdp"),
            P("fsdp", None),
            P("fsdp", None),
            P("fsdp", None),
            P("fsdp", None),
            P(None, "fsdp"),
            P("fsdp", None),
            P("fsdp", None),
            P("fsdp", None),
            P("fsdp", None),
            P(None, "fsdp"),
            P("fsdp", None),
            P("fsdp", None),
            P("fsdp", None),
            P("fsdp", None),
        ),
        out_specs=(
            P(("rep", "fsdp"), None),
            P(("rep", "fsdp"), None),
            P(None, "fsdp"),
            P("fsdp", None),
            P("fsdp", None),
            P("fsdp", None),
            P("fsdp", None),
            P(None, "fsdp"),
            P("fsdp", None),
            P("fsdp", None),
            P("fsdp", None),
            P("fsdp", None),
            P(None, "fsdp"),
            P("fsdp", None),
            P("fsdp", None),
            P("fsdp", None),
            P("fsdp", None),
            P(None, "fsdp"),
            P("fsdp", None),
            P("fsdp", None),
            P("fsdp", None),
            P("fsdp", None),
        ),
        check_vma=False,
    )
```

```python
import math

import jax
import jax.numpy as jnp
from jax import lax
from jax.experimental import pallas as pl
from jax.experimental.pallas import tpu as pltpu
from jax.sharding import PartitionSpec as P
D = 960
HEADS = 15
KV_HEADS = 5
HEAD = 64
FF = 2560
STEP = 4


NORM_EPS = 1e-05
ROPE_BASE = 100000.0
LEARN_RATE = 0.03
BETA_ONE = 0.9
BETA_TWO = 0.95
ADAM_EPS = 1e-08
DECAY_RATE = 0.1
NEG_LARGE = -1e30


def positions(sequence_ids):
    row_index = jnp.arange(sequence_ids.shape[0], dtype=jnp.int32)
    prior_ids = jnp.concatenate([jnp.full((1,), -1, jnp.int32), sequence_ids[:-1]])
    seq_starts = jnp.where(sequence_ids != prior_ids, row_index, 0)
    first_row = lax.cummax(seq_starts, axis=0)
    return (row_index - first_row).astype(jnp.float32)


def causal_mask(sequence_ids):
    row_index = jnp.arange(sequence_ids.shape[0], dtype=jnp.int32)
    return (sequence_ids[:, None] == sequence_ids[None, :]) & (
        row_index[None, :] <= row_index[:, None]
    )


def rope_tables(places):
    half_size = HEAD // 2
    freq_table = ROPE_BASE ** (-2.0 * jnp.arange(half_size, dtype=jnp.float32) / HEAD)
    angles = places[:, None] * freq_table[None, :]
    return (jnp.cos(angles), jnp.sin(angles))


def rotate(vectors, cosine_table, sine_table):
    half_size = vectors.shape[-1] // 2
    first_half = vectors[..., :half_size]
    second_half = vectors[..., half_size:]
    cosine_wide = cosine_table[:, None, :]
    sine_wide = sine_table[:, None, :]
    return jnp.concatenate(
        [
            first_half * cosine_wide - second_half * sine_wide,
            second_half * cosine_wide + first_half * sine_wide,
        ],
        axis=-1,
    )


def rms_norm(values, gain_row):
    row_scale = lax.rsqrt(jnp.mean(values * values, axis=-1, keepdims=True) + NORM_EPS)
    return values * row_scale * gain_row


def swiglu(gate_part, up_part):
    return gate_part * jax.nn.sigmoid(gate_part) * up_part


def adamw_update(weight, moment_one, moment_two, gradient, decay_rate):
    first_new = BETA_ONE * moment_one + (1.0 - BETA_ONE) * gradient
    second_new = BETA_TWO * moment_two + (1.0 - BETA_TWO) * gradient * gradient
    fix_one = 1.0 - BETA_ONE**STEP
    fix_two = 1.0 - BETA_TWO**STEP
    update_dir = (
        first_new / fix_one / (jnp.sqrt(second_new / fix_two) + ADAM_EPS) + decay_rate * weight
    )
    return (-LEARN_RATE * update_dir, first_new, second_new)


def split_groups(queries, keys_rot, values_kv):
    count_rows = queries.shape[0]
    group_size = HEADS // KV_HEADS
    query_groups = queries.reshape(count_rows, KV_HEADS, group_size, HEAD).transpose(1, 2, 0, 3)
    return (query_groups, keys_rot.transpose(1, 0, 2), values_kv.transpose(1, 0, 2))


def attend(queries, keys_rot, values_kv, mask_table):
    count_rows = queries.shape[0]
    scale_factor = 1.0 / math.sqrt(HEAD)
    query_groups, key_groups, value_groups = split_groups(queries, keys_rot, values_kv)

    def one_group(members):
        query_one, key_one, value_one = members
        scores = (
            jnp.einsum("gqd,kd->gqk", query_one, key_one, preferred_element_type=jnp.float32)
            * scale_factor
        )
        scores = jnp.where(mask_table[None], scores, NEG_LARGE)
        top_score = jnp.max(scores, axis=-1, keepdims=True)
        weights = jnp.exp(scores - top_score)
        total_sum = jnp.sum(weights, axis=-1, keepdims=True)
        prob_table = (weights / total_sum).astype(jnp.bfloat16)
        context_one = jnp.einsum(
            "gqk,kd->gqd", prob_table, value_one, preferred_element_type=jnp.float32
        )
        return (context_one.astype(jnp.bfloat16), (top_score + jnp.log(total_sum))[..., 0])

    context_groups, log_total = lax.map(one_group, (query_groups, key_groups, value_groups))
    context = context_groups.transpose(2, 0, 1, 3).reshape(count_rows, HEADS, HEAD)
    return (context, log_total)


def attend_back(queries, keys_rot, values_kv, mask_table, log_total, grad_context):
    count_rows = queries.shape[0]
    group_size = HEADS // KV_HEADS
    scale_factor = 1.0 / math.sqrt(HEAD)
    query_groups, key_groups, value_groups = split_groups(queries, keys_rot, values_kv)
    grad_groups = grad_context.reshape(count_rows, KV_HEADS, group_size, HEAD).transpose(1, 2, 0, 3)

    def one_group(members):
        query_one, key_one, value_one, log_one, grad_one = members
        scores = (
            jnp.einsum("gqd,kd->gqk", query_one, key_one, preferred_element_type=jnp.float32)
            * scale_factor
        )
        scores = jnp.where(mask_table[None], scores, NEG_LARGE)
        prob_table = jnp.exp(scores - log_one[..., None])
        grad_probs = jnp.einsum(
            "gqd,kd->gqk", grad_one, value_one, preferred_element_type=jnp.float32
        )
        grad_value = jnp.einsum(
            "gqk,gqd->kd",
            prob_table.astype(jnp.bfloat16),
            grad_one,
            preferred_element_type=jnp.float32,
        )
        row_delta = jnp.sum(prob_table * grad_probs, axis=-1, keepdims=True)
        grad_scores = (prob_table * (grad_probs - row_delta)).astype(jnp.bfloat16)
        grad_query = (
            jnp.einsum("gqk,kd->gqd", grad_scores, key_one, preferred_element_type=jnp.float32)
            * scale_factor
        )
        grad_key = (
            jnp.einsum("gqk,gqd->kd", grad_scores, query_one, preferred_element_type=jnp.float32)
            * scale_factor
        )
        return (grad_query, grad_key, grad_value)

    grad_q_groups, grad_k_groups, grad_v_groups = lax.map(
        one_group, (query_groups, key_groups, value_groups, log_total, grad_groups)
    )
    grad_queries = grad_q_groups.transpose(2, 0, 1, 3).reshape(count_rows, HEADS, HEAD)
    return (grad_queries, grad_k_groups.transpose(1, 0, 2), grad_v_groups.transpose(1, 0, 2))


def forward(tokens, sequence_ids, attn_set, mlp_set):
    gain_half, qkv_half, out_half = attn_set
    gate_up_half, down_half = mlp_set
    count_rows = tokens.shape[0]
    kv_width = KV_HEADS * HEAD
    inputs = tokens.astype(jnp.float32)
    gain_rows = gain_half.astype(jnp.float32)
    normed = rms_norm(inputs, gain_rows[0]).astype(jnp.bfloat16)
    mixed_cols = jnp.dot(normed, qkv_half, preferred_element_type=jnp.float32)
    cosine_table, sine_table = rope_tables(positions(sequence_ids))
    queries = rotate(
        mixed_cols[:, :D].reshape(count_rows, HEADS, HEAD), cosine_table, sine_table
    ).astype(jnp.bfloat16)
    keys_rot = rotate(
        mixed_cols[:, D : D + kv_width].reshape(count_rows, KV_HEADS, HEAD),
        cosine_table,
        sine_table,
    ).astype(jnp.bfloat16)
    values_kv = (
        mixed_cols[:, D + kv_width :].reshape(count_rows, KV_HEADS, HEAD).astype(jnp.bfloat16)
    )
    context, log_total = attend(queries, keys_rot, values_kv, causal_mask(sequence_ids))
    middle = inputs + jnp.dot(
        context.reshape(count_rows, D), out_half, preferred_element_type=jnp.float32
    )
    normed_two = rms_norm(middle, gain_rows[1]).astype(jnp.bfloat16)
    gate_up = jnp.dot(normed_two, gate_up_half, preferred_element_type=jnp.float32)
    hidden = swiglu(gate_up[:, :FF], gate_up[:, FF:]).astype(jnp.bfloat16)
    result = middle + jnp.dot(hidden, down_half, preferred_element_type=jnp.float32)
    kept_state = (
        inputs,
        normed,
        queries,
        keys_rot,
        values_kv,
        context,
        log_total,
        middle,
        normed_two,
        gate_up,
        hidden,
    )
    return (kept_state, result)


def mlp_backward(kept_state, cotangent, attn_set, mlp_set):
    middle, normed_two, gate_up, hidden = (
        kept_state[7],
        kept_state[8],
        kept_state[9],
        kept_state[10],
    )
    gain_rows = attn_set[0].astype(jnp.float32)
    gate_up_half, down_half = mlp_set
    grad_result = cotangent.astype(jnp.float32)
    grad_branch = grad_result.astype(jnp.bfloat16)
    down_grad = jnp.einsum("rf,rd->fd", hidden, grad_branch, preferred_element_type=jnp.float32)
    grad_hidden = jnp.einsum(
        "rd,fd->rf", grad_branch, down_half, preferred_element_type=jnp.float32
    )
    _, act_back = jax.vjp(swiglu, gate_up[:, :FF], gate_up[:, FF:])
    grad_gate, grad_up = act_back(grad_hidden)
    grad_mix_two = jnp.concatenate([grad_gate, grad_up], axis=1).astype(jnp.bfloat16)
    gate_up_grad = jnp.einsum(
        "rd,rf->df", normed_two, grad_mix_two, preferred_element_type=jnp.float32
    )
    grad_normed_two = jnp.einsum(
        "rf,df->rd", grad_mix_two, gate_up_half, preferred_element_type=jnp.float32
    )
    _, norm_back_two = jax.vjp(rms_norm, middle, gain_rows[1])
    grad_middle_norm, gain_two_grad = norm_back_two(grad_normed_two)
    grad_middle = grad_result + grad_middle_norm
    return ((gate_up_grad, down_grad), (grad_middle, gain_two_grad))


def attn_backward(kept_state, carried, sequence_ids, attn_set):
    inputs, normed, queries, keys_rot, values_kv, context, log_total = kept_state[:7]
    grad_middle, gain_two_grad = carried
    gain_half, qkv_half, out_half = attn_set
    gain_rows = gain_half.astype(jnp.float32)
    count_rows = inputs.shape[0]
    kv_width = KV_HEADS * HEAD
    grad_attn = grad_middle.astype(jnp.bfloat16)
    flat_context = context.reshape(count_rows, D)
    out_grad = jnp.einsum("rc,rd->cd", flat_context, grad_attn, preferred_element_type=jnp.float32)
    grad_context = jnp.einsum("rd,cd->rc", grad_attn, out_half, preferred_element_type=jnp.float32)
    grad_context = grad_context.astype(jnp.bfloat16).reshape(count_rows, HEADS, HEAD)
    grad_queries, grad_keys, grad_values = attend_back(
        queries, keys_rot, values_kv, causal_mask(sequence_ids), log_total, grad_context
    )
    cosine_table, sine_table = rope_tables(positions(sequence_ids))
    grad_q_raw = rotate(grad_queries, cosine_table, -sine_table).reshape(count_rows, D)
    grad_k_raw = rotate(grad_keys, cosine_table, -sine_table).reshape(count_rows, kv_width)
    grad_mixed = jnp.concatenate(
        [grad_q_raw, grad_k_raw, grad_values.reshape(count_rows, kv_width)], axis=1
    )
    grad_mixed = grad_mixed.astype(jnp.bfloat16)
    qkv_grad = jnp.einsum("rd,rc->dc", normed, grad_mixed, preferred_element_type=jnp.float32)
    grad_normed = jnp.einsum("rc,dc->rd", grad_mixed, qkv_half, preferred_element_type=jnp.float32)
    _, norm_back_one = jax.vjp(rms_norm, inputs, gain_rows[0])
    grad_inputs_norm, gain_one_grad = norm_back_one(grad_normed)
    tokens_grad = (grad_middle + grad_inputs_norm).astype(jnp.bfloat16)
    gains_grad = jnp.stack([gain_one_grad, gain_two_grad])
    return (tokens_grad, (gains_grad, qkv_grad, out_grad))


def on_device_any(
    tokens,
    sequence_ids,
    cotangent,
    norm_gains,
    qkv_weight,
    out_weight,
    gate_up_weight,
    down_weight,
    gains_first,
    qkv_first,
    out_first,
    gate_up_first,
    down_first,
    gains_second,
    qkv_second,
    out_second,
    gate_up_second,
    down_second,
):
    shares = lax.axis_size("rep")
    share = lax.axis_index("rep")
    both = ("fsdp", "rep")
    group = lax.axis_size("fsdp")

    def collect(shard):
        flat = shard.astype(jnp.bfloat16).reshape(shares, -1)
        piece = lax.dynamic_index_in_dim(flat, share, 0, keepdims=False)
        whole = lax.all_gather(piece, both, axis=0, tiled=True)
        return whole.reshape(shard.shape[0] * group, shard.shape[1])

    def total(gradient, shard):
        piece = lax.psum_scatter(
            gradient.astype(jnp.bfloat16).reshape(-1), both, scatter_dimension=0, tiled=True
        )
        flat = lax.all_gather(piece, "rep", axis=0, tiled=True)
        return flat.reshape(shard.shape).astype(jnp.float32)

    gain_full = lax.all_gather(norm_gains.astype(jnp.bfloat16), "fsdp", axis=1, tiled=True)
    qkv_full = collect(qkv_weight)
    out_full = collect(out_weight)
    mlp_set = (collect(gate_up_weight), collect(down_weight))
    attn_set = (gain_full, qkv_full, out_full)
    kept_state, result = forward(tokens, sequence_ids, attn_set, mlp_set)
    block_out = result.astype(jnp.bfloat16)
    mlp_grads, carried = mlp_backward(kept_state, cotangent, attn_set, mlp_set)
    down_total = total(mlp_grads[1], down_weight)
    gate_up_total = total(mlp_grads[0], gate_up_weight)
    tokens_grad, attn_grads = attn_backward(kept_state, carried, sequence_ids, attn_set)
    gains_part = lax.psum_scatter(attn_grads[0], "fsdp", scatter_dimension=1, tiled=True)
    gains_total = lax.psum(gains_part, "rep")
    qkv_total = total(attn_grads[1], qkv_weight)
    out_total = total(attn_grads[2], out_weight)
    gains_delta, gains_first_new, gains_second_new = adamw_update(
        norm_gains, gains_first, gains_second, gains_total, 0.0
    )
    qkv_delta, qkv_first_new, qkv_second_new = adamw_update(
        qkv_weight, qkv_first, qkv_second, qkv_total, DECAY_RATE
    )
    out_delta, out_first_new, out_second_new = adamw_update(
        out_weight, out_first, out_second, out_total, DECAY_RATE
    )
    gate_up_delta, gate_up_first_new, gate_up_second_new = adamw_update(
        gate_up_weight, gate_up_first, gate_up_second, gate_up_total, DECAY_RATE
    )
    down_delta, down_first_new, down_second_new = adamw_update(
        down_weight, down_first, down_second, down_total, DECAY_RATE
    )
    return (
        block_out,
        tokens_grad,
        gains_total,
        qkv_total,
        out_total,
        gate_up_total,
        down_total,
        gains_delta,
        qkv_delta,
        out_delta,
        gate_up_delta,
        down_delta,
        gains_first_new,
        qkv_first_new,
        out_first_new,
        gate_up_first_new,
        down_first_new,
        gains_second_new,
        qkv_second_new,
        out_second_new,
        gate_up_second_new,
        down_second_new,
    )


MESH = pl.DeviceIdType.MESH
bf16, f32 = jnp.bfloat16, jnp.float32
ROWS = 2560
GATHER_UNITS = [(0, 128, 64), (128, 112, 64), (240, 240, 128), (480, 240, 128)] + [(720 + 368 * j, 368, 192) for j in range(5)]
REDUCE_UNITS = [(720 + 368 * j, 368, 192) for j in range(5)] + [(480, 240, 128), (0, 240, 128), (240, 128, 64), (368, 112, 64)]
NT = (((1,), (1,)), ((), ()))
NN = (((1,), (0,)), ((), ()))
TN = (((0,), (0,)), ((), ()))


def mm(a, b, dims=NN):
    return lax.dot_general(a, b, dims, preferred_element_type=f32)


def lanes(n=128):
    return lax.broadcasted_iota(jnp.int32, (1, n), 1)


def spread(k):
    return jnp.where(k < 3, k, k - 1)


def param_specs():
    return [
        pl.BlockSpec((2, 240), lambda k: (0, 0)),
        pl.BlockSpec((240, 256), lambda k: (0, spread(k))),
        pl.BlockSpec((240, 128), lambda k: (0, k)),
        pl.BlockSpec((240, 640), lambda k: (0, k)),
        pl.BlockSpec((128, 640), lambda k: (k, 0)),
    ]


def adam_kernel(FIN, *refs):
    weight, first, second = refs[0:5], refs[5:10], refs[10:15]
    grad, delta, first_new, second_new = refs[15:20], refs[20:25], refs[25:30], refs[30:35]
    k = pl.program_id(0)
    every = slice(None)

    def update(i, at, g, rate):
        m = BETA_ONE * first[i][at] + (1.0 - BETA_ONE) * g
        v = BETA_TWO * second[i][at] + (1.0 - BETA_TWO) * g * g
        fixed = v * (1.0 / (1.0 - BETA_TWO**STEP))
        root = fixed * lax.rsqrt(fixed)
        step = m * (1.0 / (1.0 - BETA_ONE**STEP)) / (root + ADAM_EPS)
        if rate:
            step = step + rate * weight[i][at]
        grad[i][at] = g
        delta[i][at] = -LEARN_RATE * step
        first_new[i][at] = m
        second_new[i][at] = v

    def rows(a, b):
        return FIN[0, a:b].astype(f32)

    @pl.when(k != 3)
    def _():
        update(1, (every, slice(0, 128)), rows(0, 240), DECAY_RATE)
        update(1, (every, slice(128, 256)), rows(240, 480), DECAY_RATE)

    for i in range(2):

        @pl.when(k == 3 + 4 * i)
        def _():
            update(0, (slice(i, i + 1), every), jnp.swapaxes(rows(240, 480), 0, 1)[0:1], 0.0)

    update(2, (every, every), rows(480, 720), DECAY_RATE)
    for j in range(5):
        c = slice(j * 128, (j + 1) * 128)
        update(3, (every, c), rows(720 + 368 * j, 960 + 368 * j), DECAY_RATE)
        turned = jnp.swapaxes(FIN[0, 960 + 368 * j : 1088 + 368 * j], 0, 1).astype(f32)
        update(4, (every, c), turned, DECAY_RATE)


def adam(FIN, weights, moments):
    def five(group):
        return [*group[:4], group[4].T]

    ins = five(weights) + five(moments[:5]) + five(moments[5:])
    shapes = [jax.ShapeDtypeStruct(a.shape, f32) for a in ins[:5]] * 4
    outs = pl.pallas_call(
        adam_kernel,
        name="adam",
        grid=(8,),
        out_shape=shapes,
        in_specs=[pl.BlockSpec((1, ROWS, 128), lambda k: (k, 0, 0))] + param_specs() * 3,
        out_specs=param_specs() * 4,
    )(FIN, *ins)
    return [o.T if i % 5 == 4 else o for i, o in enumerate(outs)]


class Where:
    def __init__(w):
        rep, z = lax.axis_index("rep"), lax.axis_index("fsdp")
        c, x, y = rep % 2, (rep // 2) % 2, rep // 4
        w.rep, w.z, w.c, w.x, w.y = rep, z, c, x, y
        w.partner, w.xn, w.yn = {"rep": rep + 1 - 2 * c}, {"rep": rep + 2 - 4 * x}, {"rep": rep + 4 - 8 * y}
        w.dn = {"rep": rep + 6 - 4 * x - 8 * y}
        w.zn = [{"fsdp": (z + d) % 4} for d in (1, 2, 3)]
        w.q, w.qx, w.qy, w.qd = y * 2 + x, y * 2 + 1 - x, (1 - y) * 2 + x, (1 - y) * 2 + 1 - x
        w.k, w.kx, w.ky, w.kd = c * 4 + w.q, c * 4 + w.qx, c * 4 + w.qy, c * 4 + w.qd
        o = (1 - c) * 4
        w.kp, w.kpx, w.kpy, w.kpd = o + w.q, o + w.qx, o + w.qy, o + w.qd

    def peers(w):
        return [w.partner, w.xn, w.yn, w.dn] + w.zn


class Link:
    def __init__(g, w, sems):
        g.w, g.sems, g.ran, g.waiting = w, sems, [], False

    def copy(g, src, dst, s, r, dev):
        return pltpu.make_async_remote_copy(
            src_ref=src, dst_ref=dst, send_sem=s, recv_sem=r, device_id=dev, device_id_type=MESH
        )

    def send(g, u, i, src, dst, r, dev):
        cp = g.copy(src, dst, g.sems[0].at[u, i], r, dev)
        if g.waiting:
            cp.wait_send()
        else:
            cp.start()

    def got(g, ref, r):
        if not g.waiting:
            g.copy(ref, ref, g.sems[0].at[0, 0], r, g.w.partner).wait_recv()

    def add(g, ref, at, *parts):
        if not g.waiting:
            t = ref[at].astype(f32)
            for p, where in parts:
                t = t + p[where].astype(f32)
            ref[at] = t.astype(bf16)

    def step(g, name, u):
        getattr(g, name)(u)
        if name != "g0":
            g.ran.append((name, u))

    def finish(g):
        g.waiting = True
        for name, u in g.ran:
            getattr(g, name)(u)


class Gather(Link):
    def __init__(g, w, own, W, sems):
        super().__init__(w, sems)
        g.own, g.W = own, W
        g.rz, g.rx, g.ry, g.rp = sems[1:]

    def reg(g, k, u, a=0, b=None):
        r0, n, h = GATHER_UNITS[u]
        return g.W.at[k, :, pl.ds(r0 + a, (n if b is None else b) - a)]

    def g0(g, u):
        r0, n, h = GATHER_UNITS[u]

        def out(d):
            g.send(u, d, g.own(u, g.w.k), g.W.at[g.w.k, d, pl.ds(r0, n)], g.rz.at[u, d], g.w.zn[d])

        pl.when(g.w.z != 3)(lambda: out(0))
        out(1)
        pl.when(g.w.z != 0)(lambda: out(2))

    def gr(g, u):
        r0, n, h = GATHER_UNITS[u]
        z = g.w.z

        @pl.when((z == 1) | (z == 2))
        def _():
            src = g.W.at[g.w.k, 1, pl.ds(r0, n)]
            g.got(src, g.rz.at[u, 1])
            d = 2 * (z - 1)
            g.send(u, 11, src, g.W.at[g.w.k, d, pl.ds(r0, n)], g.rz.at[u, d], {"fsdp": 3 * (z - 1)})

    def g1(g, u):
        r0, n, h = GATHER_UNITS[u]

        def block(d):
            g.got(g.W.at[g.w.k, d, pl.ds(r0, n)], g.rz.at[u, d])

        block(0)
        pl.when((g.w.z == 0) | (g.w.z == 3))(lambda: block(1))
        block(2)
        b = g.reg(g.w.k, u)
        g.send(u, 3, b, b, g.rx.at[u, 0], g.w.xn)
        g.send(u, 4, b, b, g.ry.at[u, 0], g.w.yn)
        g.send(u, 5, b, b, g.rp.at[u, 0], g.w.partner)

    def g2a(g, u):
        h = GATHER_UNITS[u][2]
        g.got(g.reg(g.w.kx, u), g.rx.at[u, 0])
        b = g.reg(g.w.kx, u, 0, h)
        g.send(u, 6, b, b, g.ry.at[u, 1], g.w.yn)
        b = g.reg(g.w.kx, u)
        g.send(u, 7, b, b, g.rp.at[u, 1], g.w.partner)

    def g2b(g, u):
        h = GATHER_UNITS[u][2]
        g.got(g.reg(g.w.ky, u), g.ry.at[u, 0])
        b = g.reg(g.w.ky, u, h)
        g.send(u, 8, b, b, g.rx.at[u, 1], g.w.xn)
        b = g.reg(g.w.ky, u)
        g.send(u, 9, b, b, g.rp.at[u, 2], g.w.partner)

    def g3(g, u):
        h = GATHER_UNITS[u][2]
        g.got(g.reg(g.w.kd, u, 0, h), g.ry.at[u, 1])
        g.got(g.reg(g.w.kd, u, h), g.rx.at[u, 1])
        b = g.reg(g.w.kd, u)
        g.send(u, 10, b, b, g.rp.at[u, 3], g.w.partner)

    def g4(g, u):
        for i, k in enumerate((g.w.kp, g.w.kpx, g.w.kpy, g.w.kpd)):
            g.got(g.reg(k, u), g.rp.at[u, i])


class Reduce(Link):
    def __init__(g, w, S, RX3, RY3, RX, RY, RZ, FIN, sems):
        super().__init__(w, sems)
        g.S, g.RX3, g.RY3, g.RX, g.RY, g.RZ, g.FIN = S, RX3, RY3, RX, RY, RZ, FIN
        g.r3, g.rxy, g.rz, g.rf, g.lf = sems[1:]

    def at(g, u):
        r0, n, h = REDUCE_UNITS[u]
        return pl.ds(r0, n), g.S(u), g.w

    def z1(g, u):
        R, S, w = g.at(u)
        landing = ((slice(0, 4), g.RX), (slice(0, 4), g.RY), (slice(0, 2), g.RX3), (slice(2, 4), g.RY3))
        for i, (part, buf) in enumerate(landing):
            d = min(i, 2)
            g.send(u, i, S.at[part, (w.z + d + 1) % 4], buf.at[:, R], g.rxy.at[u, i], w.zn[d])

    def z2(g, u):
        r0, n, h = REDUCE_UNITS[u]
        R, S, w = g.at(u)
        for i, buf in enumerate((g.RX, g.RY, g.RX3, g.RY3)):
            g.got(buf.at[:, R], g.rxy.at[u, i])
        for a, third in ((0, g.RX3), (2, g.RY3)):
            part = slice(a, a + 2)
            g.add(S, (part, w.z), (g.RX, (part, R)), (g.RY, (part, R)), (third, (slice(None), R)))
        up, low = (pl.ds(0, h), pl.ds(r0, h)), (pl.ds(h, n - h), pl.ds(r0 + h, n - h))
        g.send(u, 4, S.at[w.qd, w.z, up[0]], g.RZ.at[0, up[1]], g.r3.at[u, 0], w.xn)
        g.send(u, 5, S.at[w.qd, w.z, low[0]], g.RZ.at[0, low[1]], g.r3.at[u, 1], w.yn)
        g.send(u, 6, S.at[w.qx, w.z, up[0]], g.RZ.at[1, up[1]], g.rz.at[u, 0], w.xn)
        g.send(u, 7, S.at[w.qy, w.z, low[0]], g.RZ.at[2, low[1]], g.rz.at[u, 1], w.yn)

    def z3a(g, u):
        r0, n, h = REDUCE_UNITS[u]
        R, S, w = g.at(u)
        low = (pl.ds(h, n - h), pl.ds(r0 + h, n - h))
        g.got(g.RZ.at[0, low[1]], g.r3.at[u, 1])
        g.add(S, (w.qx, w.z, low[0]), (g.RZ, (0, low[1])))
        g.send(u, 8, S.at[w.qx, w.z, low[0]], g.RZ.at[1, low[1]], g.rz.at[u, 2], w.xn)

    def z3b(g, u):
        r0, n, h = REDUCE_UNITS[u]
        R, S, w = g.at(u)
        up = (pl.ds(0, h), pl.ds(r0, h))
        g.got(g.RZ.at[0, up[1]], g.r3.at[u, 0])
        g.add(S, (w.qy, w.z, up[0]), (g.RZ, (0, up[1])))
        g.send(u, 17, S.at[w.qy, w.z, up[0]], g.RZ.at[2, up[1]], g.rz.at[u, 3], w.yn)

    def z4(g, u):
        r0, n, h = REDUCE_UNITS[u]
        R, S, w = g.at(u)
        up, low = pl.ds(r0, h), pl.ds(r0 + h, n - h)
        g.got(g.RZ.at[1, up], g.rz.at[u, 0])
        g.got(g.RZ.at[1, low], g.rz.at[u, 2])
        g.got(g.RZ.at[2, low], g.rz.at[u, 1])
        g.got(g.RZ.at[2, up], g.rz.at[u, 3])
        g.add(S, (w.q, w.z), (g.RZ, (1, R)), (g.RZ, (2, R)))
        g.share(u)

    def c1(g, u):
        R, S, w = g.at(u)
        g.send(u, 0, S.at[w.qd, 0:2], g.RX3.at[:, R], g.r3.at[u, 0], w.xn)
        g.send(u, 1, S.at[w.qd, 2:4], g.RY3.at[:, R], g.r3.at[u, 1], w.yn)
        g.send(u, 2, S.at[w.qx, 0:2], g.RX.at[0:2, R], g.rxy.at[u, 0], w.xn)
        g.send(u, 3, S.at[w.qy, 2:4], g.RY.at[2:4, R], g.rxy.at[u, 1], w.yn)

    def c2a(g, u):
        R, S, w = g.at(u)
        g.got(g.RY3.at[:, R], g.r3.at[u, 1])
        g.add(S, (w.qx, slice(2, 4)), (g.RY3, (slice(None), R)))
        g.send(u, 4, S.at[w.qx, 2:4], g.RX.at[2:4, R], g.rxy.at[u, 2], w.xn)

    def c2b(g, u):
        R, S, w = g.at(u)
        g.got(g.RX3.at[:, R], g.r3.at[u, 0])
        g.add(S, (w.qy, slice(0, 2)), (g.RX3, (slice(None), R)))
        g.send(u, 5, S.at[w.qy, 0:2], g.RY.at[0:2, R], g.rxy.at[u, 3], w.yn)

    def c3(g, u):
        R, S, w = g.at(u)
        g.got(g.RX.at[0:2, R], g.rxy.at[u, 0])
        g.got(g.RX.at[2:4, R], g.rxy.at[u, 2])
        g.got(g.RY.at[2:4, R], g.rxy.at[u, 1])
        g.got(g.RY.at[0:2, R], g.rxy.at[u, 3])
        g.add(S, (w.q,), (g.RX, (slice(None), R)), (g.RY, (slice(None), R)))
        for d in range(3):
            zt = (w.z + d + 1) % 4
            g.send(u, 6 + d, S.at[w.q, zt], g.RZ.at[d, R], g.rz.at[u, d], w.zn[d])

    def c4(g, u):
        R, S, w = g.at(u)
        for d in range(3):
            g.got(g.RZ.at[d, R], g.rz.at[u, d])
        g.add(S, (w.q, w.z), *[(g.RZ, (d, R)) for d in range(3)])
        g.share(u)

    def share(g, u):
        R, S, w = g.at(u)
        src, dst = S.at[w.q, w.z], g.FIN.at[w.k, R]
        if u in DIAGONAL:
            g.send(u, 12, src, dst, g.rf.at[u, 2], w.dn)
        g.send(u, 9, src, dst, g.rf.at[u, 0], w.xn)
        g.send(u, 10, src, dst, g.rf.at[u, 1], w.yn)
        g.send(u, 11, src, dst, g.rf.at[u, 4], w.partner)
        if not g.waiting:
            pltpu.make_async_copy(src, dst, g.lf.at[u]).start()

    def fin(g, k, u, a=0, b=None):
        r0, n, h = REDUCE_UNITS[u]
        return g.FIN.at[k, pl.ds(r0 + a, (n if b is None else b) - a)]

    def c5a(g, u):
        h, w = REDUCE_UNITS[u][2], g.w
        g.got(g.fin(w.kx, u), g.rf.at[u, 0])
        if u not in DIAGONAL:
            b = g.fin(w.kx, u, 0, h)
            g.send(u, 12, b, b, g.rf.at[u, 3], w.yn)
        b = g.fin(w.kx, u)
        g.send(u, 13, b, b, g.rf.at[u, 5], w.partner)

    def c5b(g, u):
        h, w = REDUCE_UNITS[u][2], g.w
        g.got(g.fin(w.ky, u), g.rf.at[u, 1])
        if u not in DIAGONAL:
            b = g.fin(w.ky, u, h)
            g.send(u, 14, b, b, g.rf.at[u, 2], w.xn)
        b = g.fin(w.ky, u)
        g.send(u, 15, b, b, g.rf.at[u, 6], w.partner)

    def c6(g, u):
        h, w = REDUCE_UNITS[u][2], g.w
        if u in DIAGONAL:
            g.got(g.fin(w.kd, u), g.rf.at[u, 2])
        else:
            g.got(g.fin(w.kd, u, 0, h), g.rf.at[u, 3])
            g.got(g.fin(w.kd, u, h), g.rf.at[u, 2])
        b = g.fin(w.kd, u)
        g.send(u, 16, b, b, g.rf.at[u, 7], w.partner)

    def c7(g, u):
        R, S, w = g.at(u)
        for i, k in enumerate((w.kp, w.kpx, w.kpy, w.kpd)):
            g.got(g.fin(k, u), g.rf.at[u, 4 + i])
        if not g.waiting:
            pltpu.make_async_copy(S.at[w.q, w.z], g.fin(w.k, u), g.lf.at[u]).wait()


def load_unit(w, own, W, dst, sem, u0, n, row0=0, halves=False):
    def block(k, _):
        def one(r, s, view, c0):
            def put(src, zs):
                rows = pl.ds(pl.multiple_of(row0 + zs * n, 16), n)
                pltpu.make_async_copy(src, view.at[rows, pl.ds(pl.multiple_of(c0, 128), 128)], sem).start()

            put(own(k, s), w.z)
            for d in range(3):
                put(W.at[k, d, pl.ds(r, n)], (w.z + 3 - d) % 4)

        if halves:
            for s in range(2):
                one(u0 + s * n, s, dst.at[k // 4], (k % 4) * 256 + s * 128)
        else:
            one(u0, 0, dst, k * 128)
        return 0

    lax.fori_loop(0, 8, block, 0)


def rope(t, c, s):
    first = (lanes() % 64) < 32
    return t * c + jnp.where(first, pltpu.roll(t, 96, 1), pltpu.roll(t, 32, 1)) * s


def dup(t, half):
    return jnp.where((lanes() < 64) == (half == 0), t, pltpu.roll(t, 64, 1))


def gain_row(tile):
    at = (lax.broadcasted_iota(jnp.int32, (8, 128), 0) == 0) & (lax.broadcasted_iota(jnp.int32, (8, 128), 1) == 0)
    return mm(at.astype(f32).astype(bf16), tile, NT)[0:1]


def norm(v, g):
    return v * lax.rsqrt(jnp.mean(v * v, axis=1, keepdims=True) + NORM_EPS) * g


def norm_back(v, g, u):
    r = lax.rsqrt(jnp.mean(v * v, axis=1, keepdims=True) + NORM_EPS)
    wv = u * g
    return r * wv - v * (r * r * r) * jnp.mean(wv * v, axis=1, keepdims=True), u * v * r


def head_at(h):
    t, half = h // 2, h % 2
    mine = (lanes() // 64) == half
    return t, mine, pl.ds(pl.multiple_of(t * 128, 128), 128)


def group_fwd(g, qk, k2, v2, bias, ctx, lse):
    for i in range(2):
        rows, n = pl.ds(256 * i, 256), 256 * (i + 1)
        sums = lse[rows]
        for h in (3 * g, 3 * g + 1, 3 * g + 2):
            t, mine, col = head_at(h)
            hm = jnp.where(mine, 0.125, 0.0).astype(bf16)
            s = mm(qk[rows, col] * hm, k2[g, pl.ds(0, n)], NT) + bias[rows, pl.ds(0, n)].astype(f32)
            m = jnp.max(s, axis=1, keepdims=True)
            p = jnp.exp(s - m)
            l = jnp.sum(p, axis=1, keepdims=True)
            o = mm((p * (1.0 / l)).astype(bf16), v2[g, pl.ds(0, n)])
            ctx[rows, col] = jnp.where(mine, o, ctx[rows, col].astype(f32)).astype(bf16)
            sums = jnp.where(lanes() == h, m + jnp.log(l), sums)
        lse[rows] = sums


def group_bwd(g, qk, k2, v2, bias, lse, dctx, dq, dk, dv):
    for i in range(2):
        rows, n = pl.ds(256 * i, 256), 256 * (i + 1)
        dk_part, dv_part = 0.0, 0.0
        for h in (3 * g, 3 * g + 1, 3 * g + 2):
            t, mine, col = head_at(h)
            hm = jnp.where(mine, 0.125, 0.0).astype(bf16)
            om = jnp.where(mine, 1.0, 0.0).astype(bf16)
            qs = qk[rows, col] * hm
            do = dctx[t // 4, rows, pl.ds(pl.multiple_of((t % 4) * 128, 128), 128)] * om
            le = jnp.sum(jnp.where(lanes() == h, lse[rows], 0.0), axis=1, keepdims=True)
            s = mm(qs, k2[g, pl.ds(0, n)], NT) + bias[rows, pl.ds(0, n)].astype(f32)
            p = jnp.exp(s - le)
            dp = mm(do, v2[g, pl.ds(0, n)], NT)
            dv_part += mm(p.astype(bf16), do, TN)
            ds = (p * (dp - jnp.sum(p * dp, axis=1, keepdims=True))).astype(bf16)
            dk_part += mm(ds, qs, TN)
            dq[rows, col] = jnp.where(mine, mm(ds, k2[g, pl.ds(0, n)]) * 0.125, dq[rows, col])
        if i == 0:
            dk[g] = jnp.zeros_like(dk[g])
            dv[g] = jnp.zeros_like(dv[g])
        dk[g, pl.ds(0, n)] += dk_part
        dv[g, pl.ds(0, n)] += dv_part


KEYS = [(7, 1), (8, 0), (8, 1), (9, 0), (9, 1)]
VALUES = [(10, 0), (10, 1), (11, 0), (11, 1), (12, 0)]


def layer_kernel(
    tokT, cotT, freq, ids, norm_gains, qkv, out, gate_up, downT,
    boT, tgT, FIN, W, n1H, ctxH,
    cot, cos, sin, qk, k2, v2, lse, mid, n2, gains,
    wg, wd, bias, n2T, n2pT, cpT, dypp, hid, dgu, hidp, dgup, da, acc, dacc, dk, dv, gcol, gcolp,
    SM, SO, RX3, RY3, RX, RY, RZ, stage,
    lsem, wsem, ps, pr, *sems,
):
    w = Where()
    c = w.c
    bar = pltpu.get_barrier_semaphore()
    for p in w.peers():
        pl.semaphore_signal(bar, inc=1, device_id=p, device_id_type=MESH)
    loads = {}

    def fetch(name, *pairs):
        loads[name] = [pltpu.make_async_copy(src, dst, wsem.at[len(loads)]) for src, dst in pairs]
        for cp in loads[name]:
            cp.start()

    def fetch_unit(j):
        rows = slice(256 * (j % 2), 256 * (j % 2) + 240)
        cols = [(gate_up.at[:, k * 640 + j * 128 : k * 640 + (j + 1) * 128], acc.at[rows, k * 128 : (k + 1) * 128]) for k in range(8)]
        for k in range(8):
            pltpu.make_async_copy(*cols[k], wsem.at[2 + j]).start()
        part = downT.at[:, j * 128 : (j + 1) * 128]
        turned = (dk, dv)[j % 2]
        pltpu.make_async_copy(part.at[0:512], turned.at[0], wsem.at[7 + j]).start()
        pltpu.make_async_copy(part.at[512:960], turned.at[1, 0:448], wsem.at[12 + j]).start()

    fetch("qkv", (qkv, stage))
    fetch("out", (out, dacc.at[0:240]))
    fetch_unit(0)
    fetch_unit(1)
    tl = pltpu.make_async_copy(tokT, tgT, lsem.at[0])
    tl.start()
    cl = pltpu.make_async_copy(cotT, boT, lsem.at[1])
    cl.start()
    pl.semaphore_wait(bar, len(w.peers()))

    def summed(u):
        if u < 5:
            return SM.at[u]
        return SO.at[u - 5] if u < 7 else SO.at[2, :, :, slice(*((0, 128), (128, 240))[u - 7])]

    def held(u, k):
        at = (k // 4, k % 4)
        if u >= 4:
            return SM.at[u - 4, *at]
        return (SO.at[1, *at, 0:128], SO.at[1, *at, 128:240], SO.at[2, *at], SO.at[0, *at])[u]

    ga = Gather(w, held, W, sems[:5])
    re = Reduce(w, summed, RX3, RY3, RX, RY, RZ, FIN, sems[5:])
    live, local = {}, {}

    def psend(i, src, dst):
        live[i] = ga.copy(src, dst, ps.at[i], pr.at[i], w.partner)
        live[i].start()

    def psent(*which):
        for i in which:
            live.pop(i).wait_send()

    def pgot(i, dst):
        ga.copy(dst, dst, ps.at[0], pr.at[i], w.partner).wait_recv()

    def begin(name, src, dst, sem):
        local[name] = pltpu.make_async_copy(src, dst, sem)
        local[name].start()

    def end(name):
        local.pop(name).wait()

    other = pl.ds(pl.multiple_of((1 - c) * 512, 512), 512)
    mine = pl.ds(pl.multiple_of(c * 512, 512), 512)
    half_rows = [pl.ds(256 * i, 256) for i in range(2)]

    zero = jnp.zeros((240, 128), bf16)

    def PQ():
        loads["qkv"][0].wait()
        for t in range(13):
            k, sub = (t // 2, t % 2) if t < 6 else (4 + (t - 6) // 2, (t - 6) % 2)
            tile = SO.at[1 + sub, k // 4, k % 4]
            if t < 12:
                tile[...] = stage[:, t * 128 : (t + 1) * 128].astype(bf16)
            else:
                tile[...] = zero
                tile[:, 0:64] = stage[:, 1536:1600].astype(bf16)
        SO[1, 0, 3] = zero
        for i in range(2):
            at = lax.broadcasted_iota(jnp.int32, (128, 240), 0) == 0
            tile = jnp.where(at, norm_gains[i : i + 1], 0.0)
            SO[2, i, 3] = jnp.swapaxes(tile, 0, 1).astype(bf16)

    def PO():
        loads["out"][0].wait()
        SO[0, 1, 3] = zero
        for k in range(8):
            width = 128 if k < 7 else 64
            SO[0, k // 4, k % 4, :, 0:width] = dacc[0:240, k * 128 : k * 128 + width].astype(bf16)

    def PM(j):
        rows = slice(256 * (j % 2), 256 * (j % 2) + 240)
        turned = (dk, dv)[j % 2]
        view = acc.at[rows]
        pltpu.make_async_copy(view, view, wsem.at[2 + j]).wait()
        for i, part in enumerate((turned.at[0], turned.at[1, 0:448])):
            pltpu.make_async_copy(part, part, wsem.at[7 + 5 * i + j]).wait()
        SM[j, 1, 3, 240:368] = jnp.zeros((128, 128), bf16)
        for k in range(8):
            width = 128 if k < 7 else 64
            SM[j, k // 4, k % 4, 0:240] = acc[rows, k * 128 : (k + 1) * 128].astype(bf16)
            block = turned[k // 4, (k % 4) * 128 : (k % 4) * 128 + width].astype(bf16)
            SM[j, k // 4, k % 4, 240:368, 0:width] = jnp.swapaxes(block, 0, 1)
        if j + 2 < 5:
            fetch_unit(j + 2)

    def A0():
        seq = ids[...].astype(f32)
        column = jnp.swapaxes(jnp.broadcast_to(seq, (8, 512)), 0, 1)[:, 0:1]
        for i in range(2):
            own_seq = column[256 * i : 256 * (i + 1)]
            rows = lax.broadcasted_iota(jnp.int32, (256, 512), 0) + 256 * i
            cols = lax.broadcasted_iota(jnp.int32, (256, 512), 1)
            ok = (own_seq == seq) & (cols <= rows)
            bias[pl.ds(256 * i, 256)] = jnp.where(ok, 0.0, NEG_LARGE).astype(bf16)
            first_row = jnp.sum(jnp.where(seq < own_seq, 1.0, 0.0), axis=1, keepdims=True)
            row = (lax.broadcasted_iota(jnp.int32, (256, 1), 0) + 256 * i).astype(f32)
            angle = (row - first_row) * freq[...]
            cos[pl.ds(256 * i, 256)] = jnp.cos(angle)
            sin[pl.ds(256 * i, 256)] = jnp.where((lanes() % 64) < 32, -1.0, 1.0) * jnp.sin(angle)
        lse[...] = jnp.zeros_like(lse)
        tl.wait()
        cl.wait()
        mid[...] = jnp.swapaxes(tgT[...], 0, 1).astype(f32)
        cot[:, 896:1024] = jnp.zeros((512, 128), bf16)
        cot[:, 0:960] = jnp.swapaxes(boT[...], 0, 1)

    def LQ():
        load_unit(w, lambda k, s: SO.at[1 + s, k // 4, k % 4], W, wg, lsem.at[0], 0, 240, halves=True)

    def wait_q():
        pltpu.make_async_copy(wg, wg, lsem.at[0]).wait()

    def LO():
        load_unit(w, lambda k, s: SO.at[0, k // 4, k % 4], W, wd, lsem.at[1], 480, 240)

    def wait_o():
        view = wd.at[pl.ds(0, 960)]
        pltpu.make_async_copy(view, view, lsem.at[1]).wait()

    def A1():
        wait_q()
        acc[...] = jnp.zeros_like(acc)
        dacc[...] = jnp.zeros_like(dacc)
        gains[...] = jnp.zeros_like(gains)
        gains[0:1] = gain_row(wg[0, :, 896:1024])
        gains[1:2] = gain_row(wg[1, :, 896:1024])
        n1 = norm(mid[...], gains[0:1]).astype(bf16)
        da[:, 0:960] = n1
        tgT[...] = jnp.swapaxes(n1, 0, 1)
        for half, (lo, hi) in enumerate(((0, 6), (6, 13))):
            res = mm(da[:, 0:960], wg[half, :, 0 : (hi - lo) * 128])
            for t in range(lo, hi):
                tile = res[:, (t - lo) * 128 : (t - lo + 1) * 128]
                if t < 10:
                    tile = rope(tile, cos[...], sin[...])
                    qk[:, t * 128 : (t + 1) * 128] = tile.astype(bf16)
                for i in range(5):
                    if KEYS[i][0] == t:
                        k2[i] = dup(tile, KEYS[i][1]).astype(bf16)
                    if VALUES[i][0] == t:
                        v2[i] = dup(tile, VALUES[i][1]).astype(bf16)
        begin("n1", tgT, n1H, lsem.at[2])
        da[...] = jnp.zeros_like(da)

    def A3():
        wait_o()
        for rows in half_rows:
            m = mid[rows] + mm(da[rows, 0:960], wd[pl.ds(0, 960), 0:960])
            mid[rows] = m
            n2[rows] = norm(m, gains[1:2]).astype(bf16)
        n2T[...] = jnp.swapaxes(n2[...], 0, 1)
        boT[...] = jnp.swapaxes(da[:, 0:960], 0, 1)
        psend(0, n2T, n2pT)
        psend(1, cot.at[:, other], dypp)
        psend(2, boT, cpT)
        begin("ctx", boT, ctxH, lsem.at[3])

    def dslot(j):
        return pl.ds(pl.multiple_of(((j + 2) % 3) * 512, 512), 512)

    def L(j):
        def rows(a, b):
            return lambda k, s: SM.at[j, k // 4, k % 4, a:b]

        load_unit(w, rows(0, 240), W, wg.at[j % 2], lsem.at[4 + j % 2], 720 + 368 * j, 240)
        load_unit(w, rows(240, 368), W, wd, lsem.at[6 + j % 2], 960 + 368 * j, 128, row0=((j + 2) % 3) * 512)

    def sends(j):
        b = j % 2
        return (
            ga.copy(hid.at[b], hidp.at[b], ps.at[4 + j], pr.at[4 + j], w.partner),
            ga.copy(dgu.at[b, 1 - c], dgup.at[b], ps.at[9 + j], pr.at[9 + j], w.partner),
        )

    def F(j):
        b = j % 2
        pltpu.make_async_copy(wg.at[b], wg.at[b], lsem.at[4 + b]).wait()
        view = wd.at[dslot(j)]
        pltpu.make_async_copy(view, view, lsem.at[6 + b]).wait()

        @pl.when(j >= 2)
        def _():
            sends(j - 2)[0].wait_send()
            sends(j - 2)[1].wait_send()

        def half(i, _):
            rows = pl.ds(pl.multiple_of(i * 256, 256), 256)
            gu = mm(n2[rows], wg[b])
            gate, up = gu[:, :512], gu[:, 512:]
            sg = jax.nn.sigmoid(gate)
            a = gate * sg
            hb = (a * up).astype(bf16)
            hid[b, rows] = hb
            acc[rows, 0:960] += mm(hb, wd[dslot(j), 0:960])
            dh = mm(cot[rows, 0:960], wd[dslot(j), 0:960], NT)
            dgate = (dh * up * (sg * (1.0 + gate * (1.0 - sg)))).astype(bf16)
            dup_ = (dh * a).astype(bf16)
            dgu[b, 0, rows] = dgate
            dgu[b, 1, rows] = dup_
            dacc[rows] += mm(dgate, wg[b, :, 0:512], NT) + mm(dup_, wg[b, :, 512:1024], NT)
            return 0

        lax.fori_loop(0, 2, half, 0)
        for cp in sends(j):
            cp.start()

    def cut(S, G, n, r0=0):
        for q in range(4):
            for z in range(4):
                S[q, z, r0 : r0 + n] = G[z * n : (z + 1) * n, q * 128 : (q + 1) * 128].astype(bf16)

    def R(j):
        b = j % 2

        @pl.when(j == 0)
        def _():
            pgot(0, n2pT)
            pgot(1, dypp)

        pgot(4 + j, hidp.at[b])
        pgot(9 + j, dgup.at[b])
        cut(SM.at[j], mm(n2T[...], dgu[b, c]) + mm(n2pT[...], dgup[b]), 240)
        cut(SM.at[j], mm(hid[b], cot[:, mine], TN) + mm(hidp[b], dypp[...], TN), 128, 240)

    def B1():
        for cp in sends(3) + sends(4):
            cp.wait_send()
        psent(0, 1, 2)
        LO()
        LQ()
        end("ctx")
        begin("ctxT", ctxH, n2T, lsem.at[3])
        ones = jnp.ones((256, 128), bf16)
        da[:, 896:1024] = jnp.zeros((512, 128), bf16)
        gc = 0.0
        for i, rows in enumerate(half_rows):
            m = mid[rows]
            boT[:, 256 * i : 256 * (i + 1)] = jnp.swapaxes((m + acc[rows, 0:960]).astype(bf16), 0, 1)
            dv_, gp = norm_back(m, gains[1:2], dacc[rows])
            dmid = cot[rows, 0:960].astype(f32) + dv_
            dacc[rows] = dmid
            da[rows, 0:960] = dmid.astype(bf16)
            gc = gc + mm(gp.astype(bf16), ones, TN)
        gcol[1] = gc.astype(bf16)
        psend(14, da.at[:, other], hidp.at[1])

    def B2():
        wait_o()
        hid[1, :, 384:512] = jnp.zeros((512, 128), bf16)
        hid[0] = mm(da[:, 0:960], wd[pl.ds(0, 512), 0:960], NT).astype(bf16)
        hid[1, :, 0:448] = mm(da[:, 0:960], wd[pl.ds(512, 448), 0:960], NT).astype(bf16)
        end("ctxT")
        pgot(2, cpT)
        pgot(14, hidp.at[1])
        end("n1")
        psend(3, n1H, n2pT)
        cut(SO.at[0], mm(n2T[...], da[:, mine]) + mm(cpT[...], hidp[1]), 240)
        acc[...] = jnp.zeros_like(acc)
        psent(14)
        begin("n1T", n1H, n2T, lsem.at[2])
        begin("tok", tokT, tgT, lsem.at[3])

    def D1():
        def put(half, t, tile):
            dgu[half, t // 4, :, (t % 4) * 128 : (t % 4 + 1) * 128] = tile.astype(bf16)

        first = lanes() < 64
        nsin = -sin[...]

        def fold(ref, i):
            return ref[i] + pltpu.roll(ref[i], 64, 1)

        for t in range(7):
            put(t // 6, t % 6, rope(acc[:, t * 128 : (t + 1) * 128], cos[...], nsin))
        zero = jnp.zeros((512, 128), f32)
        for half, t in ((0, 6), (0, 7), (1, 7)):
            put(half, t, zero)
        kk, vv = [fold(dk, i) for i in range(5)], [fold(dv, i) for i in range(5)]
        put(1, 1, rope(jnp.where(first, acc[:, 896:1024], kk[0]), cos[...], nsin))
        put(1, 2, rope(jnp.where(first, kk[1], kk[2]), cos[...], nsin))
        put(1, 3, rope(jnp.where(first, kk[3], kk[4]), cos[...], nsin))
        put(1, 4, jnp.where(first, vv[0], vv[1]))
        put(1, 5, jnp.where(first, vv[2], vv[3]))
        put(1, 6, jnp.where(first, vv[4], 0.0))
        psend(15, dgu.at[1 - c], dgup)

    def qgrad(sub):
        for q in range(4):
            t = 2 * q + sub
            if t == 7:
                G = gcol[c].astype(f32) + gcolp[...].astype(f32)
            else:
                at = slice((t % 4) * 128, (t % 4 + 1) * 128)
                G = mm(n2T[...], dgu[c, t // 4, :, at]) + mm(n2pT[...], dgup[t // 4, :, at])
            for z in range(4):
                SO[1 + sub, q, z] = G[z * 240 : (z + 1) * 240].astype(bf16)

    def D2():
        end("n1T")
        pgot(3, n2pT)
        pgot(15, dgup)
        qgrad(0)

    def D3():
        wait_q()
        end("tok")
        da[:, 0:960] = jnp.swapaxes(tgT[...], 0, 1)
        ones = jnp.ones((256, 128), bf16)
        gc = 0.0
        for i, rows in enumerate(half_rows):
            dn1 = mm(dgu[0, 0, rows], wg[0, :, 0:512], NT) + mm(dgu[0, 1, rows, 0:256], wg[0, :, 512:768], NT)
            dn1 += mm(dgu[1, 0, rows], wg[1, :, 0:512], NT) + mm(dgu[1, 1, rows, 0:384], wg[1, :, 512:896], NT)
            dv_, gp = norm_back(da[rows, 0:960].astype(f32), gains[0:1], dn1)
            tgT[:, 256 * i : 256 * (i + 1)] = jnp.swapaxes((dacc[rows] + dv_).astype(bf16), 0, 1)
            gc = gc + mm(gp.astype(bf16), ones, TN)
        gcol[0] = gc.astype(bf16)
        psend(16, gcol.at[1 - c], gcolp)

    def D4():
        pgot(16, gcolp)
        qgrad(1)

    steps = dict(PQ=PQ, PO=PO, PM=PM, A0=A0, LQ=LQ, A1=A1, LO=LO, A3=A3, L=L, B1=B1, B2=B2, D1=D1, D2=D2, D3=D3, D4=D4)

    def run(part):
        for name, at in part:
            if name in steps:
                steps[name](*([] if at is None else [at]))
            else:
                (ga if name[0] == "g" else re).step(name, at)

    def after(i, parts):
        for n, part in enumerate(parts):
            if part:
                pl.when(i == n)(lambda part=part: run(part))

    def heads(group, parts):
        def turn(g, _):
            group(g)
            after(g, parts)
            return 0

        lax.fori_loop(0, 5, turn, 0)

    def unit(j, _):
        F(j)
        after(j, PARTS["F"])
        R(j)
        after(j, PARTS["R"])
        return 0

    run(PARTS["start"])
    heads(lambda g: group_fwd(g, qk, k2, v2, bias, da, lse), PARTS["H"])
    run(PARTS["A3"])
    ga.waiting = True
    for u in range(len(GATHER_UNITS)):
        ga.g0(u)
    ga.waiting = False
    lax.fori_loop(0, 5, unit, 0)
    run(PARTS["B1"])
    heads(lambda g: group_bwd(g, qk, k2, v2, bias, lse, hid, acc, dk, dv), PARTS["K"])
    run(PARTS["D1"])
    for i in list(live):
        psent(i)
    ga.finish()
    re.finish()


def layer(tok, cot, ids, weights):
    freq = ROPE_BASE ** (-2.0 * (jnp.arange(128) % 32).astype(f32) / HEAD)
    S, D = jax.ShapeDtypeStruct, pltpu.SemaphoreType.DMA

    def V(*shape, dt=bf16):
        return pltpu.VMEM(shape, dt)

    vm = pl.BlockSpec(memory_space=pltpu.VMEM)
    hb = pl.BlockSpec(memory_space=pl.ANY)
    outs = pl.pallas_call(
        layer_kernel,
        name="layer",
        out_shape=[
            S((960, 512), bf16), S((960, 512), bf16), S((8, ROWS, 128), bf16),
            S((8, 3, ROWS, 128), bf16), S((960, 512), bf16), S((960, 512), bf16),
        ],
        in_specs=[hb, hb, vm, vm, vm, hb, hb, hb, hb],
        out_specs=[vm, vm, hb, hb, hb, hb],
        scratch_shapes=[
            V(512, 1024), V(512, 128, dt=f32), V(512, 128, dt=f32), V(512, 1280), V(5, 512, 128), V(5, 512, 128), V(512, 128, dt=f32), V(512, 960, dt=f32),
            V(512, 960), V(8, 960, dt=f32),
            V(2, 960, 1024), V(1536, 1024), V(512, 512), V(960, 512), V(960, 512), V(960, 512), V(512, 512),
            V(2, 512, 512), V(2, 2, 512, 512), V(2, 512, 512), V(2, 512, 512), V(512, 1024),
            V(512, 1024, dt=f32), V(512, 960, dt=f32), V(5, 512, 128, dt=f32), V(5, 512, 128, dt=f32),
            V(2, 960, 128), V(960, 128),
            V(5, 4, 4, 368, 128), V(3, 4, 4, 240, 128),
            V(2, ROWS, 128), V(2, ROWS, 128), V(4, ROWS, 128), V(4, ROWS, 128), V(3, ROWS, 128), V(240, 1600, dt=f32),
            D((8,)), D((17,)), D((17,)), D((17,)),
            D((9, 12)), D((9, 3)), D((9, 2)), D((9, 2)), D((9, 4)),
            D((9, 18)), D((9, 2)), D((9, 4)), D((9, 4)), D((9, 8)), D((9,)),
        ],
        compiler_params=pltpu.CompilerParams(
            collective_id=0, has_side_effects=True, vmem_limit_bytes=67043328
        ),
    )(tok.T, cot.T, freq[None, :], ids[None, :], *weights[:4], weights[4].T)
    return outs[:3]


PARTS = {
    "start": [
        ("PQ", None), ("g0", 0), ("g0", 1), ("g0", 2), ("PO", None), ("PM", 0), ("PM", 1), ("A0", None),
        ("gr", 0), ("gr", 1), ("PM", 2), ("PM", 3), ("PM", 4), ("gr", 2), ("g1", 0), ("g0", 3), ("g1", 1),
        ("g0", 4), ("g1", 2), ("g0", 5), ("g2a", 0), ("g2b", 0), ("gr", 3), ("g2a", 1), ("g2b", 1), ("gr", 4),
        ("g2a", 2), ("g2b", 2), ("g3", 0), ("g3", 1), ("g4", 0), ("g4", 1), ("gr", 5), ("g3", 2), ("g1", 3),
        ("g0", 6), ("g4", 2), ("LQ", None), ("g1", 4), ("g0", 7), ("g1", 5), ("g0", 8), ("A1", None),
        ("gr", 6), ("gr", 7), ("g2a", 3), ("g2b", 3), ("g2a", 4), ("g2b", 4),
    ],
    "H": [
        [
            ("gr", 8),
        ],
        [
            ("g2a", 5), ("g2b", 5), ("g1", 6),
        ],
        [
            ("g3", 3), ("g1", 7), ("g1", 8),
        ],
        [
            ("g3", 4), ("g4", 3), ("LO", None),
        ],
        [
            ("g3", 5), ("g4", 4), ("L", 0),
        ],
    ],
    "A3": [
        ("A3", None), ("g2a", 6), ("g2b", 6), ("g4", 5), ("L", 1),
    ],
    "F": [
        [
            ("g2a", 7), ("g2b", 7),
        ],
        [
            ("g2a", 8), ("g2b", 8),
        ],
        [
            ("L", 4), ("c2a", 1), ("c2b", 1),
        ],
        [
            ("c3", 1),
        ],
        [
            ("z2", 0),
        ],
    ],
    "R": [
        [
            ("z1", 0),
        ],
        [
            ("g3", 6), ("c1", 1), ("g3", 7), ("g4", 6), ("L", 2), ("g4", 7), ("L", 3), ("g3", 8), ("g4", 8),
        ],
        [
            ("c1", 2),
        ],
        [
            ("c2a", 2), ("c2b", 2), ("c1", 3),
        ],
        [
            ("c3", 2), ("c1", 4),
        ],
    ],
    "B1": [
        ("B1", None), ("c4", 1), ("c2a", 3), ("c2b", 3), ("B2", None), ("z3a", 0), ("z3b", 0), ("c1", 5),
    ],
    "K": [
        [
            ("c4", 2), ("c2a", 4), ("c2b", 4),
        ],
        [],
        [
            ("c5a", 1), ("c5b", 1),
        ],
        [
            ("z4", 0), ("c3", 3), ("c2b", 5), ("c2a", 5),
        ],
        [
            ("c5a", 2),
        ],
    ],
    "D1": [
        ("D1", None), ("c5b", 2), ("D3", None), ("c6", 1), ("c3", 4), ("c4", 3), ("D2", None), ("c5a", 0),
        ("c5b", 0), ("c1", 6), ("D4", None), ("c6", 2), ("c3", 5), ("c1", 7), ("c1", 8), ("c7", 1),
        ("c5a", 3), ("c7", 2), ("c5b", 3), ("c6", 0), ("c7", 0), ("c2b", 6), ("c2a", 6), ("c4", 4),
        ("c2b", 7), ("c2a", 7), ("c4", 5), ("c2b", 8), ("c2a", 8), ("c6", 3), ("c7", 3), ("c3", 6),
        ("c5a", 4), ("c5b", 4), ("c3", 7), ("c5a", 5), ("c5b", 5), ("c3", 8), ("c6", 4), ("c6", 5), ("c4", 6),
        ("c7", 4), ("c7", 5), ("c4", 7), ("c5a", 6), ("c5b", 6), ("c4", 8), ("c6", 6), ("c5a", 7), ("c5b", 7),
        ("c7", 6), ("c6", 7), ("c7", 7), ("c5a", 8), ("c5b", 8), ("c6", 8), ("c7", 8),
    ],
}

DIAGONAL = (6, 7, 8)

def on_device(tokens, sequence_ids, cotangent, norm_gains, qkv_weight, out_weight, gate_up_weight, down_weight, *moments):
    weights = (norm_gains, qkv_weight, out_weight, gate_up_weight, down_weight)
    block_out, tokens_grad, packed = layer(tokens, cotangent, sequence_ids, weights)
    return (block_out.T, tokens_grad.T, *adam(packed, weights, moments))


def solution(mesh):
    fits = mesh.shape["rep"] == 8 and mesh.shape["fsdp"] == 4
    return jax.shard_map(
        on_device if fits else on_device_any,
        mesh=mesh,
        in_specs=(
            P(("rep", "fsdp"), None),
            P(("rep", "fsdp")),
            P(("rep", "fsdp"), None),
            P(None, "fsdp"),
            P("fsdp", None),
            P("fsdp", None),
            P("fsdp", None),
            P("fsdp", None),
            P(None, "fsdp"),
            P("fsdp", None),
            P("fsdp", None),
            P("fsdp", None),
            P("fsdp", None),
            P(None, "fsdp"),
            P("fsdp", None),
            P("fsdp", None),
            P("fsdp", None),
            P("fsdp", None),
        ),
        out_specs=(
            P(("rep", "fsdp"), None),
            P(("rep", "fsdp"), None),
            P(None, "fsdp"),
            P("fsdp", None),
            P("fsdp", None),
            P("fsdp", None),
            P("fsdp", None),
            P(None, "fsdp"),
            P("fsdp", None),
            P("fsdp", None),
            P("fsdp", None),
            P("fsdp", None),
            P(None, "fsdp"),
            P("fsdp", None),
            P("fsdp", None),
            P("fsdp", None),
            P("fsdp", None),
            P(None, "fsdp"),
            P("fsdp", None),
            P("fsdp", None),
            P("fsdp", None),
            P("fsdp", None),
        ),
        check_vma=False,
    )
```
